32 devices in a mesh: obs: 16 (over z, x, core), sp: 2 (over y).
Axes of the slice: x: 2, y: 2, z: 4, core: 2. Of those that a mesh axis runs over, the one named last changes fastest.
Arguments:
- descriptors: bfloat16 [16384, 512], P('obs'), may hold values from -10 to 10
- candidates: bfloat16 [8192, 512], P('obs'), may hold values from -10 to 10
- sparse_index: int32 [4096], replicated, may hold values from 0 to 8191, as said below
- targets: bfloat16 [16384], P('obs'), may hold values from -12 to 12
- regularizer: float32 [4096], replicated, may hold values from 0.25 to 1
Outputs:
- inverse: float32 [4096, 4096], P('sp', 'obs')
- weights: float32 [4096], P('sp')
The draws below stay inside these ranges and needn't reach their ends.
Inputs may be any that keep to these rules, and one draw needn't show every extreme that they name: `sparse_index`: the 4096 indices are distinct.
All inputs are finite; a program needn't handle non-finite values.
Results may differ from the reference program's by a relative error of at most 0.012.
Values may be sent and summed in bfloat16 or wider, within the bound.
A program may use at most 128 MiB of HBM per device.

```python
import math
import jax
import jax.numpy as jnp
from jax import lax

D = 512
M = 4096
OBS_DEV = 1024
ROWS = 16384
CAND = 8192
N_OBS = 16


def draw_descriptors(key, part):
    own_key = jax.random.fold_in(key, 31)
    values = jnp.clip(jax.random.normal(own_key, (ROWS, D), jnp.float32), -6.0, 6.0)
    return values.astype(jnp.bfloat16)


def draw_candidates(key, part):
    own_key = jax.random.fold_in(key, 72)
    values = jnp.clip(jax.random.normal(own_key, (CAND, D), jnp.float32), -6.0, 6.0)
    return values.astype(jnp.bfloat16)


def draw_sparse_index(key, part):
    own_key = jax.random.fold_in(key, 17)
    return jax.random.permutation(own_key, CAND)[:M].astype(jnp.int32)


def draw_targets(key, part):
    own_key = jax.random.fold_in(key, 53)
    ramp_up = 1.0 + 2.0 * jnp.arange(ROWS, dtype=jnp.float32) / ROWS
    values = jnp.clip(jax.random.normal(own_key, (ROWS,), jnp.float32), -4.0, 4.0)
    return (values * ramp_up).astype(jnp.bfloat16)


def setup_inputs(seed: int = 0) -> dict:
    arg_keys = jax.random.split(jax.random.key(seed), 6)
    descriptors = draw_descriptors(jax.random.fold_in(arg_keys[5], 71), 0)
    candidates = draw_candidates(jax.random.fold_in(arg_keys[5], 71), 0)
    sparse_index = draw_sparse_index(jax.random.fold_in(arg_keys[5], 71), 0)
    targets = draw_targets(jax.random.fold_in(arg_keys[5], 71), 0)
    regularizer = jnp.clip(jnp.exp(jax.random.uniform(arg_keys[4], (M,), jnp.float32, math.log(0.25), math.log(1.0))), 0.25, 1.0)
    return {"descriptors": descriptors, "candidates": candidates, "sparse_index": sparse_index, "targets": targets, "regularizer": regularizer}


epsilon = 1e-06

def unit_rows(row_block):
    values = row_block.astype(jnp.float32)
    return (values * lax.rsqrt(lax.optimization_barrier(jnp.sum(values * values, axis=1, keepdims=True)) + epsilon)).astype(jnp.bfloat16)

def kernel_block(normed, sparse):
    inner = lax.dot_general(normed, sparse, (((1,), (1,)), ((), ())), preferred_element_type=jnp.float32)
    scaled = inner * math.sqrt(normed.shape[1])
    squared = scaled * scaled
    return (squared * squared - 6.0 * squared + 3.0).astype(jnp.bfloat16)

def reference(descriptors, candidates, sparse_index, targets, regularizer):
    normed = unit_rows(descriptors)
    sparse = unit_rows(candidates)[sparse_index]

    def accumulate(running, begin_at):
        gram_sum, weighted = running
        row_block = lax.dynamic_slice_in_dim(normed, begin_at, OBS_DEV)
        values = lax.dynamic_slice_in_dim(targets, begin_at, OBS_DEV)
        block_kernel = kernel_block(row_block, sparse)
        gram_sum = gram_sum + lax.dot_general(block_kernel, block_kernel, (((0,), (0,)), ((), ())), preferred_element_type=jnp.float32)
        weighted = weighted + jnp.dot(values, block_kernel, preferred_element_type=jnp.float32)
        return ((gram_sum, weighted), None)
    starts = (jnp.arange(N_OBS) * OBS_DEV).astype(jnp.int32)
    initial = (jnp.zeros((M, M), jnp.float32), jnp.zeros((M,), jnp.float32))
    (gram_sum, weighted), _ = lax.scan(accumulate, initial, starts)
    normalizer = 24.0 * ROWS
    projected = weighted / math.sqrt(normalizer)
    system = gram_sum / normalizer + jnp.diag(regularizer)
    recip = 1.0 / jnp.diagonal(system)
    first = jnp.diag(2.0 * recip) - system * recip[:, None] * recip[None, :]
    highest = lax.Precision.HIGHEST
    product = jnp.dot(system, first, precision=highest)
    inverse = 2.0 * first - jnp.dot(first, product, precision=highest)
    weights = jnp.dot(inverse, projected, precision=highest)
    return (inverse, weights)
```

```python
import functools
import math

import jax
import jax.numpy as jnp
from jax import lax
from jax.experimental import pallas as pl
from jax.experimental.pallas import tpu as pltpu
from jax.sharding import PartitionSpec as P

epsilon = 1e-06
LANES = 128
VMEM_BYTES = 58 * 2**20


def unit_rows(row_block):
    values = row_block.astype(jnp.float32)
    return (values * lax.rsqrt(jnp.sum(values * values, axis=1, keepdims=True) + epsilon)).astype(
        jnp.bfloat16
    )


def gram_body(blocks, tile, share, ext, root, s_ref, norm_ref, sp_ref, tgt_ref, gram_ref, ws_ref, kext):
    step = pl.program_id(0)
    width = blocks * tile

    @pl.when(step < blocks)
    def _():
        inner = lax.dot_general(
            norm_ref[...], sp_ref[...], (((1,), (1,)), ((), ())), preferred_element_type=jnp.float32
        )
        scaled = inner * root
        squared = scaled * scaled
        kb = ((squared - 6.0) * squared + 3.0).astype(jnp.bfloat16)
        kext[:, pl.ds(pl.multiple_of(step * tile, tile), tile)] = kb

        @pl.when(step < ext)
        def _():
            kext[:, pl.ds(pl.multiple_of(width + step * tile, tile), tile)] = kb

        kf = kb.astype(jnp.float32)
        weighted = jnp.dot(tgt_ref[...], kb, preferred_element_type=jnp.float32)
        ws_ref[0:1, :] = weighted[0:1, :]
        ws_ref[1:2, :] = jnp.sum(kf * kf, axis=0, keepdims=True)

    @pl.when(step >= blocks)
    def _():
        j = step - blocks
        cols = pl.ds(pl.multiple_of(j * tile, tile), tile)
        window = pl.ds(pl.multiple_of(j * tile + s_ref[0] * share, LANES), share)
        gram_ref[...] = lax.dot_general(
            kext[:, cols], kext[:, window], (((0,), (0,)), ((), ())), preferred_element_type=jnp.float32
        ).astype(jnp.bfloat16)


def gram_call(s_pos, normed, sparse, targets, blocks, tile, share, sp_count):
    rows, depth = normed.shape
    width = blocks * tile
    ext = -(-((blocks - 1) * tile + sp_count * share - width) // tile)
    last = blocks - 1
    return pl.pallas_call(
        functools.partial(gram_body, blocks, tile, share, ext, math.sqrt(depth)),
        grid_spec=pltpu.PrefetchScalarGridSpec(
            num_scalar_prefetch=1,
            grid=(2 * blocks,),
            in_specs=[
                pl.BlockSpec((rows, depth), lambda g, s: (0, 0)),
                pl.BlockSpec((tile, depth), lambda g, s: (jnp.minimum(g, last), 0)),
                pl.BlockSpec((16, rows), lambda g, s: (0, 0)),
            ],
            out_specs=[
                pl.BlockSpec((tile, share), lambda g, s: (jnp.maximum(g - blocks, 0), 0)),
                pl.BlockSpec((2, tile), lambda g, s: (0, jnp.minimum(g, last))),
            ],
            scratch_shapes=[pltpu.VMEM((rows, width + ext * tile), jnp.bfloat16)],
        ),
        out_shape=[
            jax.ShapeDtypeStruct((width, share), jnp.bfloat16),
            jax.ShapeDtypeStruct((2, width), jnp.float32),
        ],
        compiler_params=pltpu.CompilerParams(vmem_limit_bytes=VMEM_BYTES),
    )(s_pos, normed, sparse, jnp.broadcast_to(targets[None, :], (16, rows)))


def newton_body(
    blocks, tile, share, sp_count, chunk, block_rows,
    pos_ref, packed_ref, rcol_ref, rrow_ref, y_ref, inv_ref, w_ref, dense, prod,
):
    step = pl.program_id(0)
    width = blocks * tile
    half = blocks // 2
    p_steps = width // chunk
    my_cols = pl.ds(pl.multiple_of(pos_ref[1] * tile, tile), tile)

    @pl.when(step < blocks)
    def _():
        rows = pl.ds(pl.multiple_of(step * tile, tile), tile)
        for s in range(sp_count):
            for q in range(share // LANES):
                offset = s * share + q * LANES
                if offset >= (half + 1) * tile:
                    continue
                col = lax.rem(step * tile + offset, width)
                cols = pl.ds(pl.multiple_of(col, LANES), LANES)
                block = packed_ref[s * tile : (s + 1) * tile, q * LANES : (q + 1) * LANES]
                dense[rows, cols] = block
                if tile <= offset < half * tile:
                    dense[cols, rows] = block.T

    @pl.when((step >= blocks) & (step < blocks + p_steps))
    def _():
        rows = pl.ds(pl.multiple_of((step - blocks) * chunk, chunk), chunk)
        prod[rows, :] = jnp.dot(
            dense[rows, :], dense[:, my_cols], preferred_element_type=jnp.float32
        ).astype(jnp.bfloat16)

    @pl.when(step >= blocks + p_steps)
    def _():
        local = pl.multiple_of((step - blocks - p_steps) * chunk, chunk)
        start = pl.multiple_of(pos_ref[0] * block_rows + local, chunk)
        rows = pl.ds(start, chunk)
        cubic = jnp.dot(dense[rows, :], prod[...], preferred_element_type=jnp.float32)
        on_diag = (start + lax.broadcasted_iota(jnp.int32, (chunk, tile), 0)) == (
            pos_ref[1] * tile + lax.broadcasted_iota(jnp.int32, (chunk, tile), 1)
        )
        series = (
            jnp.where(on_diag, 1.0, 0.0)
            - dense[rows, my_cols].astype(jnp.float32)
            + prod[rows, :].astype(jnp.float32)
            - cubic
        )
        out = series * rcol_ref[rows, :] * rrow_ref[...]
        inv_ref[pl.ds(local, chunk), :] = out
        w_ref[:, pl.ds(local, chunk)] = lax.dot_general(
            y_ref[...], out, (((1,), (1,)), ((), ())),
            precision=lax.Precision.HIGHEST, preferred_element_type=jnp.float32,
        )


def newton_call(pos, packed, root_recip, rrow, y, blocks, tile, share, sp_count):
    width = blocks * tile
    block_rows = width // sp_count
    chunk = min(512, block_rows)
    grid = blocks + width // chunk + block_rows // chunk
    last = blocks - 1
    return pl.pallas_call(
        functools.partial(newton_body, blocks, tile, share, sp_count, chunk, block_rows),
        grid_spec=pltpu.PrefetchScalarGridSpec(
            num_scalar_prefetch=1,
            grid=(grid,),
            in_specs=[
                pl.BlockSpec((sp_count * tile, share), lambda g, p: (jnp.minimum(g, last), 0)),
                pl.BlockSpec((width, 1), lambda g, p: (0, 0)),
                pl.BlockSpec((1, tile), lambda g, p: (0, 0)),
                pl.BlockSpec((8, tile), lambda g, p: (0, 0)),
            ],
            out_specs=[
                pl.BlockSpec((block_rows, tile), lambda g, p: (0, 0)),
                pl.BlockSpec((8, block_rows), lambda g, p: (0, 0)),
            ],
            scratch_shapes=[
                pltpu.VMEM((width, width), jnp.bfloat16),
                pltpu.VMEM((width, tile), jnp.bfloat16),
            ],
        ),
        out_shape=[
            jax.ShapeDtypeStruct((block_rows, tile), jnp.float32),
            jax.ShapeDtypeStruct((8, block_rows), jnp.float32),
        ],
        compiler_params=pltpu.CompilerParams(vmem_limit_bytes=VMEM_BYTES),
    )(pos, packed, root_recip[:, None], rrow[None, :], jnp.broadcast_to(y[None, :], (8, tile)))


def add_body(count, in_ref, out_ref, slots, send_sem, recv_sem):
    me = lax.axis_index("obs")
    barrier = pltpu.get_barrier_semaphore()
    for k in range(1, count):
        pl.semaphore_signal(
            barrier, inc=1, device_id={"obs": lax.rem(me + k, count)}, device_id_type=pl.DeviceIdType.MESH
        )
    pl.semaphore_wait(barrier, count - 1)
    copies = []
    for k in range(1, count):
        copy = pltpu.make_async_remote_copy(
            src_ref=in_ref,
            dst_ref=slots.at[me],
            send_sem=send_sem.at[k],
            recv_sem=recv_sem.at[k],
            device_id={"obs": lax.rem(me + k, count)},
            device_id_type=pl.DeviceIdType.MESH,
        )
        copy.start()
        copies.append(copy)
    slots[me] = in_ref[...]
    for copy in copies:
        copy.wait()
    total = slots[0]
    for k in range(1, count):
        total = total + slots[k]
    out_ref[...] = total


def add_over_obs(values, count, collective_id):
    shape = values.shape
    flat = values.reshape(values.size // LANES, LANES)
    total = pl.pallas_call(
        functools.partial(add_body, count),
        out_shape=jax.ShapeDtypeStruct(flat.shape, flat.dtype),
        in_specs=[pl.BlockSpec(memory_space=pltpu.VMEM)],
        out_specs=pl.BlockSpec(memory_space=pltpu.VMEM),
        scratch_shapes=[
            pltpu.VMEM((count,) + flat.shape, flat.dtype),
            pltpu.SemaphoreType.DMA((count,)),
            pltpu.SemaphoreType.DMA((count,)),
        ],
        cost_estimate=pl.CostEstimate(
            flops=count * flat.size, bytes_accessed=400 * flat.size, transcendentals=0
        ),
        compiler_params=pltpu.CompilerParams(collective_id=collective_id, has_side_effects=True),
    )(flat)
    return total.reshape(shape)


def spread_keys(z_count, sp_count):
    keys = [("z", k) for k in range(1, z_count)]
    for k in range(z_count):
        keys += [("x", k), ("core", k), ("core_x", k)]
        for d in range(1, sp_count):
            keys += [(name, k, d) for name in ("sp", "sp_a", "x_b", "core_sp", "core_a", "core_b")]
    return {key: place for place, key in enumerate(keys)}


def spread_body(z_count, sp_count, with_slab, *refs):
    if with_slab:
        in_ref, own_slab, out_ref, slab_ref = refs[:4]
    else:
        in_ref, out_ref = refs[:2]
    send_sem, recv_sem, own_sem = refs[-3:]
    places = spread_keys(z_count, sp_count)
    obs = lax.axis_index("obs")
    s = lax.axis_index("sp")
    z, x, c = lax.div(obs, 4), lax.rem(lax.div(obs, 2), 2), lax.rem(obs, 2)
    half = in_ref.shape[0] // 2
    upper, lower = pl.ds(0, half), pl.ds(half, half)
    zs = [lax.bitwise_xor(z, k) for k in range(z_count)]
    to_sp = [lax.rem(s + d, sp_count) for d in range(sp_count)]
    from_sp = [lax.rem(s - d + sp_count, sp_count) for d in range(sp_count)]

    def device(z_to, x_to, c_to, s_to):
        return {"obs": z_to * 4 + x_to * 2 + c_to, "sp": s_to}

    def slot(z_of, x_of, s_of):
        return ((z_of * 2 + x_of) * 2 + c) * sp_count + s_of

    own_slot = slot(z, x, s)
    across, sibling = device(z, 1 - x, c, s), device(z, x, 1 - c, s)
    others = [device(zs[k], x, c, s) for k in range(1, z_count)]
    others += [device(z, x, c, to_sp[d]) for d in range(1, sp_count)]
    others += [across, sibling]
    barrier = pltpu.get_barrier_semaphore()
    for other in others:
        pl.semaphore_signal(barrier, inc=1, device_id=other, device_id_type=pl.DeviceIdType.MESH)
    pl.semaphore_wait(barrier, len(others))

    sent = {}

    def send(key, place, target, rows=None, own=False):
        src = in_ref if own else out_ref.at[place]
        dst = out_ref.at[place]
        if rows is not None:
            src, dst = src.at[rows], dst.at[rows]
        copy = pltpu.make_async_remote_copy(
            src_ref=src,
            dst_ref=dst,
            send_sem=send_sem.at[places[key]],
            recv_sem=recv_sem.at[places[key]],
            device_id=target,
            device_id_type=pl.DeviceIdType.MESH,
        )
        copy.start()
        sent[key] = copy

    keep = pltpu.make_async_copy(in_ref, out_ref.at[own_slot], own_sem.at[0])
    keep.start()
    for k in range(1, z_count):
        send(("z", k), own_slot, others[k - 1], own=True)

    shared = []
    if with_slab:
        q, q_across = x * 2 + c, (1 - x) * 2 + c
        near = pl.multiple_of(s * (own_slab.shape[0] // 2), 16)
        far = pl.multiple_of((1 - s) * (own_slab.shape[0] // 2), 16)
        near, far = pl.ds(near, own_slab.shape[0] // 2), pl.ds(far, own_slab.shape[0] // 2)
        keep_slab = pltpu.make_async_copy(own_slab, slab_ref.at[q], own_sem.at[1])
        keep_slab.start()

        def share(src, place, piece, target):
            at = len(places) + len(shared)
            dst = slab_ref.at[place]
            if piece is not None:
                src, dst = src.at[piece], dst.at[piece]
            copy = pltpu.make_async_remote_copy(
                src_ref=src, dst_ref=dst, send_sem=send_sem.at[at], recv_sem=recv_sem.at[at],
                device_id=target, device_id_type=pl.DeviceIdType.MESH,
            )
            copy.start()
            shared.append(copy)

        share(own_slab, q, near, across)
        share(own_slab, q, None, sibling)

    def fan_out(k):
        place = slot(zs[k], x, s)
        send(("x", k), place, across, own=k == 0)
        for d in range(1, sp_count):
            send(("sp", k, d), place, device(z, x, c, to_sp[d]), own=k == 0)
        send(("core", k), place, sibling, own=k == 0)

    def relay(k):
        sent[("x", k)].wait_recv()
        place = slot(zs[k], 1 - x, s)
        for d in range(1, sp_count):
            send(("sp_a", k, d), place, device(z, x, c, to_sp[d]), upper)
        send(("core_x", k), place, sibling)
        for d in range(1, sp_count):
            sent[("sp", k, d)].wait_recv()
            place = slot(zs[k], x, from_sp[d])
            send(("x_b", k, d), place, across, lower)
            send(("core_sp", k, d), place, sibling)

    def finish(k):
        for d in range(1, sp_count):
            place = slot(zs[k], 1 - x, from_sp[d])
            sent[("sp_a", k, d)].wait_recv()
            send(("core_a", k, d), place, sibling, upper)
            sent[("x_b", k, d)].wait_recv()
            send(("core_b", k, d), place, sibling, lower)

    fan_out(0)
    for k in range(1, z_count):
        sent[("z", k)].wait_recv()
        fan_out(k)
        relay(k - 1)
        if k > 1:
            finish(k - 2)
    relay(z_count - 1)
    if with_slab:
        shared[0].wait_recv()
        share(slab_ref.at[q_across], q_across, near, device(z, x, c, 1 - s))
        share(slab_ref.at[q_across], q_across, near, sibling)
        shared[2].wait_recv()
        share(slab_ref.at[q_across], q_across, far, sibling)
    if z_count > 1:
        finish(z_count - 2)
    finish(z_count - 1)
    keep.wait()
    if with_slab:
        keep_slab.wait()
        for at in (1, 3, 4):
            shared[at].wait_recv()
        for copy in shared:
            copy.wait_send()
    for key, copy in sent.items():
        copy.wait_send()
        if key[0].startswith("core"):
            copy.wait_recv()


def spread(shard, obs_count, sp_count, collective_id, own_slab=None):
    rows, cols = shard.shape
    z_count = obs_count // 4
    total = obs_count * sp_count
    sems = len(spread_keys(z_count, sp_count))
    operands = [shard]
    out_shape = [jax.ShapeDtypeStruct((total, rows, cols), shard.dtype)]
    if own_slab is not None:
        sems += 5
        operands.append(own_slab)
        out_shape.append(jax.ShapeDtypeStruct((4,) + own_slab.shape, own_slab.dtype))
    anywhere = pl.BlockSpec(memory_space=pl.ANY)
    gathered = pl.pallas_call(
        functools.partial(spread_body, z_count, sp_count, own_slab is not None),
        out_shape=out_shape,
        in_specs=[anywhere] * len(operands),
        out_specs=[anywhere] * len(operands),
        scratch_shapes=[
            pltpu.SemaphoreType.DMA((sems,)),
            pltpu.SemaphoreType.DMA((sems,)),
            pltpu.SemaphoreType.DMA((2,)),
        ],
        compiler_params=pltpu.CompilerParams(collective_id=collective_id, has_side_effects=True),
    )(*operands)
    table = gathered[0].reshape(total * rows, cols)
    return table if own_slab is None else (table, gathered[1])


def slab_body(z_count, sp_count, strip, span, tile, chunk, root, *refs):
    norm_ref, sp_ref, tgt_ref, part_ref, sums_ref = refs[:5]
    kbuf, ktr, parts, from_low, from_high, zsums, gsums = refs[5:12]
    up_send, up_recv, down_send, down_recv, zs_send, zs_recv, gs_send, gs_recv = refs[12:]
    obs = lax.axis_index("obs")
    s = lax.axis_index("sp")
    z, q = lax.div(obs, 4), lax.rem(obs, 4)
    group = 4 * sp_count
    p = q * sp_count + s
    last = z_count - 1
    shard = tgt_ref.shape[1] // 4
    per = tile // strip
    own_blocks = z_count // per
    mine = strip * z_count
    lines = mine // LANES

    z_others = [{"obs": lax.rem(z + k, z_count) * 4 + q, "sp": s} for k in range(1, z_count)]
    group_others = []
    for k in range(1, group):
        to = lax.rem(p + k, group)
        group_others.append({"obs": z * 4 + lax.div(to, sp_count), "sp": lax.rem(to, sp_count)})
    barrier = pltpu.get_barrier_semaphore()
    for other in z_others + group_others:
        pl.semaphore_signal(barrier, inc=1, device_id=other, device_id_type=pl.DeviceIdType.MESH)
    pl.semaphore_wait(barrier, len(z_others) + len(group_others))

    def remote(src, dst, send_sem, recv_sem, target):
        return pltpu.make_async_remote_copy(
            src_ref=src, dst_ref=dst, send_sem=send_sem, recv_sem=recv_sem,
            device_id=target, device_id_type=pl.DeviceIdType.MESH,
        )

    def kernel_tile(t, own):
        cols = pl.ds(pl.multiple_of(t * tile, tile), tile)
        for k in range(4):
            rows = pl.ds(k * shard, shard)
            inner = lax.dot_general(
                norm_ref[k, :shard, :], sp_ref[cols, :], (((1,), (1,)), ((), ())),
                preferred_element_type=jnp.float32,
            )
            scaled = inner * root
            squared = scaled * scaled
            kb = ((squared - 6.0) * squared + 3.0).astype(jnp.bfloat16)
            kbuf[rows, cols] = kb
            if own:
                ktr[cols, rows] = kb.T

    for t in range(own_blocks):
        kernel_tile(t, True)
        cols = slice(t * tile, (t + 1) * tile)
        weighted = jnp.dot(tgt_ref[...], kbuf[:, cols], preferred_element_type=jnp.float32)
        square = jnp.zeros((1, tile), jnp.float32)
        for k in range(4):
            kf = kbuf[k * shard : (k + 1) * shard, cols].astype(jnp.float32)
            square = square + jnp.sum(kf * kf, axis=0, keepdims=True)
        for h in range(tile // LANES):
            line = t * (tile // LANES) + h
            zsums[z, line : line + 1, :] = weighted[0:1, h * LANES : (h + 1) * LANES]
            zsums[z, lines + line : lines + line + 1, :] = square[:, h * LANES : (h + 1) * LANES]
    z_copies = []
    for k in range(1, z_count):
        copy = remote(zsums.at[z], zsums.at[z], zs_send.at[k], zs_recv.at[k], z_others[k - 1])
        copy.start()
        z_copies.append(copy)

    @pl.loop(own_blocks, kbuf.shape[1] // tile)
    def _(t):
        kernel_tile(t, False)

    def block(b):
        start = pl.multiple_of(b * tile, tile)
        for j in range(0, span + tile - strip, chunk):
            cols = pl.ds(pl.multiple_of(start + j, LANES), chunk)
            g = jnp.dot(
                ktr[pl.ds(start, tile), :], kbuf[:, cols], preferred_element_type=jnp.float32
            ).astype(jnp.bfloat16)
            for h in range(per):
                lo, hi = max(j, h * strip), min(j + chunk, h * strip + span)
                parts[b * per + h, :, lo - h * strip : hi - h * strip] = g[
                    h * strip : (h + 1) * strip, lo - j : hi - j
                ]

    def up(t):
        return remote(
            parts.at[t], from_low.at[t], up_send.at[t], up_recv.at[t],
            {"obs": lax.rem(z + 1, z_count) * 4 + q, "sp": s},
        )

    def down(t):
        return remote(
            parts.at[t], from_high.at[t], down_send.at[t], down_recv.at[t],
            {"obs": lax.rem(z + last, z_count) * 4 + q, "sp": s},
        )

    for k in range(own_blocks):
        block(jnp.where(z < z_count // 2, own_blocks - 1 - k, k))
        for h in range(per):
            high, low = last - (k * per + h), k * per + h
            if high > 0:
                pl.when(z == 0)(lambda t=high: up(t).start())
            if low < last:
                pl.when(z == last)(lambda t=low: down(t).start())
        if k == 0:
            for copy in z_copies:
                copy.wait_recv()
            total = zsums[0]
            for m in range(1, z_count):
                total = total + zsums[m]
            gsums[p] = total
            g_copies = []
            for m in range(1, group):
                copy = remote(gsums.at[p], gsums.at[p], gs_send.at[m], gs_recv.at[m], group_others[m - 1])
                copy.start()
                g_copies.append(copy)

    for k in range(last):
        high, low = last - k, k

        @pl.when((z > 0) & (z < high))
        def _(t=high):
            up(t).wait_recv()
            parts[t] = parts[t] + from_low[t]
            up(t).start()

        @pl.when((z < last) & (z > low))
        def _(t=low):
            down(t).wait_recv()
            parts[t] = parts[t] + from_high[t]
            down(t).start()

    def finish(below, above):
        total = parts[z].astype(jnp.float32)
        if below:
            up(z).wait_recv()
            total = total + from_low[z].astype(jnp.float32)
        if above:
            down(z).wait_recv()
            total = total + from_high[z].astype(jnp.float32)
        row = lax.broadcasted_iota(jnp.int32, total.shape, 0)
        col = lax.broadcasted_iota(jnp.int32, total.shape, 1)
        part_ref[...] = jnp.where(row == col, 0.0, total).astype(jnp.bfloat16)

    pl.when(z == 0)(lambda: finish(False, True))
    pl.when((z > 0) & (z < last))(lambda: finish(True, True))
    pl.when(z == last)(lambda: finish(True, False))

    for copy in g_copies:
        copy.wait()
    for copy in z_copies:
        copy.wait_send()
    sums_ref[...] = gsums[...]
    for t in range(z_count):
        pl.when(z < t)(lambda t=t: up(t).wait_send())
        pl.when(z > t)(lambda t=t: down(t).wait_send())


def slab_gram(slab, sparse, targets, z_count, sp_count, strip, span, tile, rows, collective_id):
    depth = slab.shape[2]
    window = sparse.shape[0]
    group = 4 * sp_count
    mine = strip * z_count
    lines = 2 * mine // LANES
    wide = span + tile - strip
    chunk = max(c for c in range(LANES, 1025, LANES) if wide % c == 0)
    vmem = pl.BlockSpec(memory_space=pltpu.VMEM)
    part = (z_count, strip, span)
    sems = [pltpu.SemaphoreType.DMA((z_count,))] * 6 + [pltpu.SemaphoreType.DMA((group,))] * 2
    return pl.pallas_call(
        functools.partial(slab_body, z_count, sp_count, strip, span, tile, chunk, math.sqrt(depth)),
        out_shape=[
            jax.ShapeDtypeStruct((strip, span), jnp.bfloat16),
            jax.ShapeDtypeStruct((group, lines, LANES), jnp.float32),
        ],
        in_specs=[vmem, vmem, vmem],
        out_specs=[vmem, vmem],
        scratch_shapes=[
            pltpu.VMEM((4 * rows, window), jnp.bfloat16),
            pltpu.VMEM((mine, 4 * rows), jnp.bfloat16),
            pltpu.VMEM(part, jnp.bfloat16),
            pltpu.VMEM(part, jnp.bfloat16),
            pltpu.VMEM(part, jnp.bfloat16),
            pltpu.VMEM((z_count, lines, LANES), jnp.float32),
            pltpu.VMEM((group, lines, LANES), jnp.float32),
        ] + sems,
        compiler_params=pltpu.CompilerParams(
            collective_id=collective_id, has_side_effects=True, vmem_limit_bytes=VMEM_BYTES
        ),
    )(slab, sparse, jnp.broadcast_to(targets[None, :], (16, 4 * rows)))


def strips_body(
    strips, strip, span, tile, chunk, block_rows, normalizer,
    pos_ref, even_ref, odd_ref, rcol_ref, rrow_ref, y_ref, inv_ref, w_ref, dense, first, second,
):
    step = pl.program_id(0)
    width = strips * strip
    half = strips // 2
    pairs = strips // 2
    p_steps = width // chunk
    my_cols = pl.ds(pl.multiple_of(pos_ref[1] * tile, tile), tile)
    fold = 1.0 / normalizer

    @pl.when(step < pairs)
    def _():
        for h, ref in enumerate((even_ref, odd_ref)):
            place = step * 2 + h
            rows = pl.ds(pl.multiple_of(place * strip, strip), strip)
            for k in range(span // strip):
                col = lax.rem(place + k, strips) * strip
                cols = pl.ds(pl.multiple_of(col, strip), strip)
                block = ref[:, k * strip : (k + 1) * strip]
                dense[rows, cols] = block
                if 0 < k < half:
                    dense[cols, rows] = block.T

    @pl.when(step == pairs)
    def _():
        for begin in range(0, width, chunk):
            rows = pl.ds(begin, chunk)
            first[rows, :] = (
                dense[rows, my_cols].astype(jnp.float32) * (rcol_ref[rows, :] * fold)
            ).astype(jnp.bfloat16)

    @pl.when((step >= pairs) & (step < pairs + p_steps))
    def _():
        rows = pl.ds(pl.multiple_of((step - pairs) * chunk, chunk), chunk)
        prod = jnp.dot(dense[rows, :], first[...], preferred_element_type=jnp.float32)
        second[rows, :] = (prod * (rcol_ref[rows, :] * fold)).astype(jnp.bfloat16)

    @pl.when(step >= pairs + p_steps)
    def _():
        local = pl.multiple_of((step - pairs - p_steps) * chunk, chunk)
        start = pl.multiple_of(pos_ref[0] * block_rows + local, chunk)
        rows = pl.ds(start, chunk)
        cubic = jnp.dot(dense[rows, :], second[...], preferred_element_type=jnp.float32)
        on_diag = (start + lax.broadcasted_iota(jnp.int32, (chunk, tile), 0)) == (
            pos_ref[1] * tile + lax.broadcasted_iota(jnp.int32, (chunk, tile), 1)
        )
        series = second[rows, :].astype(jnp.float32) - (
            dense[rows, my_cols].astype(jnp.float32) + cubic
        ) * (rcol_ref[rows, :] * fold)
        out = (jnp.where(on_diag, 1.0, 0.0) + series) * rrow_ref[...]
        inv_ref[pl.ds(local, chunk), :] = out
        w_ref[:, pl.ds(local, chunk)] = lax.dot_general(
            y_ref[...], out, (((1,), (1,)), ((), ())),
            precision=lax.Precision.HIGHEST, preferred_element_type=jnp.float32,
        )


def strips_newton(pos, packed, recip, rrow, y, z_count, sp_count, strip, tile, normalizer):
    strips = packed.shape[0] // strip
    span = packed.shape[1]
    width = strips * strip
    group = 4 * sp_count
    block_rows = width // sp_count
    chunk = min(512, block_rows)
    grid = strips // 2 + width // chunk + block_rows // chunk
    last = strips // 2 - 1

    def slot(h):
        def index(g, p):
            place = jnp.minimum(g, last) * 2 + h
            return (lax.rem(place, z_count) * group + lax.div(place, z_count), 0)

        return index

    return pl.pallas_call(
        functools.partial(strips_body, strips, strip, span, tile, chunk, block_rows, normalizer),
        grid_spec=pltpu.PrefetchScalarGridSpec(
            num_scalar_prefetch=1,
            grid=(grid,),
            in_specs=[
                pl.BlockSpec((strip, span), slot(0)),
                pl.BlockSpec((strip, span), slot(1)),
                pl.BlockSpec((width, 1), lambda g, p: (0, 0)),
                pl.BlockSpec((1, tile), lambda g, p: (0, 0)),
                pl.BlockSpec((8, tile), lambda g, p: (0, 0)),
            ],
            out_specs=[
                pl.BlockSpec((block_rows, tile), lambda g, p: (0, 0)),
                pl.BlockSpec((8, block_rows), lambda g, p: (0, 0)),
            ],
            scratch_shapes=[
                pltpu.VMEM((width, width), jnp.bfloat16),
                pltpu.VMEM((width, tile), jnp.bfloat16),
                pltpu.VMEM((width, tile), jnp.bfloat16),
            ],
        ),
        out_shape=[
            jax.ShapeDtypeStruct((block_rows, tile), jnp.float32),
            jax.ShapeDtypeStruct((8, block_rows), jnp.float32),
        ],
        compiler_params=pltpu.CompilerParams(vmem_limit_bytes=VMEM_BYTES),
    )(pos, packed, packed, recip[:, None], rrow[None, :], jnp.broadcast_to(y[None, :], (8, tile)))


def by_strips(descriptors, candidates, sparse_index, targets, regularizer):
    obs_count = lax.axis_size("obs")
    sp_count = lax.axis_size("sp")
    obs_pos = lax.axis_index("obs")
    sp_pos = lax.axis_index("sp")
    z_count = obs_count // 4
    group = 4 * sp_count
    width = sparse_index.shape[0]
    tile = width // obs_count
    strip = width // (obs_count * sp_count)
    mine = strip * z_count
    span = width // 2 + strip
    window = mine - strip + span
    window = -(-window // tile) * tile
    rows, depth = descriptors.shape
    normalizer = 24.0 * rows * obs_count

    extra = jnp.pad(targets.reshape(rows // depth, depth), ((0, 32 - rows // depth), (0, 0)))
    shard = jnp.concatenate([unit_rows(descriptors), extra])
    piece = candidates.shape[0] // sp_count
    own = lax.dynamic_slice_in_dim(candidates, sp_pos * piece, piece)
    table, slab = spread(unit_rows(own), obs_count, sp_count, 2, shard)
    place = lax.rem(obs_pos, 4) * sp_count + sp_pos
    wanted = lax.dynamic_slice_in_dim(
        jnp.concatenate([sparse_index, sparse_index]), place * mine, window
    )
    sparse = table.at[wanted].get(mode="promise_in_bounds")
    slab_targets = slab[:, rows : rows + rows // depth].reshape(4 * rows)
    part, sums = slab_gram(
        slab, sparse, slab_targets, z_count, sp_count, strip, span, tile, rows, 0
    )
    packed = spread(part, obs_count, sp_count, 3)

    lines = mine // LANES
    projected = sums[:, :lines].reshape(width) / math.sqrt(normalizer)
    recip = 1.0 / (sums[:, lines:].reshape(width) / normalizer + regularizer)
    col_start = obs_pos * tile
    rrow = lax.dynamic_slice_in_dim(recip, col_start, tile)
    y = lax.dynamic_slice_in_dim(projected, col_start, tile)
    pos = jnp.stack([sp_pos, obs_pos]).astype(jnp.int32)
    inverse_tile, part_w = strips_newton(
        pos, packed, recip, rrow, y, z_count, sp_count, strip, tile, normalizer
    )
    return inverse_tile, add_over_obs(part_w[0], obs_count, 1)


def on_device(descriptors, candidates, sparse_index, targets, regularizer):
    obs_count = lax.axis_size("obs")
    sp_count = lax.axis_size("sp")
    obs_pos = lax.axis_index("obs")
    sp_pos = lax.axis_index("sp")
    width = sparse_index.shape[0]
    if sp_count == 2 and width % (obs_count * sp_count * LANES) == 0:
        return by_strips(descriptors, candidates, sparse_index, targets, regularizer)
    tile = width // obs_count
    share = -(-((obs_count // 2 + 1) * tile) // (sp_count * LANES)) * LANES
    normalizer = 24.0 * descriptors.shape[0] * obs_count

    normed = unit_rows(descriptors)
    piece = candidates.shape[0] // sp_count
    own = lax.dynamic_slice_in_dim(candidates, sp_pos * piece, piece)
    table = spread(unit_rows(own), obs_count, sp_count, 2)
    sparse = table.at[sparse_index].get(mode="promise_in_bounds")

    gram, sums = gram_call(
        sp_pos[None].astype(jnp.int32), normed, sparse, targets, obs_count, tile, share, sp_count
    )
    sums = add_over_obs(sums, obs_count, 0)
    part = lax.psum_scatter(gram, "obs", scatter_dimension=0, tiled=True)

    projected = sums[0] / math.sqrt(normalizer)
    root = lax.rsqrt(sums[1] / normalizer + regularizer)
    col_start = obs_pos * tile
    rrow = lax.dynamic_slice_in_dim(root, col_start, tile)
    window_start = col_start + sp_pos * share
    rwin = lax.dynamic_slice_in_dim(jnp.concatenate([root, root]), window_start, share)
    offset = sp_pos * share + lax.iota(jnp.int32, share)
    on_diag = lax.iota(jnp.int32, tile)[:, None] == offset[None, :]
    scaled = jnp.where(
        on_diag, 0.0, part.astype(jnp.float32) * (rrow[:, None] / normalizer) * rwin[None, :]
    ).astype(jnp.bfloat16)
    packed = spread(scaled, obs_count, sp_count, 3)

    y = lax.dynamic_slice_in_dim(projected, col_start, tile)
    pos = jnp.stack([sp_pos, obs_pos]).astype(jnp.int32)
    inverse_tile, part_w = newton_call(
        pos, packed, root, rrow, y, obs_count, tile, share, sp_count
    )
    return inverse_tile, add_over_obs(part_w[0], obs_count, 1)


def solution(mesh):
    in_specs = (P("obs", None), P("obs", None), P(), P("obs"), P())
    out_specs = (P("sp", "obs"), P("sp"))
    return jax.shard_map(
        on_device, mesh=mesh, in_specs=in_specs, out_specs=out_specs, check_vma=False
    )
```

```python
import functools
import math

import jax
import jax.numpy as jnp
from jax import lax
from jax.experimental import pallas as pl
from jax.experimental.pallas import tpu as pltpu
from jax.sharding import PartitionSpec as P

epsilon = 1e-06
LANES = 128
VMEM_BYTES = 58 * 2**20


def unit_rows(row_block):
    values = row_block.astype(jnp.float32)
    return (values * lax.rsqrt(jnp.sum(values * values, axis=1, keepdims=True) + epsilon)).astype(
        jnp.bfloat16
    )


def gram_body(blocks, tile, share, ext, root, s_ref, norm_ref, sp_ref, tgt_ref, gram_ref, ws_ref, kext):
    step = pl.program_id(0)
    width = blocks * tile

    @pl.when(step < blocks)
    def _():
        inner = lax.dot_general(
            norm_ref[...], sp_ref[...], (((1,), (1,)), ((), ())), preferred_element_type=jnp.float32
        )
        scaled = inner * root
        squared = scaled * scaled
        kb = ((squared - 6.0) * squared + 3.0).astype(jnp.bfloat16)
        kext[:, pl.ds(pl.multiple_of(step * tile, tile), tile)] = kb

        @pl.when(step < ext)
        def _():
            kext[:, pl.ds(pl.multiple_of(width + step * tile, tile), tile)] = kb

        kf = kb.astype(jnp.float32)
        weighted = jnp.dot(tgt_ref[...], kb, preferred_element_type=jnp.float32)
        ws_ref[0:1, :] = weighted[0:1, :]
        ws_ref[1:2, :] = jnp.sum(kf * kf, axis=0, keepdims=True)

    @pl.when(step >= blocks)
    def _():
        j = step - blocks
        cols = pl.ds(pl.multiple_of(j * tile, tile), tile)
        window = pl.ds(pl.multiple_of(j * tile + s_ref[0] * share, LANES), share)
        gram_ref[...] = lax.dot_general(
            kext[:, cols], kext[:, window], (((0,), (0,)), ((), ())), preferred_element_type=jnp.float32
        ).astype(jnp.bfloat16)


def gram_call(s_pos, normed, sparse, targets, blocks, tile, share, sp_count):
    rows, depth = normed.shape
    width = blocks * tile
    ext = -(-((blocks - 1) * tile + sp_count * share - width) // tile)
    last = blocks - 1
    return pl.pallas_call(
        functools.partial(gram_body, blocks, tile, share, ext, math.sqrt(depth)),
        grid_spec=pltpu.PrefetchScalarGridSpec(
            num_scalar_prefetch=1,
            grid=(2 * blocks,),
            in_specs=[
                pl.BlockSpec((rows, depth), lambda g, s: (0, 0)),
                pl.BlockSpec((tile, depth), lambda g, s: (jnp.minimum(g, last), 0)),
                pl.BlockSpec((16, rows), lambda g, s: (0, 0)),
            ],
            out_specs=[
                pl.BlockSpec((tile, share), lambda g, s: (jnp.maximum(g - blocks, 0), 0)),
                pl.BlockSpec((2, tile), lambda g, s: (0, jnp.minimum(g, last))),
            ],
            scratch_shapes=[pltpu.VMEM((rows, width + ext * tile), jnp.bfloat16)],
        ),
        out_shape=[
            jax.ShapeDtypeStruct((width, share), jnp.bfloat16),
            jax.ShapeDtypeStruct((2, width), jnp.float32),
        ],
        compiler_params=pltpu.CompilerParams(vmem_limit_bytes=VMEM_BYTES),
    )(s_pos, normed, sparse, jnp.broadcast_to(targets[None, :], (16, rows)))


def newton_body(
    blocks, tile, share, sp_count, chunk, block_rows,
    pos_ref, packed_ref, rcol_ref, rrow_ref, y_ref, inv_ref, w_ref, dense, prod,
):
    step = pl.program_id(0)
    width = blocks * tile
    half = blocks // 2
    p_steps = width // chunk
    my_cols = pl.ds(pl.multiple_of(pos_ref[1] * tile, tile), tile)

    @pl.when(step < blocks)
    def _():
        rows = pl.ds(pl.multiple_of(step * tile, tile), tile)
        for s in range(sp_count):
            for q in range(share // LANES):
                offset = s * share + q * LANES
                if offset >= (half + 1) * tile:
                    continue
                col = lax.rem(step * tile + offset, width)
                cols = pl.ds(pl.multiple_of(col, LANES), LANES)
                block = packed_ref[s * tile : (s + 1) * tile, q * LANES : (q + 1) * LANES]
                dense[rows, cols] = block
                if tile <= offset < half * tile:
                    dense[cols, rows] = block.T

    @pl.when((step >= blocks) & (step < blocks + p_steps))
    def _():
        rows = pl.ds(pl.multiple_of((step - blocks) * chunk, chunk), chunk)
        prod[rows, :] = jnp.dot(
            dense[rows, :], dense[:, my_cols], preferred_element_type=jnp.float32
        ).astype(jnp.bfloat16)

    @pl.when(step >= blocks + p_steps)
    def _():
        local = pl.multiple_of((step - blocks - p_steps) * chunk, chunk)
        start = pl.multiple_of(pos_ref[0] * block_rows + local, chunk)
        rows = pl.ds(start, chunk)
        cubic = jnp.dot(dense[rows, :], prod[...], preferred_element_type=jnp.float32)
        on_diag = (start + lax.broadcasted_iota(jnp.int32, (chunk, tile), 0)) == (
            pos_ref[1] * tile + lax.broadcasted_iota(jnp.int32, (chunk, tile), 1)
        )
        series = (
            jnp.where(on_diag, 1.0, 0.0)
            - dense[rows, my_cols].astype(jnp.float32)
            + prod[rows, :].astype(jnp.float32)
            - cubic
        )
        out = series * rcol_ref[rows, :] * rrow_ref[...]
        inv_ref[pl.ds(local, chunk), :] = out
        w_ref[:, pl.ds(local, chunk)] = lax.dot_general(
            y_ref[...], out, (((1,), (1,)), ((), ())),
            precision=lax.Precision.HIGHEST, preferred_element_type=jnp.float32,
        )


def newton_call(pos, packed, root_recip, rrow, y, blocks, tile, share, sp_count):
    width = blocks * tile
    block_rows = width // sp_count
    chunk = min(512, block_rows)
    grid = blocks + width // chunk + block_rows // chunk
    last = blocks - 1
    return pl.pallas_call(
        functools.partial(newton_body, blocks, tile, share, sp_count, chunk, block_rows),
        grid_spec=pltpu.PrefetchScalarGridSpec(
            num_scalar_prefetch=1,
            grid=(grid,),
            in_specs=[
                pl.BlockSpec((sp_count * tile, share), lambda g, p: (jnp.minimum(g, last), 0)),
                pl.BlockSpec((width, 1), lambda g, p: (0, 0)),
                pl.BlockSpec((1, tile), lambda g, p: (0, 0)),
                pl.BlockSpec((8, tile), lambda g, p: (0, 0)),
            ],
            out_specs=[
                pl.BlockSpec((block_rows, tile), lambda g, p: (0, 0)),
                pl.BlockSpec((8, block_rows), lambda g, p: (0, 0)),
            ],
            scratch_shapes=[
                pltpu.VMEM((width, width), jnp.bfloat16),
                pltpu.VMEM((width, tile), jnp.bfloat16),
            ],
        ),
        out_shape=[
            jax.ShapeDtypeStruct((block_rows, tile), jnp.float32),
            jax.ShapeDtypeStruct((8, block_rows), jnp.float32),
        ],
        compiler_params=pltpu.CompilerParams(vmem_limit_bytes=VMEM_BYTES),
    )(pos, packed, root_recip[:, None], rrow[None, :], jnp.broadcast_to(y[None, :], (8, tile)))


def add_body(count, in_ref, out_ref, slots, send_sem, recv_sem):
    me = lax.axis_index("obs")
    barrier = pltpu.get_barrier_semaphore()
    for k in range(1, count):
        pl.semaphore_signal(
            barrier, inc=1, device_id={"obs": lax.rem(me + k, count)}, device_id_type=pl.DeviceIdType.MESH
        )
    pl.semaphore_wait(barrier, count - 1)
    copies = []
    for k in range(1, count):
        copy = pltpu.make_async_remote_copy(
            src_ref=in_ref,
            dst_ref=slots.at[me],
            send_sem=send_sem.at[k],
            recv_sem=recv_sem.at[k],
            device_id={"obs": lax.rem(me + k, count)},
            device_id_type=pl.DeviceIdType.MESH,
        )
        copy.start()
        copies.append(copy)
    slots[me] = in_ref[...]
    for copy in copies:
        copy.wait()
    total = slots[0]
    for k in range(1, count):
        total = total + slots[k]
    out_ref[...] = total


def add_over_obs(values, count, collective_id):
    shape = values.shape
    flat = values.reshape(values.size // LANES, LANES)
    total = pl.pallas_call(
        functools.partial(add_body, count),
        out_shape=jax.ShapeDtypeStruct(flat.shape, flat.dtype),
        in_specs=[pl.BlockSpec(memory_space=pltpu.VMEM)],
        out_specs=pl.BlockSpec(memory_space=pltpu.VMEM),
        scratch_shapes=[
            pltpu.VMEM((count,) + flat.shape, flat.dtype),
            pltpu.SemaphoreType.DMA((count,)),
            pltpu.SemaphoreType.DMA((count,)),
        ],
        cost_estimate=pl.CostEstimate(
            flops=count * flat.size, bytes_accessed=400 * flat.size, transcendentals=0
        ),
        compiler_params=pltpu.CompilerParams(collective_id=collective_id, has_side_effects=True),
    )(flat)
    return total.reshape(shape)


def spread_keys(z_count, sp_count):
    keys = [("z", k) for k in range(1, z_count)]
    for k in range(z_count):
        keys += [("x", k), ("core", k), ("core_x", k)]
        for d in range(1, sp_count):
            keys += [(name, k, d) for name in ("sp", "sp_a", "x_b", "core_sp", "core_a", "core_b")]
    return {key: place for place, key in enumerate(keys)}


def spread_body(z_count, sp_count, in_ref, out_ref, send_sem, recv_sem, own_sem):
    places = spread_keys(z_count, sp_count)
    obs = lax.axis_index("obs")
    s = lax.axis_index("sp")
    z, x, c = lax.div(obs, 4), lax.rem(lax.div(obs, 2), 2), lax.rem(obs, 2)
    half = in_ref.shape[0] // 2
    upper, lower = pl.ds(0, half), pl.ds(half, half)
    zs = [lax.bitwise_xor(z, k) for k in range(z_count)]
    to_sp = [lax.rem(s + d, sp_count) for d in range(sp_count)]
    from_sp = [lax.rem(s - d + sp_count, sp_count) for d in range(sp_count)]

    def device(z_to, x_to, c_to, s_to):
        return {"obs": z_to * 4 + x_to * 2 + c_to, "sp": s_to}

    def slot(z_of, x_of, s_of):
        return ((z_of * 2 + x_of) * 2 + c) * sp_count + s_of

    own_slot = slot(z, x, s)
    across, sibling = device(z, 1 - x, c, s), device(z, x, 1 - c, s)
    others = [device(zs[k], x, c, s) for k in range(1, z_count)]
    others += [device(z, x, c, to_sp[d]) for d in range(1, sp_count)]
    others += [across, sibling]
    barrier = pltpu.get_barrier_semaphore()
    for other in others:
        pl.semaphore_signal(barrier, inc=1, device_id=other, device_id_type=pl.DeviceIdType.MESH)
    pl.semaphore_wait(barrier, len(others))

    sent = {}

    def send(key, place, target, rows=None, own=False):
        src = in_ref if own else out_ref.at[place]
        dst = out_ref.at[place]
        if rows is not None:
            src, dst = src.at[rows], dst.at[rows]
        copy = pltpu.make_async_remote_copy(
            src_ref=src,
            dst_ref=dst,
            send_sem=send_sem.at[places[key]],
            recv_sem=recv_sem.at[places[key]],
            device_id=target,
            device_id_type=pl.DeviceIdType.MESH,
        )
        copy.start()
        sent[key] = copy

    keep = pltpu.make_async_copy(in_ref, out_ref.at[own_slot], own_sem)
    keep.start()
    for k in range(1, z_count):
        send(("z", k), own_slot, others[k - 1], own=True)

    def fan_out(k):
        place = slot(zs[k], x, s)
        send(("x", k), place, across, own=k == 0)
        for d in range(1, sp_count):
            send(("sp", k, d), place, device(z, x, c, to_sp[d]), own=k == 0)
        send(("core", k), place, sibling, own=k == 0)

    def relay(k):
        sent[("x", k)].wait_recv()
        place = slot(zs[k], 1 - x, s)
        for d in range(1, sp_count):
            send(("sp_a", k, d), place, device(z, x, c, to_sp[d]), upper)
        send(("core_x", k), place, sibling)
        for d in range(1, sp_count):
            sent[("sp", k, d)].wait_recv()
            place = slot(zs[k], x, from_sp[d])
            send(("x_b", k, d), place, across, lower)
            send(("core_sp", k, d), place, sibling)

    def finish(k):
        for d in range(1, sp_count):
            place = slot(zs[k], 1 - x, from_sp[d])
            sent[("sp_a", k, d)].wait_recv()
            send(("core_a", k, d), place, sibling, upper)
            sent[("x_b", k, d)].wait_recv()
            send(("core_b", k, d), place, sibling, lower)

    fan_out(0)
    for k in range(1, z_count):
        sent[("z", k)].wait_recv()
        fan_out(k)
        relay(k - 1)
        if k > 1:
            finish(k - 2)
    relay(z_count - 1)
    if z_count > 1:
        finish(z_count - 2)
    finish(z_count - 1)
    keep.wait()
    for key, copy in sent.items():
        copy.wait_send()
        if key[0].startswith("core"):
            copy.wait_recv()


def spread(shard, obs_count, sp_count, collective_id):
    rows, cols = shard.shape
    z_count = obs_count // 4
    total = obs_count * sp_count
    sems = len(spread_keys(z_count, sp_count))
    gathered = pl.pallas_call(
        functools.partial(spread_body, z_count, sp_count),
        out_shape=jax.ShapeDtypeStruct((total, rows, cols), shard.dtype),
        in_specs=[pl.BlockSpec(memory_space=pl.ANY)],
        out_specs=pl.BlockSpec(memory_space=pl.ANY),
        scratch_shapes=[
            pltpu.SemaphoreType.DMA((sems,)),
            pltpu.SemaphoreType.DMA((sems,)),
            pltpu.SemaphoreType.DMA,
        ],
        compiler_params=pltpu.CompilerParams(collective_id=collective_id, has_side_effects=True),
    )(shard)
    return gathered.reshape(total * rows, cols)


def position():
    obs = lax.axis_index("obs")
    return lax.div(obs, 4), lax.rem(lax.div(obs, 2), 2), lax.rem(obs, 2), lax.axis_index("sp")


def device(z, x, c, s):
    return {"obs": z * 4 + x * 2 + c, "sp": s}


def remote(src, dst, send_sem, recv_sem, target):
    return pltpu.make_async_remote_copy(
        src_ref=src, dst_ref=dst, send_sem=send_sem, recv_sem=recv_sem,
        device_id=target, device_id_type=pl.DeviceIdType.MESH,
    )


def route_sems(z_count):
    return [
        pltpu.SemaphoreType.DMA((z_count + 1,)),
        pltpu.SemaphoreType.DMA((z_count,)),
        pltpu.SemaphoreType.DMA((9 * z_count,)),
        pltpu.SemaphoreType.DMA((9 * z_count,)),
    ]


def route_greet(z_count):
    z, x, c, s = position()
    barrier = pltpu.get_barrier_semaphore()
    others = [device(z, 1 - x, c, s), device(z, x, 1 - c, s), device(z, x, c, 1 - s)]
    others += [device(lax.rem(z + k, z_count), x, c, s) for k in range(1, z_count)]
    for other in others:
        pl.semaphore_signal(barrier, inc=1, device_id=other, device_id_type=pl.DeviceIdType.MESH)
    pl.semaphore_wait(barrier, len(others))


def route(z_count, in_ref, out_ref, z_send, z_recv, send_sem, recv_sem, arrive, begin=None, late=None):
    z, x, c, s = position()
    last = z_count - 1
    half = in_ref.shape[0] // 2
    upper, lower = pl.ds(0, half), pl.ds(half, half)
    across, beside, sibling = device(z, 1 - x, c, s), device(z, x, c, 1 - s), device(z, x, 1 - c, s)

    def slot(z_of, x_of, c_of, s_of):
        return ((z_of * 2 + x_of) * 2 + c_of) * 2 + s_of

    nearer = jnp.minimum(z, last - z)
    origins = [z]
    for a in range(last):
        both = jnp.where(a % 2 == 0, z - (a // 2 + 1), z + (a // 2 + 1))
        single = jnp.where(z <= last - z, z + (a - nearer + 1), z - (a - nearer + 1))
        origins.append(jnp.where(a < 2 * nearer, both, single))

    sent = {}

    def send(key, src, place, target, rows=None):
        dst = out_ref.at[place]
        if rows is not None:
            src, dst = src.at[rows], dst.at[rows]
        n = len(sent)
        sent[key] = remote(src, dst, send_sem.at[n], recv_sem.at[n], target)
        sent[key].start()

    def hop(src, origin, sem, target_z):
        return remote(
            src, out_ref.at[slot(origin, x, c, s)], z_send.at[sem], z_recv.at[origin], device(target_z, x, c, s)
        )

    hops = []

    def start_hop(when, copy):
        pl.when(when)(copy.start)
        hops.append((when, copy))

    start_hop(z < last, hop(in_ref, z, 0, jnp.minimum(z + 1, last)))
    start_hop(z > 0, hop(in_ref, z, 1, jnp.maximum(z - 1, 0)))

    def fan_out(a, src):
        place = slot(origins[a], x, c, s)
        send(("x", a), src, place, across)
        send(("y", a), src, place, beside)
        send(("core", a), src, place, sibling)

    def relay(a):
        sent[("x", a)].wait_recv()
        place = slot(origins[a], 1 - x, c, s)
        send(("ya", a), out_ref.at[place], place, beside, upper)
        send(("core_x", a), out_ref.at[place], place, sibling)
        arrive(out_ref.at[place], place)
        sent[("y", a)].wait_recv()
        place = slot(origins[a], x, c, 1 - s)
        send(("xb", a), out_ref.at[place], place, across, lower)
        send(("core_y", a), out_ref.at[place], place, sibling)
        arrive(out_ref.at[place], place)

    def finish(a):
        place = slot(origins[a], 1 - x, c, 1 - s)
        sent[("ya", a)].wait_recv()
        send(("core_a", a), out_ref.at[place], place, sibling, upper)
        sent[("xb", a)].wait_recv()
        send(("core_b", a), out_ref.at[place], place, sibling, lower)
        arrive(out_ref.at[place], place)

    def from_sibling(a, keys, x_of, s_of):
        for key in keys:
            sent[(key, a)].wait_recv()
        place = slot(origins[a], x_of, 1 - c, s_of)
        arrive(out_ref.at[place], place)

    fan_out(0, in_ref)
    if begin is not None:
        begin()
    arrive(in_ref, slot(z, x, c, s))
    for a in range(1, z_count + 3):
        if a < z_count:
            origin = origins[a]
            place = slot(origin, x, c, s)
            held = out_ref.at[place]
            rising = origin < z
            target_z = jnp.where(rising, z + 1, z - 1)
            remote(held, held, z_send.at[0], z_recv.at[origin], across).wait_recv()
            start_hop(
                (target_z >= 0) & (target_z <= last), hop(held, origin, a + 1, jnp.clip(target_z, 0, last))
            )
            fan_out(a, held)
            arrive(held, place)
        if a - 1 < z_count:
            relay(a - 1)
            from_sibling(a - 1, ("core",), x, s)
        if a == z_count and late is not None:
            late()
        if 0 <= a - 2 < z_count:
            finish(a - 2)
            from_sibling(a - 2, ("core_x",), 1 - x, s)
            from_sibling(a - 2, ("core_y",), x, 1 - s)
        if 0 <= a - 3 < z_count:
            from_sibling(a - 3, ("core_a", "core_b"), 1 - x, 1 - s)
    for copy in sent.values():
        copy.wait_send()
    for when, copy in hops:
        pl.when(when)(copy.wait_send)


def share_body(z_count, own_ref, own_slab, out_ref, slab_ref, z_send, z_recv, send_sem, recv_sem, slab_send, slab_recv, keep_sem):
    z, x, c, s = position()
    q, q_across = x * 2 + c, (1 - x) * 2 + c
    half = own_slab.shape[0] // 2
    near, far = pl.ds(pl.multiple_of(s * half, 16), half), pl.ds(pl.multiple_of((1 - s) * half, 16), half)
    route_greet(z_count)
    keep = pltpu.make_async_copy(own_ref, out_ref.at[((z * 2 + x) * 2 + c) * 2 + s], keep_sem.at[0])
    keep_slab = pltpu.make_async_copy(own_slab, slab_ref.at[q], keep_sem.at[1])
    keep.start()
    keep_slab.start()
    shared = []

    def share(src, place, piece, target):
        n = len(shared)
        dst = slab_ref.at[place]
        if piece is not None:
            src, dst = src.at[piece], dst.at[piece]
        shared.append(remote(src, dst, slab_send.at[n], slab_recv.at[n], target))
        shared[-1].start()

    def begin():
        share(own_slab, q, near, device(z, 1 - x, c, s))
        share(own_slab, q, None, device(z, x, 1 - c, s))

    def late():
        shared[0].wait_recv()
        share(slab_ref.at[q_across], q_across, near, device(z, x, c, 1 - s))
        share(slab_ref.at[q_across], q_across, near, device(z, x, 1 - c, s))

    route(
        z_count, own_ref, out_ref, z_send, z_recv, send_sem, recv_sem, lambda src, place: None, begin, late
    )
    shared[2].wait_recv()
    share(slab_ref.at[q_across], q_across, far, device(z, x, 1 - c, s))
    for n in (1, 3, 4):
        shared[n].wait_recv()
    for copy in shared:
        copy.wait_send()
    keep.wait()
    keep_slab.wait()


def share(own, own_slab, z_count, collective_id):
    anywhere = pl.BlockSpec(memory_space=pl.ANY)
    return pl.pallas_call(
        functools.partial(share_body, z_count),
        out_shape=[
            jax.ShapeDtypeStruct((8 * z_count,) + own.shape, own.dtype),
            jax.ShapeDtypeStruct((4,) + own_slab.shape, own_slab.dtype),
        ],
        in_specs=[anywhere, anywhere],
        out_specs=[anywhere, anywhere],
        scratch_shapes=route_sems(z_count)
        + [pltpu.SemaphoreType.DMA((5,)), pltpu.SemaphoreType.DMA((5,)), pltpu.SemaphoreType.DMA((2,))],
        compiler_params=pltpu.CompilerParams(collective_id=collective_id, has_side_effects=True),
    )(own, own_slab)


def series_body(
    z_count, strip, tile, chunk, normalizer,
    part_ref, sums_ref, reg_ref, inv_ref, w_ref, gathered,
    dense, first, second, stage, recip, spread_recip, out_buf, w_own, w_slots,
    z_send, z_recv, send_sem, recv_sem, stage_sem, out_sem, w_send, w_recv,
):
    z, x, c, s = position()
    obs = lax.axis_index("obs")
    obs_count = 4 * z_count
    strips = 8 * z_count
    width = strips * strip
    half = strips // 2
    span = part_ref.shape[1]
    block_rows = width // 2
    lines = tile // LANES
    fold = 1.0 / normalizer

    barrier = pltpu.get_barrier_semaphore()
    peers = [
        {"obs": lax.rem(obs + k, obs_count), "sp": s} for k in range(1, obs_count)
    ]
    for peer in peers + [device(z, x, c, 1 - s)]:
        pl.semaphore_signal(barrier, inc=1, device_id=peer, device_id_type=pl.DeviceIdType.MESH)
    pl.semaphore_wait(barrier, obs_count)

    slots = stage.shape[0]
    waiting = []

    def lay_out(n):
        copy, place = waiting[n]
        copy.wait()
        place = lax.rem(place, 8) * z_count + lax.div(place, 8)
        rows = pl.ds(pl.multiple_of(place * strip, strip), strip)

        def put(k, turn):
            cols = pl.ds(pl.multiple_of(lax.rem(place + k, strips) * strip, strip), strip)
            block = stage[n % slots, :, pl.ds(pl.multiple_of(k * strip, strip), strip)]
            dense[rows, cols] = block
            if turn:
                dense[cols, rows] = block.T

        put(0, False)
        put(half, False)

        @pl.loop(0, half // 4)
        def _(m):
            for k in range(4):
                pl.when(m * 4 + k > 0)(lambda k=k: put(m * 4 + k, True))

    def arrive(src, place):
        n = len(waiting)
        if n >= slots:
            lay_out(n - slots)
        copy = pltpu.make_async_copy(src, stage.at[n % slots], stage_sem.at[n % slots])
        copy.start()
        waiting.append((copy, place))

    def begin():
        per = sums_ref.shape[1] // 2
        for p in range(sums_ref.shape[0]):
            lane = slice(p * per, (p + 1) * per)
            recip[lane, :] = 1.0 / (sums_ref[p, per:, :] * fold + reg_ref[lane, :])

        @pl.loop(0, width // LANES)
        def _(m):
            row = jnp.broadcast_to(recip[pl.ds(m, 1), :], (LANES, LANES))
            spread_recip[pl.ds(pl.multiple_of(m * LANES, LANES), LANES), :] = row.T

    route(z_count, part_ref, gathered, z_send, z_recv, send_sem, recv_sem, arrive, begin)
    for n in range(len(waiting) - slots, len(waiting)):
        lay_out(n)

    my_cols = pl.ds(pl.multiple_of(obs * tile, tile), tile)

    def by_row(values, rows):
        scale = spread_recip[rows, :]
        return values * jnp.concatenate([scale] * lines, axis=1)

    @pl.loop(0, width // chunk)
    def _(m):
        rows = pl.ds(pl.multiple_of(m * chunk, chunk), chunk)
        first[rows, :] = by_row(dense[rows, my_cols].astype(jnp.float32) * fold, rows).astype(jnp.bfloat16)

    @pl.loop(0, width // chunk)
    def _(m):
        rows = pl.ds(pl.multiple_of(m * chunk, chunk), chunk)
        prod = jnp.dot(dense[rows, :], first[...], preferred_element_type=jnp.float32)
        second[rows, :] = by_row(prod * fold, rows).astype(jnp.bfloat16)

    def my_lines(ref, at):
        return jnp.concatenate([ref[pl.ds(at + h, 1), :] for h in range(lines)], axis=1)

    per = sums_ref.shape[1] // 2
    r_row = my_lines(recip, obs * lines)
    y = my_lines(sums_ref.at[lax.div(obs * lines, per)], lax.rem(obs * lines, per))
    y = jnp.broadcast_to(y * (1.0 / math.sqrt(normalizer)), (8, tile))

    def emit(m):
        return pltpu.make_async_copy(
            out_buf.at[m], inv_ref.at[pl.ds(pl.multiple_of(m * chunk, chunk), chunk)], out_sem.at[m]
        )

    @pl.loop(0, block_rows // chunk)
    def _(m):
        begin_at = s * block_rows + m * chunk
        rows = pl.ds(pl.multiple_of(begin_at, chunk), chunk)
        cubic = jnp.dot(dense[rows, :], second[...], preferred_element_type=jnp.float32)
        on_diag = (begin_at + lax.broadcasted_iota(jnp.int32, (chunk, tile), 0)) == (
            obs * tile + lax.broadcasted_iota(jnp.int32, (chunk, tile), 1)
        )
        series = second[rows, :].astype(jnp.float32) - by_row(
            (dense[rows, my_cols].astype(jnp.float32) + cubic) * fold, rows
        )
        out = (jnp.where(on_diag, 1.0, 0.0) + series) * r_row
        out_buf[m] = out
        emit(m).start()
        part_w = lax.dot_general(
            y, out, (((1,), (1,)), ((), ())),
            precision=lax.Precision.HIGHEST, preferred_element_type=jnp.float32,
        )
        for h in range(chunk // LANES):
            w_own[pl.ds(m * (chunk // LANES) + h, 1), :] = part_w[0:1, h * LANES : (h + 1) * LANES]

    copies = []
    for k in range(1, obs_count):
        copies.append(remote(w_own, w_slots.at[obs], w_send.at[k], w_recv.at[k], peers[k - 1]))
        copies[-1].start()
    w_slots[obs] = w_own[...]
    for copy in copies:
        copy.wait()
    total = w_slots[0]
    for k in range(1, obs_count):
        total = total + w_slots[k]
    w_ref[...] = total
    for m in range(block_rows // chunk):
        emit(m).wait()


def series_tile(part, sums, regularizer, z_count, tile, normalizer, collective_id):
    strip, span = part.shape
    strips = 8 * z_count
    width = strips * strip
    block_rows = width // 2
    chunk = min(512, block_rows)
    obs_count = 4 * z_count
    w_shape = (block_rows // LANES, LANES)
    anywhere = pl.BlockSpec(memory_space=pl.ANY)
    vmem = pl.BlockSpec(memory_space=pltpu.VMEM)
    inverse_tile, weights, _ = pl.pallas_call(
        functools.partial(series_body, z_count, strip, tile, chunk, normalizer),
        out_shape=[
            jax.ShapeDtypeStruct((block_rows, tile), jnp.float32),
            jax.ShapeDtypeStruct(w_shape, jnp.float32),
            jax.ShapeDtypeStruct((strips, strip, span), part.dtype),
        ],
        in_specs=[anywhere, vmem, vmem],
        out_specs=[anywhere, vmem, anywhere],
        scratch_shapes=[
            pltpu.VMEM((width, width), jnp.bfloat16),
            pltpu.VMEM((width, tile), jnp.bfloat16),
            pltpu.VMEM((width, tile), jnp.bfloat16),
            pltpu.VMEM((2, strip, span), jnp.bfloat16),
            pltpu.VMEM((width // LANES, LANES), jnp.float32),
            pltpu.VMEM((width, LANES), jnp.float32),
            pltpu.VMEM((block_rows // chunk, chunk, tile), jnp.float32),
            pltpu.VMEM(w_shape, jnp.float32),
            pltpu.VMEM((obs_count,) + w_shape, jnp.float32),
        ]
        + route_sems(z_count)
        + [
            pltpu.SemaphoreType.DMA((2,)),
            pltpu.SemaphoreType.DMA((block_rows // chunk,)),
            pltpu.SemaphoreType.DMA((obs_count,)),
            pltpu.SemaphoreType.DMA((obs_count,)),
        ],
        compiler_params=pltpu.CompilerParams(
            collective_id=collective_id, has_side_effects=True, vmem_limit_bytes=VMEM_BYTES
        ),
    )(part, sums, regularizer.reshape(width // LANES, LANES))
    return inverse_tile, weights.reshape(block_rows)


def by_strips(descriptors, candidates, sparse_index, targets, regularizer):
    obs_count = lax.axis_size("obs")
    sp_count = lax.axis_size("sp")
    obs_pos = lax.axis_index("obs")
    sp_pos = lax.axis_index("sp")
    z_count = obs_count // 4
    width = sparse_index.shape[0]
    tile = width // obs_count
    strip = width // (obs_count * sp_count)
    mine = strip * z_count
    span = width // 2 + strip
    window = mine - strip + span
    window = -(-window // tile) * tile
    rows, depth = descriptors.shape
    normalizer = 24.0 * rows * obs_count

    extra = jnp.pad(targets.reshape(rows // depth, depth), ((0, 32 - rows // depth), (0, 0)))
    shard = jnp.concatenate([unit_rows(descriptors), extra])
    piece = candidates.shape[0] // sp_count
    own = lax.dynamic_slice_in_dim(candidates, sp_pos * piece, piece)
    table, slab = share(unit_rows(own), shard, z_count, 2)
    table = table.reshape(-1, depth)
    place = lax.rem(obs_pos, 4) * sp_count + sp_pos
    wanted = lax.dynamic_slice_in_dim(
        jnp.concatenate([sparse_index, sparse_index]), place * mine, window
    )
    sparse = table.at[wanted].get(mode="promise_in_bounds")
    slab_targets = slab[:, rows : rows + rows // depth].reshape(4 * rows)
    part, sums = slab_gram(
        slab, sparse, slab_targets, z_count, sp_count, strip, span, tile, rows, 0
    )
    return series_tile(part, sums, regularizer, z_count, tile, normalizer, 3)


def slab_body(z_count, sp_count, strip, span, tile, chunk, root, *refs):
    norm_ref, sp_ref, tgt_ref, part_ref, sums_ref = refs[:5]
    kbuf, ktr, parts, from_low, from_high, zsums, gsums = refs[5:12]
    up_send, up_recv, down_send, down_recv, zs_send, zs_recv, gs_send, gs_recv = refs[12:]
    obs = lax.axis_index("obs")
    s = lax.axis_index("sp")
    z, q = lax.div(obs, 4), lax.rem(obs, 4)
    group = 4 * sp_count
    p = q * sp_count + s
    last = z_count - 1
    shard = tgt_ref.shape[1] // 4
    per = tile // strip
    own_blocks = z_count // per
    mine = strip * z_count
    lines = mine // LANES

    z_others = [{"obs": lax.rem(z + k, z_count) * 4 + q, "sp": s} for k in range(1, z_count)]
    group_others = []
    for k in range(1, group):
        to = lax.rem(p + k, group)
        group_others.append({"obs": z * 4 + lax.div(to, sp_count), "sp": lax.rem(to, sp_count)})
    barrier = pltpu.get_barrier_semaphore()
    for other in z_others + group_others:
        pl.semaphore_signal(barrier, inc=1, device_id=other, device_id_type=pl.DeviceIdType.MESH)
    pl.semaphore_wait(barrier, len(z_others) + len(group_others))

    def remote(src, dst, send_sem, recv_sem, target):
        return pltpu.make_async_remote_copy(
            src_ref=src, dst_ref=dst, send_sem=send_sem, recv_sem=recv_sem,
            device_id=target, device_id_type=pl.DeviceIdType.MESH,
        )

    def kernel_tile(t, own):
        cols = pl.ds(pl.multiple_of(t * tile, tile), tile)
        for k in range(4):
            rows = pl.ds(k * shard, shard)
            inner = lax.dot_general(
                norm_ref[k, :shard, :], sp_ref[cols, :], (((1,), (1,)), ((), ())),
                preferred_element_type=jnp.float32,
            )
            scaled = inner * root
            squared = scaled * scaled
            kb = ((squared - 6.0) * squared + 3.0).astype(jnp.bfloat16)
            kbuf[rows, cols] = kb
            if own:
                ktr[cols, rows] = kb.T

    for t in range(own_blocks):
        kernel_tile(t, True)
        cols = slice(t * tile, (t + 1) * tile)
        weighted = jnp.dot(tgt_ref[...], kbuf[:, cols], preferred_element_type=jnp.float32)
        square = jnp.zeros((1, tile), jnp.float32)
        for k in range(4):
            kf = kbuf[k * shard : (k + 1) * shard, cols].astype(jnp.float32)
            square = square + jnp.sum(kf * kf, axis=0, keepdims=True)
        for h in range(tile // LANES):
            line = t * (tile // LANES) + h
            zsums[z, line : line + 1, :] = weighted[0:1, h * LANES : (h + 1) * LANES]
            zsums[z, lines + line : lines + line + 1, :] = square[:, h * LANES : (h + 1) * LANES]
    z_copies = []
    for k in range(1, z_count):
        copy = remote(zsums.at[z], zsums.at[z], zs_send.at[k], zs_recv.at[k], z_others[k - 1])
        copy.start()
        z_copies.append(copy)

    @pl.loop(own_blocks, kbuf.shape[1] // tile)
    def _(t):
        kernel_tile(t, False)

    def block(b):
        start = pl.multiple_of(b * tile, tile)
        for j in range(0, span + tile - strip, chunk):
            cols = pl.ds(pl.multiple_of(start + j, LANES), chunk)
            g = jnp.dot(
                ktr[pl.ds(start, tile), :], kbuf[:, cols], preferred_element_type=jnp.float32
            ).astype(jnp.bfloat16)
            for h in range(per):
                lo, hi = max(j, h * strip), min(j + chunk, h * strip + span)
                parts[b * per + h, :, lo - h * strip : hi - h * strip] = g[
                    h * strip : (h + 1) * strip, lo - j : hi - j
                ]

    def up(t):
        return remote(
            parts.at[t], from_low.at[t], up_send.at[t], up_recv.at[t],
            {"obs": lax.rem(z + 1, z_count) * 4 + q, "sp": s},
        )

    def down(t):
        return remote(
            parts.at[t], from_high.at[t], down_send.at[t], down_recv.at[t],
            {"obs": lax.rem(z + last, z_count) * 4 + q, "sp": s},
        )

    for k in range(own_blocks):
        block(jnp.where(z < z_count // 2, own_blocks - 1 - k, k))
        for h in range(per):
            high, low = last - (k * per + h), k * per + h
            if high > 0:
                pl.when(z == 0)(lambda t=high: up(t).start())
            if low < last:
                pl.when(z == last)(lambda t=low: down(t).start())
        if k == 0:
            for copy in z_copies:
                copy.wait_recv()
            total = zsums[0]
            for m in range(1, z_count):
                total = total + zsums[m]
            gsums[p] = total
            g_copies = []
            for m in range(1, group):
                copy = remote(gsums.at[p], gsums.at[p], gs_send.at[m], gs_recv.at[m], group_others[m - 1])
                copy.start()
                g_copies.append(copy)

    for k in range(last):
        high, low = last - k, k

        @pl.when((z > 0) & (z < high))
        def _(t=high):
            up(t).wait_recv()
            parts[t] = parts[t] + from_low[t]
            up(t).start()

        @pl.when((z < last) & (z > low))
        def _(t=low):
            down(t).wait_recv()
            parts[t] = parts[t] + from_high[t]
            down(t).start()

    def finish(below, above):
        total = parts[z].astype(jnp.float32)
        if below:
            up(z).wait_recv()
            total = total + from_low[z].astype(jnp.float32)
        if above:
            down(z).wait_recv()
            total = total + from_high[z].astype(jnp.float32)
        row = lax.broadcasted_iota(jnp.int32, total.shape, 0)
        col = lax.broadcasted_iota(jnp.int32, total.shape, 1)
        part_ref[...] = jnp.where(row == col, 0.0, total).astype(jnp.bfloat16)

    pl.when(z == 0)(lambda: finish(False, True))
    pl.when((z > 0) & (z < last))(lambda: finish(True, True))
    pl.when(z == last)(lambda: finish(True, False))

    for copy in g_copies:
        copy.wait()
    for copy in z_copies:
        copy.wait_send()
    sums_ref[...] = gsums[...]
    for t in range(z_count):
        pl.when(z < t)(lambda t=t: up(t).wait_send())
        pl.when(z > t)(lambda t=t: down(t).wait_send())


def slab_gram(slab, sparse, targets, z_count, sp_count, strip, span, tile, rows, collective_id):
    depth = slab.shape[2]
    window = sparse.shape[0]
    group = 4 * sp_count
    mine = strip * z_count
    lines = 2 * mine // LANES
    wide = span + tile - strip
    chunk = max(c for c in range(LANES, 1025, LANES) if wide % c == 0)
    vmem = pl.BlockSpec(memory_space=pltpu.VMEM)
    part = (z_count, strip, span)
    sems = [pltpu.SemaphoreType.DMA((z_count,))] * 6 + [pltpu.SemaphoreType.DMA((group,))] * 2
    return pl.pallas_call(
        functools.partial(slab_body, z_count, sp_count, strip, span, tile, chunk, math.sqrt(depth)),
        out_shape=[
            jax.ShapeDtypeStruct((strip, span), jnp.bfloat16),
            jax.ShapeDtypeStruct((group, lines, LANES), jnp.float32),
        ],
        in_specs=[vmem, vmem, vmem],
        out_specs=[vmem, vmem],
        scratch_shapes=[
            pltpu.VMEM((4 * rows, window), jnp.bfloat16),
            pltpu.VMEM((mine, 4 * rows), jnp.bfloat16),
            pltpu.VMEM(part, jnp.bfloat16),
            pltpu.VMEM(part, jnp.bfloat16),
            pltpu.VMEM(part, jnp.bfloat16),
            pltpu.VMEM((z_count, lines, LANES), jnp.float32),
            pltpu.VMEM((group, lines, LANES), jnp.float32),
        ] + sems,
        compiler_params=pltpu.CompilerParams(
            collective_id=collective_id, has_side_effects=True, vmem_limit_bytes=VMEM_BYTES
        ),
    )(slab, sparse, jnp.broadcast_to(targets[None, :], (16, 4 * rows)))


def on_device(descriptors, candidates, sparse_index, targets, regularizer):
    obs_count = lax.axis_size("obs")
    sp_count = lax.axis_size("sp")
    obs_pos = lax.axis_index("obs")
    sp_pos = lax.axis_index("sp")
    width = sparse_index.shape[0]
    if sp_count == 2 and width % (obs_count * sp_count * LANES) == 0:
        return by_strips(descriptors, candidates, sparse_index, targets, regularizer)
    tile = width // obs_count
    share = -(-((obs_count // 2 + 1) * tile) // (sp_count * LANES)) * LANES
    normalizer = 24.0 * descriptors.shape[0] * obs_count

    normed = unit_rows(descriptors)
    piece = candidates.shape[0] // sp_count
    own = lax.dynamic_slice_in_dim(candidates, sp_pos * piece, piece)
    table = spread(unit_rows(own), obs_count, sp_count, 2)
    sparse = table.at[sparse_index].get(mode="promise_in_bounds")

    gram, sums = gram_call(
        sp_pos[None].astype(jnp.int32), normed, sparse, targets, obs_count, tile, share, sp_count
    )
    sums = add_over_obs(sums, obs_count, 0)
    part = lax.psum_scatter(gram, "obs", scatter_dimension=0, tiled=True)

    projected = sums[0] / math.sqrt(normalizer)
    root = lax.rsqrt(sums[1] / normalizer + regularizer)
    col_start = obs_pos * tile
    rrow = lax.dynamic_slice_in_dim(root, col_start, tile)
    window_start = col_start + sp_pos * share
    rwin = lax.dynamic_slice_in_dim(jnp.concatenate([root, root]), window_start, share)
    offset = sp_pos * share + lax.iota(jnp.int32, share)
    on_diag = lax.iota(jnp.int32, tile)[:, None] == offset[None, :]
    scaled = jnp.where(
        on_diag, 0.0, part.astype(jnp.float32) * (rrow[:, None] / normalizer) * rwin[None, :]
    ).astype(jnp.bfloat16)
    packed = spread(scaled, obs_count, sp_count, 3)

    y = lax.dynamic_slice_in_dim(projected, col_start, tile)
    pos = jnp.stack([sp_pos, obs_pos]).astype(jnp.int32)
    inverse_tile, part_w = newton_call(
        pos, packed, root, rrow, y, obs_count, tile, share, sp_count
    )
    return inverse_tile, add_over_obs(part_w[0], obs_count, 1)


def solution(mesh):
    in_specs = (P("obs", None), P("obs", None), P(), P("obs"), P())
    out_specs = (P("sp", "obs"), P("sp"))
    return jax.shard_map(
        on_device, mesh=mesh, in_specs=in_specs, out_specs=out_specs, check_vma=False
    )
```

```python
import functools
import math

import jax
import jax.numpy as jnp
from jax import lax
from jax.experimental import pallas as pl
from jax.experimental.pallas import tpu as pltpu
from jax.sharding import PartitionSpec as P

epsilon = 1e-06
LANES = 128
VMEM_BYTES = 58 * 2**20


def unit_rows(row_block):
    values = row_block.astype(jnp.float32)
    return (values * lax.rsqrt(jnp.sum(values * values, axis=1, keepdims=True) + epsilon)).astype(
        jnp.bfloat16
    )


def gram_body(blocks, tile, share, ext, root, s_ref, norm_ref, sp_ref, tgt_ref, gram_ref, ws_ref, kext):
    step = pl.program_id(0)
    width = blocks * tile

    @pl.when(step < blocks)
    def _():
        inner = lax.dot_general(
            norm_ref[...], sp_ref[...], (((1,), (1,)), ((), ())), preferred_element_type=jnp.float32
        )
        scaled = inner * root
        squared = scaled * scaled
        kb = ((squared - 6.0) * squared + 3.0).astype(jnp.bfloat16)
        kext[:, pl.ds(pl.multiple_of(step * tile, tile), tile)] = kb

        @pl.when(step < ext)
        def _():
            kext[:, pl.ds(pl.multiple_of(width + step * tile, tile), tile)] = kb

        kf = kb.astype(jnp.float32)
        weighted = jnp.dot(tgt_ref[...], kb, preferred_element_type=jnp.float32)
        ws_ref[0:1, :] = weighted[0:1, :]
        ws_ref[1:2, :] = jnp.sum(kf * kf, axis=0, keepdims=True)

    @pl.when(step >= blocks)
    def _():
        j = step - blocks
        cols = pl.ds(pl.multiple_of(j * tile, tile), tile)
        window = pl.ds(pl.multiple_of(j * tile + s_ref[0] * share, LANES), share)
        gram_ref[...] = lax.dot_general(
            kext[:, cols], kext[:, window], (((0,), (0,)), ((), ())), preferred_element_type=jnp.float32
        ).astype(jnp.bfloat16)


def gram_call(s_pos, normed, sparse, targets, blocks, tile, share, sp_count):
    rows, depth = normed.shape
    width = blocks * tile
    ext = -(-((blocks - 1) * tile + sp_count * share - width) // tile)
    last = blocks - 1
    return pl.pallas_call(
        functools.partial(gram_body, blocks, tile, share, ext, math.sqrt(depth)),
        grid_spec=pltpu.PrefetchScalarGridSpec(
            num_scalar_prefetch=1,
            grid=(2 * blocks,),
            in_specs=[
                pl.BlockSpec((rows, depth), lambda g, s: (0, 0)),
                pl.BlockSpec((tile, depth), lambda g, s: (jnp.minimum(g, last), 0)),
                pl.BlockSpec((16, rows), lambda g, s: (0, 0)),
            ],
            out_specs=[
                pl.BlockSpec((tile, share), lambda g, s: (jnp.maximum(g - blocks, 0), 0)),
                pl.BlockSpec((2, tile), lambda g, s: (0, jnp.minimum(g, last))),
            ],
            scratch_shapes=[pltpu.VMEM((rows, width + ext * tile), jnp.bfloat16)],
        ),
        out_shape=[
            jax.ShapeDtypeStruct((width, share), jnp.bfloat16),
            jax.ShapeDtypeStruct((2, width), jnp.float32),
        ],
        compiler_params=pltpu.CompilerParams(vmem_limit_bytes=VMEM_BYTES),
    )(s_pos, normed, sparse, jnp.broadcast_to(targets[None, :], (16, rows)))


def newton_body(
    blocks, tile, share, sp_count, chunk, block_rows,
    pos_ref, packed_ref, rcol_ref, rrow_ref, y_ref, inv_ref, w_ref, dense, prod,
):
    step = pl.program_id(0)
    width = blocks * tile
    half = blocks // 2
    p_steps = width // chunk
    my_cols = pl.ds(pl.multiple_of(pos_ref[1] * tile, tile), tile)

    @pl.when(step < blocks)
    def _():
        rows = pl.ds(pl.multiple_of(step * tile, tile), tile)
        for s in range(sp_count):
            for q in range(share // LANES):
                offset = s * share + q * LANES
                if offset >= (half + 1) * tile:
                    continue
                col = lax.rem(step * tile + offset, width)
                cols = pl.ds(pl.multiple_of(col, LANES), LANES)
                block = packed_ref[s * tile : (s + 1) * tile, q * LANES : (q + 1) * LANES]
                dense[rows, cols] = block
                if tile <= offset < half * tile:
                    dense[cols, rows] = block.T

    @pl.when((step >= blocks) & (step < blocks + p_steps))
    def _():
        rows = pl.ds(pl.multiple_of((step - blocks) * chunk, chunk), chunk)
        prod[rows, :] = jnp.dot(
            dense[rows, :], dense[:, my_cols], preferred_element_type=jnp.float32
        ).astype(jnp.bfloat16)

    @pl.when(step >= blocks + p_steps)
    def _():
        local = pl.multiple_of((step - blocks - p_steps) * chunk, chunk)
        start = pl.multiple_of(pos_ref[0] * block_rows + local, chunk)
        rows = pl.ds(start, chunk)
        cubic = jnp.dot(dense[rows, :], prod[...], preferred_element_type=jnp.float32)
        on_diag = (start + lax.broadcasted_iota(jnp.int32, (chunk, tile), 0)) == (
            pos_ref[1] * tile + lax.broadcasted_iota(jnp.int32, (chunk, tile), 1)
        )
        series = (
            jnp.where(on_diag, 1.0, 0.0)
            - dense[rows, my_cols].astype(jnp.float32)
            + prod[rows, :].astype(jnp.float32)
            - cubic
        )
        out = series * rcol_ref[rows, :] * rrow_ref[...]
        inv_ref[pl.ds(local, chunk), :] = out
        w_ref[:, pl.ds(local, chunk)] = lax.dot_general(
            y_ref[...], out, (((1,), (1,)), ((), ())),
            precision=lax.Precision.HIGHEST, preferred_element_type=jnp.float32,
        )


def newton_call(pos, packed, root_recip, rrow, y, blocks, tile, share, sp_count):
    width = blocks * tile
    block_rows = width // sp_count
    chunk = min(512, block_rows)
    grid = blocks + width // chunk + block_rows // chunk
    last = blocks - 1
    return pl.pallas_call(
        functools.partial(newton_body, blocks, tile, share, sp_count, chunk, block_rows),
        grid_spec=pltpu.PrefetchScalarGridSpec(
            num_scalar_prefetch=1,
            grid=(grid,),
            in_specs=[
                pl.BlockSpec((sp_count * tile, share), lambda g, p: (jnp.minimum(g, last), 0)),
                pl.BlockSpec((width, 1), lambda g, p: (0, 0)),
                pl.BlockSpec((1, tile), lambda g, p: (0, 0)),
                pl.BlockSpec((8, tile), lambda g, p: (0, 0)),
            ],
            out_specs=[
                pl.BlockSpec((block_rows, tile), lambda g, p: (0, 0)),
                pl.BlockSpec((8, block_rows), lambda g, p: (0, 0)),
            ],
            scratch_shapes=[
                pltpu.VMEM((width, width), jnp.bfloat16),
                pltpu.VMEM((width, tile), jnp.bfloat16),
            ],
        ),
        out_shape=[
            jax.ShapeDtypeStruct((block_rows, tile), jnp.float32),
            jax.ShapeDtypeStruct((8, block_rows), jnp.float32),
        ],
        compiler_params=pltpu.CompilerParams(vmem_limit_bytes=VMEM_BYTES),
    )(pos, packed, root_recip[:, None], rrow[None, :], jnp.broadcast_to(y[None, :], (8, tile)))


def add_body(count, in_ref, out_ref, slots, send_sem, recv_sem):
    me = lax.axis_index("obs")
    barrier = pltpu.get_barrier_semaphore()
    for k in range(1, count):
        pl.semaphore_signal(
            barrier, inc=1, device_id={"obs": lax.rem(me + k, count)}, device_id_type=pl.DeviceIdType.MESH
        )
    pl.semaphore_wait(barrier, count - 1)
    copies = []
    for k in range(1, count):
        copy = pltpu.make_async_remote_copy(
            src_ref=in_ref,
            dst_ref=slots.at[me],
            send_sem=send_sem.at[k],
            recv_sem=recv_sem.at[k],
            device_id={"obs": lax.rem(me + k, count)},
            device_id_type=pl.DeviceIdType.MESH,
        )
        copy.start()
        copies.append(copy)
    slots[me] = in_ref[...]
    for copy in copies:
        copy.wait()
    total = slots[0]
    for k in range(1, count):
        total = total + slots[k]
    out_ref[...] = total


def add_over_obs(values, count, collective_id):
    shape = values.shape
    flat = values.reshape(values.size // LANES, LANES)
    total = pl.pallas_call(
        functools.partial(add_body, count),
        out_shape=jax.ShapeDtypeStruct(flat.shape, flat.dtype),
        in_specs=[pl.BlockSpec(memory_space=pltpu.VMEM)],
        out_specs=pl.BlockSpec(memory_space=pltpu.VMEM),
        scratch_shapes=[
            pltpu.VMEM((count,) + flat.shape, flat.dtype),
            pltpu.SemaphoreType.DMA((count,)),
            pltpu.SemaphoreType.DMA((count,)),
        ],
        cost_estimate=pl.CostEstimate(
            flops=count * flat.size, bytes_accessed=400 * flat.size, transcendentals=0
        ),
        compiler_params=pltpu.CompilerParams(collective_id=collective_id, has_side_effects=True),
    )(flat)
    return total.reshape(shape)


def spread_keys(z_count, sp_count):
    keys = [("z", k) for k in range(1, z_count)]
    for k in range(z_count):
        keys += [("x", k), ("core", k), ("core_x", k)]
        for d in range(1, sp_count):
            keys += [(name, k, d) for name in ("sp", "sp_a", "x_b", "core_sp", "core_a", "core_b")]
    return {key: place for place, key in enumerate(keys)}


def spread_body(z_count, sp_count, in_ref, out_ref, send_sem, recv_sem, own_sem):
    places = spread_keys(z_count, sp_count)
    obs = lax.axis_index("obs")
    s = lax.axis_index("sp")
    z, x, c = lax.div(obs, 4), lax.rem(lax.div(obs, 2), 2), lax.rem(obs, 2)
    half = in_ref.shape[0] // 2
    upper, lower = pl.ds(0, half), pl.ds(half, half)
    zs = [lax.bitwise_xor(z, k) for k in range(z_count)]
    to_sp = [lax.rem(s + d, sp_count) for d in range(sp_count)]
    from_sp = [lax.rem(s - d + sp_count, sp_count) for d in range(sp_count)]

    def device(z_to, x_to, c_to, s_to):
        return {"obs": z_to * 4 + x_to * 2 + c_to, "sp": s_to}

    def slot(z_of, x_of, s_of):
        return ((z_of * 2 + x_of) * 2 + c) * sp_count + s_of

    own_slot = slot(z, x, s)
    across, sibling = device(z, 1 - x, c, s), device(z, x, 1 - c, s)
    others = [device(zs[k], x, c, s) for k in range(1, z_count)]
    others += [device(z, x, c, to_sp[d]) for d in range(1, sp_count)]
    others += [across, sibling]
    barrier = pltpu.get_barrier_semaphore()
    for other in others:
        pl.semaphore_signal(barrier, inc=1, device_id=other, device_id_type=pl.DeviceIdType.MESH)
    pl.semaphore_wait(barrier, len(others))

    sent = {}

    def send(key, place, target, rows=None, own=False):
        src = in_ref if own else out_ref.at[place]
        dst = out_ref.at[place]
        if rows is not None:
            src, dst = src.at[rows], dst.at[rows]
        copy = pltpu.make_async_remote_copy(
            src_ref=src,
            dst_ref=dst,
            send_sem=send_sem.at[places[key]],
            recv_sem=recv_sem.at[places[key]],
            device_id=target,
            device_id_type=pl.DeviceIdType.MESH,
        )
        copy.start()
        sent[key] = copy

    keep = pltpu.make_async_copy(in_ref, out_ref.at[own_slot], own_sem)
    keep.start()
    for k in range(1, z_count):
        send(("z", k), own_slot, others[k - 1], own=True)

    def fan_out(k):
        place = slot(zs[k], x, s)
        send(("x", k), place, across, own=k == 0)
        for d in range(1, sp_count):
            send(("sp", k, d), place, device(z, x, c, to_sp[d]), own=k == 0)
        send(("core", k), place, sibling, own=k == 0)

    def relay(k):
        sent[("x", k)].wait_recv()
        place = slot(zs[k], 1 - x, s)
        for d in range(1, sp_count):
            send(("sp_a", k, d), place, device(z, x, c, to_sp[d]), upper)
        send(("core_x", k), place, sibling)
        for d in range(1, sp_count):
            sent[("sp", k, d)].wait_recv()
            place = slot(zs[k], x, from_sp[d])
            send(("x_b", k, d), place, across, lower)
            send(("core_sp", k, d), place, sibling)

    def finish(k):
        for d in range(1, sp_count):
            place = slot(zs[k], 1 - x, from_sp[d])
            sent[("sp_a", k, d)].wait_recv()
            send(("core_a", k, d), place, sibling, upper)
            sent[("x_b", k, d)].wait_recv()
            send(("core_b", k, d), place, sibling, lower)

    fan_out(0)
    for k in range(1, z_count):
        sent[("z", k)].wait_recv()
        fan_out(k)
        relay(k - 1)
        if k > 1:
            finish(k - 2)
    relay(z_count - 1)
    if z_count > 1:
        finish(z_count - 2)
    finish(z_count - 1)
    keep.wait()
    for key, copy in sent.items():
        copy.wait_send()
        if key[0].startswith("core"):
            copy.wait_recv()


def spread(shard, obs_count, sp_count, collective_id):
    rows, cols = shard.shape
    z_count = obs_count // 4
    total = obs_count * sp_count
    sems = len(spread_keys(z_count, sp_count))
    gathered = pl.pallas_call(
        functools.partial(spread_body, z_count, sp_count),
        out_shape=jax.ShapeDtypeStruct((total, rows, cols), shard.dtype),
        in_specs=[pl.BlockSpec(memory_space=pl.ANY)],
        out_specs=pl.BlockSpec(memory_space=pl.ANY),
        scratch_shapes=[
            pltpu.SemaphoreType.DMA((sems,)),
            pltpu.SemaphoreType.DMA((sems,)),
            pltpu.SemaphoreType.DMA,
        ],
        compiler_params=pltpu.CompilerParams(collective_id=collective_id, has_side_effects=True),
    )(shard)
    return gathered.reshape(total * rows, cols)


def position():
    obs = lax.axis_index("obs")
    return lax.div(obs, 4), lax.rem(lax.div(obs, 2), 2), lax.rem(obs, 2), lax.axis_index("sp")


def device(z, x, c, s):
    return {"obs": z * 4 + x * 2 + c, "sp": s}


def remote(src, dst, send_sem, recv_sem, target):
    return pltpu.make_async_remote_copy(
        src_ref=src, dst_ref=dst, send_sem=send_sem, recv_sem=recv_sem,
        device_id=target, device_id_type=pl.DeviceIdType.MESH,
    )


def route_sems(z_count):
    return [
        pltpu.SemaphoreType.DMA((z_count + 1,)),
        pltpu.SemaphoreType.DMA((z_count,)),
        pltpu.SemaphoreType.DMA((9 * z_count,)),
        pltpu.SemaphoreType.DMA((9 * z_count,)),
    ]


def route_greet(z_count):
    z, x, c, s = position()
    barrier = pltpu.get_barrier_semaphore()
    others = [device(z, 1 - x, c, s), device(z, x, 1 - c, s), device(z, x, c, 1 - s)]
    others += [device(lax.rem(z + k, z_count), x, c, s) for k in range(1, z_count)]
    for other in others:
        pl.semaphore_signal(barrier, inc=1, device_id=other, device_id_type=pl.DeviceIdType.MESH)
    pl.semaphore_wait(barrier, len(others))


def route(z_count, in_ref, out_ref, z_send, z_recv, send_sem, recv_sem, arrive, begin=None, late=None):
    z, x, c, s = position()
    last = z_count - 1
    half = in_ref.shape[0] // 2
    upper, lower = pl.ds(0, half), pl.ds(half, half)
    across, beside, sibling = device(z, 1 - x, c, s), device(z, x, c, 1 - s), device(z, x, 1 - c, s)

    def slot(z_of, x_of, c_of, s_of):
        return ((z_of * 2 + x_of) * 2 + c_of) * 2 + s_of

    nearer = jnp.minimum(z, last - z)
    origins = [z]
    for a in range(last):
        both = jnp.where(a % 2 == 0, z - (a // 2 + 1), z + (a // 2 + 1))
        single = jnp.where(z <= last - z, z + (a - nearer + 1), z - (a - nearer + 1))
        origins.append(jnp.where(a < 2 * nearer, both, single))

    sent = {}

    def send(key, src, place, target, rows=None):
        dst = out_ref.at[place]
        if rows is not None:
            src, dst = src.at[rows], dst.at[rows]
        n = len(sent)
        sent[key] = remote(src, dst, send_sem.at[n], recv_sem.at[n], target)
        sent[key].start()

    def hop(src, origin, sem, target_z):
        return remote(
            src, out_ref.at[slot(origin, x, c, s)], z_send.at[sem], z_recv.at[origin], device(target_z, x, c, s)
        )

    hops = []

    def start_hop(when, copy):
        pl.when(when)(copy.start)
        hops.append((when, copy))

    start_hop(z < last, hop(in_ref, z, 0, jnp.minimum(z + 1, last)))
    start_hop(z > 0, hop(in_ref, z, 1, jnp.maximum(z - 1, 0)))

    def fan_out(a, src):
        place = slot(origins[a], x, c, s)
        send(("x", a), src, place, across)
        send(("y", a), src, place, beside)
        send(("core", a), src, place, sibling)

    def relay(a):
        sent[("x", a)].wait_recv()
        place = slot(origins[a], 1 - x, c, s)
        send(("ya", a), out_ref.at[place], place, beside, upper)
        send(("core_x", a), out_ref.at[place], place, sibling)
        arrive(out_ref.at[place], place)
        sent[("y", a)].wait_recv()
        place = slot(origins[a], x, c, 1 - s)
        send(("xb", a), out_ref.at[place], place, across, lower)
        send(("core_y", a), out_ref.at[place], place, sibling)
        arrive(out_ref.at[place], place)

    def finish(a):
        place = slot(origins[a], 1 - x, c, 1 - s)
        sent[("ya", a)].wait_recv()
        send(("core_a", a), out_ref.at[place], place, sibling, upper)
        sent[("xb", a)].wait_recv()
        send(("core_b", a), out_ref.at[place], place, sibling, lower)
        arrive(out_ref.at[place], place)

    def from_sibling(a, keys, x_of, s_of):
        for key in keys:
            sent[(key, a)].wait_recv()
        place = slot(origins[a], x_of, 1 - c, s_of)
        arrive(out_ref.at[place], place)

    fan_out(0, in_ref)
    if begin is not None:
        begin()
    arrive(in_ref, slot(z, x, c, s))
    for a in range(1, z_count + 3):
        if a < z_count:
            origin = origins[a]
            place = slot(origin, x, c, s)
            held = out_ref.at[place]
            rising = origin < z
            target_z = jnp.where(rising, z + 1, z - 1)
            remote(held, held, z_send.at[0], z_recv.at[origin], across).wait_recv()
            start_hop(
                (target_z >= 0) & (target_z <= last), hop(held, origin, a + 1, jnp.clip(target_z, 0, last))
            )
            fan_out(a, held)
            arrive(held, place)
        if a - 1 < z_count:
            relay(a - 1)
            from_sibling(a - 1, ("core",), x, s)
        if a == 2 and late is not None:
            late()
        if 0 <= a - 2 < z_count:
            finish(a - 2)
            from_sibling(a - 2, ("core_x",), 1 - x, s)
            from_sibling(a - 2, ("core_y",), x, 1 - s)
        if 0 <= a - 3 < z_count:
            from_sibling(a - 3, ("core_a", "core_b"), 1 - x, 1 - s)
    for copy in sent.values():
        copy.wait_send()
    for when, copy in hops:
        pl.when(when)(copy.wait_send)


def share_body(z_count, own_ref, own_slab, out_ref, slab_ref, z_send, z_recv, send_sem, recv_sem, slab_send, slab_recv, keep_sem):
    z, x, c, s = position()
    q, q_across = x * 2 + c, (1 - x) * 2 + c
    half = own_slab.shape[0] // 2
    near, far = pl.ds(pl.multiple_of(s * half, 16), half), pl.ds(pl.multiple_of((1 - s) * half, 16), half)
    route_greet(z_count)
    keep = pltpu.make_async_copy(own_ref, out_ref.at[((z * 2 + x) * 2 + c) * 2 + s], keep_sem.at[0])
    keep_slab = pltpu.make_async_copy(own_slab, slab_ref.at[q], keep_sem.at[1])
    keep.start()
    keep_slab.start()
    shared = []

    def share(src, place, piece, target):
        n = len(shared)
        dst = slab_ref.at[place]
        if piece is not None:
            src, dst = src.at[piece], dst.at[piece]
        shared.append(remote(src, dst, slab_send.at[n], slab_recv.at[n], target))
        shared[-1].start()

    def begin():
        share(own_slab, q, near, device(z, 1 - x, c, s))
        share(own_slab, q, None, device(z, x, 1 - c, s))

    def late():
        shared[0].wait_recv()
        share(slab_ref.at[q_across], q_across, near, device(z, x, c, 1 - s))
        share(slab_ref.at[q_across], q_across, near, device(z, x, 1 - c, s))

    route(
        z_count, own_ref, out_ref, z_send, z_recv, send_sem, recv_sem, lambda src, place: None, begin, late
    )
    shared[2].wait_recv()
    share(slab_ref.at[q_across], q_across, far, device(z, x, 1 - c, s))
    for n in (1, 3, 4):
        shared[n].wait_recv()
    for copy in shared:
        copy.wait_send()
    keep.wait()
    keep_slab.wait()


def share(own, own_slab, z_count, collective_id):
    anywhere = pl.BlockSpec(memory_space=pl.ANY)
    return pl.pallas_call(
        functools.partial(share_body, z_count),
        out_shape=[
            jax.ShapeDtypeStruct((8 * z_count,) + own.shape, own.dtype),
            jax.ShapeDtypeStruct((4,) + own_slab.shape, own_slab.dtype),
        ],
        in_specs=[anywhere, anywhere],
        out_specs=[anywhere, anywhere],
        scratch_shapes=route_sems(z_count)
        + [pltpu.SemaphoreType.DMA((5,)), pltpu.SemaphoreType.DMA((5,)), pltpu.SemaphoreType.DMA((2,))],
        compiler_params=pltpu.CompilerParams(collective_id=collective_id, has_side_effects=True),
    )(own, own_slab)


def series_body(
    z_count, strip, tile, chunk, normalizer,
    part_ref, sums_ref, reg_ref, inv_ref, w_ref, gathered,
    dense, first, second, stage, recip, spread_recip, out_buf, w_own, w_slots,
    z_send, z_recv, send_sem, recv_sem, stage_sem, out_sem, w_send, w_recv,
):
    z, x, c, s = position()
    obs = lax.axis_index("obs")
    obs_count = 4 * z_count
    strips = 8 * z_count
    width = strips * strip
    half = strips // 2
    span = part_ref.shape[1]
    block_rows = width // 2
    lines = tile // LANES
    fold = 1.0 / normalizer

    barrier = pltpu.get_barrier_semaphore()
    peers = [
        {"obs": lax.rem(obs + k, obs_count), "sp": s} for k in range(1, obs_count)
    ]
    for peer in peers + [device(z, x, c, 1 - s)]:
        pl.semaphore_signal(barrier, inc=1, device_id=peer, device_id_type=pl.DeviceIdType.MESH)
    pl.semaphore_wait(barrier, obs_count)

    slots = stage.shape[0]
    waiting = []

    def lay_out(n):
        copy, place = waiting[n]
        copy.wait()
        place = lax.rem(place, 8) * z_count + lax.div(place, 8)
        rows = pl.ds(pl.multiple_of(place * strip, strip), strip)

        def put(k, turn):
            cols = pl.ds(pl.multiple_of(lax.rem(place + k, strips) * strip, strip), strip)
            block = stage[n % slots, :, pl.ds(pl.multiple_of(k * strip, strip), strip)]
            dense[rows, cols] = block
            if turn:
                dense[cols, rows] = block.T

        put(0, False)
        put(half, False)

        @pl.loop(0, half // 4)
        def _(m):
            for k in range(4):
                pl.when(m * 4 + k > 0)(lambda k=k: put(m * 4 + k, True))

    def arrive(src, place):
        n = len(waiting)
        if n >= slots:
            lay_out(n - slots)
        copy = pltpu.make_async_copy(src, stage.at[n % slots], stage_sem.at[n % slots])
        copy.start()
        waiting.append((copy, place))

    def begin():
        per = sums_ref.shape[1] // 2
        for p in range(sums_ref.shape[0]):
            lane = slice(p * per, (p + 1) * per)
            recip[lane, :] = 1.0 / (sums_ref[p, per:, :] * fold + reg_ref[lane, :])

        @pl.loop(0, width // LANES)
        def _(m):
            row = jnp.broadcast_to(recip[pl.ds(m, 1), :], (LANES, LANES))
            spread_recip[pl.ds(pl.multiple_of(m * LANES, LANES), LANES), :] = row.T

    route(z_count, part_ref, gathered, z_send, z_recv, send_sem, recv_sem, arrive, begin)
    for n in range(len(waiting) - slots, len(waiting)):
        lay_out(n)

    my_cols = pl.ds(pl.multiple_of(obs * tile, tile), tile)

    def by_row(values, rows):
        scale = spread_recip[rows, :]
        return values * jnp.concatenate([scale] * lines, axis=1)

    @pl.loop(0, width // chunk)
    def _(m):
        rows = pl.ds(pl.multiple_of(m * chunk, chunk), chunk)
        first[rows, :] = by_row(dense[rows, my_cols].astype(jnp.float32) * fold, rows).astype(jnp.bfloat16)

    @pl.loop(0, width // chunk)
    def _(m):
        rows = pl.ds(pl.multiple_of(m * chunk, chunk), chunk)
        prod = jnp.dot(dense[rows, :], first[...], preferred_element_type=jnp.float32)
        second[rows, :] = by_row(prod * fold, rows).astype(jnp.bfloat16)

    def my_lines(ref, at):
        return jnp.concatenate([ref[pl.ds(at + h, 1), :] for h in range(lines)], axis=1)

    per = sums_ref.shape[1] // 2
    r_row = my_lines(recip, obs * lines)
    y = my_lines(sums_ref.at[lax.div(obs * lines, per)], lax.rem(obs * lines, per))
    y = jnp.broadcast_to(y * (1.0 / math.sqrt(normalizer)), (8, tile))

    def emit(m):
        return pltpu.make_async_copy(
            out_buf.at[m], inv_ref.at[pl.ds(pl.multiple_of(m * chunk, chunk), chunk)], out_sem.at[m]
        )

    @pl.loop(0, block_rows // chunk)
    def _(m):
        begin_at = s * block_rows + m * chunk
        rows = pl.ds(pl.multiple_of(begin_at, chunk), chunk)
        cubic = jnp.dot(dense[rows, :], second[...], preferred_element_type=jnp.float32)
        on_diag = (begin_at + lax.broadcasted_iota(jnp.int32, (chunk, tile), 0)) == (
            obs * tile + lax.broadcasted_iota(jnp.int32, (chunk, tile), 1)
        )
        series = second[rows, :].astype(jnp.float32) - by_row(
            (dense[rows, my_cols].astype(jnp.float32) + cubic) * fold, rows
        )
        out = (jnp.where(on_diag, 1.0, 0.0) + series) * r_row
        out_buf[m] = out
        emit(m).start()
        part_w = lax.dot_general(
            y, out, (((1,), (1,)), ((), ())),
            precision=lax.Precision.HIGHEST, preferred_element_type=jnp.float32,
        )
        for h in range(chunk // LANES):
            w_own[pl.ds(m * (chunk // LANES) + h, 1), :] = part_w[0:1, h * LANES : (h + 1) * LANES]

    copies = []
    for k in range(1, obs_count):
        copies.append(remote(w_own, w_slots.at[obs], w_send.at[k], w_recv.at[k], peers[k - 1]))
        copies[-1].start()
    w_slots[obs] = w_own[...]
    for copy in copies:
        copy.wait()
    total = w_slots[0]
    for k in range(1, obs_count):
        total = total + w_slots[k]
    w_ref[...] = total
    for m in range(block_rows // chunk):
        emit(m).wait()


def series_tile(part, sums, regularizer, z_count, tile, normalizer, collective_id):
    strip, span = part.shape
    strips = 8 * z_count
    width = strips * strip
    block_rows = width // 2
    chunk = min(512, block_rows)
    obs_count = 4 * z_count
    w_shape = (block_rows // LANES, LANES)
    anywhere = pl.BlockSpec(memory_space=pl.ANY)
    vmem = pl.BlockSpec(memory_space=pltpu.VMEM)
    inverse_tile, weights, _ = pl.pallas_call(
        functools.partial(series_body, z_count, strip, tile, chunk, normalizer),
        out_shape=[
            jax.ShapeDtypeStruct((block_rows, tile), jnp.float32),
            jax.ShapeDtypeStruct(w_shape, jnp.float32),
            jax.ShapeDtypeStruct((strips, strip, span), part.dtype),
        ],
        in_specs=[anywhere, vmem, vmem],
        out_specs=[anywhere, vmem, anywhere],
        scratch_shapes=[
            pltpu.VMEM((width, width), jnp.bfloat16),
            pltpu.VMEM((width, tile), jnp.bfloat16),
            pltpu.VMEM((width, tile), jnp.bfloat16),
            pltpu.VMEM((2, strip, span), jnp.bfloat16),
            pltpu.VMEM((width // LANES, LANES), jnp.float32),
            pltpu.VMEM((width, LANES), jnp.float32),
            pltpu.VMEM((block_rows // chunk, chunk, tile), jnp.float32),
            pltpu.VMEM(w_shape, jnp.float32),
            pltpu.VMEM((obs_count,) + w_shape, jnp.float32),
        ]
        + route_sems(z_count)
        + [
            pltpu.SemaphoreType.DMA((2,)),
            pltpu.SemaphoreType.DMA((block_rows // chunk,)),
            pltpu.SemaphoreType.DMA((obs_count,)),
            pltpu.SemaphoreType.DMA((obs_count,)),
        ],
        compiler_params=pltpu.CompilerParams(
            collective_id=collective_id, has_side_effects=True, vmem_limit_bytes=VMEM_BYTES
        ),
    )(part, sums, regularizer.reshape(width // LANES, LANES))
    return inverse_tile, weights.reshape(block_rows)


def by_strips(descriptors, candidates, sparse_index, targets, regularizer):
    obs_count = lax.axis_size("obs")
    sp_count = lax.axis_size("sp")
    obs_pos = lax.axis_index("obs")
    sp_pos = lax.axis_index("sp")
    z_count = obs_count // 4
    width = sparse_index.shape[0]
    tile = width // obs_count
    strip = width // (obs_count * sp_count)
    mine = strip * z_count
    span = width // 2 + strip
    window = width // 2 + mine
    rows, depth = descriptors.shape
    normalizer = 24.0 * rows * obs_count

    extra = jnp.pad(targets.reshape(rows // depth, depth), ((0, 32 - rows // depth), (0, 0)))
    shard = jnp.concatenate([unit_rows(descriptors), extra])
    piece = candidates.shape[0] // sp_count
    own = lax.dynamic_slice_in_dim(candidates, sp_pos * piece, piece)
    table, slab = share(unit_rows(own), shard, z_count, 2)
    table = table.reshape(-1, depth)
    place = lax.rem(obs_pos, 4) * sp_count + sp_pos
    wanted = lax.dynamic_slice_in_dim(
        jnp.concatenate([sparse_index, sparse_index]), place * mine, window
    )
    sparse = table.at[wanted].get(mode="promise_in_bounds")
    slab_targets = slab[:, rows : rows + rows // depth].reshape(4 * rows)
    part, sums = slab_gram(
        slab, sparse, slab_targets, z_count, sp_count, strip, span, tile, rows, 0
    )
    return series_tile(part, sums, regularizer, z_count, tile, normalizer, 3)


def slab_body(z_count, sp_count, strip, tile, root, *refs):
    norm_ref, sp_ref, tgt_ref, part_ref, sums_ref = refs[:5]
    kbuf, ktr, parts, from_low, from_high, zsums, gsums = refs[5:12]
    up_send, up_recv, down_send, down_recv, zs_send, zs_recv, gs_send, gs_recv = refs[12:]
    obs = lax.axis_index("obs")
    s = lax.axis_index("sp")
    z, q = lax.div(obs, 4), lax.rem(obs, 4)
    group = 4 * sp_count
    p = q * sp_count + s
    last = z_count - 1
    shard = tgt_ref.shape[1] // 4
    mine = strip * z_count
    lines = mine // LANES

    z_others = [{"obs": lax.rem(z + k, z_count) * 4 + q, "sp": s} for k in range(1, z_count)]
    group_others = []
    for k in range(1, group):
        to = lax.rem(p + k, group)
        group_others.append({"obs": z * 4 + lax.div(to, sp_count), "sp": lax.rem(to, sp_count)})
    barrier = pltpu.get_barrier_semaphore()
    for other in z_others + group_others:
        pl.semaphore_signal(barrier, inc=1, device_id=other, device_id_type=pl.DeviceIdType.MESH)
    pl.semaphore_wait(barrier, len(z_others) + len(group_others))

    def kernel_tile(t, own):
        cols = pl.ds(pl.multiple_of(t * tile, tile), tile)
        for k in range(4):
            rows = pl.ds(k * shard, shard)
            inner = lax.dot_general(
                norm_ref[k, :shard, :], sp_ref[cols, :], (((1,), (1,)), ((), ())),
                preferred_element_type=jnp.float32,
            )
            scaled = inner * root
            squared = scaled * scaled
            kb = ((squared - 6.0) * squared + 3.0).astype(jnp.bfloat16)
            kbuf[rows, cols] = kb
            if own:
                ktr[cols, rows] = kb.T

    def row_sums():
        for t in range(mine // tile):
            cols = slice(t * tile, (t + 1) * tile)
            weighted = jnp.dot(tgt_ref[...], kbuf[:, cols], preferred_element_type=jnp.float32)
            square = jnp.zeros((1, tile), jnp.float32)
            for k in range(4):
                kf = kbuf[k * shard : (k + 1) * shard, cols].astype(jnp.float32)
                square = square + jnp.sum(kf * kf, axis=0, keepdims=True)
            for h in range(tile // LANES):
                line = t * (tile // LANES) + h
                lane = slice(h * LANES, (h + 1) * LANES)
                zsums[z, line : line + 1, :] = weighted[0:1, lane]
                zsums[z, lines + line : lines + line + 1, :] = square[:, lane]

    groups = kbuf.shape[1] // mine

    def piece(t, g):
        begin = t * strip if g == 0 else 0
        end = mine if g < groups - 1 else (t + 1) * strip
        return begin, g * mine + begin - t * strip, end - begin

    def cut(t, g):
        _, begin, size = piece(t, g)
        return pl.ds(begin, size)

    def up(t, g):
        n, at = t * groups + g, (t, slice(None), cut(t, g))
        return remote(
            parts.at[at], from_low.at[at], up_send.at[n], up_recv.at[n],
            {"obs": lax.rem(z + 1, z_count) * 4 + q, "sp": s},
        )

    def down(t, g):
        n, at = t * groups + g, (t, slice(None), cut(t, g))
        return remote(
            parts.at[at], from_high.at[at], down_send.at[n], down_recv.at[n],
            {"obs": lax.rem(z + last, z_count) * 4 + q, "sp": s},
        )

    def gram_group(g):
        cols = slice(g * mine, (g + 1) * mine)
        made = jnp.dot(ktr[...], kbuf[:, cols], preferred_element_type=jnp.float32).astype(jnp.bfloat16)
        for t in range(z_count):
            begin, at, size = piece(t, g)
            parts[t, :, at : at + size] = made[t * strip : (t + 1) * strip, begin : begin + size]

    def pass_on(place, n):
        if 0 <= n - place < groups:
            for t in range(last, place, -1):
                g = n - place
                up(t, g).wait_recv()
                parts[t, :, cut(t, g)] = parts[t, :, cut(t, g)] + from_low[t, :, cut(t, g)]
                up(t, g).start()
        if 0 <= n - (last - place) < groups:
            for t in range(place):
                g = n - (last - place)
                down(t, g).wait_recv()
                parts[t, :, cut(t, g)] = parts[t, :, cut(t, g)] + from_high[t, :, cut(t, g)]
                down(t, g).start()

    z_copies, g_copies = [], []
    for n in range(groups + last - 1):
        if n < groups:

            @pl.loop(n * mine // tile, (n + 1) * mine // tile)
            def _(t):
                kernel_tile(t, n == 0)

            gram_group(n)

            @pl.when(z == 0)
            def _():
                for t in range(last, 0, -1):
                    up(t, n).start()

            @pl.when(z == last)
            def _():
                for t in range(last):
                    down(t, n).start()

        if n == 0:
            row_sums()
            for k in range(1, z_count):
                z_copies.append(remote(zsums.at[z], zsums.at[z], zs_send.at[k], zs_recv.at[k], z_others[k - 1]))
                z_copies[-1].start()
        if n == 1:
            for copy in z_copies:
                copy.wait_recv()
            total = zsums[0]
            for m in range(1, z_count):
                total = total + zsums[m]
            gsums[p] = total
            for m in range(1, group):
                g_copies.append(
                    remote(gsums.at[p], gsums.at[p], gs_send.at[m], gs_recv.at[m], group_others[m - 1])
                )
                g_copies[-1].start()
        for place in range(1, last):
            pl.when(z == place)(functools.partial(pass_on, place, n))

    def finish(place):
        for g in range(groups):
            total = parts[place, :, cut(place, g)].astype(jnp.float32)
            if place > 0:
                up(place, g).wait_recv()
                total = total + from_low[place, :, cut(place, g)].astype(jnp.float32)
            if place < last:
                down(place, g).wait_recv()
                total = total + from_high[place, :, cut(place, g)].astype(jnp.float32)
            if g == 0:
                row = lax.broadcasted_iota(jnp.int32, total.shape, 0)
                col = lax.broadcasted_iota(jnp.int32, total.shape, 1)
                total = jnp.where(row == col, 0.0, total)
            part_ref[:, cut(place, g)] = total.astype(jnp.bfloat16)
        for t in range(z_count):
            for g in range(groups):
                if t > place:
                    up(t, g).wait_send()
                if t < place:
                    down(t, g).wait_send()

    for place in range(z_count):
        pl.when(z == place)(functools.partial(finish, place))

    for copy in g_copies:
        copy.wait()
    for copy in z_copies:
        copy.wait_send()
    sums_ref[...] = gsums[...]


def slab_gram(slab, sparse, targets, z_count, sp_count, strip, span, tile, rows, collective_id):
    depth = slab.shape[2]
    window = sparse.shape[0]
    group = 4 * sp_count
    mine = strip * z_count
    lines = 2 * mine // LANES
    pieces = z_count * (window // mine)
    vmem = pl.BlockSpec(memory_space=pltpu.VMEM)
    part = (z_count, strip, span)
    sems = [pltpu.SemaphoreType.DMA((pieces,))] * 4
    sems += [pltpu.SemaphoreType.DMA((z_count,))] * 2 + [pltpu.SemaphoreType.DMA((group,))] * 2
    return pl.pallas_call(
        functools.partial(slab_body, z_count, sp_count, strip, tile, math.sqrt(depth)),
        out_shape=[
            jax.ShapeDtypeStruct((strip, span), jnp.bfloat16),
            jax.ShapeDtypeStruct((group, lines, LANES), jnp.float32),
        ],
        in_specs=[vmem, vmem, vmem],
        out_specs=[vmem, vmem],
        scratch_shapes=[
            pltpu.VMEM((4 * rows, window), jnp.bfloat16),
            pltpu.VMEM((mine, 4 * rows), jnp.bfloat16),
            pltpu.VMEM(part, jnp.bfloat16),
            pltpu.VMEM(part, jnp.bfloat16),
            pltpu.VMEM(part, jnp.bfloat16),
            pltpu.VMEM((z_count, lines, LANES), jnp.float32),
            pltpu.VMEM((group, lines, LANES), jnp.float32),
        ] + sems,
        compiler_params=pltpu.CompilerParams(
            collective_id=collective_id, has_side_effects=True, vmem_limit_bytes=VMEM_BYTES
        ),
    )(slab, sparse, jnp.broadcast_to(targets[None, :], (16, 4 * rows)))


def on_device(descriptors, candidates, sparse_index, targets, regularizer):
    obs_count = lax.axis_size("obs")
    sp_count = lax.axis_size("sp")
    obs_pos = lax.axis_index("obs")
    sp_pos = lax.axis_index("sp")
    width = sparse_index.shape[0]
    if sp_count == 2 and width % (obs_count * sp_count * LANES) == 0:
        return by_strips(descriptors, candidates, sparse_index, targets, regularizer)
    tile = width // obs_count
    share = -(-((obs_count // 2 + 1) * tile) // (sp_count * LANES)) * LANES
    normalizer = 24.0 * descriptors.shape[0] * obs_count

    normed = unit_rows(descriptors)
    piece = candidates.shape[0] // sp_count
    own = lax.dynamic_slice_in_dim(candidates, sp_pos * piece, piece)
    table = spread(unit_rows(own), obs_count, sp_count, 2)
    sparse = table.at[sparse_index].get(mode="promise_in_bounds")

    gram, sums = gram_call(
        sp_pos[None].astype(jnp.int32), normed, sparse, targets, obs_count, tile, share, sp_count
    )
    sums = add_over_obs(sums, obs_count, 0)
    part = lax.psum_scatter(gram, "obs", scatter_dimension=0, tiled=True)

    projected = sums[0] / math.sqrt(normalizer)
    root = lax.rsqrt(sums[1] / normalizer + regularizer)
    col_start = obs_pos * tile
    rrow = lax.dynamic_slice_in_dim(root, col_start, tile)
    window_start = col_start + sp_pos * share
    rwin = lax.dynamic_slice_in_dim(jnp.concatenate([root, root]), window_start, share)
    offset = sp_pos * share + lax.iota(jnp.int32, share)
    on_diag = lax.iota(jnp.int32, tile)[:, None] == offset[None, :]
    scaled = jnp.where(
        on_diag, 0.0, part.astype(jnp.float32) * (rrow[:, None] / normalizer) * rwin[None, :]
    ).astype(jnp.bfloat16)
    packed = spread(scaled, obs_count, sp_count, 3)

    y = lax.dynamic_slice_in_dim(projected, col_start, tile)
    pos = jnp.stack([sp_pos, obs_pos]).astype(jnp.int32)
    inverse_tile, part_w = newton_call(
        pos, packed, root, rrow, y, obs_count, tile, share, sp_count
    )
    return inverse_tile, add_over_obs(part_w[0], obs_count, 1)


def solution(mesh):
    in_specs = (P("obs", None), P("obs", None), P(), P("obs"), P())
    out_specs = (P("sp", "obs"), P("sp"))
    return jax.shard_map(
        on_device, mesh=mesh, in_specs=in_specs, out_specs=out_specs, check_vma=False
    )
```

```python
import functools
import math

import jax
import jax.numpy as jnp
from jax import lax
from jax.experimental import pallas as pl
from jax.experimental.pallas import tpu as pltpu
from jax.sharding import PartitionSpec as P

epsilon = 1e-06
LANES = 128
VMEM_BYTES = 58 * 2**20


def unit_rows(row_block):
    values = row_block.astype(jnp.float32)
    return (values * lax.rsqrt(jnp.sum(values * values, axis=1, keepdims=True) + epsilon)).astype(
        jnp.bfloat16
    )


def gram_body(blocks, tile, share, ext, root, s_ref, norm_ref, sp_ref, tgt_ref, gram_ref, ws_ref, kext):
    step = pl.program_id(0)
    width = blocks * tile

    @pl.when(step < blocks)
    def _():
        inner = lax.dot_general(
            norm_ref[...], sp_ref[...], (((1,), (1,)), ((), ())), preferred_element_type=jnp.float32
        )
        scaled = inner * root
        squared = scaled * scaled
        kb = ((squared - 6.0) * squared + 3.0).astype(jnp.bfloat16)
        kext[:, pl.ds(pl.multiple_of(step * tile, tile), tile)] = kb

        @pl.when(step < ext)
        def _():
            kext[:, pl.ds(pl.multiple_of(width + step * tile, tile), tile)] = kb

        kf = kb.astype(jnp.float32)
        weighted = jnp.dot(tgt_ref[...], kb, preferred_element_type=jnp.float32)
        ws_ref[0:1, :] = weighted[0:1, :]
        ws_ref[1:2, :] = jnp.sum(kf * kf, axis=0, keepdims=True)

    @pl.when(step >= blocks)
    def _():
        j = step - blocks
        cols = pl.ds(pl.multiple_of(j * tile, tile), tile)
        window = pl.ds(pl.multiple_of(j * tile + s_ref[0] * share, LANES), share)
        gram_ref[...] = lax.dot_general(
            kext[:, cols], kext[:, window], (((0,), (0,)), ((), ())), preferred_element_type=jnp.float32
        ).astype(jnp.bfloat16)


def gram_call(s_pos, normed, sparse, targets, blocks, tile, share, sp_count):
    rows, depth = normed.shape
    width = blocks * tile
    ext = -(-((blocks - 1) * tile + sp_count * share - width) // tile)
    last = blocks - 1
    return pl.pallas_call(
        functools.partial(gram_body, blocks, tile, share, ext, math.sqrt(depth)),
        grid_spec=pltpu.PrefetchScalarGridSpec(
            num_scalar_prefetch=1,
            grid=(2 * blocks,),
            in_specs=[
                pl.BlockSpec((rows, depth), lambda g, s: (0, 0)),
                pl.BlockSpec((tile, depth), lambda g, s: (jnp.minimum(g, last), 0)),
                pl.BlockSpec((16, rows), lambda g, s: (0, 0)),
            ],
            out_specs=[
                pl.BlockSpec((tile, share), lambda g, s: (jnp.maximum(g - blocks, 0), 0)),
                pl.BlockSpec((2, tile), lambda g, s: (0, jnp.minimum(g, last))),
            ],
            scratch_shapes=[pltpu.VMEM((rows, width + ext * tile), jnp.bfloat16)],
        ),
        out_shape=[
            jax.ShapeDtypeStruct((width, share), jnp.bfloat16),
            jax.ShapeDtypeStruct((2, width), jnp.float32),
        ],
        compiler_params=pltpu.CompilerParams(vmem_limit_bytes=VMEM_BYTES),
    )(s_pos, normed, sparse, jnp.broadcast_to(targets[None, :], (16, rows)))


def newton_body(
    blocks, tile, share, sp_count, chunk, block_rows,
    pos_ref, packed_ref, rcol_ref, rrow_ref, y_ref, inv_ref, w_ref, dense, prod,
):
    step = pl.program_id(0)
    width = blocks * tile
    half = blocks // 2
    p_steps = width // chunk
    my_cols = pl.ds(pl.multiple_of(pos_ref[1] * tile, tile), tile)

    @pl.when(step < blocks)
    def _():
        rows = pl.ds(pl.multiple_of(step * tile, tile), tile)
        for s in range(sp_count):
            for q in range(share // LANES):
                offset = s * share + q * LANES
                if offset >= (half + 1) * tile:
                    continue
                col = lax.rem(step * tile + offset, width)
                cols = pl.ds(pl.multiple_of(col, LANES), LANES)
                block = packed_ref[s * tile : (s + 1) * tile, q * LANES : (q + 1) * LANES]
                dense[rows, cols] = block
                if tile <= offset < half * tile:
                    dense[cols, rows] = block.T

    @pl.when((step >= blocks) & (step < blocks + p_steps))
    def _():
        rows = pl.ds(pl.multiple_of((step - blocks) * chunk, chunk), chunk)
        prod[rows, :] = jnp.dot(
            dense[rows, :], dense[:, my_cols], preferred_element_type=jnp.float32
        ).astype(jnp.bfloat16)

    @pl.when(step >= blocks + p_steps)
    def _():
        local = pl.multiple_of((step - blocks - p_steps) * chunk, chunk)
        start = pl.multiple_of(pos_ref[0] * block_rows + local, chunk)
        rows = pl.ds(start, chunk)
        cubic = jnp.dot(dense[rows, :], prod[...], preferred_element_type=jnp.float32)
        on_diag = (start + lax.broadcasted_iota(jnp.int32, (chunk, tile), 0)) == (
            pos_ref[1] * tile + lax.broadcasted_iota(jnp.int32, (chunk, tile), 1)
        )
        series = (
            jnp.where(on_diag, 1.0, 0.0)
            - dense[rows, my_cols].astype(jnp.float32)
            + prod[rows, :].astype(jnp.float32)
            - cubic
        )
        out = series * rcol_ref[rows, :] * rrow_ref[...]
        inv_ref[pl.ds(local, chunk), :] = out
        w_ref[:, pl.ds(local, chunk)] = lax.dot_general(
            y_ref[...], out, (((1,), (1,)), ((), ())),
            precision=lax.Precision.HIGHEST, preferred_element_type=jnp.float32,
        )


def newton_call(pos, packed, root_recip, rrow, y, blocks, tile, share, sp_count):
    width = blocks * tile
    block_rows = width // sp_count
    chunk = min(512, block_rows)
    grid = blocks + width // chunk + block_rows // chunk
    last = blocks - 1
    return pl.pallas_call(
        functools.partial(newton_body, blocks, tile, share, sp_count, chunk, block_rows),
        grid_spec=pltpu.PrefetchScalarGridSpec(
            num_scalar_prefetch=1,
            grid=(grid,),
            in_specs=[
                pl.BlockSpec((sp_count * tile, share), lambda g, p: (jnp.minimum(g, last), 0)),
                pl.BlockSpec((width, 1), lambda g, p: (0, 0)),
                pl.BlockSpec((1, tile), lambda g, p: (0, 0)),
                pl.BlockSpec((8, tile), lambda g, p: (0, 0)),
            ],
            out_specs=[
                pl.BlockSpec((block_rows, tile), lambda g, p: (0, 0)),
                pl.BlockSpec((8, block_rows), lambda g, p: (0, 0)),
            ],
            scratch_shapes=[
                pltpu.VMEM((width, width), jnp.bfloat16),
                pltpu.VMEM((width, tile), jnp.bfloat16),
            ],
        ),
        out_shape=[
            jax.ShapeDtypeStruct((block_rows, tile), jnp.float32),
            jax.ShapeDtypeStruct((8, block_rows), jnp.float32),
        ],
        compiler_params=pltpu.CompilerParams(vmem_limit_bytes=VMEM_BYTES),
    )(pos, packed, root_recip[:, None], rrow[None, :], jnp.broadcast_to(y[None, :], (8, tile)))


def add_body(count, in_ref, out_ref, slots, send_sem, recv_sem):
    me = lax.axis_index("obs")
    barrier = pltpu.get_barrier_semaphore()
    for k in range(1, count):
        pl.semaphore_signal(
            barrier, inc=1, device_id={"obs": lax.rem(me + k, count)}, device_id_type=pl.DeviceIdType.MESH
        )
    pl.semaphore_wait(barrier, count - 1)
    copies = []
    for k in range(1, count):
        copy = pltpu.make_async_remote_copy(
            src_ref=in_ref,
            dst_ref=slots.at[me],
            send_sem=send_sem.at[k],
            recv_sem=recv_sem.at[k],
            device_id={"obs": lax.rem(me + k, count)},
            device_id_type=pl.DeviceIdType.MESH,
        )
        copy.start()
        copies.append(copy)
    slots[me] = in_ref[...]
    for copy in copies:
        copy.wait()
    total = slots[0]
    for k in range(1, count):
        total = total + slots[k]
    out_ref[...] = total


def add_over_obs(values, count, collective_id):
    shape = values.shape
    flat = values.reshape(values.size // LANES, LANES)
    total = pl.pallas_call(
        functools.partial(add_body, count),
        out_shape=jax.ShapeDtypeStruct(flat.shape, flat.dtype),
        in_specs=[pl.BlockSpec(memory_space=pltpu.VMEM)],
        out_specs=pl.BlockSpec(memory_space=pltpu.VMEM),
        scratch_shapes=[
            pltpu.VMEM((count,) + flat.shape, flat.dtype),
            pltpu.SemaphoreType.DMA((count,)),
            pltpu.SemaphoreType.DMA((count,)),
        ],
        cost_estimate=pl.CostEstimate(
            flops=count * flat.size, bytes_accessed=400 * flat.size, transcendentals=0
        ),
        compiler_params=pltpu.CompilerParams(collective_id=collective_id, has_side_effects=True),
    )(flat)
    return total.reshape(shape)


def spread_keys(z_count, sp_count):
    keys = [("z", k) for k in range(1, z_count)]
    for k in range(z_count):
        keys += [("x", k), ("core", k), ("core_x", k)]
        for d in range(1, sp_count):
            keys += [(name, k, d) for name in ("sp", "sp_a", "x_b", "core_sp", "core_a", "core_b")]
    return {key: place for place, key in enumerate(keys)}


def spread_body(z_count, sp_count, in_ref, out_ref, send_sem, recv_sem, own_sem):
    places = spread_keys(z_count, sp_count)
    obs = lax.axis_index("obs")
    s = lax.axis_index("sp")
    z, x, c = lax.div(obs, 4), lax.rem(lax.div(obs, 2), 2), lax.rem(obs, 2)
    half = in_ref.shape[0] // 2
    upper, lower = pl.ds(0, half), pl.ds(half, half)
    zs = [lax.bitwise_xor(z, k) for k in range(z_count)]
    to_sp = [lax.rem(s + d, sp_count) for d in range(sp_count)]
    from_sp = [lax.rem(s - d + sp_count, sp_count) for d in range(sp_count)]

    def device(z_to, x_to, c_to, s_to):
        return {"obs": z_to * 4 + x_to * 2 + c_to, "sp": s_to}

    def slot(z_of, x_of, s_of):
        return ((z_of * 2 + x_of) * 2 + c) * sp_count + s_of

    own_slot = slot(z, x, s)
    across, sibling = device(z, 1 - x, c, s), device(z, x, 1 - c, s)
    others = [device(zs[k], x, c, s) for k in range(1, z_count)]
    others += [device(z, x, c, to_sp[d]) for d in range(1, sp_count)]
    others += [across, sibling]
    barrier = pltpu.get_barrier_semaphore()
    for other in others:
        pl.semaphore_signal(barrier, inc=1, device_id=other, device_id_type=pl.DeviceIdType.MESH)
    pl.semaphore_wait(barrier, len(others))

    sent = {}

    def send(key, place, target, rows=None, own=False):
        src = in_ref if own else out_ref.at[place]
        dst = out_ref.at[place]
        if rows is not None:
            src, dst = src.at[rows], dst.at[rows]
        copy = pltpu.make_async_remote_copy(
            src_ref=src,
            dst_ref=dst,
            send_sem=send_sem.at[places[key]],
            recv_sem=recv_sem.at[places[key]],
            device_id=target,
            device_id_type=pl.DeviceIdType.MESH,
        )
        copy.start()
        sent[key] = copy

    keep = pltpu.make_async_copy(in_ref, out_ref.at[own_slot], own_sem)
    keep.start()
    for k in range(1, z_count):
        send(("z", k), own_slot, others[k - 1], own=True)

    def fan_out(k):
        place = slot(zs[k], x, s)
        send(("x", k), place, across, own=k == 0)
        for d in range(1, sp_count):
            send(("sp", k, d), place, device(z, x, c, to_sp[d]), own=k == 0)
        send(("core", k), place, sibling, own=k == 0)

    def relay(k):
        sent[("x", k)].wait_recv()
        place = slot(zs[k], 1 - x, s)
        for d in range(1, sp_count):
            send(("sp_a", k, d), place, device(z, x, c, to_sp[d]), upper)
        send(("core_x", k), place, sibling)
        for d in range(1, sp_count):
            sent[("sp", k, d)].wait_recv()
            place = slot(zs[k], x, from_sp[d])
            send(("x_b", k, d), place, across, lower)
            send(("core_sp", k, d), place, sibling)

    def finish(k):
        for d in range(1, sp_count):
            place = slot(zs[k], 1 - x, from_sp[d])
            sent[("sp_a", k, d)].wait_recv()
            send(("core_a", k, d), place, sibling, upper)
            sent[("x_b", k, d)].wait_recv()
            send(("core_b", k, d), place, sibling, lower)

    fan_out(0)
    for k in range(1, z_count):
        sent[("z", k)].wait_recv()
        fan_out(k)
        relay(k - 1)
        if k > 1:
            finish(k - 2)
    relay(z_count - 1)
    if z_count > 1:
        finish(z_count - 2)
    finish(z_count - 1)
    keep.wait()
    for key, copy in sent.items():
        copy.wait_send()
        if key[0].startswith("core"):
            copy.wait_recv()


def spread(shard, obs_count, sp_count, collective_id):
    rows, cols = shard.shape
    z_count = obs_count // 4
    total = obs_count * sp_count
    sems = len(spread_keys(z_count, sp_count))
    gathered = pl.pallas_call(
        functools.partial(spread_body, z_count, sp_count),
        out_shape=jax.ShapeDtypeStruct((total, rows, cols), shard.dtype),
        in_specs=[pl.BlockSpec(memory_space=pl.ANY)],
        out_specs=pl.BlockSpec(memory_space=pl.ANY),
        scratch_shapes=[
            pltpu.SemaphoreType.DMA((sems,)),
            pltpu.SemaphoreType.DMA((sems,)),
            pltpu.SemaphoreType.DMA,
        ],
        compiler_params=pltpu.CompilerParams(collective_id=collective_id, has_side_effects=True),
    )(shard)
    return gathered.reshape(total * rows, cols)


def position():
    obs = lax.axis_index("obs")
    return lax.div(obs, 4), lax.rem(lax.div(obs, 2), 2), lax.rem(obs, 2), lax.axis_index("sp")


def device(z, x, c, s):
    return {"obs": z * 4 + x * 2 + c, "sp": s}


def remote(src, dst, send_sem, recv_sem, target):
    return pltpu.make_async_remote_copy(
        src_ref=src, dst_ref=dst, send_sem=send_sem, recv_sem=recv_sem,
        device_id=target, device_id_type=pl.DeviceIdType.MESH,
    )


def route_sems(z_count):
    return [
        pltpu.SemaphoreType.DMA((4 * (z_count + 1),)),
        pltpu.SemaphoreType.DMA((4 * z_count,)),
        pltpu.SemaphoreType.DMA((8 * z_count,)),
        pltpu.SemaphoreType.DMA((8 * z_count,)),
    ]


def route_greet(z_count):
    z, x, c, s = position()
    barrier = pltpu.get_barrier_semaphore()
    others = [device(z, 1 - x, c, s), device(z, x, 1 - c, s), device(z, x, c, 1 - s)]
    others += [device(lax.rem(z + k, z_count), x, c, s) for k in range(1, z_count)]
    for other in others:
        pl.semaphore_signal(barrier, inc=1, device_id=other, device_id_type=pl.DeviceIdType.MESH)
    pl.semaphore_wait(barrier, len(others))


OWN, ACROSS, BESIDE, DIAGONAL = range(4)


def route(z_count, home, level, out_ref, sems, arrive, side_rows, diagonal_rows, begin=None, late=None):
    z_send, z_recv, send_sem, recv_sem = sems
    z, x, c, s = position()
    last = z_count - 1
    rows = home.shape[0]
    middle = diagonal_rows + (rows - diagonal_rows) // 2
    across, beside, sibling = device(z, 1 - x, c, s), device(z, x, c, 1 - s), device(z, x, 1 - c, s)

    nearer = jnp.minimum(z, last - z)
    origins = [z]
    for a in range(last):
        both = jnp.where(a % 2 == 0, z - (a // 2 + 1), z + (a // 2 + 1))
        single = jnp.where(z <= last - z, z + (a - nearer + 1), z - (a - nearer + 1))
        origins.append(jnp.where(a < 2 * nearer, both, single))

    def slot(col, a, c_of=c):
        x_of = 1 - x if col in (ACROSS, DIAGONAL) else x
        s_of = 1 - s if col in (BESIDE, DIAGONAL) else s
        return ((origins[a] * 2 + x_of) * 2 + c_of) * 2 + s_of

    def shard(col, a):
        if a == 0 and col == OWN:
            return home
        if a == 0 and level is not None:
            x_of = 1 - x if col in (ACROSS, DIAGONAL) else x
            s_of = 1 - s if col in (BESIDE, DIAGONAL) else s
            return level.at[x_of * 2 + s_of]
        return out_ref.at[slot(col, a)]

    sent = {}

    def send(key, src, place, target, begin_row=0, end_row=rows):
        cut = pl.ds(begin_row, end_row - begin_row)
        n = len(sent)
        sent[key] = remote(src.at[cut], out_ref.at[place].at[cut], send_sem.at[n], recv_sem.at[n], target)
        sent[key].start()

    along = {OWN: rows, ACROSS: side_rows, BESIDE: side_rows, DIAGONAL: diagonal_rows}
    hops = []

    def hop(col, a, n, target_z, when):
        cut = pl.ds(0, along[col])
        copy = remote(
            shard(col, a).at[cut], out_ref.at[slot(col, a)].at[cut],
            z_send.at[col * (z_count + 1) + n], z_recv.at[col * z_count + origins[a]],
            device(jnp.clip(target_z, 0, last), x, c, s),
        )
        pl.when(when)(copy.start)
        hops.append((when, copy))

    def set_off(*cols):
        for col in cols:
            if along[col]:
                hop(col, 0, 0, z + 1, z < last)
                hop(col, 0, 1, z - 1, z > 0)

    def pass_on(a, *cols):
        for col in cols:
            if along[col]:
                cut = pl.ds(0, along[col])
                held = out_ref.at[slot(col, a)].at[cut]
                remote(held, held, z_send.at[0], z_recv.at[col * z_count + origins[a]], across).wait_recv()
                target_z = jnp.where(origins[a] < z, z + 1, z - 1)
                hop(col, a, a + 1, target_z, (target_z >= 0) & (target_z <= last))

    def complete(a, *cols):
        for col in cols:
            send(("core", col, a), shard(col, a), slot(col, a), sibling)
            arrive(shard(col, a), slot(col, a))

    def from_sibling(a, *cols):
        for col in cols:
            sent[("core", col, a)].wait_recv()
            place = slot(col, a, 1 - c)
            arrive(out_ref.at[place], place)

    def fan_out(a):
        first_row = side_rows if a else 0
        send(("x", a), shard(OWN, a), slot(OWN, a), across, first_row)
        send(("y", a), shard(OWN, a), slot(OWN, a), beside, first_row)

    def relay(a):
        first_row, split = (diagonal_rows, middle) if a else (0, rows // 2)
        sent[("x", a)].wait_recv()
        send(("ya", a), shard(ACROSS, a), slot(ACROSS, a), beside, first_row, split)
        sent[("y", a)].wait_recv()
        send(("xb", a), shard(BESIDE, a), slot(BESIDE, a), across, split)

    set_off(OWN)
    if level is not None:
        set_off(ACROSS, BESIDE, DIAGONAL)
        if begin is not None:
            begin()
        complete(0, OWN, ACROSS, BESIDE, DIAGONAL)
    else:
        fan_out(0)
        if begin is not None:
            begin()
        complete(0, OWN)
    for n in range(1, z_count + 3):
        if n < z_count:
            pass_on(n, OWN)
            fan_out(n)
            complete(n, OWN)
        a = n - 1
        if a < z_count and (a or level is None):
            relay(a)
            if a == 0:
                set_off(ACROSS, BESIDE)
                complete(0, ACROSS, BESIDE)
        if n == 2 and late is not None:
            late()
        if a < z_count:
            from_sibling(a, OWN)
        a = n - 2
        if 0 <= a < z_count and (a or level is None):
            sent[("ya", a)].wait_recv()
            sent[("xb", a)].wait_recv()
            if a == 0:
                set_off(DIAGONAL)
                complete(0, DIAGONAL)
            else:
                pass_on(a, ACROSS, BESIDE, DIAGONAL)
                complete(a, ACROSS, BESIDE, DIAGONAL)
        a = n - 3
        if 0 <= a < z_count:
            from_sibling(a, ACROSS, BESIDE, DIAGONAL)
    for copy in sent.values():
        copy.wait_send()
    for when, copy in hops:
        pl.when(when)(copy.wait_send)


def share_body(z_count, own_ref, own_slab, out_ref, slab_ref, z_send, z_recv, send_sem, recv_sem, slab_send, slab_recv, keep_sem):
    z, x, c, s = position()
    q, q_across = x * 2 + c, (1 - x) * 2 + c
    half = own_slab.shape[0] // 2
    near, far = pl.ds(pl.multiple_of(s * half, 16), half), pl.ds(pl.multiple_of((1 - s) * half, 16), half)
    route_greet(z_count)
    keep = pltpu.make_async_copy(own_ref, out_ref.at[((z * 2 + x) * 2 + c) * 2 + s], keep_sem.at[0])
    keep_slab = pltpu.make_async_copy(own_slab, slab_ref.at[q], keep_sem.at[1])
    keep.start()
    keep_slab.start()
    shared = []

    def share(src, place, piece, target):
        n = len(shared)
        dst = slab_ref.at[place]
        if piece is not None:
            src, dst = src.at[piece], dst.at[piece]
        shared.append(remote(src, dst, slab_send.at[n], slab_recv.at[n], target))
        shared[-1].start()

    def begin():
        share(own_slab, q, near, device(z, 1 - x, c, s))
        share(own_slab, q, None, device(z, x, 1 - c, s))

    def late():
        shared[0].wait_recv()
        share(slab_ref.at[q_across], q_across, near, device(z, x, c, 1 - s))
        share(slab_ref.at[q_across], q_across, near, device(z, x, 1 - c, s))

    along = own_ref.shape[0] * 3 // 8 // 16 * 16
    sems = z_send, z_recv, send_sem, recv_sem
    route(z_count, own_ref, None, out_ref, sems, lambda src, place: None, along, along, begin, late)
    shared[2].wait_recv()
    share(slab_ref.at[q_across], q_across, far, device(z, x, 1 - c, s))
    for n in (1, 3, 4):
        shared[n].wait_recv()
    for copy in shared:
        copy.wait_send()
    keep.wait()
    keep_slab.wait()


def share(own, own_slab, z_count, collective_id):
    anywhere = pl.BlockSpec(memory_space=pl.ANY)
    return pl.pallas_call(
        functools.partial(share_body, z_count),
        out_shape=[
            jax.ShapeDtypeStruct((8 * z_count,) + own.shape, own.dtype),
            jax.ShapeDtypeStruct((4,) + own_slab.shape, own_slab.dtype),
        ],
        in_specs=[anywhere, anywhere],
        out_specs=[anywhere, anywhere],
        scratch_shapes=route_sems(z_count)
        + [pltpu.SemaphoreType.DMA((5,)), pltpu.SemaphoreType.DMA((5,)), pltpu.SemaphoreType.DMA((2,))],
        compiler_params=pltpu.CompilerParams(collective_id=collective_id, has_side_effects=True),
    )(own, own_slab)


def series_body(
    z_count, strip, tile, chunk, normalizer,
    level_ref, sums_ref, reg_ref, inv_ref, w_ref, gathered,
    dense, first, second, stage, recip, spread_recip, out_buf, w_own, w_slots,
    z_send, z_recv, send_sem, recv_sem, stage_sem, out_sem, w_send, w_recv,
):
    z, x, c, s = position()
    obs = lax.axis_index("obs")
    obs_count = 4 * z_count
    strips = 8 * z_count
    width = strips * strip
    half = strips // 2
    span = level_ref.shape[2]
    block_rows = width // 2
    lines = tile // LANES
    fold = 1.0 / normalizer

    barrier = pltpu.get_barrier_semaphore()
    peers = [
        {"obs": lax.rem(obs + k, obs_count), "sp": s} for k in range(1, obs_count)
    ]
    for peer in peers + [device(z, x, c, 1 - s)]:
        pl.semaphore_signal(barrier, inc=1, device_id=peer, device_id_type=pl.DeviceIdType.MESH)
    pl.semaphore_wait(barrier, obs_count)

    slots = stage.shape[0]
    waiting = []

    def lay_out(n):
        copy, place = waiting[n]
        copy.wait()
        place = lax.rem(place, 8) * z_count + lax.div(place, 8)
        rows = pl.ds(pl.multiple_of(place * strip, strip), strip)

        def put(k, turn):
            cols = pl.ds(pl.multiple_of(lax.rem(place + k, strips) * strip, strip), strip)
            block = stage[n % slots, :, pl.ds(pl.multiple_of(k * strip, strip), strip)]
            dense[rows, cols] = block
            if turn:
                dense[cols, rows] = block.T

        put(0, False)
        put(half, False)

        @pl.loop(0, half // 4)
        def _(m):
            for k in range(4):
                pl.when(m * 4 + k > 0)(lambda k=k: put(m * 4 + k, True))

    def arrive(src, place):
        n = len(waiting)
        if n >= slots:
            lay_out(n - slots)
        copy = pltpu.make_async_copy(src, stage.at[n % slots], stage_sem.at[n % slots])
        copy.start()
        waiting.append((copy, place))

    def begin():
        per = sums_ref.shape[1] // 2
        for p in range(sums_ref.shape[0]):
            lane = slice(p * per, (p + 1) * per)
            recip[lane, :] = 1.0 / (sums_ref[p, per:, :] * fold + reg_ref[lane, :])

        @pl.loop(0, width // LANES)
        def _(m):
            row = jnp.broadcast_to(recip[pl.ds(m, 1), :], (LANES, LANES))
            spread_recip[pl.ds(pl.multiple_of(m * LANES, LANES), LANES), :] = row.T

    sems = z_send, z_recv, send_sem, recv_sem
    route(z_count, level_ref.at[x * 2 + s], level_ref, gathered, sems, arrive, 0, strip // 64 * 16, begin)
    for n in range(len(waiting) - slots, len(waiting)):
        lay_out(n)

    my_cols = pl.ds(pl.multiple_of(obs * tile, tile), tile)

    def by_row(values, rows):
        scale = spread_recip[rows, :]
        return values * jnp.concatenate([scale] * lines, axis=1)

    @pl.loop(0, width // chunk)
    def _(m):
        rows = pl.ds(pl.multiple_of(m * chunk, chunk), chunk)
        first[rows, :] = by_row(dense[rows, my_cols].astype(jnp.float32) * fold, rows).astype(jnp.bfloat16)

    @pl.loop(0, width // chunk)
    def _(m):
        rows = pl.ds(pl.multiple_of(m * chunk, chunk), chunk)
        prod = jnp.dot(dense[rows, :], first[...], preferred_element_type=jnp.float32)
        second[rows, :] = by_row(prod * fold, rows).astype(jnp.bfloat16)

    def my_lines(ref, at):
        return jnp.concatenate([ref[pl.ds(at + h, 1), :] for h in range(lines)], axis=1)

    per = sums_ref.shape[1] // 2
    r_row = my_lines(recip, obs * lines)
    y = my_lines(sums_ref.at[lax.div(obs * lines, per)], lax.rem(obs * lines, per))
    y = jnp.broadcast_to(y * (1.0 / math.sqrt(normalizer)), (8, tile))

    def emit(m):
        return pltpu.make_async_copy(
            out_buf.at[m], inv_ref.at[pl.ds(pl.multiple_of(m * chunk, chunk), chunk)], out_sem.at[m]
        )

    @pl.loop(0, block_rows // chunk)
    def _(m):
        begin_at = s * block_rows + m * chunk
        rows = pl.ds(pl.multiple_of(begin_at, chunk), chunk)
        cubic = jnp.dot(dense[rows, :], second[...], preferred_element_type=jnp.float32)
        on_diag = (begin_at + lax.broadcasted_iota(jnp.int32, (chunk, tile), 0)) == (
            obs * tile + lax.broadcasted_iota(jnp.int32, (chunk, tile), 1)
        )
        series = second[rows, :].astype(jnp.float32) - by_row(
            (dense[rows, my_cols].astype(jnp.float32) + cubic) * fold, rows
        )
        out = (jnp.where(on_diag, 1.0, 0.0) + series) * r_row
        out_buf[m] = out
        emit(m).start()
        part_w = lax.dot_general(
            y, out, (((1,), (1,)), ((), ())),
            precision=lax.Precision.HIGHEST, preferred_element_type=jnp.float32,
        )
        for h in range(chunk // LANES):
            w_own[pl.ds(m * (chunk // LANES) + h, 1), :] = part_w[0:1, h * LANES : (h + 1) * LANES]

    copies = []
    for k in range(1, obs_count):
        copies.append(remote(w_own, w_slots.at[obs], w_send.at[k], w_recv.at[k], peers[k - 1]))
        copies[-1].start()
    w_slots[obs] = w_own[...]
    for copy in copies:
        copy.wait()
    total = w_slots[0]
    for k in range(1, obs_count):
        total = total + w_slots[k]
    w_ref[...] = total
    for m in range(block_rows // chunk):
        emit(m).wait()


def series_tile(level, sums, regularizer, z_count, tile, normalizer, collective_id):
    _, strip, span = level.shape
    strips = 8 * z_count
    width = strips * strip
    block_rows = width // 2
    chunk = min(512, block_rows)
    obs_count = 4 * z_count
    w_shape = (block_rows // LANES, LANES)
    anywhere = pl.BlockSpec(memory_space=pl.ANY)
    vmem = pl.BlockSpec(memory_space=pltpu.VMEM)
    inverse_tile, weights, _ = pl.pallas_call(
        functools.partial(series_body, z_count, strip, tile, chunk, normalizer),
        out_shape=[
            jax.ShapeDtypeStruct((block_rows, tile), jnp.float32),
            jax.ShapeDtypeStruct(w_shape, jnp.float32),
            jax.ShapeDtypeStruct((strips, strip, span), level.dtype),
        ],
        in_specs=[anywhere, vmem, vmem],
        out_specs=[anywhere, vmem, anywhere],
        scratch_shapes=[
            pltpu.VMEM((width, width), jnp.bfloat16),
            pltpu.VMEM((width, tile), jnp.bfloat16),
            pltpu.VMEM((width, tile), jnp.bfloat16),
            pltpu.VMEM((2, strip, span), jnp.bfloat16),
            pltpu.VMEM((width // LANES, LANES), jnp.float32),
            pltpu.VMEM((width, LANES), jnp.float32),
            pltpu.VMEM((block_rows // chunk, chunk, tile), jnp.float32),
            pltpu.VMEM(w_shape, jnp.float32),
            pltpu.VMEM((obs_count,) + w_shape, jnp.float32),
        ]
        + route_sems(z_count)
        + [
            pltpu.SemaphoreType.DMA((2,)),
            pltpu.SemaphoreType.DMA((block_rows // chunk,)),
            pltpu.SemaphoreType.DMA((obs_count,)),
            pltpu.SemaphoreType.DMA((obs_count,)),
        ],
        compiler_params=pltpu.CompilerParams(
            collective_id=collective_id, has_side_effects=True, vmem_limit_bytes=VMEM_BYTES
        ),
    )(level, sums, regularizer.reshape(width // LANES, LANES))
    return inverse_tile, weights.reshape(block_rows)


def by_strips(descriptors, candidates, sparse_index, targets, regularizer):
    obs_count = lax.axis_size("obs")
    sp_count = lax.axis_size("sp")
    obs_pos = lax.axis_index("obs")
    sp_pos = lax.axis_index("sp")
    z_count = obs_count // 4
    width = sparse_index.shape[0]
    tile = width // obs_count
    strip = width // (obs_count * sp_count)
    mine = strip * z_count
    span = width // 2 + strip
    window = width // 2 + mine
    rows, depth = descriptors.shape
    normalizer = 24.0 * rows * obs_count

    extra = jnp.pad(targets.reshape(rows // depth, depth), ((0, 32 - rows // depth), (0, 0)))
    shard = jnp.concatenate([unit_rows(descriptors), extra])
    piece = candidates.shape[0] // sp_count
    own = lax.dynamic_slice_in_dim(candidates, sp_pos * piece, piece)
    table, slab = share(unit_rows(own), shard, z_count, 2)
    table = table.reshape(-1, depth)
    place = lax.rem(obs_pos, 4) * sp_count + sp_pos
    wanted = lax.dynamic_slice_in_dim(
        jnp.concatenate([sparse_index, sparse_index]), place * mine, window
    )
    sparse = table.at[wanted].get(mode="promise_in_bounds")
    slab_targets = slab[:, rows : rows + rows // depth].reshape(4 * rows)
    level, sums = slab_gram(
        slab, sparse, slab_targets, z_count, sp_count, strip, span, tile, rows, 0
    )
    return series_tile(level, sums, regularizer, z_count, tile, normalizer, 3)


def slab_body(z_count, sp_count, strip, tile, root, *refs):
    norm_ref, sp_ref, tgt_ref, level_ref, sums_ref = refs[:5]
    kbuf, ktr, parts, from_low, from_high, done, zsums, gsums = refs[5:13]
    up_send, up_recv, down_send, down_recv, side_send, side_recv, zs_send, zs_recv, gs_send, gs_recv, keep_sem = refs[13:]
    obs = lax.axis_index("obs")
    s = lax.axis_index("sp")
    z, x, c, _ = position()
    q = x * 2 + c
    group = 4 * sp_count
    p = q * sp_count + s
    last = z_count - 1
    shard = tgt_ref.shape[1] // 4
    mine = strip * z_count
    lines = mine // LANES

    z_others = [{"obs": lax.rem(z + k, z_count) * 4 + q, "sp": s} for k in range(1, z_count)]
    group_others = []
    for k in range(1, group):
        to = lax.rem(p + k, group)
        group_others.append({"obs": z * 4 + lax.div(to, sp_count), "sp": lax.rem(to, sp_count)})
    barrier = pltpu.get_barrier_semaphore()
    for other in z_others + group_others:
        pl.semaphore_signal(barrier, inc=1, device_id=other, device_id_type=pl.DeviceIdType.MESH)
    pl.semaphore_wait(barrier, len(z_others) + len(group_others))

    def kernel_tile(t, own):
        cols = pl.ds(pl.multiple_of(t * tile, tile), tile)
        for k in range(4):
            rows = pl.ds(k * shard, shard)
            inner = lax.dot_general(
                norm_ref[k, :shard, :], sp_ref[cols, :], (((1,), (1,)), ((), ())),
                preferred_element_type=jnp.float32,
            )
            scaled = inner * root
            squared = scaled * scaled
            kb = ((squared - 6.0) * squared + 3.0).astype(jnp.bfloat16)
            kbuf[rows, cols] = kb
            if own:
                ktr[cols, rows] = kb.T

    def row_sums():
        for t in range(mine // tile):
            cols = slice(t * tile, (t + 1) * tile)
            weighted = jnp.dot(tgt_ref[...], kbuf[:, cols], preferred_element_type=jnp.float32)
            square = jnp.zeros((1, tile), jnp.float32)
            for k in range(4):
                kf = kbuf[k * shard : (k + 1) * shard, cols].astype(jnp.float32)
                square = square + jnp.sum(kf * kf, axis=0, keepdims=True)
            for h in range(tile // LANES):
                line = t * (tile // LANES) + h
                lane = slice(h * LANES, (h + 1) * LANES)
                zsums[z, line : line + 1, :] = weighted[0:1, lane]
                zsums[z, lines + line : lines + line + 1, :] = square[:, lane]

    groups = kbuf.shape[1] // mine

    def piece(t, g):
        begin = t * strip if g == 0 else 0
        end = mine if g < groups - 1 else (t + 1) * strip
        return begin, g * mine + begin - t * strip, end - begin

    def cut(t, g):
        _, begin, size = piece(t, g)
        return pl.ds(begin, size)

    def up(t, g):
        n, at = t * groups + g, (t, slice(None), cut(t, g))
        return remote(
            parts.at[at], from_low.at[at], up_send.at[n], up_recv.at[n],
            {"obs": lax.rem(z + 1, z_count) * 4 + q, "sp": s},
        )

    def down(t, g):
        n, at = t * groups + g, (t, slice(None), cut(t, g))
        return remote(
            parts.at[at], from_high.at[at], down_send.at[n], down_recv.at[n],
            {"obs": lax.rem(z + last, z_count) * 4 + q, "sp": s},
        )

    def gram_group(g):
        cols = slice(g * mine, (g + 1) * mine)
        made = jnp.dot(ktr[...], kbuf[:, cols], preferred_element_type=jnp.float32).astype(jnp.bfloat16)
        for t in range(z_count):
            begin, at, size = piece(t, g)
            parts[t, :, at : at + size] = made[t * strip : (t + 1) * strip, begin : begin + size]

    def pass_on(place, n):
        if place > 0 and 0 <= n - place < groups:
            for t in range(last, place, -1):
                g = n - place
                up(t, g).wait_recv()
                parts[t, :, cut(t, g)] = parts[t, :, cut(t, g)] + from_low[t, :, cut(t, g)]
                up(t, g).start()
        if place < last and 0 <= n - (last - place) < groups:
            for t in range(place):
                g = n - (last - place)
                down(t, g).wait_recv()
                parts[t, :, cut(t, g)] = parts[t, :, cut(t, g)] + from_high[t, :, cut(t, g)]
                down(t, g).start()

    mine_at, across_at, beside_at = x * 2 + s, (1 - x) * 2 + s, x * 2 + 1 - s
    across, beside = device(z, 1 - x, c, s), device(z, x, c, 1 - s)
    half = strip // 2

    def side(place, g, k):
        rows = (slice(None), slice(None), pl.ds(0, half), pl.ds(half, half))[k]
        at = (mine_at, mine_at, across_at, beside_at)[k]
        src = done.at[:, cut(place, g)] if k < 2 else level_ref.at[at, rows, cut(place, g)]
        return remote(
            src, level_ref.at[at, rows, cut(place, g)], side_send.at[g * 4 + k], side_recv.at[g * 4 + k],
            (across, beside, beside, across)[k],
        )

    def keep(place, g):
        return pltpu.make_async_copy(
            done.at[:, cut(place, g)], level_ref.at[mine_at, :, cut(place, g)], keep_sem.at[g]
        )

    def close(place, g):
        total = parts[place, :, cut(place, g)].astype(jnp.float32)
        if place > 0:
            up(place, g).wait_recv()
            total = total + from_low[place, :, cut(place, g)].astype(jnp.float32)
        if place < last:
            down(place, g).wait_recv()
            total = total + from_high[place, :, cut(place, g)].astype(jnp.float32)
        if g == 0:
            row = lax.broadcasted_iota(jnp.int32, total.shape, 0)
            col = lax.broadcasted_iota(jnp.int32, total.shape, 1)
            total = jnp.where(row == col, 0.0, total)
        done[:, cut(place, g)] = total.astype(jnp.bfloat16)
        side(place, g, 0).start()
        side(place, g, 1).start()
        keep(place, g).start()

    def progress(place, n):
        pass_on(place, n)
        g = n - max(place, last - place)
        if 0 <= g < groups:
            close(place, g)
        if 0 <= g - 1 < groups:
            for k in range(2):
                side(place, g - 1, k).wait_recv()
                side(place, g - 1, k + 2).start()
        if 0 <= g - 2 < groups:
            for k in range(2):
                side(place, g - 2, k + 2).wait_recv()

    z_copies, g_copies = [], []
    for n in range(groups + last + 2):
        if n < groups:

            @pl.loop(n * mine // tile, (n + 1) * mine // tile)
            def _(t):
                kernel_tile(t, n == 0)

            gram_group(n)

            @pl.when(z == 0)
            def _():
                for t in range(last, 0, -1):
                    up(t, n).start()

            @pl.when(z == last)
            def _():
                for t in range(last):
                    down(t, n).start()

        if n == 0:
            row_sums()
            for k in range(1, z_count):
                z_copies.append(remote(zsums.at[z], zsums.at[z], zs_send.at[k], zs_recv.at[k], z_others[k - 1]))
                z_copies[-1].start()
        if n == 1:
            for copy in z_copies:
                copy.wait_recv()
            total = zsums[0]
            for m in range(1, z_count):
                total = total + zsums[m]
            gsums[p] = total
            for m in range(1, group):
                g_copies.append(
                    remote(gsums.at[p], gsums.at[p], gs_send.at[m], gs_recv.at[m], group_others[m - 1])
                )
                g_copies[-1].start()
        for place in range(z_count):
            pl.when(z == place)(functools.partial(progress, place, n))

    def finish(place):
        for g in range(groups):
            for k in range(4):
                side(place, g, k).wait_send()
            keep(place, g).wait()
            for t in range(z_count):
                if t > place:
                    up(t, g).wait_send()
                if t < place:
                    down(t, g).wait_send()

    for place in range(z_count):
        pl.when(z == place)(functools.partial(finish, place))

    for copy in g_copies:
        copy.wait()
    for copy in z_copies:
        copy.wait_send()
    sums_ref[...] = gsums[...]


def slab_gram(slab, sparse, targets, z_count, sp_count, strip, span, tile, rows, collective_id):
    depth = slab.shape[2]
    window = sparse.shape[0]
    group = 4 * sp_count
    mine = strip * z_count
    lines = 2 * mine // LANES
    vmem = pl.BlockSpec(memory_space=pltpu.VMEM)
    part = (z_count, strip, span)
    groups = window // mine
    sems = [pltpu.SemaphoreType.DMA((z_count * groups,))] * 4 + [pltpu.SemaphoreType.DMA((4 * groups,))] * 2
    sems += [pltpu.SemaphoreType.DMA((z_count,))] * 2 + [pltpu.SemaphoreType.DMA((group,))] * 2
    sems += [pltpu.SemaphoreType.DMA((groups,))]
    return pl.pallas_call(
        functools.partial(slab_body, z_count, sp_count, strip, tile, math.sqrt(depth)),
        out_shape=[
            jax.ShapeDtypeStruct((4, strip, span), jnp.bfloat16),
            jax.ShapeDtypeStruct((group, lines, LANES), jnp.float32),
        ],
        in_specs=[vmem, vmem, vmem],
        out_specs=[pl.BlockSpec(memory_space=pl.ANY), vmem],
        scratch_shapes=[
            pltpu.VMEM((4 * rows, window), jnp.bfloat16),
            pltpu.VMEM((mine, 4 * rows), jnp.bfloat16),
            pltpu.VMEM(part, jnp.bfloat16),
            pltpu.VMEM(part, jnp.bfloat16),
            pltpu.VMEM(part, jnp.bfloat16),
            pltpu.VMEM(part[1:], jnp.bfloat16),
            pltpu.VMEM((z_count, lines, LANES), jnp.float32),
            pltpu.VMEM((group, lines, LANES), jnp.float32),
        ] + sems,
        compiler_params=pltpu.CompilerParams(
            collective_id=collective_id, has_side_effects=True, vmem_limit_bytes=VMEM_BYTES
        ),
    )(slab, sparse, jnp.broadcast_to(targets[None, :], (16, 4 * rows)))


def on_device(descriptors, candidates, sparse_index, targets, regularizer):
    obs_count = lax.axis_size("obs")
    sp_count = lax.axis_size("sp")
    obs_pos = lax.axis_index("obs")
    sp_pos = lax.axis_index("sp")
    width = sparse_index.shape[0]
    if sp_count == 2 and width % (obs_count * sp_count * LANES) == 0:
        return by_strips(descriptors, candidates, sparse_index, targets, regularizer)
    tile = width // obs_count
    share = -(-((obs_count // 2 + 1) * tile) // (sp_count * LANES)) * LANES
    normalizer = 24.0 * descriptors.shape[0] * obs_count

    normed = unit_rows(descriptors)
    piece = candidates.shape[0] // sp_count
    own = lax.dynamic_slice_in_dim(candidates, sp_pos * piece, piece)
    table = spread(unit_rows(own), obs_count, sp_count, 2)
    sparse = table.at[sparse_index].get(mode="promise_in_bounds")

    gram, sums = gram_call(
        sp_pos[None].astype(jnp.int32), normed, sparse, targets, obs_count, tile, share, sp_count
    )
    sums = add_over_obs(sums, obs_count, 0)
    part = lax.psum_scatter(gram, "obs", scatter_dimension=0, tiled=True)

    projected = sums[0] / math.sqrt(normalizer)
    root = lax.rsqrt(sums[1] / normalizer + regularizer)
    col_start = obs_pos * tile
    rrow = lax.dynamic_slice_in_dim(root, col_start, tile)
    window_start = col_start + sp_pos * share
    rwin = lax.dynamic_slice_in_dim(jnp.concatenate([root, root]), window_start, share)
    offset = sp_pos * share + lax.iota(jnp.int32, share)
    on_diag = lax.iota(jnp.int32, tile)[:, None] == offset[None, :]
    scaled = jnp.where(
        on_diag, 0.0, part.astype(jnp.float32) * (rrow[:, None] / normalizer) * rwin[None, :]
    ).astype(jnp.bfloat16)
    packed = spread(scaled, obs_count, sp_count, 3)

    y = lax.dynamic_slice_in_dim(projected, col_start, tile)
    pos = jnp.stack([sp_pos, obs_pos]).astype(jnp.int32)
    inverse_tile, part_w = newton_call(
        pos, packed, root, rrow, y, obs_count, tile, share, sp_count
    )
    return inverse_tile, add_over_obs(part_w[0], obs_count, 1)


def solution(mesh):
    in_specs = (P("obs", None), P("obs", None), P(), P("obs"), P())
    out_specs = (P("sp", "obs"), P("sp"))
    return jax.shard_map(
        on_device, mesh=mesh, in_specs=in_specs, out_specs=out_specs, check_vma=False
    )
```

```python
import functools
import math

import jax
import jax.numpy as jnp
from jax import lax
from jax.experimental import pallas as pl
from jax.experimental.pallas import tpu as pltpu
from jax.sharding import PartitionSpec as P

epsilon = 1e-06
LANES = 128
VMEM_BYTES = 58 * 2**20


def unit_rows(row_block):
    values = row_block.astype(jnp.float32)
    return (values * lax.rsqrt(jnp.sum(values * values, axis=1, keepdims=True) + epsilon)).astype(
        jnp.bfloat16
    )


def gram_body(blocks, tile, share, ext, root, s_ref, norm_ref, sp_ref, tgt_ref, gram_ref, ws_ref, kext):
    step = pl.program_id(0)
    width = blocks * tile

    @pl.when(step < blocks)
    def _():
        inner = lax.dot_general(
            norm_ref[...], sp_ref[...], (((1,), (1,)), ((), ())), preferred_element_type=jnp.float32
        )
        scaled = inner * root
        squared = scaled * scaled
        kb = ((squared - 6.0) * squared + 3.0).astype(jnp.bfloat16)
        kext[:, pl.ds(pl.multiple_of(step * tile, tile), tile)] = kb

        @pl.when(step < ext)
        def _():
            kext[:, pl.ds(pl.multiple_of(width + step * tile, tile), tile)] = kb

        kf = kb.astype(jnp.float32)
        weighted = jnp.dot(tgt_ref[...], kb, preferred_element_type=jnp.float32)
        ws_ref[0:1, :] = weighted[0:1, :]
        ws_ref[1:2, :] = jnp.sum(kf * kf, axis=0, keepdims=True)

    @pl.when(step >= blocks)
    def _():
        j = step - blocks
        cols = pl.ds(pl.multiple_of(j * tile, tile), tile)
        window = pl.ds(pl.multiple_of(j * tile + s_ref[0] * share, LANES), share)
        gram_ref[...] = lax.dot_general(
            kext[:, cols], kext[:, window], (((0,), (0,)), ((), ())), preferred_element_type=jnp.float32
        ).astype(jnp.bfloat16)


def gram_call(s_pos, normed, sparse, targets, blocks, tile, share, sp_count):
    rows, depth = normed.shape
    width = blocks * tile
    ext = -(-((blocks - 1) * tile + sp_count * share - width) // tile)
    last = blocks - 1
    return pl.pallas_call(
        functools.partial(gram_body, blocks, tile, share, ext, math.sqrt(depth)),
        grid_spec=pltpu.PrefetchScalarGridSpec(
            num_scalar_prefetch=1,
            grid=(2 * blocks,),
            in_specs=[
                pl.BlockSpec((rows, depth), lambda g, s: (0, 0)),
                pl.BlockSpec((tile, depth), lambda g, s: (jnp.minimum(g, last), 0)),
                pl.BlockSpec((16, rows), lambda g, s: (0, 0)),
            ],
            out_specs=[
                pl.BlockSpec((tile, share), lambda g, s: (jnp.maximum(g - blocks, 0), 0)),
                pl.BlockSpec((2, tile), lambda g, s: (0, jnp.minimum(g, last))),
            ],
            scratch_shapes=[pltpu.VMEM((rows, width + ext * tile), jnp.bfloat16)],
        ),
        out_shape=[
            jax.ShapeDtypeStruct((width, share), jnp.bfloat16),
            jax.ShapeDtypeStruct((2, width), jnp.float32),
        ],
        compiler_params=pltpu.CompilerParams(vmem_limit_bytes=VMEM_BYTES),
    )(s_pos, normed, sparse, jnp.broadcast_to(targets[None, :], (16, rows)))


def newton_body(
    blocks, tile, share, sp_count, chunk, block_rows,
    pos_ref, packed_ref, rcol_ref, rrow_ref, y_ref, inv_ref, w_ref, dense, prod,
):
    step = pl.program_id(0)
    width = blocks * tile
    half = blocks // 2
    p_steps = width // chunk
    my_cols = pl.ds(pl.multiple_of(pos_ref[1] * tile, tile), tile)

    @pl.when(step < blocks)
    def _():
        rows = pl.ds(pl.multiple_of(step * tile, tile), tile)
        for s in range(sp_count):
            for q in range(share // LANES):
                offset = s * share + q * LANES
                if offset >= (half + 1) * tile:
                    continue
                col = lax.rem(step * tile + offset, width)
                cols = pl.ds(pl.multiple_of(col, LANES), LANES)
                block = packed_ref[s * tile : (s + 1) * tile, q * LANES : (q + 1) * LANES]
                dense[rows, cols] = block
                if tile <= offset < half * tile:
                    dense[cols, rows] = block.T

    @pl.when((step >= blocks) & (step < blocks + p_steps))
    def _():
        rows = pl.ds(pl.multiple_of((step - blocks) * chunk, chunk), chunk)
        prod[rows, :] = jnp.dot(
            dense[rows, :], dense[:, my_cols], preferred_element_type=jnp.float32
        ).astype(jnp.bfloat16)

    @pl.when(step >= blocks + p_steps)
    def _():
        local = pl.multiple_of((step - blocks - p_steps) * chunk, chunk)
        start = pl.multiple_of(pos_ref[0] * block_rows + local, chunk)
        rows = pl.ds(start, chunk)
        cubic = jnp.dot(dense[rows, :], prod[...], preferred_element_type=jnp.float32)
        on_diag = (start + lax.broadcasted_iota(jnp.int32, (chunk, tile), 0)) == (
            pos_ref[1] * tile + lax.broadcasted_iota(jnp.int32, (chunk, tile), 1)
        )
        series = (
            jnp.where(on_diag, 1.0, 0.0)
            - dense[rows, my_cols].astype(jnp.float32)
            + prod[rows, :].astype(jnp.float32)
            - cubic
        )
        out = series * rcol_ref[rows, :] * rrow_ref[...]
        inv_ref[pl.ds(local, chunk), :] = out
        w_ref[:, pl.ds(local, chunk)] = lax.dot_general(
            y_ref[...], out, (((1,), (1,)), ((), ())),
            precision=lax.Precision.HIGHEST, preferred_element_type=jnp.float32,
        )


def newton_call(pos, packed, root_recip, rrow, y, blocks, tile, share, sp_count):
    width = blocks * tile
    block_rows = width // sp_count
    chunk = min(512, block_rows)
    grid = blocks + width // chunk + block_rows // chunk
    last = blocks - 1
    return pl.pallas_call(
        functools.partial(newton_body, blocks, tile, share, sp_count, chunk, block_rows),
        grid_spec=pltpu.PrefetchScalarGridSpec(
            num_scalar_prefetch=1,
            grid=(grid,),
            in_specs=[
                pl.BlockSpec((sp_count * tile, share), lambda g, p: (jnp.minimum(g, last), 0)),
                pl.BlockSpec((width, 1), lambda g, p: (0, 0)),
                pl.BlockSpec((1, tile), lambda g, p: (0, 0)),
                pl.BlockSpec((8, tile), lambda g, p: (0, 0)),
            ],
            out_specs=[
                pl.BlockSpec((block_rows, tile), lambda g, p: (0, 0)),
                pl.BlockSpec((8, block_rows), lambda g, p: (0, 0)),
            ],
            scratch_shapes=[
                pltpu.VMEM((width, width), jnp.bfloat16),
                pltpu.VMEM((width, tile), jnp.bfloat16),
            ],
        ),
        out_shape=[
            jax.ShapeDtypeStruct((block_rows, tile), jnp.float32),
            jax.ShapeDtypeStruct((8, block_rows), jnp.float32),
        ],
        compiler_params=pltpu.CompilerParams(vmem_limit_bytes=VMEM_BYTES),
    )(pos, packed, root_recip[:, None], rrow[None, :], jnp.broadcast_to(y[None, :], (8, tile)))


def add_body(count, in_ref, out_ref, slots, send_sem, recv_sem):
    me = lax.axis_index("obs")
    barrier = pltpu.get_barrier_semaphore()
    for k in range(1, count):
        pl.semaphore_signal(
            barrier, inc=1, device_id={"obs": lax.rem(me + k, count)}, device_id_type=pl.DeviceIdType.MESH
        )
    pl.semaphore_wait(barrier, count - 1)
    copies = []
    for k in range(1, count):
        copy = pltpu.make_async_remote_copy(
            src_ref=in_ref,
            dst_ref=slots.at[me],
            send_sem=send_sem.at[k],
            recv_sem=recv_sem.at[k],
            device_id={"obs": lax.rem(me + k, count)},
            device_id_type=pl.DeviceIdType.MESH,
        )
        copy.start()
        copies.append(copy)
    slots[me] = in_ref[...]
    for copy in copies:
        copy.wait()
    total = slots[0]
    for k in range(1, count):
        total = total + slots[k]
    out_ref[...] = total


def add_over_obs(values, count, collective_id):
    shape = values.shape
    flat = values.reshape(values.size // LANES, LANES)
    total = pl.pallas_call(
        functools.partial(add_body, count),
        out_shape=jax.ShapeDtypeStruct(flat.shape, flat.dtype),
        in_specs=[pl.BlockSpec(memory_space=pltpu.VMEM)],
        out_specs=pl.BlockSpec(memory_space=pltpu.VMEM),
        scratch_shapes=[
            pltpu.VMEM((count,) + flat.shape, flat.dtype),
            pltpu.SemaphoreType.DMA((count,)),
            pltpu.SemaphoreType.DMA((count,)),
        ],
        cost_estimate=pl.CostEstimate(
            flops=count * flat.size, bytes_accessed=400 * flat.size, transcendentals=0
        ),
        compiler_params=pltpu.CompilerParams(collective_id=collective_id, has_side_effects=True),
    )(flat)
    return total.reshape(shape)


def spread_keys(z_count, sp_count):
    keys = [("z", k) for k in range(1, z_count)]
    for k in range(z_count):
        keys += [("x", k), ("core", k), ("core_x", k)]
        for d in range(1, sp_count):
            keys += [(name, k, d) for name in ("sp", "sp_a", "x_b", "core_sp", "core_a", "core_b")]
    return {key: place for place, key in enumerate(keys)}


def spread_body(z_count, sp_count, in_ref, out_ref, send_sem, recv_sem, own_sem):
    places = spread_keys(z_count, sp_count)
    obs = lax.axis_index("obs")
    s = lax.axis_index("sp")
    z, x, c = lax.div(obs, 4), lax.rem(lax.div(obs, 2), 2), lax.rem(obs, 2)
    half = in_ref.shape[0] // 2
    upper, lower = pl.ds(0, half), pl.ds(half, half)
    zs = [lax.bitwise_xor(z, k) for k in range(z_count)]
    to_sp = [lax.rem(s + d, sp_count) for d in range(sp_count)]
    from_sp = [lax.rem(s - d + sp_count, sp_count) for d in range(sp_count)]

    def device(z_to, x_to, c_to, s_to):
        return {"obs": z_to * 4 + x_to * 2 + c_to, "sp": s_to}

    def slot(z_of, x_of, s_of):
        return ((z_of * 2 + x_of) * 2 + c) * sp_count + s_of

    own_slot = slot(z, x, s)
    across, sibling = device(z, 1 - x, c, s), device(z, x, 1 - c, s)
    others = [device(zs[k], x, c, s) for k in range(1, z_count)]
    others += [device(z, x, c, to_sp[d]) for d in range(1, sp_count)]
    others += [across, sibling]
    barrier = pltpu.get_barrier_semaphore()
    for other in others:
        pl.semaphore_signal(barrier, inc=1, device_id=other, device_id_type=pl.DeviceIdType.MESH)
    pl.semaphore_wait(barrier, len(others))

    sent = {}

    def send(key, place, target, rows=None, own=False):
        src = in_ref if own else out_ref.at[place]
        dst = out_ref.at[place]
        if rows is not None:
            src, dst = src.at[rows], dst.at[rows]
        copy = pltpu.make_async_remote_copy(
            src_ref=src,
            dst_ref=dst,
            send_sem=send_sem.at[places[key]],
            recv_sem=recv_sem.at[places[key]],
            device_id=target,
            device_id_type=pl.DeviceIdType.MESH,
        )
        copy.start()
        sent[key] = copy

    keep = pltpu.make_async_copy(in_ref, out_ref.at[own_slot], own_sem)
    keep.start()
    for k in range(1, z_count):
        send(("z", k), own_slot, others[k - 1], own=True)

    def fan_out(k):
        place = slot(zs[k], x, s)
        send(("x", k), place, across, own=k == 0)
        for d in range(1, sp_count):
            send(("sp", k, d), place, device(z, x, c, to_sp[d]), own=k == 0)
        send(("core", k), place, sibling, own=k == 0)

    def relay(k):
        sent[("x", k)].wait_recv()
        place = slot(zs[k], 1 - x, s)
        for d in range(1, sp_count):
            send(("sp_a", k, d), place, device(z, x, c, to_sp[d]), upper)
        send(("core_x", k), place, sibling)
        for d in range(1, sp_count):
            sent[("sp", k, d)].wait_recv()
            place = slot(zs[k], x, from_sp[d])
            send(("x_b", k, d), place, across, lower)
            send(("core_sp", k, d), place, sibling)

    def finish(k):
        for d in range(1, sp_count):
            place = slot(zs[k], 1 - x, from_sp[d])
            sent[("sp_a", k, d)].wait_recv()
            send(("core_a", k, d), place, sibling, upper)
            sent[("x_b", k, d)].wait_recv()
            send(("core_b", k, d), place, sibling, lower)

    fan_out(0)
    for k in range(1, z_count):
        sent[("z", k)].wait_recv()
        fan_out(k)
        relay(k - 1)
        if k > 1:
            finish(k - 2)
    relay(z_count - 1)
    if z_count > 1:
        finish(z_count - 2)
    finish(z_count - 1)
    keep.wait()
    for key, copy in sent.items():
        copy.wait_send()
        if key[0].startswith("core"):
            copy.wait_recv()


def spread(shard, obs_count, sp_count, collective_id):
    rows, cols = shard.shape
    z_count = obs_count // 4
    total = obs_count * sp_count
    sems = len(spread_keys(z_count, sp_count))
    gathered = pl.pallas_call(
        functools.partial(spread_body, z_count, sp_count),
        out_shape=jax.ShapeDtypeStruct((total, rows, cols), shard.dtype),
        in_specs=[pl.BlockSpec(memory_space=pl.ANY)],
        out_specs=pl.BlockSpec(memory_space=pl.ANY),
        scratch_shapes=[
            pltpu.SemaphoreType.DMA((sems,)),
            pltpu.SemaphoreType.DMA((sems,)),
            pltpu.SemaphoreType.DMA,
        ],
        compiler_params=pltpu.CompilerParams(collective_id=collective_id, has_side_effects=True),
    )(shard)
    return gathered.reshape(total * rows, cols)


def position():
    obs = lax.axis_index("obs")
    return lax.div(obs, 4), lax.rem(lax.div(obs, 2), 2), lax.rem(obs, 2), lax.axis_index("sp")


def device(z, x, c, s):
    return {"obs": z * 4 + x * 2 + c, "sp": s}


def remote(src, dst, send_sem, recv_sem, target):
    return pltpu.make_async_remote_copy(
        src_ref=src, dst_ref=dst, send_sem=send_sem, recv_sem=recv_sem,
        device_id=target, device_id_type=pl.DeviceIdType.MESH,
    )


def route_sems(z_count, chunks):
    return [
        pltpu.SemaphoreType.DMA((4 * chunks * (z_count + 1),)),
        pltpu.SemaphoreType.DMA((4 * chunks * z_count,)),
        pltpu.SemaphoreType.DMA((4 * (chunks + 1) * z_count,)),
        pltpu.SemaphoreType.DMA((4 * (chunks + 1) * z_count,)),
    ]


def route_greet(z_count):
    z, x, c, s = position()
    barrier = pltpu.get_barrier_semaphore()
    others = [device(z, 1 - x, c, s), device(z, x, 1 - c, s), device(z, x, c, 1 - s)]
    others += [device(lax.rem(z + k, z_count), x, c, s) for k in range(1, z_count)]
    for other in others:
        pl.semaphore_signal(barrier, inc=1, device_id=other, device_id_type=pl.DeviceIdType.MESH)
    pl.semaphore_wait(barrier, len(others))


OWN, ACROSS, BESIDE, DIAGONAL = range(4)


def route(z_count, home, level, out_ref, sems, arrive, chunks, diagonal, lag, begin, late=None):
    z_send, z_recv, send_sem, recv_sem = sems
    z, x, c, s = position()
    last = z_count - 1
    rows = home.shape[0]
    high = rows // chunks
    across, beside, sibling = device(z, 1 - x, c, s), device(z, x, c, 1 - s), device(z, x, 1 - c, s)
    along = {OWN: chunks, ACROSS: 0, BESIDE: 0, DIAGONAL: diagonal}

    nearer = jnp.minimum(z, last - z)
    origins = [z]
    for a in range(last):
        both = jnp.where(a % 2 == 0, z - (a // 2 + 1), z + (a // 2 + 1))
        single = jnp.where(z <= last - z, z + (a - nearer + 1), z - (a - nearer + 1))
        origins.append(jnp.where(a < 2 * nearer, both, single))

    def place_of(col, a, c_of):
        x_of = 1 - x if col in (ACROSS, DIAGONAL) else x
        s_of = 1 - s if col in (BESIDE, DIAGONAL) else s
        return origins[a] * 2 + x_of, c_of, s_of

    def slot(col, a, c_of=c):
        zx, c_of, s_of = place_of(col, a, c_of)
        return (zx * 2 + c_of) * 2 + s_of

    def shard(col, a):
        if a == 0 and col == OWN:
            return home
        if a == 0 and level is not None:
            zx, _, s_of = place_of(col, a, c)
            return level.at[(zx - z * 2) * 2 + s_of]
        return out_ref.at[slot(col, a)]

    sent = {}

    def send(key, col, a, target, begin=0, size=rows):
        cut = pl.ds(begin, size)
        n = len(sent)
        sent[key] = remote(
            shard(col, a).at[cut], out_ref.at[slot(col, a)].at[cut], send_sem.at[n], recv_sem.at[n], target
        )
        sent[key].start()

    hops = []

    def hop(col, a, j, n, target_z, when):
        cut = pl.ds(j * high, high)
        copy = remote(
            shard(col, a).at[cut], out_ref.at[slot(col, a)].at[cut],
            z_send.at[(col * chunks + j) * (z_count + 1) + n], z_recv.at[(col * chunks + j) * z_count + origins[a]],
            device(jnp.clip(target_z, 0, last), x, c, s),
        )
        pl.when(when)(copy.start)
        hops.append((when, copy))

    def set_off(col, j):
        if j < along[col]:
            hop(col, 0, j, 0, z + 1, z < last)
            hop(col, 0, j, 1, z - 1, z > 0)

    def pass_on(col, a, j):
        if j < along[col]:
            held = out_ref.at[slot(col, a)].at[pl.ds(j * high, high)]
            remote(held, held, z_send.at[0], z_recv.at[(col * chunks + j) * z_count + origins[a]], across).wait_recv()
            target_z = jnp.where(origins[a] < z, z + 1, z - 1)
            hop(col, a, j, a + 1, target_z, (target_z >= 0) & (target_z <= last))

    finished = []

    def complete(now, a, *cols):
        for col in cols:
            send(("core", col, a), col, a, sibling)
            arrive(shard(col, a), slot(col, a))
            finished.append((now, a, col))

    def from_sibling(before):
        while finished and finished[0][0] < before:
            _, a, col = finished.pop(0)
            sent[("core", col, a)].wait_recv()
            place = slot(col, a, 1 - c)
            arrive(out_ref.at[place], place)

    def fan_out(a, j):
        send(("x", a, j), OWN, a, across, j * high, high)
        send(("y", a, j), OWN, a, beside, j * high, high)

    def relay(a, j):
        direct = a == 0 or j >= diagonal
        sent[("x", a, j)].wait_recv()
        if direct:
            send(("ya", a, j), ACROSS, a, beside, j * high, high // 2)
        sent[("y", a, j)].wait_recv()
        if direct:
            send(("xb", a, j), BESIDE, a, across, j * high + high // 2, high // 2)

    def finish(a, j):
        if ("ya", a, j) in sent:
            sent[("ya", a, j)].wait_recv()
            sent[("xb", a, j)].wait_recv()

    first = 1
    for j in range(chunks):
        set_off(OWN, j)
    if level is None:
        first = 0
        for j in range(chunks):
            fan_out(0, j)
    else:
        for j in range(chunks):
            set_off(DIAGONAL, j)
    begin()
    complete(-1, 0, OWN)
    if level is not None:
        complete(-1, 0, ACROSS, BESIDE, DIAGONAL)
    items = [(a, j) for j in range(chunks) for a in range(first, 2)]
    items += [(a, j) for a in range(2, z_count) for j in range(chunks)]
    ends = [items.index((a, chunks - 1)) for a in range(1, z_count)]
    ready = set()
    for now in range(len(items) + max(sum(lag), 3)):
        if now < len(items):
            a, j = items[now]
            if a:
                pass_on(OWN, a, j)
                fan_out(a, j)
                if j == chunks - 1:
                    complete(now, a, OWN)
        if 0 <= now - lag[0] < len(items):
            a, j = items[now - lag[0]]
            relay(a, j)
            if j == chunks - 1:
                complete(now, a, ACROSS, BESIDE)
        if now - 3 in ends:
            a = ends.index(now - 3) + 1
            for j in range(chunks):
                pass_on(DIAGONAL, a, j)
            ready.add(a)
        if 0 <= now - sum(lag) < len(items):
            a, j = items[now - sum(lag)]
            finish(a, j)
            if a == 0:
                set_off(DIAGONAL, j)
            if j == chunks - 1:
                assert a in ready or not a
                complete(now, a, DIAGONAL)
        if now == len(items) - 2 and late is not None:
            late()
        from_sibling(now - 2)
    from_sibling(now + 1)
    for copy in sent.values():
        copy.wait_send()
    for when, copy in hops:
        pl.when(when)(copy.wait_send)


def share_body(z_count, own_ref, own_slab, out_ref, slab_ref, z_send, z_recv, send_sem, recv_sem, slab_send, slab_recv, keep_sem):
    z, x, c, s = position()
    q, q_across = x * 2 + c, (1 - x) * 2 + c
    half = own_slab.shape[0] // 2
    near, far = pl.ds(pl.multiple_of(s * half, 16), half), pl.ds(pl.multiple_of((1 - s) * half, 16), half)
    route_greet(z_count)
    keep = pltpu.make_async_copy(own_ref, out_ref.at[((z * 2 + x) * 2 + c) * 2 + s], keep_sem.at[0])
    keep_slab = pltpu.make_async_copy(own_slab, slab_ref.at[q], keep_sem.at[1])
    keep.start()
    keep_slab.start()
    shared = []

    def share(src, place, piece, target):
        n = len(shared)
        dst = slab_ref.at[place]
        if piece is not None:
            src, dst = src.at[piece], dst.at[piece]
        shared.append(remote(src, dst, slab_send.at[n], slab_recv.at[n], target))
        shared[-1].start()

    def begin():
        share(own_slab, q, near, device(z, 1 - x, c, s))
        share(own_slab, q, None, device(z, x, 1 - c, s))

    def late():
        shared[0].wait_recv()
        share(slab_ref.at[q_across], q_across, near, device(z, x, c, 1 - s))
        share(slab_ref.at[q_across], q_across, near, device(z, x, 1 - c, s))

    sems = z_send, z_recv, send_sem, recv_sem
    route(z_count, own_ref, None, out_ref, sems, lambda src, place: None, 2, 0, (5, 3), begin, late)
    shared[2].wait_recv()
    share(slab_ref.at[q_across], q_across, far, device(z, x, 1 - c, s))
    for n in (1, 3, 4):
        shared[n].wait_recv()
    for copy in shared:
        copy.wait_send()
    keep.wait()
    keep_slab.wait()


def share(own, own_slab, z_count, collective_id):
    anywhere = pl.BlockSpec(memory_space=pl.ANY)
    return pl.pallas_call(
        functools.partial(share_body, z_count),
        out_shape=[
            jax.ShapeDtypeStruct((8 * z_count,) + own.shape, own.dtype),
            jax.ShapeDtypeStruct((4,) + own_slab.shape, own_slab.dtype),
        ],
        in_specs=[anywhere, anywhere],
        out_specs=[anywhere, anywhere],
        scratch_shapes=route_sems(z_count, 2)
        + [pltpu.SemaphoreType.DMA((5,)), pltpu.SemaphoreType.DMA((5,)), pltpu.SemaphoreType.DMA((2,))],
        compiler_params=pltpu.CompilerParams(collective_id=collective_id, has_side_effects=True),
    )(own, own_slab)


def series_body(
    z_count, strip, tile, chunk, normalizer,
    level_ref, sums_ref, reg_ref, inv_ref, w_ref, gathered,
    dense, first, second, stage, recip, spread_recip, out_buf, w_own, w_slots,
    z_send, z_recv, send_sem, recv_sem, stage_sem, out_sem, w_send, w_recv,
):
    z, x, c, s = position()
    obs = lax.axis_index("obs")
    obs_count = 4 * z_count
    strips = 8 * z_count
    width = strips * strip
    half = strips // 2
    span = level_ref.shape[2]
    block_rows = width // 2
    lines = tile // LANES
    fold = 1.0 / normalizer

    barrier = pltpu.get_barrier_semaphore()
    peers = [
        {"obs": lax.rem(obs + k, obs_count), "sp": s} for k in range(1, obs_count)
    ]
    for peer in peers + [device(z, x, c, 1 - s)]:
        pl.semaphore_signal(barrier, inc=1, device_id=peer, device_id_type=pl.DeviceIdType.MESH)
    pl.semaphore_wait(barrier, obs_count)

    slots = stage.shape[0]
    waiting = []

    def lay_out(n):
        copy, place = waiting[n]
        copy.wait()
        place = lax.rem(place, 8) * z_count + lax.div(place, 8)
        rows = pl.ds(pl.multiple_of(place * strip, strip), strip)

        def put(k, turn):
            cols = pl.ds(pl.multiple_of(lax.rem(place + k, strips) * strip, strip), strip)
            block = stage[n % slots, :, pl.ds(pl.multiple_of(k * strip, strip), strip)]
            dense[rows, cols] = block
            if turn:
                dense[cols, rows] = block.T

        put(0, False)
        put(half, False)

        @pl.loop(0, half // 4)
        def _(m):
            for k in range(4):
                pl.when(m * 4 + k > 0)(lambda k=k: put(m * 4 + k, True))

    def arrive(src, place):
        n = len(waiting)
        if n >= slots:
            lay_out(n - slots)
        copy = pltpu.make_async_copy(src, stage.at[n % slots], stage_sem.at[n % slots])
        copy.start()
        waiting.append((copy, place))

    def begin():
        per = sums_ref.shape[1] // 2
        for p in range(sums_ref.shape[0]):
            lane = slice(p * per, (p + 1) * per)
            recip[lane, :] = 1.0 / (sums_ref[p, per:, :] * fold + reg_ref[lane, :])

        @pl.loop(0, width // LANES)
        def _(m):
            row = jnp.broadcast_to(recip[pl.ds(m, 1), :], (LANES, LANES))
            spread_recip[pl.ds(pl.multiple_of(m * LANES, LANES), LANES), :] = row.T

    sems = z_send, z_recv, send_sem, recv_sem
    route(z_count, level_ref.at[x * 2 + s], level_ref, gathered, sems, arrive, 4, 1, (2, 3), begin)
    for n in range(len(waiting) - slots, len(waiting)):
        lay_out(n)

    my_cols = pl.ds(pl.multiple_of(obs * tile, tile), tile)

    def by_row(values, rows):
        scale = spread_recip[rows, :]
        return values * jnp.concatenate([scale] * lines, axis=1)

    @pl.loop(0, width // chunk)
    def _(m):
        rows = pl.ds(pl.multiple_of(m * chunk, chunk), chunk)
        first[rows, :] = by_row(dense[rows, my_cols].astype(jnp.float32) * fold, rows).astype(jnp.bfloat16)

    @pl.loop(0, width // chunk)
    def _(m):
        rows = pl.ds(pl.multiple_of(m * chunk, chunk), chunk)
        prod = jnp.dot(dense[rows, :], first[...], preferred_element_type=jnp.float32)
        second[rows, :] = by_row(prod * fold, rows).astype(jnp.bfloat16)

    def my_lines(ref, at):
        return jnp.concatenate([ref[pl.ds(at + h, 1), :] for h in range(lines)], axis=1)

    per = sums_ref.shape[1] // 2
    r_row = my_lines(recip, obs * lines)
    y = my_lines(sums_ref.at[lax.div(obs * lines, per)], lax.rem(obs * lines, per))
    y = y * (1.0 / math.sqrt(normalizer))

    def emit(m):
        return pltpu.make_async_copy(
            out_buf.at[m], inv_ref.at[pl.ds(pl.multiple_of(m * chunk, chunk), chunk)], out_sem.at[m]
        )

    @pl.loop(0, block_rows // chunk)
    def _(m):
        begin_at = s * block_rows + m * chunk
        rows = pl.ds(pl.multiple_of(begin_at, chunk), chunk)
        cubic = jnp.dot(dense[rows, :], second[...], preferred_element_type=jnp.float32)
        on_diag = (begin_at + lax.broadcasted_iota(jnp.int32, (chunk, tile), 0)) == (
            obs * tile + lax.broadcasted_iota(jnp.int32, (chunk, tile), 1)
        )
        series = second[rows, :].astype(jnp.float32) - by_row(
            (dense[rows, my_cols].astype(jnp.float32) + cubic) * fold, rows
        )
        out = (jnp.where(on_diag, 1.0, 0.0) + series) * r_row
        out_buf[m] = out
        emit(m).start()
        weighted = out * y
        weighted = sum(weighted[:, h * LANES : (h + 1) * LANES] for h in range(lines))
        for h in range(chunk // LANES):
            turned = weighted[h * LANES : (h + 1) * LANES, :].T
            w_own[pl.ds(m * (chunk // LANES) + h, 1), :] = jnp.sum(turned, axis=0, keepdims=True)

    copies = []
    for k in range(1, obs_count):
        copies.append(remote(w_own, w_slots.at[obs], w_send.at[k], w_recv.at[k], peers[k - 1]))
        copies[-1].start()
    w_slots[obs] = w_own[...]
    for copy in copies:
        copy.wait()
    total = w_slots[0]
    for k in range(1, obs_count):
        total = total + w_slots[k]
    w_ref[...] = total
    for m in range(block_rows // chunk):
        emit(m).wait()


def series_tile(level, sums, regularizer, z_count, tile, normalizer, collective_id):
    _, strip, span = level.shape
    strips = 8 * z_count
    width = strips * strip
    block_rows = width // 2
    chunk = min(512, block_rows)
    obs_count = 4 * z_count
    w_shape = (block_rows // LANES, LANES)
    anywhere = pl.BlockSpec(memory_space=pl.ANY)
    vmem = pl.BlockSpec(memory_space=pltpu.VMEM)
    inverse_tile, weights, _ = pl.pallas_call(
        functools.partial(series_body, z_count, strip, tile, chunk, normalizer),
        out_shape=[
            jax.ShapeDtypeStruct((block_rows, tile), jnp.float32),
            jax.ShapeDtypeStruct(w_shape, jnp.float32),
            jax.ShapeDtypeStruct((strips, strip, span), level.dtype),
        ],
        in_specs=[anywhere, vmem, vmem],
        out_specs=[anywhere, vmem, anywhere],
        scratch_shapes=[
            pltpu.VMEM((width, width), jnp.bfloat16),
            pltpu.VMEM((width, tile), jnp.bfloat16),
            pltpu.VMEM((width, tile), jnp.bfloat16),
            pltpu.VMEM((2, strip, span), jnp.bfloat16),
            pltpu.VMEM((width // LANES, LANES), jnp.float32),
            pltpu.VMEM((width, LANES), jnp.float32),
            pltpu.VMEM((block_rows // chunk, chunk, tile), jnp.float32),
            pltpu.VMEM(w_shape, jnp.float32),
            pltpu.VMEM((obs_count,) + w_shape, jnp.float32),
        ]
        + route_sems(z_count, 4)
        + [
            pltpu.SemaphoreType.DMA((2,)),
            pltpu.SemaphoreType.DMA((block_rows // chunk,)),
            pltpu.SemaphoreType.DMA((obs_count,)),
            pltpu.SemaphoreType.DMA((obs_count,)),
        ],
        compiler_params=pltpu.CompilerParams(
            collective_id=collective_id, has_side_effects=True, vmem_limit_bytes=VMEM_BYTES
        ),
    )(level, sums, regularizer.reshape(width // LANES, LANES))
    return inverse_tile, weights.reshape(block_rows)


def by_strips(descriptors, candidates, sparse_index, targets, regularizer):
    obs_count = lax.axis_size("obs")
    sp_count = lax.axis_size("sp")
    obs_pos = lax.axis_index("obs")
    sp_pos = lax.axis_index("sp")
    z_count = obs_count // 4
    width = sparse_index.shape[0]
    tile = width // obs_count
    strip = width // (obs_count * sp_count)
    mine = strip * z_count
    span = width // 2 + strip
    window = width // 2 + mine
    rows, depth = descriptors.shape
    normalizer = 24.0 * rows * obs_count

    extra = jnp.pad(targets.reshape(rows // depth, depth), ((0, 32 - rows // depth), (0, 0)))
    shard = jnp.concatenate([unit_rows(descriptors), extra])
    piece = candidates.shape[0] // sp_count
    own = lax.dynamic_slice_in_dim(candidates, sp_pos * piece, piece)
    table, slab = share(unit_rows(own), shard, z_count, 2)
    table = table.reshape(-1, depth)
    place = lax.rem(obs_pos, 4) * sp_count + sp_pos
    wanted = lax.dynamic_slice_in_dim(
        jnp.concatenate([sparse_index, sparse_index]), place * mine, window
    )
    sparse = table.at[wanted].get(mode="promise_in_bounds")
    slab_targets = slab[:, rows : rows + rows // depth].reshape(4 * rows)
    level, sums = slab_gram(
        slab, sparse, slab_targets, z_count, sp_count, strip, span, tile, rows, 0
    )
    return series_tile(level, sums, regularizer, z_count, tile, normalizer, 3)


def slab_body(z_count, sp_count, strip, tile, root, *refs):
    norm_ref, sp_ref, tgt_ref, level_ref, sums_ref = refs[:5]
    kbuf, ktr, parts, from_low, from_high, done, zsums, gsums = refs[5:13]
    up_send, up_recv, down_send, down_recv, side_send, side_recv, zs_send, zs_recv, gs_send, gs_recv, keep_sem = refs[13:]
    obs = lax.axis_index("obs")
    s = lax.axis_index("sp")
    z, x, c, _ = position()
    q = x * 2 + c
    group = 4 * sp_count
    p = q * sp_count + s
    last = z_count - 1
    shard = tgt_ref.shape[1] // 4
    mine = strip * z_count
    lines = mine // LANES

    z_others = [{"obs": lax.rem(z + k, z_count) * 4 + q, "sp": s} for k in range(1, z_count)]
    group_others = []
    for k in range(1, group):
        to = lax.rem(p + k, group)
        group_others.append({"obs": z * 4 + lax.div(to, sp_count), "sp": lax.rem(to, sp_count)})
    barrier = pltpu.get_barrier_semaphore()
    for other in z_others + group_others:
        pl.semaphore_signal(barrier, inc=1, device_id=other, device_id_type=pl.DeviceIdType.MESH)
    pl.semaphore_wait(barrier, len(z_others) + len(group_others))

    def kernel_tile(t, own):
        cols = pl.ds(pl.multiple_of(t * tile, tile), tile)
        for k in range(4):
            rows = pl.ds(k * shard, shard)
            inner = lax.dot_general(
                norm_ref[k, :shard, :], sp_ref[cols, :], (((1,), (1,)), ((), ())),
                preferred_element_type=jnp.float32,
            )
            scaled = inner * root
            squared = scaled * scaled
            kb = ((squared - 6.0) * squared + 3.0).astype(jnp.bfloat16)
            kbuf[rows, cols] = kb
            if own:
                ktr[cols, rows] = kb.T

    def row_sums():
        for t in range(mine // tile):
            cols = slice(t * tile, (t + 1) * tile)
            weighted = jnp.dot(tgt_ref[...], kbuf[:, cols], preferred_element_type=jnp.float32)
            square = jnp.zeros((1, tile), jnp.float32)
            for k in range(4):
                kf = kbuf[k * shard : (k + 1) * shard, cols].astype(jnp.float32)
                square = square + jnp.sum(kf * kf, axis=0, keepdims=True)
            for h in range(tile // LANES):
                line = t * (tile // LANES) + h
                lane = slice(h * LANES, (h + 1) * LANES)
                zsums[z, line : line + 1, :] = weighted[0:1, lane]
                zsums[z, lines + line : lines + line + 1, :] = square[:, lane]

    groups = kbuf.shape[1] // mine

    def piece(t, g):
        begin = t * strip if g == 0 else 0
        end = mine if g < groups - 1 else (t + 1) * strip
        return begin, g * mine + begin - t * strip, end - begin

    def cut(t, g):
        _, begin, size = piece(t, g)
        return pl.ds(begin, size)

    def up(t, g):
        n, at = t * groups + g, (t, slice(None), cut(t, g))
        return remote(
            parts.at[at], from_low.at[at], up_send.at[n], up_recv.at[n],
            {"obs": lax.rem(z + 1, z_count) * 4 + q, "sp": s},
        )

    def down(t, g):
        n, at = t * groups + g, (t, slice(None), cut(t, g))
        return remote(
            parts.at[at], from_high.at[at], down_send.at[n], down_recv.at[n],
            {"obs": lax.rem(z + last, z_count) * 4 + q, "sp": s},
        )

    def gram_group(g):
        cols = slice(g * mine, (g + 1) * mine)
        made = jnp.dot(ktr[...], kbuf[:, cols], preferred_element_type=jnp.float32).astype(jnp.bfloat16)
        for t in range(z_count):
            begin, at, size = piece(t, g)
            parts[t, :, at : at + size] = made[t * strip : (t + 1) * strip, begin : begin + size]

    def pass_on(place, n):
        if place > 0 and 0 <= n - place < groups:
            for t in range(last, place, -1):
                g = n - place
                up(t, g).wait_recv()
                parts[t, :, cut(t, g)] = parts[t, :, cut(t, g)] + from_low[t, :, cut(t, g)]
                up(t, g).start()
        if place < last and 0 <= n - (last - place) < groups:
            for t in range(place):
                g = n - (last - place)
                down(t, g).wait_recv()
                parts[t, :, cut(t, g)] = parts[t, :, cut(t, g)] + from_high[t, :, cut(t, g)]
                down(t, g).start()

    mine_at, across_at, beside_at = x * 2 + s, (1 - x) * 2 + s, x * 2 + 1 - s
    across, beside = device(z, 1 - x, c, s), device(z, x, c, 1 - s)
    half = strip // 2

    def side(place, g, k):
        rows = (slice(None), slice(None), pl.ds(0, half), pl.ds(half, half))[k]
        at = (mine_at, mine_at, across_at, beside_at)[k]
        src = done.at[:, cut(place, g)] if k < 2 else level_ref.at[at, rows, cut(place, g)]
        return remote(
            src, level_ref.at[at, rows, cut(place, g)], side_send.at[g * 4 + k], side_recv.at[g * 4 + k],
            (across, beside, beside, across)[k],
        )

    def keep(place, g):
        return pltpu.make_async_copy(
            done.at[:, cut(place, g)], level_ref.at[mine_at, :, cut(place, g)], keep_sem.at[g]
        )

    def close(place, g):
        total = parts[place, :, cut(place, g)].astype(jnp.float32)
        if place > 0:
            up(place, g).wait_recv()
            total = total + from_low[place, :, cut(place, g)].astype(jnp.float32)
        if place < last:
            down(place, g).wait_recv()
            total = total + from_high[place, :, cut(place, g)].astype(jnp.float32)
        if g == 0:
            row = lax.broadcasted_iota(jnp.int32, total.shape, 0)
            col = lax.broadcasted_iota(jnp.int32, total.shape, 1)
            total = jnp.where(row == col, 0.0, total)
        done[:, cut(place, g)] = total.astype(jnp.bfloat16)
        side(place, g, 0).start()
        side(place, g, 1).start()
        keep(place, g).start()

    def progress(place, n):
        pass_on(place, n)
        g = n - max(place, last - place)
        if 0 <= g < groups:
            close(place, g)
        if 0 <= g - 1 < groups:
            for k in range(2):
                side(place, g - 1, k).wait_recv()
                side(place, g - 1, k + 2).start()
        if 0 <= g - 2 < groups:
            for k in range(2):
                side(place, g - 2, k + 2).wait_recv()

    z_copies, g_copies = [], []
    for n in range(groups + last + 2):
        if n < groups:

            @pl.loop(n * mine // tile, (n + 1) * mine // tile)
            def _(t):
                kernel_tile(t, n == 0)

            gram_group(n)

            @pl.when(z == 0)
            def _():
                for t in range(last, 0, -1):
                    up(t, n).start()

            @pl.when(z == last)
            def _():
                for t in range(last):
                    down(t, n).start()

        if n == 0:
            row_sums()
            for k in range(1, z_count):
                z_copies.append(remote(zsums.at[z], zsums.at[z], zs_send.at[k], zs_recv.at[k], z_others[k - 1]))
                z_copies[-1].start()
        if n == 1:
            for copy in z_copies:
                copy.wait_recv()
            total = zsums[0]
            for m in range(1, z_count):
                total = total + zsums[m]
            gsums[p] = total
            for m in range(1, group):
                g_copies.append(
                    remote(gsums.at[p], gsums.at[p], gs_send.at[m], gs_recv.at[m], group_others[m - 1])
                )
                g_copies[-1].start()
        for place in range(z_count):
            pl.when(z == place)(functools.partial(progress, place, n))

    def finish(place):
        for g in range(groups):
            for k in range(4):
                side(place, g, k).wait_send()
            keep(place, g).wait()
            for t in range(z_count):
                if t > place:
                    up(t, g).wait_send()
                if t < place:
                    down(t, g).wait_send()

    for place in range(z_count):
        pl.when(z == place)(functools.partial(finish, place))

    for copy in g_copies:
        copy.wait()
    for copy in z_copies:
        copy.wait_send()
    sums_ref[...] = gsums[...]


def slab_gram(slab, sparse, targets, z_count, sp_count, strip, span, tile, rows, collective_id):
    depth = slab.shape[2]
    window = sparse.shape[0]
    group = 4 * sp_count
    mine = strip * z_count
    lines = 2 * mine // LANES
    vmem = pl.BlockSpec(memory_space=pltpu.VMEM)
    part = (z_count, strip, span)
    groups = window // mine
    sems = [pltpu.SemaphoreType.DMA((z_count * groups,))] * 4 + [pltpu.SemaphoreType.DMA((4 * groups,))] * 2
    sems += [pltpu.SemaphoreType.DMA((z_count,))] * 2 + [pltpu.SemaphoreType.DMA((group,))] * 2
    sems += [pltpu.SemaphoreType.DMA((groups,))]
    return pl.pallas_call(
        functools.partial(slab_body, z_count, sp_count, strip, tile, math.sqrt(depth)),
        out_shape=[
            jax.ShapeDtypeStruct((4, strip, span), jnp.bfloat16),
            jax.ShapeDtypeStruct((group, lines, LANES), jnp.float32),
        ],
        in_specs=[vmem, vmem, vmem],
        out_specs=[pl.BlockSpec(memory_space=pl.ANY), vmem],
        scratch_shapes=[
            pltpu.VMEM((4 * rows, window), jnp.bfloat16),
            pltpu.VMEM((mine, 4 * rows), jnp.bfloat16),
            pltpu.VMEM(part, jnp.bfloat16),
            pltpu.VMEM(part, jnp.bfloat16),
            pltpu.VMEM(part, jnp.bfloat16),
            pltpu.VMEM(part[1:], jnp.bfloat16),
            pltpu.VMEM((z_count, lines, LANES), jnp.float32),
            pltpu.VMEM((group, lines, LANES), jnp.float32),
        ] + sems,
        compiler_params=pltpu.CompilerParams(
            collective_id=collective_id, has_side_effects=True, vmem_limit_bytes=VMEM_BYTES
        ),
    )(slab, sparse, jnp.broadcast_to(targets[None, :], (16, 4 * rows)))


def on_device(descriptors, candidates, sparse_index, targets, regularizer):
    obs_count = lax.axis_size("obs")
    sp_count = lax.axis_size("sp")
    obs_pos = lax.axis_index("obs")
    sp_pos = lax.axis_index("sp")
    width = sparse_index.shape[0]
    if sp_count == 2 and width % (obs_count * sp_count * LANES) == 0:
        return by_strips(descriptors, candidates, sparse_index, targets, regularizer)
    tile = width // obs_count
    share = -(-((obs_count // 2 + 1) * tile) // (sp_count * LANES)) * LANES
    normalizer = 24.0 * descriptors.shape[0] * obs_count

    normed = unit_rows(descriptors)
    piece = candidates.shape[0] // sp_count
    own = lax.dynamic_slice_in_dim(candidates, sp_pos * piece, piece)
    table = spread(unit_rows(own), obs_count, sp_count, 2)
    sparse = table.at[sparse_index].get(mode="promise_in_bounds")

    gram, sums = gram_call(
        sp_pos[None].astype(jnp.int32), normed, sparse, targets, obs_count, tile, share, sp_count
    )
    sums = add_over_obs(sums, obs_count, 0)
    part = lax.psum_scatter(gram, "obs", scatter_dimension=0, tiled=True)

    projected = sums[0] / math.sqrt(normalizer)
    root = lax.rsqrt(sums[1] / normalizer + regularizer)
    col_start = obs_pos * tile
    rrow = lax.dynamic_slice_in_dim(root, col_start, tile)
    window_start = col_start + sp_pos * share
    rwin = lax.dynamic_slice_in_dim(jnp.concatenate([root, root]), window_start, share)
    offset = sp_pos * share + lax.iota(jnp.int32, share)
    on_diag = lax.iota(jnp.int32, tile)[:, None] == offset[None, :]
    scaled = jnp.where(
        on_diag, 0.0, part.astype(jnp.float32) * (rrow[:, None] / normalizer) * rwin[None, :]
    ).astype(jnp.bfloat16)
    packed = spread(scaled, obs_count, sp_count, 3)

    y = lax.dynamic_slice_in_dim(projected, col_start, tile)
    pos = jnp.stack([sp_pos, obs_pos]).astype(jnp.int32)
    inverse_tile, part_w = newton_call(
        pos, packed, root, rrow, y, obs_count, tile, share, sp_count
    )
    return inverse_tile, add_over_obs(part_w[0], obs_count, 1)


def solution(mesh):
    in_specs = (P("obs", None), P("obs", None), P(), P("obs"), P())
    out_specs = (P("sp", "obs"), P("sp"))
    return jax.shard_map(
        on_device, mesh=mesh, in_specs=in_specs, out_specs=out_specs, check_vma=False
    )
```

```python
import functools
import math

import jax
import jax.numpy as jnp
from jax import lax
from jax.experimental import pallas as pl
from jax.experimental.pallas import tpu as pltpu
from jax.sharding import PartitionSpec as P

epsilon = 1e-06
LANES = 128
VMEM_BYTES = 58 * 2**20


def unit_rows(row_block):
    values = row_block.astype(jnp.float32)
    return (values * lax.rsqrt(jnp.sum(values * values, axis=1, keepdims=True) + epsilon)).astype(
        jnp.bfloat16
    )


def gram_body(blocks, tile, share, ext, root, s_ref, norm_ref, sp_ref, tgt_ref, gram_ref, ws_ref, kext):
    step = pl.program_id(0)
    width = blocks * tile

    @pl.when(step < blocks)
    def _():
        inner = lax.dot_general(
            norm_ref[...], sp_ref[...], (((1,), (1,)), ((), ())), preferred_element_type=jnp.float32
        )
        scaled = inner * root
        squared = scaled * scaled
        kb = ((squared - 6.0) * squared + 3.0).astype(jnp.bfloat16)
        kext[:, pl.ds(pl.multiple_of(step * tile, tile), tile)] = kb

        @pl.when(step < ext)
        def _():
            kext[:, pl.ds(pl.multiple_of(width + step * tile, tile), tile)] = kb

        kf = kb.astype(jnp.float32)
        weighted = jnp.dot(tgt_ref[...], kb, preferred_element_type=jnp.float32)
        ws_ref[0:1, :] = weighted[0:1, :]
        ws_ref[1:2, :] = jnp.sum(kf * kf, axis=0, keepdims=True)

    @pl.when(step >= blocks)
    def _():
        j = step - blocks
        cols = pl.ds(pl.multiple_of(j * tile, tile), tile)
        window = pl.ds(pl.multiple_of(j * tile + s_ref[0] * share, LANES), share)
        gram_ref[...] = lax.dot_general(
            kext[:, cols], kext[:, window], (((0,), (0,)), ((), ())), preferred_element_type=jnp.float32
        ).astype(jnp.bfloat16)


def gram_call(s_pos, normed, sparse, targets, blocks, tile, share, sp_count):
    rows, depth = normed.shape
    width = blocks * tile
    ext = -(-((blocks - 1) * tile + sp_count * share - width) // tile)
    last = blocks - 1
    return pl.pallas_call(
        functools.partial(gram_body, blocks, tile, share, ext, math.sqrt(depth)),
        grid_spec=pltpu.PrefetchScalarGridSpec(
            num_scalar_prefetch=1,
            grid=(2 * blocks,),
            in_specs=[
                pl.BlockSpec((rows, depth), lambda g, s: (0, 0)),
                pl.BlockSpec((tile, depth), lambda g, s: (jnp.minimum(g, last), 0)),
                pl.BlockSpec((16, rows), lambda g, s: (0, 0)),
            ],
            out_specs=[
                pl.BlockSpec((tile, share), lambda g, s: (jnp.maximum(g - blocks, 0), 0)),
                pl.BlockSpec((2, tile), lambda g, s: (0, jnp.minimum(g, last))),
            ],
            scratch_shapes=[pltpu.VMEM((rows, width + ext * tile), jnp.bfloat16)],
        ),
        out_shape=[
            jax.ShapeDtypeStruct((width, share), jnp.bfloat16),
            jax.ShapeDtypeStruct((2, width), jnp.float32),
        ],
        compiler_params=pltpu.CompilerParams(vmem_limit_bytes=VMEM_BYTES),
    )(s_pos, normed, sparse, jnp.broadcast_to(targets[None, :], (16, rows)))


def newton_body(
    blocks, tile, share, sp_count, chunk, block_rows,
    pos_ref, packed_ref, rcol_ref, rrow_ref, y_ref, inv_ref, w_ref, dense, prod,
):
    step = pl.program_id(0)
    width = blocks * tile
    half = blocks // 2
    p_steps = width // chunk
    my_cols = pl.ds(pl.multiple_of(pos_ref[1] * tile, tile), tile)

    @pl.when(step < blocks)
    def _():
        rows = pl.ds(pl.multiple_of(step * tile, tile), tile)
        for s in range(sp_count):
            for q in range(share // LANES):
                offset = s * share + q * LANES
                if offset >= (half + 1) * tile:
                    continue
                col = lax.rem(step * tile + offset, width)
                cols = pl.ds(pl.multiple_of(col, LANES), LANES)
                block = packed_ref[s * tile : (s + 1) * tile, q * LANES : (q + 1) * LANES]
                dense[rows, cols] = block
                if tile <= offset < half * tile:
                    dense[cols, rows] = block.T

    @pl.when((step >= blocks) & (step < blocks + p_steps))
    def _():
        rows = pl.ds(pl.multiple_of((step - blocks) * chunk, chunk), chunk)
        prod[rows, :] = jnp.dot(
            dense[rows, :], dense[:, my_cols], preferred_element_type=jnp.float32
        ).astype(jnp.bfloat16)

    @pl.when(step >= blocks + p_steps)
    def _():
        local = pl.multiple_of((step - blocks - p_steps) * chunk, chunk)
        start = pl.multiple_of(pos_ref[0] * block_rows + local, chunk)
        rows = pl.ds(start, chunk)
        cubic = jnp.dot(dense[rows, :], prod[...], preferred_element_type=jnp.float32)
        on_diag = (start + lax.broadcasted_iota(jnp.int32, (chunk, tile), 0)) == (
            pos_ref[1] * tile + lax.broadcasted_iota(jnp.int32, (chunk, tile), 1)
        )
        series = (
            jnp.where(on_diag, 1.0, 0.0)
            - dense[rows, my_cols].astype(jnp.float32)
            + prod[rows, :].astype(jnp.float32)
            - cubic
        )
        out = series * rcol_ref[rows, :] * rrow_ref[...]
        inv_ref[pl.ds(local, chunk), :] = out
        w_ref[:, pl.ds(local, chunk)] = lax.dot_general(
            y_ref[...], out, (((1,), (1,)), ((), ())),
            precision=lax.Precision.HIGHEST, preferred_element_type=jnp.float32,
        )


def newton_call(pos, packed, root_recip, rrow, y, blocks, tile, share, sp_count):
    width = blocks * tile
    block_rows = width // sp_count
    chunk = min(512, block_rows)
    grid = blocks + width // chunk + block_rows // chunk
    last = blocks - 1
    return pl.pallas_call(
        functools.partial(newton_body, blocks, tile, share, sp_count, chunk, block_rows),
        grid_spec=pltpu.PrefetchScalarGridSpec(
            num_scalar_prefetch=1,
            grid=(grid,),
            in_specs=[
                pl.BlockSpec((sp_count * tile, share), lambda g, p: (jnp.minimum(g, last), 0)),
                pl.BlockSpec((width, 1), lambda g, p: (0, 0)),
                pl.BlockSpec((1, tile), lambda g, p: (0, 0)),
                pl.BlockSpec((8, tile), lambda g, p: (0, 0)),
            ],
            out_specs=[
                pl.BlockSpec((block_rows, tile), lambda g, p: (0, 0)),
                pl.BlockSpec((8, block_rows), lambda g, p: (0, 0)),
            ],
            scratch_shapes=[
                pltpu.VMEM((width, width), jnp.bfloat16),
                pltpu.VMEM((width, tile), jnp.bfloat16),
            ],
        ),
        out_shape=[
            jax.ShapeDtypeStruct((block_rows, tile), jnp.float32),
            jax.ShapeDtypeStruct((8, block_rows), jnp.float32),
        ],
        compiler_params=pltpu.CompilerParams(vmem_limit_bytes=VMEM_BYTES),
    )(pos, packed, root_recip[:, None], rrow[None, :], jnp.broadcast_to(y[None, :], (8, tile)))


def add_body(count, in_ref, out_ref, slots, send_sem, recv_sem):
    me = lax.axis_index("obs")
    barrier = pltpu.get_barrier_semaphore()
    for k in range(1, count):
        pl.semaphore_signal(
            barrier, inc=1, device_id={"obs": lax.rem(me + k, count)}, device_id_type=pl.DeviceIdType.MESH
        )
    pl.semaphore_wait(barrier, count - 1)
    copies = []
    for k in range(1, count):
        copy = pltpu.make_async_remote_copy(
            src_ref=in_ref,
            dst_ref=slots.at[me],
            send_sem=send_sem.at[k],
            recv_sem=recv_sem.at[k],
            device_id={"obs": lax.rem(me + k, count)},
            device_id_type=pl.DeviceIdType.MESH,
        )
        copy.start()
        copies.append(copy)
    slots[me] = in_ref[...]
    for copy in copies:
        copy.wait()
    total = slots[0]
    for k in range(1, count):
        total = total + slots[k]
    out_ref[...] = total


def add_over_obs(values, count, collective_id):
    shape = values.shape
    flat = values.reshape(values.size // LANES, LANES)
    total = pl.pallas_call(
        functools.partial(add_body, count),
        out_shape=jax.ShapeDtypeStruct(flat.shape, flat.dtype),
        in_specs=[pl.BlockSpec(memory_space=pltpu.VMEM)],
        out_specs=pl.BlockSpec(memory_space=pltpu.VMEM),
        scratch_shapes=[
            pltpu.VMEM((count,) + flat.shape, flat.dtype),
            pltpu.SemaphoreType.DMA((count,)),
            pltpu.SemaphoreType.DMA((count,)),
        ],
        cost_estimate=pl.CostEstimate(
            flops=count * flat.size, bytes_accessed=400 * flat.size, transcendentals=0
        ),
        compiler_params=pltpu.CompilerParams(collective_id=collective_id, has_side_effects=True),
    )(flat)
    return total.reshape(shape)


def spread_keys(z_count, sp_count):
    keys = [("z", k) for k in range(1, z_count)]
    for k in range(z_count):
        keys += [("x", k), ("core", k), ("core_x", k)]
        for d in range(1, sp_count):
            keys += [(name, k, d) for name in ("sp", "sp_a", "x_b", "core_sp", "core_a", "core_b")]
    return {key: place for place, key in enumerate(keys)}


def spread_body(z_count, sp_count, in_ref, out_ref, send_sem, recv_sem, own_sem):
    places = spread_keys(z_count, sp_count)
    obs = lax.axis_index("obs")
    s = lax.axis_index("sp")
    z, x, c = lax.div(obs, 4), lax.rem(lax.div(obs, 2), 2), lax.rem(obs, 2)
    half = in_ref.shape[0] // 2
    upper, lower = pl.ds(0, half), pl.ds(half, half)
    zs = [lax.bitwise_xor(z, k) for k in range(z_count)]
    to_sp = [lax.rem(s + d, sp_count) for d in range(sp_count)]
    from_sp = [lax.rem(s - d + sp_count, sp_count) for d in range(sp_count)]

    def device(z_to, x_to, c_to, s_to):
        return {"obs": z_to * 4 + x_to * 2 + c_to, "sp": s_to}

    def slot(z_of, x_of, s_of):
        return ((z_of * 2 + x_of) * 2 + c) * sp_count + s_of

    own_slot = slot(z, x, s)
    across, sibling = device(z, 1 - x, c, s), device(z, x, 1 - c, s)
    others = [device(zs[k], x, c, s) for k in range(1, z_count)]
    others += [device(z, x, c, to_sp[d]) for d in range(1, sp_count)]
    others += [across, sibling]
    barrier = pltpu.get_barrier_semaphore()
    for other in others:
        pl.semaphore_signal(barrier, inc=1, device_id=other, device_id_type=pl.DeviceIdType.MESH)
    pl.semaphore_wait(barrier, len(others))

    sent = {}

    def send(key, place, target, rows=None, own=False):
        src = in_ref if own else out_ref.at[place]
        dst = out_ref.at[place]
        if rows is not None:
            src, dst = src.at[rows], dst.at[rows]
        copy = pltpu.make_async_remote_copy(
            src_ref=src,
            dst_ref=dst,
            send_sem=send_sem.at[places[key]],
            recv_sem=recv_sem.at[places[key]],
            device_id=target,
            device_id_type=pl.DeviceIdType.MESH,
        )
        copy.start()
        sent[key] = copy

    keep = pltpu.make_async_copy(in_ref, out_ref.at[own_slot], own_sem)
    keep.start()
    for k in range(1, z_count):
        send(("z", k), own_slot, others[k - 1], own=True)

    def fan_out(k):
        place = slot(zs[k], x, s)
        send(("x", k), place, across, own=k == 0)
        for d in range(1, sp_count):
            send(("sp", k, d), place, device(z, x, c, to_sp[d]), own=k == 0)
        send(("core", k), place, sibling, own=k == 0)

    def relay(k):
        sent[("x", k)].wait_recv()
        place = slot(zs[k], 1 - x, s)
        for d in range(1, sp_count):
            send(("sp_a", k, d), place, device(z, x, c, to_sp[d]), upper)
        send(("core_x", k), place, sibling)
        for d in range(1, sp_count):
            sent[("sp", k, d)].wait_recv()
            place = slot(zs[k], x, from_sp[d])
            send(("x_b", k, d), place, across, lower)
            send(("core_sp", k, d), place, sibling)

    def finish(k):
        for d in range(1, sp_count):
            place = slot(zs[k], 1 - x, from_sp[d])
            sent[("sp_a", k, d)].wait_recv()
            send(("core_a", k, d), place, sibling, upper)
            sent[("x_b", k, d)].wait_recv()
            send(("core_b", k, d), place, sibling, lower)

    fan_out(0)
    for k in range(1, z_count):
        sent[("z", k)].wait_recv()
        fan_out(k)
        relay(k - 1)
        if k > 1:
            finish(k - 2)
    relay(z_count - 1)
    if z_count > 1:
        finish(z_count - 2)
    finish(z_count - 1)
    keep.wait()
    for key, copy in sent.items():
        copy.wait_send()
        if key[0].startswith("core"):
            copy.wait_recv()


def spread(shard, obs_count, sp_count, collective_id):
    rows, cols = shard.shape
    z_count = obs_count // 4
    total = obs_count * sp_count
    sems = len(spread_keys(z_count, sp_count))
    gathered = pl.pallas_call(
        functools.partial(spread_body, z_count, sp_count),
        out_shape=jax.ShapeDtypeStruct((total, rows, cols), shard.dtype),
        in_specs=[pl.BlockSpec(memory_space=pl.ANY)],
        out_specs=pl.BlockSpec(memory_space=pl.ANY),
        scratch_shapes=[
            pltpu.SemaphoreType.DMA((sems,)),
            pltpu.SemaphoreType.DMA((sems,)),
            pltpu.SemaphoreType.DMA,
        ],
        compiler_params=pltpu.CompilerParams(collective_id=collective_id, has_side_effects=True),
    )(shard)
    return gathered.reshape(total * rows, cols)


def position():
    obs = lax.axis_index("obs")
    return lax.div(obs, 4), lax.rem(lax.div(obs, 2), 2), lax.rem(obs, 2), lax.axis_index("sp")


def device(z, x, c, s):
    return {"obs": z * 4 + x * 2 + c, "sp": s}


def remote(src, dst, send_sem, recv_sem, target):
    return pltpu.make_async_remote_copy(
        src_ref=src, dst_ref=dst, send_sem=send_sem, recv_sem=recv_sem,
        device_id=target, device_id_type=pl.DeviceIdType.MESH,
    )


def route_sems(z_count, chunks):
    return [
        pltpu.SemaphoreType.DMA((4 * chunks * (z_count + 1),)),
        pltpu.SemaphoreType.DMA((4 * chunks * z_count,)),
        pltpu.SemaphoreType.DMA((4 * (chunks + 1) * z_count,)),
        pltpu.SemaphoreType.DMA((4 * (chunks + 1) * z_count,)),
    ]


def route_greet(z_count):
    z, x, c, s = position()
    barrier = pltpu.get_barrier_semaphore()
    others = [device(z, 1 - x, c, s), device(z, x, 1 - c, s), device(z, x, c, 1 - s)]
    others += [device(lax.rem(z + k, z_count), x, c, s) for k in range(1, z_count)]
    for other in others:
        pl.semaphore_signal(barrier, inc=1, device_id=other, device_id_type=pl.DeviceIdType.MESH)
    pl.semaphore_wait(barrier, len(others))


OWN, ACROSS, BESIDE, DIAGONAL = range(4)


def route(z_count, home, out_ref, sems, arrive, chunks, diagonal, lag, begin, late=None):
    z_send, z_recv, send_sem, recv_sem = sems
    z, x, c, s = position()
    last = z_count - 1
    rows = out_ref.shape[1]
    high = rows // chunks
    known = home is None
    across, beside, sibling = device(z, 1 - x, c, s), device(z, x, c, 1 - s), device(z, x, 1 - c, s)
    along = {OWN: chunks, ACROSS: 0, BESIDE: 0, DIAGONAL: diagonal}

    nearer = jnp.minimum(z, last - z)
    origins = [z]
    for a in range(last):
        both = jnp.where(a % 2 == 0, z - (a // 2 + 1), z + (a // 2 + 1))
        single = jnp.where(z <= last - z, z + (a - nearer + 1), z - (a - nearer + 1))
        origins.append(jnp.where(a < 2 * nearer, both, single))

    def slot(col, a, c_of=c):
        x_of = 1 - x if col in (ACROSS, DIAGONAL) else x
        s_of = 1 - s if col in (BESIDE, DIAGONAL) else s
        return ((origins[a] * 2 + x_of) * 2 + c_of) * 2 + s_of

    def shard(col, a):
        return out_ref.at[slot(col, a)] if a or col != OWN or known else home

    sent = {}

    def send(key, col, a, target, begin=0, size=rows):
        cut = pl.ds(begin, size)
        n = len(sent)
        sent[key] = remote(
            shard(col, a).at[cut], out_ref.at[slot(col, a)].at[cut], send_sem.at[n], recv_sem.at[n], target
        )
        sent[key].start()

    hops = []

    def hop(col, a, j, n, target_z, when):
        cut = pl.ds(j * high, high)
        copy = remote(
            shard(col, a).at[cut], out_ref.at[slot(col, a)].at[cut],
            z_send.at[(col * chunks + j) * (z_count + 1) + n], z_recv.at[(col * chunks + j) * z_count + origins[a]],
            device(jnp.clip(target_z, 0, last), x, c, s),
        )
        pl.when(when)(copy.start)
        hops.append((when, copy))

    def set_off(col, j):
        if j < along[col]:
            hop(col, 0, j, 0, z + 1, z < last)
            hop(col, 0, j, 1, z - 1, z > 0)

    def pass_on(col, a, j):
        if j < along[col]:
            held = out_ref.at[slot(col, a)].at[pl.ds(j * high, high)]
            arrival = remote(
                held, held, z_send.at[0], z_recv.at[(col * chunks + j) * z_count + origins[a]], across
            ).wait_recv
            if not known or col != OWN:
                arrival()
            elif a > 1:
                pl.when((origins[a] > z + 1) | (origins[a] < z - 1))(arrival)
            target_z = jnp.where(origins[a] < z, z + 1, z - 1)
            hop(col, a, j, a + 1, target_z, (target_z >= 0) & (target_z <= last))

    finished = []

    def complete(now, a, *cols):
        for col in cols:
            send(("core", col, a), col, a, sibling)
            arrive(shard(col, a), slot(col, a))
            finished.append((now, a, col))

    def from_sibling(before):
        while finished and finished[0][0] < before:
            _, a, col = finished.pop(0)
            sent[("core", col, a)].wait_recv()
            place = slot(col, a, 1 - c)
            arrive(out_ref.at[place], place)

    def fan_out(a, j):
        send(("x", a, j), OWN, a, across, j * high, high)
        send(("y", a, j), OWN, a, beside, j * high, high)

    def relay(a, j):
        direct = a == 0 or j >= diagonal
        sent[("x", a, j)].wait_recv()
        if direct:
            send(("ya", a, j), ACROSS, a, beside, j * high, high // 2)
        sent[("y", a, j)].wait_recv()
        if direct:
            send(("xb", a, j), BESIDE, a, across, j * high + high // 2, high // 2)

    def finish(a, j):
        if ("ya", a, j) in sent:
            sent[("ya", a, j)].wait_recv()
            sent[("xb", a, j)].wait_recv()

    first = 1 if known else 0
    for j in range(chunks):
        if known:
            set_off(DIAGONAL, j)
        else:
            set_off(OWN, j)
            fan_out(0, j)
    begin()
    complete(-1, 0, OWN)
    if known:
        complete(-1, 0, ACROSS, BESIDE, DIAGONAL)
    items = [(a, j) for j in range(chunks) for a in range(first, 2)]
    items += [(a, j) for a in range(2, z_count) for j in range(chunks)]
    ends = [items.index((a, chunks - 1)) for a in range(1, z_count)]
    ready = set()
    for now in range(len(items) + max(sum(lag), 3)):
        if now < len(items):
            a, j = items[now]
            if a:
                pass_on(OWN, a, j)
                fan_out(a, j)
                if j == chunks - 1:
                    complete(now, a, OWN)
        if 0 <= now - lag[0] < len(items):
            a, j = items[now - lag[0]]
            relay(a, j)
            if j == chunks - 1:
                complete(now, a, ACROSS, BESIDE)
        if now - 3 in ends:
            a = ends.index(now - 3) + 1
            for j in range(chunks):
                pass_on(DIAGONAL, a, j)
            ready.add(a)
        if 0 <= now - sum(lag) < len(items):
            a, j = items[now - sum(lag)]
            finish(a, j)
            if a == 0:
                set_off(DIAGONAL, j)
            if j == chunks - 1:
                assert a in ready or not a
                complete(now, a, DIAGONAL)
        if now == len(items) - 2 and late is not None:
            late()
        from_sibling(now - 2)
    from_sibling(now + 1)
    for copy in sent.values():
        copy.wait_send()
    for when, copy in hops:
        pl.when(when)(copy.wait_send)


def share_body(z_count, own_ref, own_slab, out_ref, slab_ref, z_send, z_recv, send_sem, recv_sem, slab_send, slab_recv, keep_sem):
    z, x, c, s = position()
    q, q_across = x * 2 + c, (1 - x) * 2 + c
    half = own_slab.shape[0] // 2
    near, far = pl.ds(pl.multiple_of(s * half, 16), half), pl.ds(pl.multiple_of((1 - s) * half, 16), half)
    route_greet(z_count)
    keep = pltpu.make_async_copy(own_ref, out_ref.at[((z * 2 + x) * 2 + c) * 2 + s], keep_sem.at[0])
    keep_slab = pltpu.make_async_copy(own_slab, slab_ref.at[q], keep_sem.at[1])
    keep.start()
    keep_slab.start()
    shared = []

    def share(src, place, piece, target):
        n = len(shared)
        dst = slab_ref.at[place]
        if piece is not None:
            src, dst = src.at[piece], dst.at[piece]
        shared.append(remote(src, dst, slab_send.at[n], slab_recv.at[n], target))
        shared[-1].start()

    def begin():
        share(own_slab, q, near, device(z, 1 - x, c, s))
        share(own_slab, q, None, device(z, x, 1 - c, s))

    def late():
        shared[0].wait_recv()
        share(slab_ref.at[q_across], q_across, near, device(z, x, c, 1 - s))
        share(slab_ref.at[q_across], q_across, near, device(z, x, 1 - c, s))

    sems = z_send, z_recv, send_sem, recv_sem
    route(z_count, own_ref, out_ref, sems, lambda src, place: None, 2, 0, (5, 3), begin, late)
    shared[2].wait_recv()
    share(slab_ref.at[q_across], q_across, far, device(z, x, 1 - c, s))
    for n in (1, 3, 4):
        shared[n].wait_recv()
    for copy in shared:
        copy.wait_send()
    keep.wait()
    keep_slab.wait()


def share(own, own_slab, z_count, collective_id):
    anywhere = pl.BlockSpec(memory_space=pl.ANY)
    return pl.pallas_call(
        functools.partial(share_body, z_count),
        out_shape=[
            jax.ShapeDtypeStruct((8 * z_count,) + own.shape, own.dtype),
            jax.ShapeDtypeStruct((4,) + own_slab.shape, own_slab.dtype),
        ],
        in_specs=[anywhere, anywhere],
        out_specs=[anywhere, anywhere],
        scratch_shapes=route_sems(z_count, 2)
        + [pltpu.SemaphoreType.DMA((5,)), pltpu.SemaphoreType.DMA((5,)), pltpu.SemaphoreType.DMA((2,))],
        compiler_params=pltpu.CompilerParams(collective_id=collective_id, has_side_effects=True),
    )(own, own_slab)


def series_body(
    z_count, strip, tile, chunk, normalizer,
    begun_ref, sums_ref, reg_ref, inv_ref, w_ref, gathered,
    dense, first, second, stage, recip, spread_recip, out_buf, w_own, w_slots,
    z_send, z_recv, send_sem, recv_sem, stage_sem, out_sem, w_send, w_recv,
):
    z, x, c, s = position()
    obs = lax.axis_index("obs")
    obs_count = 4 * z_count
    strips = 8 * z_count
    width = strips * strip
    half = strips // 2
    span = begun_ref.shape[2]
    block_rows = width // 2
    lines = tile // LANES
    fold = 1.0 / normalizer

    barrier = pltpu.get_barrier_semaphore()
    peers = [
        {"obs": lax.rem(obs + k, obs_count), "sp": s} for k in range(1, obs_count)
    ]
    for peer in peers + [device(z, x, c, 1 - s)]:
        pl.semaphore_signal(barrier, inc=1, device_id=peer, device_id_type=pl.DeviceIdType.MESH)
    pl.semaphore_wait(barrier, obs_count)

    slots = stage.shape[0]
    waiting = []

    def lay_out(n):
        copy, place = waiting[n]
        copy.wait()
        place = lax.rem(place, 8) * z_count + lax.div(place, 8)
        rows = pl.ds(pl.multiple_of(place * strip, strip), strip)

        def put(k, turn):
            cols = pl.ds(pl.multiple_of(lax.rem(place + k, strips) * strip, strip), strip)
            block = stage[n % slots, :, pl.ds(pl.multiple_of(k * strip, strip), strip)]
            dense[rows, cols] = block
            if turn:
                dense[cols, rows] = block.T

        for k in range(half + 1):
            put(k, 0 < k < half)

    def arrive(src, place):
        n = len(waiting)
        if n >= slots:
            lay_out(n - slots)
        copy = pltpu.make_async_copy(src, stage.at[n % slots], stage_sem.at[n % slots])
        copy.start()
        waiting.append((copy, place))

    def begin():
        per = sums_ref.shape[1] // 2
        for p in range(sums_ref.shape[0]):
            lane = slice(p * per, (p + 1) * per)
            recip[lane, :] = 1.0 / (sums_ref[p, per:, :] * fold + reg_ref[lane, :])

        @pl.loop(0, width // LANES)
        def _(m):
            row = jnp.broadcast_to(recip[pl.ds(m, 1), :], (LANES, LANES))
            spread_recip[pl.ds(pl.multiple_of(m * LANES, LANES), LANES), :] = row.T

    sems = z_send, z_recv, send_sem, recv_sem
    route(z_count, None, gathered, sems, arrive, 4, 2, (2, 3), begin)
    for n in range(len(waiting) - slots, len(waiting)):
        lay_out(n)

    my_cols = pl.ds(pl.multiple_of(obs * tile, tile), tile)

    def by_row(values, rows):
        scale = spread_recip[rows, :]
        return values * jnp.concatenate([scale] * lines, axis=1)

    @pl.loop(0, width // chunk)
    def _(m):
        rows = pl.ds(pl.multiple_of(m * chunk, chunk), chunk)
        first[rows, :] = by_row(dense[rows, my_cols].astype(jnp.float32) * fold, rows).astype(jnp.bfloat16)

    @pl.loop(0, width // chunk)
    def _(m):
        rows = pl.ds(pl.multiple_of(m * chunk, chunk), chunk)
        prod = jnp.dot(dense[rows, :], first[...], preferred_element_type=jnp.float32)
        second[rows, :] = by_row(prod * fold, rows).astype(jnp.bfloat16)

    def my_lines(ref, at):
        return jnp.concatenate([ref[pl.ds(at + h, 1), :] for h in range(lines)], axis=1)

    per = sums_ref.shape[1] // 2
    r_row = my_lines(recip, obs * lines)
    y = my_lines(sums_ref.at[lax.div(obs * lines, per)], lax.rem(obs * lines, per))
    y = y * (1.0 / math.sqrt(normalizer))

    def emit(m):
        return pltpu.make_async_copy(
            out_buf.at[m], inv_ref.at[pl.ds(pl.multiple_of(m * chunk, chunk), chunk)], out_sem.at[m]
        )

    @pl.loop(0, block_rows // chunk)
    def _(m):
        begin_at = s * block_rows + m * chunk
        rows = pl.ds(pl.multiple_of(begin_at, chunk), chunk)
        cubic = jnp.dot(dense[rows, :], second[...], preferred_element_type=jnp.float32)
        on_diag = (begin_at + lax.broadcasted_iota(jnp.int32, (chunk, tile), 0)) == (
            obs * tile + lax.broadcasted_iota(jnp.int32, (chunk, tile), 1)
        )
        series = second[rows, :].astype(jnp.float32) - by_row(
            (dense[rows, my_cols].astype(jnp.float32) + cubic) * fold, rows
        )
        out = (jnp.where(on_diag, 1.0, 0.0) + series) * r_row
        out_buf[m] = out
        emit(m).start()
        weighted = out * y
        weighted = sum(weighted[:, h * LANES : (h + 1) * LANES] for h in range(lines))
        for h in range(chunk // LANES):
            turned = weighted[h * LANES : (h + 1) * LANES, :].T
            w_own[pl.ds(m * (chunk // LANES) + h, 1), :] = jnp.sum(turned, axis=0, keepdims=True)

    copies = []
    for k in range(1, obs_count):
        copies.append(remote(w_own, w_slots.at[obs], w_send.at[k], w_recv.at[k], peers[k - 1]))
        copies[-1].start()
    w_slots[obs] = w_own[...]
    for copy in copies:
        copy.wait()
    total = w_slots[0]
    for k in range(1, obs_count):
        total = total + w_slots[k]
    w_ref[...] = total
    for m in range(block_rows // chunk):
        emit(m).wait()


def series_tile(begun, sums, regularizer, z_count, tile, normalizer, collective_id):
    strips, strip, span = begun.shape
    width = strips * strip
    block_rows = width // 2
    chunk = min(512, block_rows)
    obs_count = 4 * z_count
    w_shape = (block_rows // LANES, LANES)
    anywhere = pl.BlockSpec(memory_space=pl.ANY)
    vmem = pl.BlockSpec(memory_space=pltpu.VMEM)
    inverse_tile, weights, _ = pl.pallas_call(
        functools.partial(series_body, z_count, strip, tile, chunk, normalizer),
        out_shape=[
            jax.ShapeDtypeStruct((block_rows, tile), jnp.float32),
            jax.ShapeDtypeStruct(w_shape, jnp.float32),
            jax.ShapeDtypeStruct(begun.shape, begun.dtype),
        ],
        in_specs=[anywhere, vmem, vmem],
        out_specs=[anywhere, vmem, anywhere],
        scratch_shapes=[
            pltpu.VMEM((width, width), jnp.bfloat16),
            pltpu.VMEM((width, tile), jnp.bfloat16),
            pltpu.VMEM((width, tile), jnp.bfloat16),
            pltpu.VMEM((2, strip, span), jnp.bfloat16),
            pltpu.VMEM((width // LANES, LANES), jnp.float32),
            pltpu.VMEM((width, LANES), jnp.float32),
            pltpu.VMEM((block_rows // chunk, chunk, tile), jnp.float32),
            pltpu.VMEM(w_shape, jnp.float32),
            pltpu.VMEM((obs_count,) + w_shape, jnp.float32),
        ]
        + route_sems(z_count, 4)
        + [
            pltpu.SemaphoreType.DMA((2,)),
            pltpu.SemaphoreType.DMA((block_rows // chunk,)),
            pltpu.SemaphoreType.DMA((obs_count,)),
            pltpu.SemaphoreType.DMA((obs_count,)),
        ],
        compiler_params=pltpu.CompilerParams(
            collective_id=collective_id, has_side_effects=True, vmem_limit_bytes=VMEM_BYTES
        ),
        input_output_aliases={0: 2},
    )(begun, sums, regularizer.reshape(width // LANES, LANES))
    return inverse_tile, weights.reshape(block_rows)


def by_strips(descriptors, candidates, sparse_index, targets, regularizer):
    obs_count = lax.axis_size("obs")
    sp_count = lax.axis_size("sp")
    obs_pos = lax.axis_index("obs")
    sp_pos = lax.axis_index("sp")
    z_count = obs_count // 4
    width = sparse_index.shape[0]
    tile = width // obs_count
    strip = width // (obs_count * sp_count)
    mine = strip * z_count
    span = width // 2 + strip
    window = width // 2 + mine
    rows, depth = descriptors.shape
    normalizer = 24.0 * rows * obs_count

    extra = jnp.pad(targets.reshape(rows // depth, depth), ((0, 32 - rows // depth), (0, 0)))
    shard = jnp.concatenate([unit_rows(descriptors), extra])
    piece = candidates.shape[0] // sp_count
    own = lax.dynamic_slice_in_dim(candidates, sp_pos * piece, piece)
    table, slab = share(unit_rows(own), shard, z_count, 2)
    table = table.reshape(-1, depth)
    place = lax.rem(obs_pos, 4) * sp_count + sp_pos
    wanted = lax.dynamic_slice_in_dim(
        jnp.concatenate([sparse_index, sparse_index]), place * mine, window
    )
    sparse = table.at[wanted].get(mode="promise_in_bounds")
    slab_targets = slab[:, rows : rows + rows // depth].reshape(4 * rows)
    begun, sums = slab_gram(
        slab, sparse, slab_targets, z_count, sp_count, strip, span, tile, rows, 0
    )
    return series_tile(begun, sums, regularizer, z_count, tile, normalizer, 3)


def slab_body(z_count, sp_count, strip, tile, root, *refs):
    norm_ref, sp_ref, tgt_ref, gathered, sums_ref = refs[:5]
    kbuf, ktr, parts, from_low, from_high, done, zsums, gsums = refs[5:13]
    up_send, up_recv, down_send, down_recv, side_send, side_recv, zs_send, zs_recv, gs_send, gs_recv, keep_sem = refs[13:24]
    near_send, near_recv = refs[24:]
    obs = lax.axis_index("obs")
    s = lax.axis_index("sp")
    z, x, c, _ = position()
    q = x * 2 + c
    group = 4 * sp_count
    p = q * sp_count + s
    last = z_count - 1
    shard = tgt_ref.shape[1] // 4
    mine = strip * z_count
    lines = mine // LANES

    z_others = [{"obs": lax.rem(z + k, z_count) * 4 + q, "sp": s} for k in range(1, z_count)]
    group_others = []
    for k in range(1, group):
        to = lax.rem(p + k, group)
        group_others.append({"obs": z * 4 + lax.div(to, sp_count), "sp": lax.rem(to, sp_count)})
    barrier = pltpu.get_barrier_semaphore()
    for other in z_others + group_others:
        pl.semaphore_signal(barrier, inc=1, device_id=other, device_id_type=pl.DeviceIdType.MESH)
    pl.semaphore_wait(barrier, len(z_others) + len(group_others))

    def kernel_tile(t, own):
        cols = pl.ds(pl.multiple_of(t * tile, tile), tile)
        for k in range(4):
            rows = pl.ds(k * shard, shard)
            inner = lax.dot_general(
                norm_ref[k, :shard, :], sp_ref[cols, :], (((1,), (1,)), ((), ())),
                preferred_element_type=jnp.float32,
            )
            scaled = inner * root
            squared = scaled * scaled
            kb = ((squared - 6.0) * squared + 3.0).astype(jnp.bfloat16)
            kbuf[rows, cols] = kb
            if own:
                ktr[cols, rows] = kb.T

    def row_sums():
        for t in range(mine // tile):
            cols = slice(t * tile, (t + 1) * tile)
            weighted = jnp.dot(tgt_ref[...], kbuf[:, cols], preferred_element_type=jnp.float32)
            square = jnp.zeros((1, tile), jnp.float32)
            for k in range(4):
                kf = kbuf[k * shard : (k + 1) * shard, cols].astype(jnp.float32)
                square = square + jnp.sum(kf * kf, axis=0, keepdims=True)
            for h in range(tile // LANES):
                line = t * (tile // LANES) + h
                lane = slice(h * LANES, (h + 1) * LANES)
                zsums[z, line : line + 1, :] = weighted[0:1, lane]
                zsums[z, lines + line : lines + line + 1, :] = square[:, lane]

    groups = kbuf.shape[1] // mine

    def piece(t, g):
        begin = t * strip if g == 0 else 0
        end = mine if g < groups - 1 else (t + 1) * strip
        return begin, g * mine + begin - t * strip, end - begin

    def cut(t, g):
        _, begin, size = piece(t, g)
        return pl.ds(begin, size)

    def up(t, g):
        n, at = t * groups + g, (t, slice(None), cut(t, g))
        return remote(
            parts.at[at], from_low.at[at], up_send.at[n], up_recv.at[n],
            {"obs": lax.rem(z + 1, z_count) * 4 + q, "sp": s},
        )

    def down(t, g):
        n, at = t * groups + g, (t, slice(None), cut(t, g))
        return remote(
            parts.at[at], from_high.at[at], down_send.at[n], down_recv.at[n],
            {"obs": lax.rem(z + last, z_count) * 4 + q, "sp": s},
        )

    def gram_group(g):
        cols = slice(g * mine, (g + 1) * mine)
        made = jnp.dot(ktr[...], kbuf[:, cols], preferred_element_type=jnp.float32).astype(jnp.bfloat16)
        for t in range(z_count):
            begin, at, size = piece(t, g)
            parts[t, :, at : at + size] = made[t * strip : (t + 1) * strip, begin : begin + size]

    def pass_on(place, n):
        if place > 0 and 0 <= n - place < groups:
            for t in range(last, place, -1):
                g = n - place
                up(t, g).wait_recv()
                parts[t, :, cut(t, g)] = parts[t, :, cut(t, g)] + from_low[t, :, cut(t, g)]
                up(t, g).start()
        if place < last and 0 <= n - (last - place) < groups:
            for t in range(place):
                g = n - (last - place)
                down(t, g).wait_recv()
                parts[t, :, cut(t, g)] = parts[t, :, cut(t, g)] + from_high[t, :, cut(t, g)]
                down(t, g).start()

    mine_at = ((z * 2 + x) * 2 + c) * 2 + s
    across_at, beside_at = ((z * 2 + 1 - x) * 2 + c) * 2 + s, ((z * 2 + x) * 2 + c) * 2 + 1 - s
    across, beside = device(z, 1 - x, c, s), device(z, x, c, 1 - s)
    half = strip // 2

    def side(place, g, k):
        rows = (slice(None), slice(None), pl.ds(0, half), pl.ds(half, half))[k]
        at = (mine_at, mine_at, across_at, beside_at)[k]
        src = done.at[:, cut(place, g)] if k < 2 else gathered.at[at, rows, cut(place, g)]
        return remote(
            src, gathered.at[at, rows, cut(place, g)], side_send.at[g * 4 + k], side_recv.at[g * 4 + k],
            (across, beside, beside, across)[k],
        )

    def keep(place, g):
        return pltpu.make_async_copy(
            done.at[:, cut(place, g)], gathered.at[mine_at, :, cut(place, g)], keep_sem.at[g]
        )

    def near(place, g, rising):
        to = lax.rem(z + (1 if rising else last), z_count)
        n = g * 2 + int(rising)
        return remote(
            done.at[:, cut(place, g)], gathered.at[mine_at, :, cut(place, g)],
            near_send.at[n], near_recv.at[n], device(to, x, c, s),
        )

    def close(place, g):
        total = parts[place, :, cut(place, g)].astype(jnp.float32)
        if place > 0:
            up(place, g).wait_recv()
            total = total + from_low[place, :, cut(place, g)].astype(jnp.float32)
        if place < last:
            down(place, g).wait_recv()
            total = total + from_high[place, :, cut(place, g)].astype(jnp.float32)
        if g == 0:
            row = lax.broadcasted_iota(jnp.int32, total.shape, 0)
            col = lax.broadcasted_iota(jnp.int32, total.shape, 1)
            total = jnp.where(row == col, 0.0, total)
        done[:, cut(place, g)] = total.astype(jnp.bfloat16)
        side(place, g, 0).start()
        side(place, g, 1).start()
        if place < last:
            near(place, g, True).start()
        if place > 0:
            near(place, g, False).start()
        keep(place, g).start()

    def progress(place, n):
        pass_on(place, n)
        g = n - max(place, last - place)
        if 0 <= g < groups:
            close(place, g)
        if 0 <= g - 1 < groups:
            for k in range(2):
                side(place, g - 1, k).wait_recv()
                side(place, g - 1, k + 2).start()
        if 0 <= g - 2 < groups:
            for k in range(2):
                side(place, g - 2, k + 2).wait_recv()

    z_copies, g_copies = [], []
    for n in range(groups + last + 2):
        if n < groups:

            @pl.loop(n * mine // tile, (n + 1) * mine // tile)
            def _(t):
                kernel_tile(t, n == 0)

            gram_group(n)

            @pl.when(z == 0)
            def _():
                for t in range(last, 0, -1):
                    up(t, n).start()

            @pl.when(z == last)
            def _():
                for t in range(last):
                    down(t, n).start()

        if n == 0:
            row_sums()
            for k in range(1, z_count):
                z_copies.append(remote(zsums.at[z], zsums.at[z], zs_send.at[k], zs_recv.at[k], z_others[k - 1]))
                z_copies[-1].start()
        if n == 1:
            for copy in z_copies:
                copy.wait_recv()
            total = zsums[0]
            for m in range(1, z_count):
                total = total + zsums[m]
            gsums[p] = total
            for m in range(1, group):
                g_copies.append(
                    remote(gsums.at[p], gsums.at[p], gs_send.at[m], gs_recv.at[m], group_others[m - 1])
                )
                g_copies[-1].start()
        for place in range(z_count):
            pl.when(z == place)(functools.partial(progress, place, n))

    def finish(place):
        for g in range(groups):
            for k in range(4):
                side(place, g, k).wait_send()
            keep(place, g).wait()
            if place < last:
                near(place, g, True).wait_send()
                near(place + 1, g, False).wait_recv()
            if place > 0:
                near(place, g, False).wait_send()
                near(place - 1, g, True).wait_recv()
            for t in range(z_count):
                if t > place:
                    up(t, g).wait_send()
                if t < place:
                    down(t, g).wait_send()

    for place in range(z_count):
        pl.when(z == place)(functools.partial(finish, place))

    for copy in g_copies:
        copy.wait()
    for copy in z_copies:
        copy.wait_send()
    sums_ref[...] = gsums[...]


def slab_gram(slab, sparse, targets, z_count, sp_count, strip, span, tile, rows, collective_id):
    depth = slab.shape[2]
    window = sparse.shape[0]
    group = 4 * sp_count
    mine = strip * z_count
    lines = 2 * mine // LANES
    vmem = pl.BlockSpec(memory_space=pltpu.VMEM)
    part = (z_count, strip, span)
    groups = window // mine
    sems = [pltpu.SemaphoreType.DMA((z_count * groups,))] * 4 + [pltpu.SemaphoreType.DMA((4 * groups,))] * 2
    sems += [pltpu.SemaphoreType.DMA((z_count,))] * 2 + [pltpu.SemaphoreType.DMA((group,))] * 2
    sems += [pltpu.SemaphoreType.DMA((groups,))] + [pltpu.SemaphoreType.DMA((2 * groups,))] * 2
    return pl.pallas_call(
        functools.partial(slab_body, z_count, sp_count, strip, tile, math.sqrt(depth)),
        out_shape=[
            jax.ShapeDtypeStruct((group * z_count, strip, span), jnp.bfloat16),
            jax.ShapeDtypeStruct((group, lines, LANES), jnp.float32),
        ],
        in_specs=[vmem, vmem, vmem],
        out_specs=[pl.BlockSpec(memory_space=pl.ANY), vmem],
        scratch_shapes=[
            pltpu.VMEM((4 * rows, window), jnp.bfloat16),
            pltpu.VMEM((mine, 4 * rows), jnp.bfloat16),
            pltpu.VMEM(part, jnp.bfloat16),
            pltpu.VMEM(part, jnp.bfloat16),
            pltpu.VMEM(part, jnp.bfloat16),
            pltpu.VMEM(part[1:], jnp.bfloat16),
            pltpu.VMEM((z_count, lines, LANES), jnp.float32),
            pltpu.VMEM((group, lines, LANES), jnp.float32),
        ] + sems,
        compiler_params=pltpu.CompilerParams(
            collective_id=collective_id, has_side_effects=True, vmem_limit_bytes=VMEM_BYTES
        ),
    )(slab, sparse, jnp.broadcast_to(targets[None, :], (16, 4 * rows)))


def on_device(descriptors, candidates, sparse_index, targets, regularizer):
    obs_count = lax.axis_size("obs")
    sp_count = lax.axis_size("sp")
    obs_pos = lax.axis_index("obs")
    sp_pos = lax.axis_index("sp")
    width = sparse_index.shape[0]
    if sp_count == 2 and width % (obs_count * sp_count * LANES) == 0:
        return by_strips(descriptors, candidates, sparse_index, targets, regularizer)
    tile = width // obs_count
    share = -(-((obs_count // 2 + 1) * tile) // (sp_count * LANES)) * LANES
    normalizer = 24.0 * descriptors.shape[0] * obs_count

    normed = unit_rows(descriptors)
    piece = candidates.shape[0] // sp_count
    own = lax.dynamic_slice_in_dim(candidates, sp_pos * piece, piece)
    table = spread(unit_rows(own), obs_count, sp_count, 2)
    sparse = table.at[sparse_index].get(mode="promise_in_bounds")

    gram, sums = gram_call(
        sp_pos[None].astype(jnp.int32), normed, sparse, targets, obs_count, tile, share, sp_count
    )
    sums = add_over_obs(sums, obs_count, 0)
    part = lax.psum_scatter(gram, "obs", scatter_dimension=0, tiled=True)

    projected = sums[0] / math.sqrt(normalizer)
    root = lax.rsqrt(sums[1] / normalizer + regularizer)
    col_start = obs_pos * tile
    rrow = lax.dynamic_slice_in_dim(root, col_start, tile)
    window_start = col_start + sp_pos * share
    rwin = lax.dynamic_slice_in_dim(jnp.concatenate([root, root]), window_start, share)
    offset = sp_pos * share + lax.iota(jnp.int32, share)
    on_diag = lax.iota(jnp.int32, tile)[:, None] == offset[None, :]
    scaled = jnp.where(
        on_diag, 0.0, part.astype(jnp.float32) * (rrow[:, None] / normalizer) * rwin[None, :]
    ).astype(jnp.bfloat16)
    packed = spread(scaled, obs_count, sp_count, 3)

    y = lax.dynamic_slice_in_dim(projected, col_start, tile)
    pos = jnp.stack([sp_pos, obs_pos]).astype(jnp.int32)
    inverse_tile, part_w = newton_call(
        pos, packed, root, rrow, y, obs_count, tile, share, sp_count
    )
    return inverse_tile, add_over_obs(part_w[0], obs_count, 1)


def solution(mesh):
    in_specs = (P("obs", None), P("obs", None), P(), P("obs"), P())
    out_specs = (P("sp", "obs"), P("sp"))
    return jax.shard_map(
        on_device, mesh=mesh, in_specs=in_specs, out_specs=out_specs, check_vma=False
    )
```

```python
import functools
import math

import jax
import jax.numpy as jnp
from jax import lax
from jax.experimental import pallas as pl
from jax.experimental.pallas import tpu as pltpu
from jax.sharding import PartitionSpec as P

epsilon = 1e-06
LANES = 128
VMEM_BYTES = 58 * 2**20


def unit_rows(row_block):
    values = row_block.astype(jnp.float32)
    return (values * lax.rsqrt(jnp.sum(values * values, axis=1, keepdims=True) + epsilon)).astype(
        jnp.bfloat16
    )


def gram_body(blocks, tile, share, ext, root, s_ref, norm_ref, sp_ref, tgt_ref, gram_ref, ws_ref, kext):
    step = pl.program_id(0)
    width = blocks * tile

    @pl.when(step < blocks)
    def _():
        inner = lax.dot_general(
            norm_ref[...], sp_ref[...], (((1,), (1,)), ((), ())), preferred_element_type=jnp.float32
        )
        scaled = inner * root
        squared = scaled * scaled
        kb = ((squared - 6.0) * squared + 3.0).astype(jnp.bfloat16)
        kext[:, pl.ds(pl.multiple_of(step * tile, tile), tile)] = kb

        @pl.when(step < ext)
        def _():
            kext[:, pl.ds(pl.multiple_of(width + step * tile, tile), tile)] = kb

        kf = kb.astype(jnp.float32)
        weighted = jnp.dot(tgt_ref[...], kb, preferred_element_type=jnp.float32)
        ws_ref[0:1, :] = weighted[0:1, :]
        ws_ref[1:2, :] = jnp.sum(kf * kf, axis=0, keepdims=True)

    @pl.when(step >= blocks)
    def _():
        j = step - blocks
        cols = pl.ds(pl.multiple_of(j * tile, tile), tile)
        window = pl.ds(pl.multiple_of(j * tile + s_ref[0] * share, LANES), share)
        gram_ref[...] = lax.dot_general(
            kext[:, cols], kext[:, window], (((0,), (0,)), ((), ())), preferred_element_type=jnp.float32
        ).astype(jnp.bfloat16)


def gram_call(s_pos, normed, sparse, targets, blocks, tile, share, sp_count):
    rows, depth = normed.shape
    width = blocks * tile
    ext = -(-((blocks - 1) * tile + sp_count * share - width) // tile)
    last = blocks - 1
    return pl.pallas_call(
        functools.partial(gram_body, blocks, tile, share, ext, math.sqrt(depth)),
        grid_spec=pltpu.PrefetchScalarGridSpec(
            num_scalar_prefetch=1,
            grid=(2 * blocks,),
            in_specs=[
                pl.BlockSpec((rows, depth), lambda g, s: (0, 0)),
                pl.BlockSpec((tile, depth), lambda g, s: (jnp.minimum(g, last), 0)),
                pl.BlockSpec((16, rows), lambda g, s: (0, 0)),
            ],
            out_specs=[
                pl.BlockSpec((tile, share), lambda g, s: (jnp.maximum(g - blocks, 0), 0)),
                pl.BlockSpec((2, tile), lambda g, s: (0, jnp.minimum(g, last))),
            ],
            scratch_shapes=[pltpu.VMEM((rows, width + ext * tile), jnp.bfloat16)],
        ),
        out_shape=[
            jax.ShapeDtypeStruct((width, share), jnp.bfloat16),
            jax.ShapeDtypeStruct((2, width), jnp.float32),
        ],
        compiler_params=pltpu.CompilerParams(vmem_limit_bytes=VMEM_BYTES),
    )(s_pos, normed, sparse, jnp.broadcast_to(targets[None, :], (16, rows)))


def newton_body(
    blocks, tile, share, sp_count, chunk, block_rows,
    pos_ref, packed_ref, rcol_ref, rrow_ref, y_ref, inv_ref, w_ref, dense, prod,
):
    step = pl.program_id(0)
    width = blocks * tile
    half = blocks // 2
    p_steps = width // chunk
    my_cols = pl.ds(pl.multiple_of(pos_ref[1] * tile, tile), tile)

    @pl.when(step < blocks)
    def _():
        rows = pl.ds(pl.multiple_of(step * tile, tile), tile)
        for s in range(sp_count):
            for q in range(share // LANES):
                offset = s * share + q * LANES
                if offset >= (half + 1) * tile:
                    continue
                col = lax.rem(step * tile + offset, width)
                cols = pl.ds(pl.multiple_of(col, LANES), LANES)
                block = packed_ref[s * tile : (s + 1) * tile, q * LANES : (q + 1) * LANES]
                dense[rows, cols] = block
                if tile <= offset < half * tile:
                    dense[cols, rows] = block.T

    @pl.when((step >= blocks) & (step < blocks + p_steps))
    def _():
        rows = pl.ds(pl.multiple_of((step - blocks) * chunk, chunk), chunk)
        prod[rows, :] = jnp.dot(
            dense[rows, :], dense[:, my_cols], preferred_element_type=jnp.float32
        ).astype(jnp.bfloat16)

    @pl.when(step >= blocks + p_steps)
    def _():
        local = pl.multiple_of((step - blocks - p_steps) * chunk, chunk)
        start = pl.multiple_of(pos_ref[0] * block_rows + local, chunk)
        rows = pl.ds(start, chunk)
        cubic = jnp.dot(dense[rows, :], prod[...], preferred_element_type=jnp.float32)
        on_diag = (start + lax.broadcasted_iota(jnp.int32, (chunk, tile), 0)) == (
            pos_ref[1] * tile + lax.broadcasted_iota(jnp.int32, (chunk, tile), 1)
        )
        series = (
            jnp.where(on_diag, 1.0, 0.0)
            - dense[rows, my_cols].astype(jnp.float32)
            + prod[rows, :].astype(jnp.float32)
            - cubic
        )
        out = series * rcol_ref[rows, :] * rrow_ref[...]
        inv_ref[pl.ds(local, chunk), :] = out
        w_ref[:, pl.ds(local, chunk)] = lax.dot_general(
            y_ref[...], out, (((1,), (1,)), ((), ())),
            precision=lax.Precision.HIGHEST, preferred_element_type=jnp.float32,
        )


def newton_call(pos, packed, root_recip, rrow, y, blocks, tile, share, sp_count):
    width = blocks * tile
    block_rows = width // sp_count
    chunk = min(512, block_rows)
    grid = blocks + width // chunk + block_rows // chunk
    last = blocks - 1
    return pl.pallas_call(
        functools.partial(newton_body, blocks, tile, share, sp_count, chunk, block_rows),
        grid_spec=pltpu.PrefetchScalarGridSpec(
            num_scalar_prefetch=1,
            grid=(grid,),
            in_specs=[
                pl.BlockSpec((sp_count * tile, share), lambda g, p: (jnp.minimum(g, last), 0)),
                pl.BlockSpec((width, 1), lambda g, p: (0, 0)),
                pl.BlockSpec((1, tile), lambda g, p: (0, 0)),
                pl.BlockSpec((8, tile), lambda g, p: (0, 0)),
            ],
            out_specs=[
                pl.BlockSpec((block_rows, tile), lambda g, p: (0, 0)),
                pl.BlockSpec((8, block_rows), lambda g, p: (0, 0)),
            ],
            scratch_shapes=[
                pltpu.VMEM((width, width), jnp.bfloat16),
                pltpu.VMEM((width, tile), jnp.bfloat16),
            ],
        ),
        out_shape=[
            jax.ShapeDtypeStruct((block_rows, tile), jnp.float32),
            jax.ShapeDtypeStruct((8, block_rows), jnp.float32),
        ],
        compiler_params=pltpu.CompilerParams(vmem_limit_bytes=VMEM_BYTES),
    )(pos, packed, root_recip[:, None], rrow[None, :], jnp.broadcast_to(y[None, :], (8, tile)))


def add_body(count, in_ref, out_ref, slots, send_sem, recv_sem):
    me = lax.axis_index("obs")
    barrier = pltpu.get_barrier_semaphore()
    for k in range(1, count):
        pl.semaphore_signal(
            barrier, inc=1, device_id={"obs": lax.rem(me + k, count)}, device_id_type=pl.DeviceIdType.MESH
        )
    pl.semaphore_wait(barrier, count - 1)
    copies = []
    for k in range(1, count):
        copy = pltpu.make_async_remote_copy(
            src_ref=in_ref,
            dst_ref=slots.at[me],
            send_sem=send_sem.at[k],
            recv_sem=recv_sem.at[k],
            device_id={"obs": lax.rem(me + k, count)},
            device_id_type=pl.DeviceIdType.MESH,
        )
        copy.start()
        copies.append(copy)
    slots[me] = in_ref[...]
    for copy in copies:
        copy.wait()
    total = slots[0]
    for k in range(1, count):
        total = total + slots[k]
    out_ref[...] = total


def add_over_obs(values, count, collective_id):
    shape = values.shape
    flat = values.reshape(values.size // LANES, LANES)
    total = pl.pallas_call(
        functools.partial(add_body, count),
        out_shape=jax.ShapeDtypeStruct(flat.shape, flat.dtype),
        in_specs=[pl.BlockSpec(memory_space=pltpu.VMEM)],
        out_specs=pl.BlockSpec(memory_space=pltpu.VMEM),
        scratch_shapes=[
            pltpu.VMEM((count,) + flat.shape, flat.dtype),
            pltpu.SemaphoreType.DMA((count,)),
            pltpu.SemaphoreType.DMA((count,)),
        ],
        cost_estimate=pl.CostEstimate(
            flops=count * flat.size, bytes_accessed=400 * flat.size, transcendentals=0
        ),
        compiler_params=pltpu.CompilerParams(collective_id=collective_id, has_side_effects=True),
    )(flat)
    return total.reshape(shape)


def spread_keys(z_count, sp_count):
    keys = [("z", k) for k in range(1, z_count)]
    for k in range(z_count):
        keys += [("x", k), ("core", k), ("core_x", k)]
        for d in range(1, sp_count):
            keys += [(name, k, d) for name in ("sp", "sp_a", "x_b", "core_sp", "core_a", "core_b")]
    return {key: place for place, key in enumerate(keys)}


def spread_body(z_count, sp_count, in_ref, out_ref, send_sem, recv_sem, own_sem):
    places = spread_keys(z_count, sp_count)
    obs = lax.axis_index("obs")
    s = lax.axis_index("sp")
    z, x, c = lax.div(obs, 4), lax.rem(lax.div(obs, 2), 2), lax.rem(obs, 2)
    half = in_ref.shape[0] // 2
    upper, lower = pl.ds(0, half), pl.ds(half, half)
    zs = [lax.bitwise_xor(z, k) for k in range(z_count)]
    to_sp = [lax.rem(s + d, sp_count) for d in range(sp_count)]
    from_sp = [lax.rem(s - d + sp_count, sp_count) for d in range(sp_count)]

    def device(z_to, x_to, c_to, s_to):
        return {"obs": z_to * 4 + x_to * 2 + c_to, "sp": s_to}

    def slot(z_of, x_of, s_of):
        return ((z_of * 2 + x_of) * 2 + c) * sp_count + s_of

    own_slot = slot(z, x, s)
    across, sibling = device(z, 1 - x, c, s), device(z, x, 1 - c, s)
    others = [device(zs[k], x, c, s) for k in range(1, z_count)]
    others += [device(z, x, c, to_sp[d]) for d in range(1, sp_count)]
    others += [across, sibling]
    barrier = pltpu.get_barrier_semaphore()
    for other in others:
        pl.semaphore_signal(barrier, inc=1, device_id=other, device_id_type=pl.DeviceIdType.MESH)
    pl.semaphore_wait(barrier, len(others))

    sent = {}

    def send(key, place, target, rows=None, own=False):
        src = in_ref if own else out_ref.at[place]
        dst = out_ref.at[place]
        if rows is not None:
            src, dst = src.at[rows], dst.at[rows]
        copy = pltpu.make_async_remote_copy(
            src_ref=src,
            dst_ref=dst,
            send_sem=send_sem.at[places[key]],
            recv_sem=recv_sem.at[places[key]],
            device_id=target,
            device_id_type=pl.DeviceIdType.MESH,
        )
        copy.start()
        sent[key] = copy

    keep = pltpu.make_async_copy(in_ref, out_ref.at[own_slot], own_sem)
    keep.start()
    for k in range(1, z_count):
        send(("z", k), own_slot, others[k - 1], own=True)

    def fan_out(k):
        place = slot(zs[k], x, s)
        send(("x", k), place, across, own=k == 0)
        for d in range(1, sp_count):
            send(("sp", k, d), place, device(z, x, c, to_sp[d]), own=k == 0)
        send(("core", k), place, sibling, own=k == 0)

    def relay(k):
        sent[("x", k)].wait_recv()
        place = slot(zs[k], 1 - x, s)
        for d in range(1, sp_count):
            send(("sp_a", k, d), place, device(z, x, c, to_sp[d]), upper)
        send(("core_x", k), place, sibling)
        for d in range(1, sp_count):
            sent[("sp", k, d)].wait_recv()
            place = slot(zs[k], x, from_sp[d])
            send(("x_b", k, d), place, across, lower)
            send(("core_sp", k, d), place, sibling)

    def finish(k):
        for d in range(1, sp_count):
            place = slot(zs[k], 1 - x, from_sp[d])
            sent[("sp_a", k, d)].wait_recv()
            send(("core_a", k, d), place, sibling, upper)
            sent[("x_b", k, d)].wait_recv()
            send(("core_b", k, d), place, sibling, lower)

    fan_out(0)
    for k in range(1, z_count):
        sent[("z", k)].wait_recv()
        fan_out(k)
        relay(k - 1)
        if k > 1:
            finish(k - 2)
    relay(z_count - 1)
    if z_count > 1:
        finish(z_count - 2)
    finish(z_count - 1)
    keep.wait()
    for key, copy in sent.items():
        copy.wait_send()
        if key[0].startswith("core"):
            copy.wait_recv()


def spread(shard, obs_count, sp_count, collective_id):
    rows, cols = shard.shape
    z_count = obs_count // 4
    total = obs_count * sp_count
    sems = len(spread_keys(z_count, sp_count))
    gathered = pl.pallas_call(
        functools.partial(spread_body, z_count, sp_count),
        out_shape=jax.ShapeDtypeStruct((total, rows, cols), shard.dtype),
        in_specs=[pl.BlockSpec(memory_space=pl.ANY)],
        out_specs=pl.BlockSpec(memory_space=pl.ANY),
        scratch_shapes=[
            pltpu.SemaphoreType.DMA((sems,)),
            pltpu.SemaphoreType.DMA((sems,)),
            pltpu.SemaphoreType.DMA,
        ],
        compiler_params=pltpu.CompilerParams(collective_id=collective_id, has_side_effects=True),
    )(shard)
    return gathered.reshape(total * rows, cols)


def position():
    obs = lax.axis_index("obs")
    return lax.div(obs, 4), lax.rem(lax.div(obs, 2), 2), lax.rem(obs, 2), lax.axis_index("sp")


def device(z, x, c, s):
    return {"obs": z * 4 + x * 2 + c, "sp": s}


def remote(src, dst, send_sem, recv_sem, target):
    return pltpu.make_async_remote_copy(
        src_ref=src, dst_ref=dst, send_sem=send_sem, recv_sem=recv_sem,
        device_id=target, device_id_type=pl.DeviceIdType.MESH,
    )


def route_sems(z_count, chunks):
    return [
        pltpu.SemaphoreType.DMA((4 * chunks * (z_count + 1),)),
        pltpu.SemaphoreType.DMA((4 * chunks * z_count,)),
        pltpu.SemaphoreType.DMA((4 * (chunks + 1) * z_count,)),
        pltpu.SemaphoreType.DMA((4 * (chunks + 1) * z_count,)),
    ]


def route_greet(z_count, meanwhile):
    z, x, c, s = position()
    barrier = pltpu.get_barrier_semaphore()
    others = [device(z, 1 - x, c, s), device(z, x, 1 - c, s), device(z, x, c, 1 - s)]
    others += [device(lax.rem(z + k, z_count), x, c, s) for k in range(1, z_count)]
    for other in others:
        pl.semaphore_signal(barrier, inc=1, device_id=other, device_id_type=pl.DeviceIdType.MESH)
    meanwhile()
    pl.semaphore_wait(barrier, len(others))


EXTRA = 32
OWN, ACROSS, BESIDE, DIAGONAL = range(4)


def route(z_count, home, out_ref, sems, arrive, chunks, diagonal, lag, begin, late=None):
    z_send, z_recv, send_sem, recv_sem = sems
    z, x, c, s = position()
    last = z_count - 1
    rows = out_ref.shape[1]
    high = rows // chunks
    known = home is None
    across, beside, sibling = device(z, 1 - x, c, s), device(z, x, c, 1 - s), device(z, x, 1 - c, s)
    along = {OWN: chunks, ACROSS: 0, BESIDE: 0, DIAGONAL: diagonal}

    nearer = jnp.minimum(z, last - z)
    origins = [z]
    for a in range(last):
        both = jnp.where(a % 2 == 0, z - (a // 2 + 1), z + (a // 2 + 1))
        single = jnp.where(z <= last - z, z + (a - nearer + 1), z - (a - nearer + 1))
        origins.append(jnp.where(a < 2 * nearer, both, single))

    def slot(col, a, c_of=c):
        x_of = 1 - x if col in (ACROSS, DIAGONAL) else x
        s_of = 1 - s if col in (BESIDE, DIAGONAL) else s
        return ((origins[a] * 2 + x_of) * 2 + c_of) * 2 + s_of

    def shard(col, a):
        return out_ref.at[slot(col, a)] if a or col != OWN or known else home

    sent = {}

    def send(key, col, a, target, begin=0, size=rows):
        cut = pl.ds(begin, size)
        n = len(sent)
        sent[key] = remote(
            shard(col, a).at[cut], out_ref.at[slot(col, a)].at[cut], send_sem.at[n], recv_sem.at[n], target
        )
        sent[key].start()

    hops = []

    def hop(col, a, j, n, target_z, when):
        cut = pl.ds(j * high, high)
        copy = remote(
            shard(col, a).at[cut], out_ref.at[slot(col, a)].at[cut],
            z_send.at[(col * chunks + j) * (z_count + 1) + n], z_recv.at[(col * chunks + j) * z_count + origins[a]],
            device(jnp.clip(target_z, 0, last), x, c, s),
        )
        pl.when(when)(copy.start)
        hops.append((when, copy))

    def set_off(col, j):
        if j < along[col]:
            hop(col, 0, j, 0, z + 1, z < last)
            hop(col, 0, j, 1, z - 1, z > 0)

    def pass_on(col, a, j):
        if j < along[col]:
            held = out_ref.at[slot(col, a)].at[pl.ds(j * high, high)]
            arrival = remote(
                held, held, z_send.at[0], z_recv.at[(col * chunks + j) * z_count + origins[a]], across
            ).wait_recv
            if not known or col != OWN:
                arrival()
            elif a > 1:
                pl.when((origins[a] > z + 1) | (origins[a] < z - 1))(arrival)
            target_z = jnp.where(origins[a] < z, z + 1, z - 1)
            hop(col, a, j, a + 1, target_z, (target_z >= 0) & (target_z <= last))

    finished = []

    def complete(now, a, *cols):
        for col in cols:
            send(("core", col, a), col, a, sibling)
            arrive(shard(col, a), slot(col, a))
            finished.append((now, a, col))

    def from_sibling(before):
        while finished and finished[0][0] < before:
            _, a, col = finished.pop(0)
            sent[("core", col, a)].wait_recv()
            place = slot(col, a, 1 - c)
            arrive(out_ref.at[place], place)

    def fan_out(a, j):
        send(("x", a, j), OWN, a, across, j * high, high)
        send(("y", a, j), OWN, a, beside, j * high, high)

    def relay(a, j):
        direct = a == 0 or j >= diagonal
        sent[("x", a, j)].wait_recv()
        if direct:
            send(("ya", a, j), ACROSS, a, beside, j * high, high // 2)
        sent[("y", a, j)].wait_recv()
        if direct:
            send(("xb", a, j), BESIDE, a, across, j * high + high // 2, high // 2)

    def finish(a, j):
        if ("ya", a, j) in sent:
            sent[("ya", a, j)].wait_recv()
            sent[("xb", a, j)].wait_recv()

    first = 1 if known else 0
    for j in range(chunks):
        if known:
            set_off(DIAGONAL, j)
        else:
            set_off(OWN, j)
            fan_out(0, j)
    begin()
    complete(-1, 0, OWN)
    if known:
        complete(-1, 0, ACROSS, BESIDE, DIAGONAL)
    items = [(a, j) for j in range(chunks) for a in range(first, 2)]
    items += [(a, j) for a in range(2, z_count) for j in range(chunks)]
    ends = [items.index((a, chunks - 1)) for a in range(1, z_count)]
    ready = set()
    for now in range(len(items) + max(sum(lag), 3)):
        if now < len(items):
            a, j = items[now]
            if a:
                pass_on(OWN, a, j)
                fan_out(a, j)
                if j == chunks - 1:
                    complete(now, a, OWN)
        if 0 <= now - lag[0] < len(items):
            a, j = items[now - lag[0]]
            relay(a, j)
            if j == chunks - 1:
                complete(now, a, ACROSS, BESIDE)
        if now - 3 in ends:
            a = ends.index(now - 3) + 1
            for j in range(chunks):
                pass_on(DIAGONAL, a, j)
            ready.add(a)
        if 0 <= now - sum(lag) < len(items):
            a, j = items[now - sum(lag)]
            finish(a, j)
            if a == 0:
                set_off(DIAGONAL, j)
            if j == chunks - 1:
                assert a in ready or not a
                complete(now, a, DIAGONAL)
        if now == len(items) - 2 and late is not None:
            late()
        from_sibling(now - 2)
    from_sibling(now + 1)
    for copy in sent.values():
        copy.wait_send()
    for when, copy in hops:
        pl.when(when)(copy.wait_send)


def share_body(
    z_count, rows_ref, targets_ref, candidates_ref, out_ref, slab_ref, own_ref, own_slab,
    z_send, z_recv, send_sem, recv_sem, slab_send, slab_recv, keep_sem,
):
    z, x, c, s = position()
    q, q_across = x * 2 + c, (1 - x) * 2 + c
    half = own_slab.shape[0] // 2
    near, far = pl.ds(pl.multiple_of(s * half, 16), half), pl.ds(pl.multiple_of((1 - s) * half, 16), half)

    def make_unit():
        piece, rows = own_ref.shape[0], rows_ref.shape[0]
        own_ref[...] = unit_rows(candidates_ref[pl.ds(pl.multiple_of(s * piece, 16), piece), :])
        step = math.gcd(rows, 256)
        for begin in range(0, rows, step):
            own_slab[begin : begin + step, :] = unit_rows(rows_ref[begin : begin + step, :])
        extra = own_slab.shape[0] - rows
        place = lax.broadcasted_iota(jnp.int32, (extra, own_slab.shape[1]), 0)
        lines = jnp.zeros(place.shape, jnp.float32)
        for k in range(targets_ref.shape[0]):
            lines = jnp.where(place == k, targets_ref[k : k + 1, :], lines)
        own_slab[rows:, :] = lines.astype(jnp.bfloat16)

    route_greet(z_count, make_unit)
    keep = pltpu.make_async_copy(own_ref, out_ref.at[((z * 2 + x) * 2 + c) * 2 + s], keep_sem.at[0])
    keep_slab = pltpu.make_async_copy(own_slab, slab_ref.at[q], keep_sem.at[1])
    keep.start()
    keep_slab.start()
    shared = []

    def share(src, place, piece, target):
        n = len(shared)
        dst = slab_ref.at[place]
        if piece is not None:
            src, dst = src.at[piece], dst.at[piece]
        shared.append(remote(src, dst, slab_send.at[n], slab_recv.at[n], target))
        shared[-1].start()

    def begin():
        share(own_slab, q, near, device(z, 1 - x, c, s))
        share(own_slab, q, None, device(z, x, 1 - c, s))

    def late():
        shared[0].wait_recv()
        share(slab_ref.at[q_across], q_across, near, device(z, x, c, 1 - s))
        share(slab_ref.at[q_across], q_across, near, device(z, x, 1 - c, s))

    sems = z_send, z_recv, send_sem, recv_sem
    route(z_count, own_ref, out_ref, sems, lambda src, place: None, 1, 0, (2, 2), begin, late)
    shared[2].wait_recv()
    share(slab_ref.at[q_across], q_across, far, device(z, x, 1 - c, s))
    for n in (1, 3, 4):
        shared[n].wait_recv()
    for copy in shared:
        copy.wait_send()
    keep.wait()
    keep_slab.wait()


def share(descriptors, targets, candidates, z_count, collective_id):
    rows, depth = descriptors.shape
    own = (candidates.shape[0] // 2, depth)
    own_slab = (rows + EXTRA, depth)
    anywhere = pl.BlockSpec(memory_space=pl.ANY)
    vmem = pl.BlockSpec(memory_space=pltpu.VMEM)
    return pl.pallas_call(
        functools.partial(share_body, z_count),
        out_shape=[
            jax.ShapeDtypeStruct((8 * z_count,) + own, jnp.bfloat16),
            jax.ShapeDtypeStruct((4,) + own_slab, jnp.bfloat16),
        ],
        in_specs=[vmem, vmem, vmem],
        out_specs=[anywhere, anywhere],
        scratch_shapes=[pltpu.VMEM(own, jnp.bfloat16), pltpu.VMEM(own_slab, jnp.bfloat16)]
        + route_sems(z_count, 1)
        + [pltpu.SemaphoreType.DMA((5,)), pltpu.SemaphoreType.DMA((5,)), pltpu.SemaphoreType.DMA((2,))],
        compiler_params=pltpu.CompilerParams(
            collective_id=collective_id, has_side_effects=True, vmem_limit_bytes=VMEM_BYTES
        ),
    )(descriptors, targets.astype(jnp.float32).reshape(rows // depth, depth), candidates)


def series_body(
    z_count, strip, tile, chunk, normalizer,
    begun_ref, sums_ref, reg_ref, inv_ref, w_ref, gathered,
    dense, first, second, stage, recip, spread_recip, out_buf, w_own, w_slots,
    z_send, z_recv, send_sem, recv_sem, stage_sem, out_sem, w_send, w_recv,
):
    z, x, c, s = position()
    obs = lax.axis_index("obs")
    obs_count = 4 * z_count
    strips = 8 * z_count
    width = strips * strip
    half = strips // 2
    span = begun_ref.shape[2]
    block_rows = width // 2
    lines = tile // LANES
    fold = 1.0 / normalizer

    barrier = pltpu.get_barrier_semaphore()
    peers = [
        {"obs": lax.rem(obs + k, obs_count), "sp": s} for k in range(1, obs_count)
    ]
    for peer in peers + [device(z, x, c, 1 - s)]:
        pl.semaphore_signal(barrier, inc=1, device_id=peer, device_id_type=pl.DeviceIdType.MESH)
    pl.semaphore_wait(barrier, obs_count)

    slots = stage.shape[0]
    waiting = []

    def lay_out(n):
        copy, place = waiting[n]
        copy.wait()
        place = lax.rem(place, 8) * z_count + lax.div(place, 8)
        rows = pl.ds(pl.multiple_of(place * strip, strip), strip)

        def put(k, turn):
            cols = pl.ds(pl.multiple_of(lax.rem(place + k, strips) * strip, strip), strip)
            block = stage[n % slots, :, pl.ds(pl.multiple_of(k * strip, strip), strip)]
            dense[rows, cols] = block
            if turn:
                dense[cols, rows] = block.T

        for k in range(half + 1):
            put(k, 0 < k < half)

    def arrive(src, place):
        n = len(waiting)
        if n >= slots:
            lay_out(n - slots)
        copy = pltpu.make_async_copy(src, stage.at[n % slots], stage_sem.at[n % slots])
        copy.start()
        waiting.append((copy, place))

    def begin():
        per = sums_ref.shape[1] // 2
        for p in range(sums_ref.shape[0]):
            lane = slice(p * per, (p + 1) * per)
            recip[lane, :] = 1.0 / (sums_ref[p, per:, :] * fold + reg_ref[lane, :])

        @pl.loop(0, width // LANES)
        def _(m):
            row = jnp.broadcast_to(recip[pl.ds(m, 1), :], (LANES, LANES))
            spread_recip[pl.ds(pl.multiple_of(m * LANES, LANES), LANES), :] = row.T

    sems = z_send, z_recv, send_sem, recv_sem
    route(z_count, None, gathered, sems, arrive, 4, 2, (2, 3), begin)
    for n in range(len(waiting) - slots, len(waiting)):
        lay_out(n)

    my_cols = pl.ds(pl.multiple_of(obs * tile, tile), tile)

    def by_row(values, rows):
        scale = spread_recip[rows, :]
        return values * jnp.concatenate([scale] * lines, axis=1)

    @pl.loop(0, width // chunk)
    def _(m):
        rows = pl.ds(pl.multiple_of(m * chunk, chunk), chunk)
        first[rows, :] = by_row(dense[rows, my_cols].astype(jnp.float32) * fold, rows).astype(jnp.bfloat16)

    @pl.loop(0, width // chunk)
    def _(m):
        rows = pl.ds(pl.multiple_of(m * chunk, chunk), chunk)
        prod = jnp.dot(dense[rows, :], first[...], preferred_element_type=jnp.float32)
        second[rows, :] = by_row(prod * fold, rows).astype(jnp.bfloat16)

    def my_lines(ref, at):
        return jnp.concatenate([ref[pl.ds(at + h, 1), :] for h in range(lines)], axis=1)

    per = sums_ref.shape[1] // 2
    r_row = my_lines(recip, obs * lines)
    y = my_lines(sums_ref.at[lax.div(obs * lines, per)], lax.rem(obs * lines, per))
    y = y * (1.0 / math.sqrt(normalizer))

    def emit(m):
        return pltpu.make_async_copy(
            out_buf.at[m], inv_ref.at[pl.ds(pl.multiple_of(m * chunk, chunk), chunk)], out_sem.at[m]
        )

    @pl.loop(0, block_rows // chunk)
    def _(m):
        begin_at = s * block_rows + m * chunk
        rows = pl.ds(pl.multiple_of(begin_at, chunk), chunk)
        cubic = jnp.dot(dense[rows, :], second[...], preferred_element_type=jnp.float32)
        on_diag = (begin_at + lax.broadcasted_iota(jnp.int32, (chunk, tile), 0)) == (
            obs * tile + lax.broadcasted_iota(jnp.int32, (chunk, tile), 1)
        )
        series = second[rows, :].astype(jnp.float32) - by_row(
            (dense[rows, my_cols].astype(jnp.float32) + cubic) * fold, rows
        )
        out = (jnp.where(on_diag, 1.0, 0.0) + series) * r_row
        out_buf[m] = out
        emit(m).start()
        weighted = out * y
        weighted = sum(weighted[:, h * LANES : (h + 1) * LANES] for h in range(lines))
        for h in range(chunk // LANES):
            turned = weighted[h * LANES : (h + 1) * LANES, :].T
            w_own[pl.ds(m * (chunk // LANES) + h, 1), :] = jnp.sum(turned, axis=0, keepdims=True)

    copies = []
    for k in range(1, obs_count):
        copies.append(remote(w_own, w_slots.at[obs], w_send.at[k], w_recv.at[k], peers[k - 1]))
        copies[-1].start()
    w_slots[obs] = w_own[...]
    for copy in copies:
        copy.wait()
    total = w_slots[0]
    for k in range(1, obs_count):
        total = total + w_slots[k]
    w_ref[...] = total
    for m in range(block_rows // chunk):
        emit(m).wait()


def series_tile(begun, sums, regularizer, z_count, tile, normalizer, collective_id):
    strips, strip, span = begun.shape
    width = strips * strip
    block_rows = width // 2
    chunk = min(512, block_rows)
    obs_count = 4 * z_count
    w_shape = (block_rows // LANES, LANES)
    anywhere = pl.BlockSpec(memory_space=pl.ANY)
    vmem = pl.BlockSpec(memory_space=pltpu.VMEM)
    inverse_tile, weights, _ = pl.pallas_call(
        functools.partial(series_body, z_count, strip, tile, chunk, normalizer),
        out_shape=[
            jax.ShapeDtypeStruct((block_rows, tile), jnp.float32),
            jax.ShapeDtypeStruct(w_shape, jnp.float32),
            jax.ShapeDtypeStruct(begun.shape, begun.dtype),
        ],
        in_specs=[anywhere, vmem, vmem],
        out_specs=[anywhere, vmem, anywhere],
        scratch_shapes=[
            pltpu.VMEM((width, width), jnp.bfloat16),
            pltpu.VMEM((width, tile), jnp.bfloat16),
            pltpu.VMEM((width, tile), jnp.bfloat16),
            pltpu.VMEM((3, strip, span), jnp.bfloat16),
            pltpu.VMEM((width // LANES, LANES), jnp.float32),
            pltpu.VMEM((width, LANES), jnp.float32),
            pltpu.VMEM((block_rows // chunk, chunk, tile), jnp.float32),
            pltpu.VMEM(w_shape, jnp.float32),
            pltpu.VMEM((obs_count,) + w_shape, jnp.float32),
        ]
        + route_sems(z_count, 4)
        + [
            pltpu.SemaphoreType.DMA((3,)),
            pltpu.SemaphoreType.DMA((block_rows // chunk,)),
            pltpu.SemaphoreType.DMA((obs_count,)),
            pltpu.SemaphoreType.DMA((obs_count,)),
        ],
        compiler_params=pltpu.CompilerParams(
            collective_id=collective_id, has_side_effects=True, vmem_limit_bytes=VMEM_BYTES
        ),
        input_output_aliases={0: 2},
    )(begun, sums, regularizer.reshape(width // LANES, LANES))
    return inverse_tile, weights.reshape(block_rows)


def by_strips(descriptors, candidates, sparse_index, targets, regularizer):
    obs_count = lax.axis_size("obs")
    sp_count = lax.axis_size("sp")
    obs_pos = lax.axis_index("obs")
    sp_pos = lax.axis_index("sp")
    z_count = obs_count // 4
    width = sparse_index.shape[0]
    tile = width // obs_count
    strip = width // (obs_count * sp_count)
    mine = strip * z_count
    span = width // 2 + strip
    window = width // 2 + mine
    rows, depth = descriptors.shape
    normalizer = 24.0 * rows * obs_count

    table, slab = share(descriptors, targets, candidates, z_count, 2)
    table = table.reshape(-1, depth)
    place = lax.rem(obs_pos, 4) * sp_count + sp_pos
    wanted = lax.dynamic_slice_in_dim(
        jnp.concatenate([sparse_index, sparse_index]), place * mine, window
    )
    sparse = table.at[wanted].get(mode="promise_in_bounds")
    begun, sums = slab_gram(
        slab, sparse, z_count, sp_count, strip, span, tile, rows, 0
    )
    return series_tile(begun, sums, regularizer, z_count, tile, normalizer, 3)


def slab_body(z_count, sp_count, strip, tile, root, *refs):
    norm_ref, sp_ref, gathered, sums_ref = refs[:4]
    kbuf, ktr, parts, from_low, from_high, done, zsums, gsums = refs[4:12]
    up_send, up_recv, down_send, down_recv, side_send, side_recv, zs_send, zs_recv, gs_send, gs_recv, keep_sem = refs[12:23]
    near_send, near_recv = refs[23:]
    obs = lax.axis_index("obs")
    s = lax.axis_index("sp")
    z, x, c, _ = position()
    q = x * 2 + c
    group = 4 * sp_count
    p = q * sp_count + s
    last = z_count - 1
    shard, depth = norm_ref.shape[1] - EXTRA, norm_ref.shape[2]
    mine = strip * z_count
    lines = mine // LANES

    z_others = [{"obs": lax.rem(z + k, z_count) * 4 + q, "sp": s} for k in range(1, z_count)]
    group_others = []
    for k in range(1, group):
        to = lax.rem(p + k, group)
        group_others.append({"obs": z * 4 + lax.div(to, sp_count), "sp": lax.rem(to, sp_count)})
    barrier = pltpu.get_barrier_semaphore()
    for other in z_others + group_others:
        pl.semaphore_signal(barrier, inc=1, device_id=other, device_id_type=pl.DeviceIdType.MESH)
    pl.semaphore_wait(barrier, len(z_others) + len(group_others))

    def kernel_tile(t, own):
        cols = pl.ds(pl.multiple_of(t * tile, tile), tile)
        for k in range(4):
            rows = pl.ds(k * shard, shard)
            inner = lax.dot_general(
                norm_ref[k, :shard, :], sp_ref[cols, :], (((1,), (1,)), ((), ())),
                preferred_element_type=jnp.float32,
            )
            scaled = inner * root
            squared = scaled * scaled
            kb = ((squared - 6.0) * squared + 3.0).astype(jnp.bfloat16)
            kbuf[rows, cols] = kb
            if own:
                ktr[cols, rows] = kb.T

    def row_sums():
        for t in range(mine // tile):
            cols = slice(t * tile, (t + 1) * tile)
            weighted = jnp.zeros((1, tile), jnp.float32)
            for k in range(4):
                for h in range(shard // depth):
                    begin = k * shard + h * depth
                    lines_of = jnp.dot(
                        norm_ref[k, shard:, :], kbuf[begin : begin + depth, cols],
                        preferred_element_type=jnp.float32,
                    )
                    weighted = weighted + lines_of[h : h + 1, :]
            square = jnp.zeros((1, tile), jnp.float32)
            for k in range(4):
                kf = kbuf[k * shard : (k + 1) * shard, cols].astype(jnp.float32)
                square = square + jnp.sum(kf * kf, axis=0, keepdims=True)
            for h in range(tile // LANES):
                line = t * (tile // LANES) + h
                lane = slice(h * LANES, (h + 1) * LANES)
                zsums[z, line : line + 1, :] = weighted[:, lane]
                zsums[z, lines + line : lines + line + 1, :] = square[:, lane]

    groups = kbuf.shape[1] // mine

    def piece(t, g):
        begin = t * strip if g == 0 else 0
        end = mine if g < groups - 1 else (t + 1) * strip
        return begin, g * mine + begin - t * strip, end - begin

    def cut(t, g):
        _, begin, size = piece(t, g)
        return pl.ds(begin, size)

    def up(t, g):
        n, at = t * groups + g, (t, slice(None), cut(t, g))
        return remote(
            parts.at[at], from_low.at[at], up_send.at[n], up_recv.at[n],
            {"obs": lax.rem(z + 1, z_count) * 4 + q, "sp": s},
        )

    def down(t, g):
        n, at = t * groups + g, (t, slice(None), cut(t, g))
        return remote(
            parts.at[at], from_high.at[at], down_send.at[n], down_recv.at[n],
            {"obs": lax.rem(z + last, z_count) * 4 + q, "sp": s},
        )

    def gram_group(g):
        cols = slice(g * mine, (g + 1) * mine)
        made = jnp.dot(ktr[...], kbuf[:, cols], preferred_element_type=jnp.float32).astype(jnp.bfloat16)
        for t in range(z_count):
            begin, at, size = piece(t, g)
            parts[t, :, at : at + size] = made[t * strip : (t + 1) * strip, begin : begin + size]

    def pass_on(place, n):
        if place > 0 and 0 <= n - place < groups:
            for t in range(last, place, -1):
                g = n - place
                up(t, g).wait_recv()
                parts[t, :, cut(t, g)] = parts[t, :, cut(t, g)] + from_low[t, :, cut(t, g)]
                up(t, g).start()
        if place < last and 0 <= n - (last - place) < groups:
            for t in range(place):
                g = n - (last - place)
                down(t, g).wait_recv()
                parts[t, :, cut(t, g)] = parts[t, :, cut(t, g)] + from_high[t, :, cut(t, g)]
                down(t, g).start()

    mine_at = ((z * 2 + x) * 2 + c) * 2 + s
    across_at, beside_at = ((z * 2 + 1 - x) * 2 + c) * 2 + s, ((z * 2 + x) * 2 + c) * 2 + 1 - s
    across, beside = device(z, 1 - x, c, s), device(z, x, c, 1 - s)
    half = strip // 2

    def side(place, g, k):
        rows = (slice(None), slice(None), pl.ds(0, half), pl.ds(half, half))[k]
        at = (mine_at, mine_at, across_at, beside_at)[k]
        src = done.at[:, cut(place, g)] if k < 2 else gathered.at[at, rows, cut(place, g)]
        return remote(
            src, gathered.at[at, rows, cut(place, g)], side_send.at[g * 4 + k], side_recv.at[g * 4 + k],
            (across, beside, beside, across)[k],
        )

    def keep(place, g):
        return pltpu.make_async_copy(
            done.at[:, cut(place, g)], gathered.at[mine_at, :, cut(place, g)], keep_sem.at[g]
        )

    def near(place, g, rising):
        to = lax.rem(z + (1 if rising else last), z_count)
        n = g * 2 + int(rising)
        return remote(
            done.at[:, cut(place, g)], gathered.at[mine_at, :, cut(place, g)],
            near_send.at[n], near_recv.at[n], device(to, x, c, s),
        )

    def close(place, g):
        total = parts[place, :, cut(place, g)].astype(jnp.float32)
        if place > 0:
            up(place, g).wait_recv()
            total = total + from_low[place, :, cut(place, g)].astype(jnp.float32)
        if place < last:
            down(place, g).wait_recv()
            total = total + from_high[place, :, cut(place, g)].astype(jnp.float32)
        if g == 0:
            row = lax.broadcasted_iota(jnp.int32, total.shape, 0)
            col = lax.broadcasted_iota(jnp.int32, total.shape, 1)
            total = jnp.where(row == col, 0.0, total)
        done[:, cut(place, g)] = total.astype(jnp.bfloat16)
        side(place, g, 0).start()
        side(place, g, 1).start()
        if place < last:
            near(place, g, True).start()
        if place > 0:
            near(place, g, False).start()
        keep(place, g).start()

    def progress(place, n):
        pass_on(place, n)
        g = n - max(place, last - place)
        if 0 <= g < groups:
            close(place, g)
        if 0 <= g - 1 < groups:
            for k in range(2):
                side(place, g - 1, k).wait_recv()
                side(place, g - 1, k + 2).start()
        if 0 <= g - 2 < groups:
            for k in range(2):
                side(place, g - 2, k + 2).wait_recv()

    z_copies, g_copies = [], []
    for n in range(groups + last + 2):
        if n < groups:

            @pl.loop(n * mine // tile, (n + 1) * mine // tile)
            def _(t):
                kernel_tile(t, n == 0)

            gram_group(n)

            @pl.when(z == 0)
            def _():
                for t in range(last, 0, -1):
                    up(t, n).start()

            @pl.when(z == last)
            def _():
                for t in range(last):
                    down(t, n).start()

        if n == 0:
            row_sums()
            for k in range(1, z_count):
                z_copies.append(remote(zsums.at[z], zsums.at[z], zs_send.at[k], zs_recv.at[k], z_others[k - 1]))
                z_copies[-1].start()
        if n == 1:
            for copy in z_copies:
                copy.wait_recv()
            total = zsums[0]
            for m in range(1, z_count):
                total = total + zsums[m]
            gsums[p] = total
            for m in range(1, group):
                g_copies.append(
                    remote(gsums.at[p], gsums.at[p], gs_send.at[m], gs_recv.at[m], group_others[m - 1])
                )
                g_copies[-1].start()
        for place in range(z_count):
            pl.when(z == place)(functools.partial(progress, place, n))

    def finish(place):
        for g in range(groups):
            for k in range(4):
                side(place, g, k).wait_send()
            keep(place, g).wait()
            if place < last:
                near(place, g, True).wait_send()
                near(place + 1, g, False).wait_recv()
            if place > 0:
                near(place, g, False).wait_send()
                near(place - 1, g, True).wait_recv()
            for t in range(z_count):
                if t > place:
                    up(t, g).wait_send()
                if t < place:
                    down(t, g).wait_send()

    for place in range(z_count):
        pl.when(z == place)(functools.partial(finish, place))

    for copy in g_copies:
        copy.wait()
    for copy in z_copies:
        copy.wait_send()
    sums_ref[...] = gsums[...]


def slab_gram(slab, sparse, z_count, sp_count, strip, span, tile, rows, collective_id):
    depth = slab.shape[2]
    window = sparse.shape[0]
    group = 4 * sp_count
    mine = strip * z_count
    lines = 2 * mine // LANES
    vmem = pl.BlockSpec(memory_space=pltpu.VMEM)
    part = (z_count, strip, span)
    groups = window // mine
    sems = [pltpu.SemaphoreType.DMA((z_count * groups,))] * 4 + [pltpu.SemaphoreType.DMA((4 * groups,))] * 2
    sems += [pltpu.SemaphoreType.DMA((z_count,))] * 2 + [pltpu.SemaphoreType.DMA((group,))] * 2
    sems += [pltpu.SemaphoreType.DMA((groups,))] + [pltpu.SemaphoreType.DMA((2 * groups,))] * 2
    return pl.pallas_call(
        functools.partial(slab_body, z_count, sp_count, strip, tile, math.sqrt(depth)),
        out_shape=[
            jax.ShapeDtypeStruct((group * z_count, strip, span), jnp.bfloat16),
            jax.ShapeDtypeStruct((group, lines, LANES), jnp.float32),
        ],
        in_specs=[vmem, vmem],
        out_specs=[pl.BlockSpec(memory_space=pl.ANY), vmem],
        scratch_shapes=[
            pltpu.VMEM((4 * rows, window), jnp.bfloat16),
            pltpu.VMEM((mine, 4 * rows), jnp.bfloat16),
            pltpu.VMEM(part, jnp.bfloat16),
            pltpu.VMEM(part, jnp.bfloat16),
            pltpu.VMEM(part, jnp.bfloat16),
            pltpu.VMEM(part[1:], jnp.bfloat16),
            pltpu.VMEM((z_count, lines, LANES), jnp.float32),
            pltpu.VMEM((group, lines, LANES), jnp.float32),
        ] + sems,
        compiler_params=pltpu.CompilerParams(
            collective_id=collective_id, has_side_effects=True, vmem_limit_bytes=VMEM_BYTES
        ),
    )(slab, sparse)


def on_device(descriptors, candidates, sparse_index, targets, regularizer):
    obs_count = lax.axis_size("obs")
    sp_count = lax.axis_size("sp")
    obs_pos = lax.axis_index("obs")
    sp_pos = lax.axis_index("sp")
    width = sparse_index.shape[0]
    if sp_count == 2 and width % (obs_count * sp_count * LANES) == 0:
        return by_strips(descriptors, candidates, sparse_index, targets, regularizer)
    tile = width // obs_count
    share = -(-((obs_count // 2 + 1) * tile) // (sp_count * LANES)) * LANES
    normalizer = 24.0 * descriptors.shape[0] * obs_count

    normed = unit_rows(descriptors)
    piece = candidates.shape[0] // sp_count
    own = lax.dynamic_slice_in_dim(candidates, sp_pos * piece, piece)
    table = spread(unit_rows(own), obs_count, sp_count, 2)
    sparse = table.at[sparse_index].get(mode="promise_in_bounds")

    gram, sums = gram_call(
        sp_pos[None].astype(jnp.int32), normed, sparse, targets, obs_count, tile, share, sp_count
    )
    sums = add_over_obs(sums, obs_count, 0)
    part = lax.psum_scatter(gram, "obs", scatter_dimension=0, tiled=True)

    projected = sums[0] / math.sqrt(normalizer)
    root = lax.rsqrt(sums[1] / normalizer + regularizer)
    col_start = obs_pos * tile
    rrow = lax.dynamic_slice_in_dim(root, col_start, tile)
    window_start = col_start + sp_pos * share
    rwin = lax.dynamic_slice_in_dim(jnp.concatenate([root, root]), window_start, share)
    offset = sp_pos * share + lax.iota(jnp.int32, share)
    on_diag = lax.iota(jnp.int32, tile)[:, None] == offset[None, :]
    scaled = jnp.where(
        on_diag, 0.0, part.astype(jnp.float32) * (rrow[:, None] / normalizer) * rwin[None, :]
    ).astype(jnp.bfloat16)
    packed = spread(scaled, obs_count, sp_count, 3)

    y = lax.dynamic_slice_in_dim(projected, col_start, tile)
    pos = jnp.stack([sp_pos, obs_pos]).astype(jnp.int32)
    inverse_tile, part_w = newton_call(
        pos, packed, root, rrow, y, obs_count, tile, share, sp_count
    )
    return inverse_tile, add_over_obs(part_w[0], obs_count, 1)


def solution(mesh):
    in_specs = (P("obs", None), P("obs", None), P(), P("obs"), P())
    out_specs = (P("sp", "obs"), P("sp"))
    return jax.shard_map(
        on_device, mesh=mesh, in_specs=in_specs, out_specs=out_specs, check_vma=False
    )
```

```python
import functools
import math

import jax
import jax.numpy as jnp
from jax import lax
from jax.experimental import pallas as pl
from jax.experimental.pallas import tpu as pltpu
from jax.sharding import PartitionSpec as P

epsilon = 1e-06
LANES = 128
VMEM_BYTES = 58 * 2**20


def unit_rows(row_block):
    values = row_block.astype(jnp.float32)
    return (values * lax.rsqrt(jnp.sum(values * values, axis=1, keepdims=True) + epsilon)).astype(
        jnp.bfloat16
    )


def gram_body(blocks, tile, share, ext, root, s_ref, norm_ref, sp_ref, tgt_ref, gram_ref, ws_ref, kext):
    step = pl.program_id(0)
    width = blocks * tile

    @pl.when(step < blocks)
    def _():
        inner = lax.dot_general(
            norm_ref[...], sp_ref[...], (((1,), (1,)), ((), ())), preferred_element_type=jnp.float32
        )
        scaled = inner * root
        squared = scaled * scaled
        kb = ((squared - 6.0) * squared + 3.0).astype(jnp.bfloat16)
        kext[:, pl.ds(pl.multiple_of(step * tile, tile), tile)] = kb

        @pl.when(step < ext)
        def _():
            kext[:, pl.ds(pl.multiple_of(width + step * tile, tile), tile)] = kb

        kf = kb.astype(jnp.float32)
        weighted = jnp.dot(tgt_ref[...], kb, preferred_element_type=jnp.float32)
        ws_ref[0:1, :] = weighted[0:1, :]
        ws_ref[1:2, :] = jnp.sum(kf * kf, axis=0, keepdims=True)

    @pl.when(step >= blocks)
    def _():
        j = step - blocks
        cols = pl.ds(pl.multiple_of(j * tile, tile), tile)
        window = pl.ds(pl.multiple_of(j * tile + s_ref[0] * share, LANES), share)
        gram_ref[...] = lax.dot_general(
            kext[:, cols], kext[:, window], (((0,), (0,)), ((), ())), preferred_element_type=jnp.float32
        ).astype(jnp.bfloat16)


def gram_call(s_pos, normed, sparse, targets, blocks, tile, share, sp_count):
    rows, depth = normed.shape
    width = blocks * tile
    ext = -(-((blocks - 1) * tile + sp_count * share - width) // tile)
    last = blocks - 1
    return pl.pallas_call(
        functools.partial(gram_body, blocks, tile, share, ext, math.sqrt(depth)),
        grid_spec=pltpu.PrefetchScalarGridSpec(
            num_scalar_prefetch=1,
            grid=(2 * blocks,),
            in_specs=[
                pl.BlockSpec((rows, depth), lambda g, s: (0, 0)),
                pl.BlockSpec((tile, depth), lambda g, s: (jnp.minimum(g, last), 0)),
                pl.BlockSpec((16, rows), lambda g, s: (0, 0)),
            ],
            out_specs=[
                pl.BlockSpec((tile, share), lambda g, s: (jnp.maximum(g - blocks, 0), 0)),
                pl.BlockSpec((2, tile), lambda g, s: (0, jnp.minimum(g, last))),
            ],
            scratch_shapes=[pltpu.VMEM((rows, width + ext * tile), jnp.bfloat16)],
        ),
        out_shape=[
            jax.ShapeDtypeStruct((width, share), jnp.bfloat16),
            jax.ShapeDtypeStruct((2, width), jnp.float32),
        ],
        compiler_params=pltpu.CompilerParams(vmem_limit_bytes=VMEM_BYTES),
    )(s_pos, normed, sparse, jnp.broadcast_to(targets[None, :], (16, rows)))


def newton_body(
    blocks, tile, share, sp_count, chunk, block_rows,
    pos_ref, packed_ref, rcol_ref, rrow_ref, y_ref, inv_ref, w_ref, dense, prod,
):
    step = pl.program_id(0)
    width = blocks * tile
    half = blocks // 2
    p_steps = width // chunk
    my_cols = pl.ds(pl.multiple_of(pos_ref[1] * tile, tile), tile)

    @pl.when(step < blocks)
    def _():
        rows = pl.ds(pl.multiple_of(step * tile, tile), tile)
        for s in range(sp_count):
            for q in range(share // LANES):
                offset = s * share + q * LANES
                if offset >= (half + 1) * tile:
                    continue
                col = lax.rem(step * tile + offset, width)
                cols = pl.ds(pl.multiple_of(col, LANES), LANES)
                block = packed_ref[s * tile : (s + 1) * tile, q * LANES : (q + 1) * LANES]
                dense[rows, cols] = block
                if tile <= offset < half * tile:
                    dense[cols, rows] = block.T

    @pl.when((step >= blocks) & (step < blocks + p_steps))
    def _():
        rows = pl.ds(pl.multiple_of((step - blocks) * chunk, chunk), chunk)
        prod[rows, :] = jnp.dot(
            dense[rows, :], dense[:, my_cols], preferred_element_type=jnp.float32
        ).astype(jnp.bfloat16)

    @pl.when(step >= blocks + p_steps)
    def _():
        local = pl.multiple_of((step - blocks - p_steps) * chunk, chunk)
        start = pl.multiple_of(pos_ref[0] * block_rows + local, chunk)
        rows = pl.ds(start, chunk)
        cubic = jnp.dot(dense[rows, :], prod[...], preferred_element_type=jnp.float32)
        on_diag = (start + lax.broadcasted_iota(jnp.int32, (chunk, tile), 0)) == (
            pos_ref[1] * tile + lax.broadcasted_iota(jnp.int32, (chunk, tile), 1)
        )
        series = (
            jnp.where(on_diag, 1.0, 0.0)
            - dense[rows, my_cols].astype(jnp.float32)
            + prod[rows, :].astype(jnp.float32)
            - cubic
        )
        out = series * rcol_ref[rows, :] * rrow_ref[...]
        inv_ref[pl.ds(local, chunk), :] = out
        w_ref[:, pl.ds(local, chunk)] = lax.dot_general(
            y_ref[...], out, (((1,), (1,)), ((), ())),
            precision=lax.Precision.HIGHEST, preferred_element_type=jnp.float32,
        )


def newton_call(pos, packed, root_recip, rrow, y, blocks, tile, share, sp_count):
    width = blocks * tile
    block_rows = width // sp_count
    chunk = min(512, block_rows)
    grid = blocks + width // chunk + block_rows // chunk
    last = blocks - 1
    return pl.pallas_call(
        functools.partial(newton_body, blocks, tile, share, sp_count, chunk, block_rows),
        grid_spec=pltpu.PrefetchScalarGridSpec(
            num_scalar_prefetch=1,
            grid=(grid,),
            in_specs=[
                pl.BlockSpec((sp_count * tile, share), lambda g, p: (jnp.minimum(g, last), 0)),
                pl.BlockSpec((width, 1), lambda g, p: (0, 0)),
                pl.BlockSpec((1, tile), lambda g, p: (0, 0)),
                pl.BlockSpec((8, tile), lambda g, p: (0, 0)),
            ],
            out_specs=[
                pl.BlockSpec((block_rows, tile), lambda g, p: (0, 0)),
                pl.BlockSpec((8, block_rows), lambda g, p: (0, 0)),
            ],
            scratch_shapes=[
                pltpu.VMEM((width, width), jnp.bfloat16),
                pltpu.VMEM((width, tile), jnp.bfloat16),
            ],
        ),
        out_shape=[
            jax.ShapeDtypeStruct((block_rows, tile), jnp.float32),
            jax.ShapeDtypeStruct((8, block_rows), jnp.float32),
        ],
        compiler_params=pltpu.CompilerParams(vmem_limit_bytes=VMEM_BYTES),
    )(pos, packed, root_recip[:, None], rrow[None, :], jnp.broadcast_to(y[None, :], (8, tile)))


def add_body(count, in_ref, out_ref, slots, send_sem, recv_sem):
    me = lax.axis_index("obs")
    barrier = pltpu.get_barrier_semaphore()
    for k in range(1, count):
        pl.semaphore_signal(
            barrier, inc=1, device_id={"obs": lax.rem(me + k, count)}, device_id_type=pl.DeviceIdType.MESH
        )
    pl.semaphore_wait(barrier, count - 1)
    copies = []
    for k in range(1, count):
        copy = pltpu.make_async_remote_copy(
            src_ref=in_ref,
            dst_ref=slots.at[me],
            send_sem=send_sem.at[k],
            recv_sem=recv_sem.at[k],
            device_id={"obs": lax.rem(me + k, count)},
            device_id_type=pl.DeviceIdType.MESH,
        )
        copy.start()
        copies.append(copy)
    slots[me] = in_ref[...]
    for copy in copies:
        copy.wait()
    total = slots[0]
    for k in range(1, count):
        total = total + slots[k]
    out_ref[...] = total


def add_over_obs(values, count, collective_id):
    shape = values.shape
    flat = values.reshape(values.size // LANES, LANES)
    total = pl.pallas_call(
        functools.partial(add_body, count),
        out_shape=jax.ShapeDtypeStruct(flat.shape, flat.dtype),
        in_specs=[pl.BlockSpec(memory_space=pltpu.VMEM)],
        out_specs=pl.BlockSpec(memory_space=pltpu.VMEM),
        scratch_shapes=[
            pltpu.VMEM((count,) + flat.shape, flat.dtype),
            pltpu.SemaphoreType.DMA((count,)),
            pltpu.SemaphoreType.DMA((count,)),
        ],
        cost_estimate=pl.CostEstimate(
            flops=count * flat.size, bytes_accessed=400 * flat.size, transcendentals=0
        ),
        compiler_params=pltpu.CompilerParams(collective_id=collective_id, has_side_effects=True),
    )(flat)
    return total.reshape(shape)


def spread_keys(z_count, sp_count):
    keys = [("z", k) for k in range(1, z_count)]
    for k in range(z_count):
        keys += [("x", k), ("core", k), ("core_x", k)]
        for d in range(1, sp_count):
            keys += [(name, k, d) for name in ("sp", "sp_a", "x_b", "core_sp", "core_a", "core_b")]
    return {key: place for place, key in enumerate(keys)}


def spread_body(z_count, sp_count, in_ref, out_ref, send_sem, recv_sem, own_sem):
    places = spread_keys(z_count, sp_count)
    obs = lax.axis_index("obs")
    s = lax.axis_index("sp")
    z, x, c = lax.div(obs, 4), lax.rem(lax.div(obs, 2), 2), lax.rem(obs, 2)
    half = in_ref.shape[0] // 2
    upper, lower = pl.ds(0, half), pl.ds(half, half)
    zs = [lax.bitwise_xor(z, k) for k in range(z_count)]
    to_sp = [lax.rem(s + d, sp_count) for d in range(sp_count)]
    from_sp = [lax.rem(s - d + sp_count, sp_count) for d in range(sp_count)]

    def device(z_to, x_to, c_to, s_to):
        return {"obs": z_to * 4 + x_to * 2 + c_to, "sp": s_to}

    def slot(z_of, x_of, s_of):
        return ((z_of * 2 + x_of) * 2 + c) * sp_count + s_of

    own_slot = slot(z, x, s)
    across, sibling = device(z, 1 - x, c, s), device(z, x, 1 - c, s)
    others = [device(zs[k], x, c, s) for k in range(1, z_count)]
    others += [device(z, x, c, to_sp[d]) for d in range(1, sp_count)]
    others += [across, sibling]
    barrier = pltpu.get_barrier_semaphore()
    for other in others:
        pl.semaphore_signal(barrier, inc=1, device_id=other, device_id_type=pl.DeviceIdType.MESH)
    pl.semaphore_wait(barrier, len(others))

    sent = {}

    def send(key, place, target, rows=None, own=False):
        src = in_ref if own else out_ref.at[place]
        dst = out_ref.at[place]
        if rows is not None:
            src, dst = src.at[rows], dst.at[rows]
        copy = pltpu.make_async_remote_copy(
            src_ref=src,
            dst_ref=dst,
            send_sem=send_sem.at[places[key]],
            recv_sem=recv_sem.at[places[key]],
            device_id=target,
            device_id_type=pl.DeviceIdType.MESH,
        )
        copy.start()
        sent[key] = copy

    keep = pltpu.make_async_copy(in_ref, out_ref.at[own_slot], own_sem)
    keep.start()
    for k in range(1, z_count):
        send(("z", k), own_slot, others[k - 1], own=True)

    def fan_out(k):
        place = slot(zs[k], x, s)
        send(("x", k), place, across, own=k == 0)
        for d in range(1, sp_count):
            send(("sp", k, d), place, device(z, x, c, to_sp[d]), own=k == 0)
        send(("core", k), place, sibling, own=k == 0)

    def relay(k):
        sent[("x", k)].wait_recv()
        place = slot(zs[k], 1 - x, s)
        for d in range(1, sp_count):
            send(("sp_a", k, d), place, device(z, x, c, to_sp[d]), upper)
        send(("core_x", k), place, sibling)
        for d in range(1, sp_count):
            sent[("sp", k, d)].wait_recv()
            place = slot(zs[k], x, from_sp[d])
            send(("x_b", k, d), place, across, lower)
            send(("core_sp", k, d), place, sibling)

    def finish(k):
        for d in range(1, sp_count):
            place = slot(zs[k], 1 - x, from_sp[d])
            sent[("sp_a", k, d)].wait_recv()
            send(("core_a", k, d), place, sibling, upper)
            sent[("x_b", k, d)].wait_recv()
            send(("core_b", k, d), place, sibling, lower)

    fan_out(0)
    for k in range(1, z_count):
        sent[("z", k)].wait_recv()
        fan_out(k)
        relay(k - 1)
        if k > 1:
            finish(k - 2)
    relay(z_count - 1)
    if z_count > 1:
        finish(z_count - 2)
    finish(z_count - 1)
    keep.wait()
    for key, copy in sent.items():
        copy.wait_send()
        if key[0].startswith("core"):
            copy.wait_recv()


def spread(shard, obs_count, sp_count, collective_id):
    rows, cols = shard.shape
    z_count = obs_count // 4
    total = obs_count * sp_count
    sems = len(spread_keys(z_count, sp_count))
    gathered = pl.pallas_call(
        functools.partial(spread_body, z_count, sp_count),
        out_shape=jax.ShapeDtypeStruct((total, rows, cols), shard.dtype),
        in_specs=[pl.BlockSpec(memory_space=pl.ANY)],
        out_specs=pl.BlockSpec(memory_space=pl.ANY),
        scratch_shapes=[
            pltpu.SemaphoreType.DMA((sems,)),
            pltpu.SemaphoreType.DMA((sems,)),
            pltpu.SemaphoreType.DMA,
        ],
        compiler_params=pltpu.CompilerParams(collective_id=collective_id, has_side_effects=True),
    )(shard)
    return gathered.reshape(total * rows, cols)


def position():
    obs = lax.axis_index("obs")
    return lax.div(obs, 4), lax.rem(lax.div(obs, 2), 2), lax.rem(obs, 2), lax.axis_index("sp")


def device(z, x, c, s):
    return {"obs": z * 4 + x * 2 + c, "sp": s}


def remote(src, dst, send_sem, recv_sem, target):
    return pltpu.make_async_remote_copy(
        src_ref=src, dst_ref=dst, send_sem=send_sem, recv_sem=recv_sem,
        device_id=target, device_id_type=pl.DeviceIdType.MESH,
    )


def route_sems(z_count, chunks):
    return [
        pltpu.SemaphoreType.DMA((4 * chunks * (z_count + 1),)),
        pltpu.SemaphoreType.DMA((4 * chunks * z_count,)),
        pltpu.SemaphoreType.DMA((4 * (chunks + 1) * z_count,)),
        pltpu.SemaphoreType.DMA((4 * (chunks + 1) * z_count,)),
    ]


def route_greet(z_count, meanwhile):
    z, x, c, s = position()
    barrier = pltpu.get_barrier_semaphore()
    others = [device(z, 1 - x, c, s), device(z, x, 1 - c, s), device(z, x, c, 1 - s)]
    others += [device(lax.rem(z + k, z_count), x, c, s) for k in range(1, z_count)]
    for other in others:
        pl.semaphore_signal(barrier, inc=1, device_id=other, device_id_type=pl.DeviceIdType.MESH)
    meanwhile()
    pl.semaphore_wait(barrier, len(others))


EXTRA = 32
OWN, ACROSS, BESIDE, DIAGONAL = range(4)


def route(z_count, home, out_ref, sems, arrive, chunks, diagonal, lag, begin, late=None):
    z_send, z_recv, send_sem, recv_sem = sems
    z, x, c, s = position()
    last = z_count - 1
    rows = out_ref.shape[1]
    high = rows // chunks
    known = home is None
    across, beside, sibling = device(z, 1 - x, c, s), device(z, x, c, 1 - s), device(z, x, 1 - c, s)
    along = {OWN: chunks, ACROSS: 0, BESIDE: 0, DIAGONAL: diagonal}

    nearer = jnp.minimum(z, last - z)
    origins = [z]
    for a in range(last):
        both = jnp.where((z <= last // 2) == (a % 2 == 0), z + (a // 2 + 1), z - (a // 2 + 1))
        single = jnp.where(z <= last - z, z + (a - nearer + 1), z - (a - nearer + 1))
        origins.append(jnp.where(a < 2 * nearer, both, single))

    def slot(col, a, c_of=c):
        x_of = 1 - x if col in (ACROSS, DIAGONAL) else x
        s_of = 1 - s if col in (BESIDE, DIAGONAL) else s
        return ((origins[a] * 2 + x_of) * 2 + c_of) * 2 + s_of

    def shard(col, a):
        return out_ref.at[slot(col, a)] if a or col != OWN or known else home

    sent = {}

    def send(key, col, a, target, begin=0, size=rows):
        cut = pl.ds(begin, size)
        n = len(sent)
        sent[key] = remote(
            shard(col, a).at[cut], out_ref.at[slot(col, a)].at[cut], send_sem.at[n], recv_sem.at[n], target
        )
        sent[key].start()

    hops = []

    def hop(col, a, j, n, target_z, when):
        cut = pl.ds(j * high, high)
        copy = remote(
            shard(col, a).at[cut], out_ref.at[slot(col, a)].at[cut],
            z_send.at[(col * chunks + j) * (z_count + 1) + n], z_recv.at[(col * chunks + j) * z_count + origins[a]],
            device(jnp.clip(target_z, 0, last), x, c, s),
        )
        pl.when(when)(copy.start)
        hops.append((when, copy))

    def set_off(col, j):
        if j < along[col]:
            hop(col, 0, j, 0, z + 1, z < last)
            hop(col, 0, j, 1, z - 1, z > 0)

    def pass_on(col, a, j):
        if j < along[col]:
            held = out_ref.at[slot(col, a)].at[pl.ds(j * high, high)]
            arrival = remote(
                held, held, z_send.at[0], z_recv.at[(col * chunks + j) * z_count + origins[a]], across
            ).wait_recv
            if not known or col != OWN or a > 1:
                arrival()
            target_z = jnp.where(origins[a] < z, z + 1, z - 1)
            hop(col, a, j, a + 1, target_z, (target_z >= 0) & (target_z <= last))

    finished = []

    def complete(now, a, *cols):
        for col in cols:
            send(("core", col, a), col, a, sibling)
            arrive(shard(col, a), slot(col, a))
            finished.append((now, a, col))

    def from_sibling(before):
        while finished and finished[0][0] < before:
            _, a, col = finished.pop(0)
            sent[("core", col, a)].wait_recv()
            place = slot(col, a, 1 - c)
            arrive(out_ref.at[place], place)

    def fan_out(a, j):
        send(("x", a, j), OWN, a, across, j * high, high)
        send(("y", a, j), OWN, a, beside, j * high, high)

    def relay(a, j):
        direct = a == 0 or j >= diagonal
        sent[("x", a, j)].wait_recv()
        if direct:
            send(("ya", a, j), ACROSS, a, beside, j * high, high // 2)
        sent[("y", a, j)].wait_recv()
        if direct:
            send(("xb", a, j), BESIDE, a, across, j * high + high // 2, high // 2)

    def finish(a, j):
        if ("ya", a, j) in sent:
            sent[("ya", a, j)].wait_recv()
            sent[("xb", a, j)].wait_recv()

    first = 1 if known else 0
    for j in range(chunks):
        if known:
            hop(OWN, 0, j, 0, jnp.where(z == 0, 1, last - 1), (z == 0) | (z == last))
        else:
            set_off(OWN, j)
            fan_out(0, j)
    for j in range(chunks if known else 0):
        set_off(DIAGONAL, j)
    begin()
    complete(-1, 0, OWN)
    if known:
        complete(-1, 0, ACROSS, BESIDE, DIAGONAL)
    items = [(a, j) for j in range(chunks) for a in range(first, 2)]
    items += [(a, j) for a in range(2, z_count) for j in range(chunks)]
    ends = [items.index((a, chunks - 1)) for a in range(1, z_count)]
    ready = set()
    for now in range(len(items) + max(sum(lag), 3)):
        if now < len(items):
            a, j = items[now]
            if a:
                pass_on(OWN, a, j)
                fan_out(a, j)
                if j == chunks - 1:
                    complete(now, a, OWN)
        if 0 <= now - lag[0] < len(items):
            a, j = items[now - lag[0]]
            relay(a, j)
            if j == chunks - 1:
                complete(now, a, ACROSS, BESIDE)
        if now - 3 in ends:
            a = ends.index(now - 3) + 1
            for j in range(chunks):
                pass_on(DIAGONAL, a, j)
            ready.add(a)
        if 0 <= now - sum(lag) < len(items):
            a, j = items[now - sum(lag)]
            finish(a, j)
            if a == 0:
                set_off(DIAGONAL, j)
            if j == chunks - 1:
                assert a in ready or not a
                complete(now, a, DIAGONAL)
        if now == len(items) - 2 and late is not None:
            late()
        from_sibling(now - 2)
    from_sibling(now + 1)
    for copy in sent.values():
        copy.wait_send()
    for when, copy in hops:
        pl.when(when)(copy.wait_send)


def share_body(
    z_count, rows_ref, targets_ref, candidates_ref, out_ref, slab_ref, own_ref, own_slab,
    z_send, z_recv, send_sem, recv_sem, slab_send, slab_recv, keep_sem,
):
    z, x, c, s = position()
    q, q_across = x * 2 + c, (1 - x) * 2 + c
    half = own_slab.shape[0] // 2
    near, far = pl.ds(pl.multiple_of(s * half, 16), half), pl.ds(pl.multiple_of((1 - s) * half, 16), half)

    def make_unit():
        piece, rows = own_ref.shape[0], rows_ref.shape[0]
        own_ref[...] = unit_rows(candidates_ref[pl.ds(pl.multiple_of(s * piece, 16), piece), :])
        step = math.gcd(rows, 256)
        for begin in range(0, rows, step):
            own_slab[begin : begin + step, :] = unit_rows(rows_ref[begin : begin + step, :])
        extra = own_slab.shape[0] - rows
        place = lax.broadcasted_iota(jnp.int32, (extra, own_slab.shape[1]), 0)
        lines = jnp.zeros(place.shape, jnp.float32)
        for k in range(rows // own_slab.shape[1]):
            line = targets_ref[:, k * own_slab.shape[1] : (k + 1) * own_slab.shape[1]].astype(jnp.float32)
            lines = jnp.where(place == k, line, lines)
        own_slab[rows:, :] = lines.astype(jnp.bfloat16)

    route_greet(z_count, make_unit)
    keep = pltpu.make_async_copy(own_ref, out_ref.at[((z * 2 + x) * 2 + c) * 2 + s], keep_sem.at[0])
    keep_slab = pltpu.make_async_copy(own_slab, slab_ref.at[q], keep_sem.at[1])
    keep.start()
    keep_slab.start()
    shared = []

    def share(src, place, piece, target):
        n = len(shared)
        dst = slab_ref.at[place]
        if piece is not None:
            src, dst = src.at[piece], dst.at[piece]
        shared.append(remote(src, dst, slab_send.at[n], slab_recv.at[n], target))
        shared[-1].start()

    def begin():
        share(own_slab, q, near, device(z, 1 - x, c, s))
        share(own_slab, q, None, device(z, x, 1 - c, s))

    def late():
        shared[0].wait_recv()
        share(slab_ref.at[q_across], q_across, near, device(z, x, c, 1 - s))
        share(slab_ref.at[q_across], q_across, near, device(z, x, 1 - c, s))

    sems = z_send, z_recv, send_sem, recv_sem
    route(z_count, own_ref, out_ref, sems, lambda src, place: None, 1, 0, (2, 2), begin, late)
    shared[2].wait_recv()
    share(slab_ref.at[q_across], q_across, far, device(z, x, 1 - c, s))
    for n in (1, 3, 4):
        shared[n].wait_recv()
    for copy in shared:
        copy.wait_send()
    keep.wait()
    keep_slab.wait()


def share(descriptors, targets, candidates, z_count, collective_id):
    rows, depth = descriptors.shape
    own = (candidates.shape[0] // 2, depth)
    own_slab = (rows + EXTRA, depth)
    anywhere = pl.BlockSpec(memory_space=pl.ANY)
    vmem = pl.BlockSpec(memory_space=pltpu.VMEM)
    return pl.pallas_call(
        functools.partial(share_body, z_count),
        out_shape=[
            jax.ShapeDtypeStruct((8 * z_count,) + own, jnp.bfloat16),
            jax.ShapeDtypeStruct((4,) + own_slab, jnp.bfloat16),
        ],
        in_specs=[vmem, vmem, vmem],
        out_specs=[anywhere, anywhere],
        scratch_shapes=[pltpu.VMEM(own, jnp.bfloat16), pltpu.VMEM(own_slab, jnp.bfloat16)]
        + route_sems(z_count, 1)
        + [pltpu.SemaphoreType.DMA((5,)), pltpu.SemaphoreType.DMA((5,)), pltpu.SemaphoreType.DMA((2,))],
        compiler_params=pltpu.CompilerParams(
            collective_id=collective_id, has_side_effects=True, vmem_limit_bytes=VMEM_BYTES
        ),
    )(descriptors, targets.reshape(1, rows), candidates)


def series_body(
    z_count, strip, tile, chunk, normalizer,
    begun_ref, sums_ref, reg_ref, inv_ref, w_ref, gathered,
    dense, first, second, stage, recip, spread_recip, out_buf, w_own, w_slots,
    z_send, z_recv, send_sem, recv_sem, stage_sem, out_sem, w_send, w_recv,
):
    z, x, c, s = position()
    obs = lax.axis_index("obs")
    obs_count = 4 * z_count
    strips = 8 * z_count
    width = strips * strip
    half = strips // 2
    span = begun_ref.shape[2]
    block_rows = width // 2
    lines = tile // LANES
    fold = 1.0 / normalizer

    barrier = pltpu.get_barrier_semaphore()
    peers = [
        {"obs": lax.rem(obs + k, obs_count), "sp": s} for k in range(1, obs_count)
    ]
    for peer in peers + [device(z, x, c, 1 - s)]:
        pl.semaphore_signal(barrier, inc=1, device_id=peer, device_id_type=pl.DeviceIdType.MESH)
    pl.semaphore_wait(barrier, obs_count)

    slots = stage.shape[0]
    waiting = []

    def lay_out(n):
        copy, place = waiting[n]
        copy.wait()
        place = lax.rem(place, 8) * z_count + lax.div(place, 8)
        rows = pl.ds(pl.multiple_of(place * strip, strip), strip)

        def put(k, turn):
            cols = pl.ds(pl.multiple_of(lax.rem(place + k, strips) * strip, strip), strip)
            block = stage[n % slots, :, pl.ds(pl.multiple_of(k * strip, strip), strip)]
            dense[rows, cols] = block
            if turn:
                dense[cols, rows] = block.T

        for k in range(half + 1):
            put(k, 0 < k < half)

    def arrive(src, place):
        n = len(waiting)
        if n >= slots:
            lay_out(n - slots)
        copy = pltpu.make_async_copy(src, stage.at[n % slots], stage_sem.at[n % slots])
        copy.start()
        waiting.append((copy, place))

    def begin():
        per = sums_ref.shape[1] // 2
        for p in range(sums_ref.shape[0]):
            lane = slice(p * per, (p + 1) * per)
            recip[lane, :] = 1.0 / (sums_ref[p, per:, :] * fold + reg_ref[lane, :])

        @pl.loop(0, width // LANES)
        def _(m):
            row = jnp.broadcast_to(recip[pl.ds(m, 1), :], (LANES, LANES))
            spread_recip[pl.ds(pl.multiple_of(m * LANES, LANES), LANES), :] = row.T

    sems = z_send, z_recv, send_sem, recv_sem
    route(z_count, None, gathered, sems, arrive, 4, 2, (2, 3), begin)
    for n in range(len(waiting) - slots, len(waiting)):
        lay_out(n)

    my_cols = pl.ds(pl.multiple_of(obs * tile, tile), tile)

    def by_row(values, rows):
        scale = spread_recip[rows, :]
        return values * jnp.concatenate([scale] * lines, axis=1)

    @pl.loop(0, width // chunk)
    def _(m):
        rows = pl.ds(pl.multiple_of(m * chunk, chunk), chunk)
        first[rows, :] = by_row(dense[rows, my_cols].astype(jnp.float32) * fold, rows).astype(jnp.bfloat16)

    @pl.loop(0, width // chunk)
    def _(m):
        rows = pl.ds(pl.multiple_of(m * chunk, chunk), chunk)
        prod = jnp.dot(dense[rows, :], first[...], preferred_element_type=jnp.float32)
        second[rows, :] = by_row(prod * fold, rows).astype(jnp.bfloat16)

    def my_lines(ref, at):
        return jnp.concatenate([ref[pl.ds(at + h, 1), :] for h in range(lines)], axis=1)

    per = sums_ref.shape[1] // 2
    r_row = my_lines(recip, obs * lines)
    y = my_lines(sums_ref.at[lax.div(obs * lines, per)], lax.rem(obs * lines, per))
    y = y * (1.0 / math.sqrt(normalizer))

    def emit(m):
        return pltpu.make_async_copy(
            out_buf.at[m], inv_ref.at[pl.ds(pl.multiple_of(m * chunk, chunk), chunk)], out_sem.at[m]
        )

    @pl.loop(0, block_rows // chunk)
    def _(m):
        begin_at = s * block_rows + m * chunk
        rows = pl.ds(pl.multiple_of(begin_at, chunk), chunk)
        cubic = jnp.dot(dense[rows, :], second[...], preferred_element_type=jnp.float32)
        on_diag = (begin_at + lax.broadcasted_iota(jnp.int32, (chunk, tile), 0)) == (
            obs * tile + lax.broadcasted_iota(jnp.int32, (chunk, tile), 1)
        )
        series = second[rows, :].astype(jnp.float32) - by_row(
            (dense[rows, my_cols].astype(jnp.float32) + cubic) * fold, rows
        )
        out = (jnp.where(on_diag, 1.0, 0.0) + series) * r_row
        out_buf[m] = out
        emit(m).start()
        weighted = out * y
        weighted = sum(weighted[:, h * LANES : (h + 1) * LANES] for h in range(lines))
        for h in range(chunk // LANES):
            turned = weighted[h * LANES : (h + 1) * LANES, :].T
            w_own[pl.ds(m * (chunk // LANES) + h, 1), :] = jnp.sum(turned, axis=0, keepdims=True)

    copies = []
    for k in range(1, obs_count):
        copies.append(remote(w_own, w_slots.at[obs], w_send.at[k], w_recv.at[k], peers[k - 1]))
        copies[-1].start()
    w_slots[obs] = w_own[...]
    for copy in copies:
        copy.wait()
    total = w_slots[0]
    for k in range(1, obs_count):
        total = total + w_slots[k]
    w_ref[...] = total
    for m in range(block_rows // chunk):
        emit(m).wait()


def series_tile(begun, sums, regularizer, z_count, tile, normalizer, collective_id):
    strips, strip, span = begun.shape
    width = strips * strip
    block_rows = width // 2
    chunk = min(512, block_rows)
    obs_count = 4 * z_count
    w_shape = (block_rows // LANES, LANES)
    anywhere = pl.BlockSpec(memory_space=pl.ANY)
    vmem = pl.BlockSpec(memory_space=pltpu.VMEM)
    inverse_tile, weights, _ = pl.pallas_call(
        functools.partial(series_body, z_count, strip, tile, chunk, normalizer),
        out_shape=[
            jax.ShapeDtypeStruct((block_rows, tile), jnp.float32),
            jax.ShapeDtypeStruct(w_shape, jnp.float32),
            jax.ShapeDtypeStruct(begun.shape, begun.dtype),
        ],
        in_specs=[anywhere, vmem, vmem],
        out_specs=[anywhere, vmem, anywhere],
        scratch_shapes=[
            pltpu.VMEM((width, width), jnp.bfloat16),
            pltpu.VMEM((width, tile), jnp.bfloat16),
            pltpu.VMEM((width, tile), jnp.bfloat16),
            pltpu.VMEM((3, strip, span), jnp.bfloat16),
            pltpu.VMEM((width // LANES, LANES), jnp.float32),
            pltpu.VMEM((width, LANES), jnp.float32),
            pltpu.VMEM((block_rows // chunk, chunk, tile), jnp.float32),
            pltpu.VMEM(w_shape, jnp.float32),
            pltpu.VMEM((obs_count,) + w_shape, jnp.float32),
        ]
        + route_sems(z_count, 4)
        + [
            pltpu.SemaphoreType.DMA((3,)),
            pltpu.SemaphoreType.DMA((block_rows // chunk,)),
            pltpu.SemaphoreType.DMA((obs_count,)),
            pltpu.SemaphoreType.DMA((obs_count,)),
        ],
        compiler_params=pltpu.CompilerParams(
            collective_id=collective_id, has_side_effects=True, vmem_limit_bytes=VMEM_BYTES
        ),
        input_output_aliases={0: 2},
    )(begun, sums, regularizer.reshape(width // LANES, LANES))
    return inverse_tile, weights.reshape(block_rows)


def by_strips(descriptors, candidates, sparse_index, targets, regularizer):
    obs_count = lax.axis_size("obs")
    sp_count = lax.axis_size("sp")
    obs_pos = lax.axis_index("obs")
    sp_pos = lax.axis_index("sp")
    z_count = obs_count // 4
    width = sparse_index.shape[0]
    tile = width // obs_count
    strip = width // (obs_count * sp_count)
    mine = strip * z_count
    span = width // 2 + strip
    window = width // 2 + mine
    rows, depth = descriptors.shape
    normalizer = 24.0 * rows * obs_count

    table, slab = share(descriptors, targets, candidates, z_count, 2)
    table = table.reshape(-1, depth)
    place = lax.rem(obs_pos, 4) * sp_count + sp_pos
    wanted = lax.dynamic_slice_in_dim(
        jnp.concatenate([sparse_index, sparse_index]), place * mine, window
    )
    sparse = table.at[wanted].get(mode="promise_in_bounds")
    begun, sums = slab_gram(
        slab, sparse, z_count, sp_count, strip, span, tile, rows, 0
    )
    return series_tile(begun, sums, regularizer, z_count, tile, normalizer, 3)


def slab_body(z_count, sp_count, strip, tile, root, *refs):
    norm_ref, sp_ref, gathered, sums_ref = refs[:4]
    kbuf, ktr, parts, from_low, from_high, done, zsums, gsums = refs[4:12]
    up_send, up_recv, down_send, down_recv, side_send, side_recv, zs_send, zs_recv, gs_send, gs_recv, keep_sem = refs[12:23]
    near_send, near_recv = refs[23:]
    obs = lax.axis_index("obs")
    s = lax.axis_index("sp")
    z, x, c, _ = position()
    q = x * 2 + c
    group = 4 * sp_count
    p = q * sp_count + s
    last = z_count - 1
    shard, depth = norm_ref.shape[1] - EXTRA, norm_ref.shape[2]
    mine = strip * z_count
    lines = mine // LANES

    z_others = [{"obs": lax.rem(z + k, z_count) * 4 + q, "sp": s} for k in range(1, z_count)]
    group_others = []
    for k in range(1, group):
        to = lax.rem(p + k, group)
        group_others.append({"obs": z * 4 + lax.div(to, sp_count), "sp": lax.rem(to, sp_count)})
    barrier = pltpu.get_barrier_semaphore()
    for other in z_others + group_others:
        pl.semaphore_signal(barrier, inc=1, device_id=other, device_id_type=pl.DeviceIdType.MESH)
    pl.semaphore_wait(barrier, len(z_others) + len(group_others))

    def kernel_tile(t, own):
        cols = pl.ds(pl.multiple_of(t * tile, tile), tile)
        for k in range(4):
            rows = pl.ds(k * shard, shard)
            inner = lax.dot_general(
                norm_ref[k, :shard, :], sp_ref[cols, :], (((1,), (1,)), ((), ())),
                preferred_element_type=jnp.float32,
            )
            scaled = inner * root
            squared = scaled * scaled
            kb = ((squared - 6.0) * squared + 3.0).astype(jnp.bfloat16)
            kbuf[rows, cols] = kb
            if own:
                ktr[cols, rows] = kb.T

    def row_sums():
        for t in range(mine // tile):
            cols = slice(t * tile, (t + 1) * tile)
            weighted = jnp.zeros((1, tile), jnp.float32)
            for k in range(4):
                for h in range(shard // depth):
                    begin = k * shard + h * depth
                    lines_of = jnp.dot(
                        norm_ref[k, shard:, :], kbuf[begin : begin + depth, cols],
                        preferred_element_type=jnp.float32,
                    )
                    weighted = weighted + lines_of[h : h + 1, :]
            square = jnp.zeros((1, tile), jnp.float32)
            for k in range(4):
                kf = kbuf[k * shard : (k + 1) * shard, cols].astype(jnp.float32)
                square = square + jnp.sum(kf * kf, axis=0, keepdims=True)
            for h in range(tile // LANES):
                line = t * (tile // LANES) + h
                lane = slice(h * LANES, (h + 1) * LANES)
                zsums[z, line : line + 1, :] = weighted[:, lane]
                zsums[z, lines + line : lines + line + 1, :] = square[:, lane]

    groups = kbuf.shape[1] // mine

    def piece(t, g):
        begin = t * strip if g == 0 else 0
        end = mine if g < groups - 1 else (t + 1) * strip
        return begin, g * mine + begin - t * strip, end - begin

    def cut(t, g):
        _, begin, size = piece(t, g)
        return pl.ds(begin, size)

    def up(t, g):
        n, at = t * groups + g, (t, slice(None), cut(t, g))
        return remote(
            parts.at[at], from_low.at[at], up_send.at[n], up_recv.at[n],
            {"obs": lax.rem(z + 1, z_count) * 4 + q, "sp": s},
        )

    def down(t, g):
        n, at = t * groups + g, (t, slice(None), cut(t, g))
        return remote(
            parts.at[at], from_high.at[at], down_send.at[n], down_recv.at[n],
            {"obs": lax.rem(z + last, z_count) * 4 + q, "sp": s},
        )

    def gram_group(g):
        cols = slice(g * mine, (g + 1) * mine)
        made = jnp.dot(ktr[...], kbuf[:, cols], preferred_element_type=jnp.float32).astype(jnp.bfloat16)
        for t in range(z_count):
            begin, at, size = piece(t, g)
            parts[t, :, at : at + size] = made[t * strip : (t + 1) * strip, begin : begin + size]

    def pass_on(place, n):
        if place > 0 and 0 <= n - place < groups:
            for t in range(last, place, -1):
                g = n - place
                up(t, g).wait_recv()
                parts[t, :, cut(t, g)] = parts[t, :, cut(t, g)] + from_low[t, :, cut(t, g)]
                up(t, g).start()
        if place < last and 0 <= n - (last - place) < groups:
            for t in range(place):
                g = n - (last - place)
                down(t, g).wait_recv()
                parts[t, :, cut(t, g)] = parts[t, :, cut(t, g)] + from_high[t, :, cut(t, g)]
                down(t, g).start()

    mine_at = ((z * 2 + x) * 2 + c) * 2 + s
    across_at, beside_at = ((z * 2 + 1 - x) * 2 + c) * 2 + s, ((z * 2 + x) * 2 + c) * 2 + 1 - s
    across, beside = device(z, 1 - x, c, s), device(z, x, c, 1 - s)
    half = strip // 2

    def side(place, g, k):
        rows = (slice(None), slice(None), pl.ds(0, half), pl.ds(half, half))[k]
        at = (mine_at, mine_at, across_at, beside_at)[k]
        src = done.at[:, cut(place, g)] if k < 2 else gathered.at[at, rows, cut(place, g)]
        return remote(
            src, gathered.at[at, rows, cut(place, g)], side_send.at[g * 4 + k], side_recv.at[g * 4 + k],
            (across, beside, beside, across)[k],
        )

    def keep(place, g):
        return pltpu.make_async_copy(
            done.at[:, cut(place, g)], gathered.at[mine_at, :, cut(place, g)], keep_sem.at[g]
        )

    def near(place, g, rising):
        to = lax.rem(z + (1 if rising else last), z_count)
        n = g * 2 + int(rising)
        return remote(
            done.at[:, cut(place, g)], gathered.at[mine_at, :, cut(place, g)],
            near_send.at[n], near_recv.at[n], device(to, x, c, s),
        )

    def close(place, g):
        total = parts[place, :, cut(place, g)].astype(jnp.float32)
        if place > 0:
            up(place, g).wait_recv()
            total = total + from_low[place, :, cut(place, g)].astype(jnp.float32)
        if place < last:
            down(place, g).wait_recv()
            total = total + from_high[place, :, cut(place, g)].astype(jnp.float32)
        if g == 0:
            row = lax.broadcasted_iota(jnp.int32, total.shape, 0)
            col = lax.broadcasted_iota(jnp.int32, total.shape, 1)
            total = jnp.where(row == col, 0.0, total)
        done[:, cut(place, g)] = total.astype(jnp.bfloat16)
        side(place, g, 0).start()
        side(place, g, 1).start()
        if 0 < place < last:
            near(place, g, True).start()
            near(place, g, False).start()
        keep(place, g).start()

    def progress(place, n):
        pass_on(place, n)
        g = n - max(place, last - place)
        if 0 <= g < groups:
            close(place, g)
        if 0 <= g - 1 < groups:
            for k in range(2):
                side(place, g - 1, k).wait_recv()
                side(place, g - 1, k + 2).start()
        if 0 <= g - 2 < groups:
            for k in range(2):
                side(place, g - 2, k + 2).wait_recv()

    z_copies, g_copies = [], []
    for n in range(groups + last + 2):
        if n < groups:

            @pl.loop(n * mine // tile, (n + 1) * mine // tile)
            def _(t):
                kernel_tile(t, n == 0)

            gram_group(n)

            @pl.when(z == 0)
            def _():
                for t in range(last, 0, -1):
                    up(t, n).start()

            @pl.when(z == last)
            def _():
                for t in range(last):
                    down(t, n).start()

        if n == 0:
            row_sums()
            for k in range(1, z_count):
                z_copies.append(remote(zsums.at[z], zsums.at[z], zs_send.at[k], zs_recv.at[k], z_others[k - 1]))
                z_copies[-1].start()
        if n == 1:
            for copy in z_copies:
                copy.wait_recv()
            total = zsums[0]
            for m in range(1, z_count):
                total = total + zsums[m]
            gsums[p] = total
            for m in range(1, group):
                g_copies.append(
                    remote(gsums.at[p], gsums.at[p], gs_send.at[m], gs_recv.at[m], group_others[m - 1])
                )
                g_copies[-1].start()
        for place in range(z_count):
            pl.when(z == place)(functools.partial(progress, place, n))

    def finish(place):
        for g in range(groups):
            for k in range(4):
                side(place, g, k).wait_send()
            keep(place, g).wait()
            if 0 < place < last:
                near(place, g, True).wait_send()
                near(place, g, False).wait_send()
            if 0 < place + 1 < last:
                near(place + 1, g, False).wait_recv()
            if 0 < place - 1 < last:
                near(place - 1, g, True).wait_recv()
            for t in range(z_count):
                if t > place:
                    up(t, g).wait_send()
                if t < place:
                    down(t, g).wait_send()

    for place in range(z_count):
        pl.when(z == place)(functools.partial(finish, place))

    for copy in g_copies:
        copy.wait()
    for copy in z_copies:
        copy.wait_send()
    sums_ref[...] = gsums[...]


def slab_gram(slab, sparse, z_count, sp_count, strip, span, tile, rows, collective_id):
    depth = slab.shape[2]
    window = sparse.shape[0]
    group = 4 * sp_count
    mine = strip * z_count
    lines = 2 * mine // LANES
    vmem = pl.BlockSpec(memory_space=pltpu.VMEM)
    part = (z_count, strip, span)
    groups = window // mine
    sems = [pltpu.SemaphoreType.DMA((z_count * groups,))] * 4 + [pltpu.SemaphoreType.DMA((4 * groups,))] * 2
    sems += [pltpu.SemaphoreType.DMA((z_count,))] * 2 + [pltpu.SemaphoreType.DMA((group,))] * 2
    sems += [pltpu.SemaphoreType.DMA((groups,))] + [pltpu.SemaphoreType.DMA((2 * groups,))] * 2
    return pl.pallas_call(
        functools.partial(slab_body, z_count, sp_count, strip, tile, math.sqrt(depth)),
        out_shape=[
            jax.ShapeDtypeStruct((group * z_count, strip, span), jnp.bfloat16),
            jax.ShapeDtypeStruct((group, lines, LANES), jnp.float32),
        ],
        in_specs=[vmem, vmem],
        out_specs=[pl.BlockSpec(memory_space=pl.ANY), vmem],
        scratch_shapes=[
            pltpu.VMEM((4 * rows, window), jnp.bfloat16),
            pltpu.VMEM((mine, 4 * rows), jnp.bfloat16),
            pltpu.VMEM(part, jnp.bfloat16),
            pltpu.VMEM(part, jnp.bfloat16),
            pltpu.VMEM(part, jnp.bfloat16),
            pltpu.VMEM(part[1:], jnp.bfloat16),
            pltpu.VMEM((z_count, lines, LANES), jnp.float32),
            pltpu.VMEM((group, lines, LANES), jnp.float32),
        ] + sems,
        compiler_params=pltpu.CompilerParams(
            collective_id=collective_id, has_side_effects=True, vmem_limit_bytes=VMEM_BYTES
        ),
    )(slab, sparse)


def on_device(descriptors, candidates, sparse_index, targets, regularizer):
    obs_count = lax.axis_size("obs")
    sp_count = lax.axis_size("sp")
    obs_pos = lax.axis_index("obs")
    sp_pos = lax.axis_index("sp")
    width = sparse_index.shape[0]
    if sp_count == 2 and obs_count == 16 and width % (obs_count * sp_count * LANES) == 0:
        return by_strips(descriptors, candidates, sparse_index, targets, regularizer)
    tile = width // obs_count
    share = -(-((obs_count // 2 + 1) * tile) // (sp_count * LANES)) * LANES
    normalizer = 24.0 * descriptors.shape[0] * obs_count

    normed = unit_rows(descriptors)
    piece = candidates.shape[0] // sp_count
    own = lax.dynamic_slice_in_dim(candidates, sp_pos * piece, piece)
    table = spread(unit_rows(own), obs_count, sp_count, 2)
    sparse = table.at[sparse_index].get(mode="promise_in_bounds")

    gram, sums = gram_call(
        sp_pos[None].astype(jnp.int32), normed, sparse, targets, obs_count, tile, share, sp_count
    )
    sums = add_over_obs(sums, obs_count, 0)
    part = lax.psum_scatter(gram, "obs", scatter_dimension=0, tiled=True)

    projected = sums[0] / math.sqrt(normalizer)
    root = lax.rsqrt(sums[1] / normalizer + regularizer)
    col_start = obs_pos * tile
    rrow = lax.dynamic_slice_in_dim(root, col_start, tile)
    window_start = col_start + sp_pos * share
    rwin = lax.dynamic_slice_in_dim(jnp.concatenate([root, root]), window_start, share)
    offset = sp_pos * share + lax.iota(jnp.int32, share)
    on_diag = lax.iota(jnp.int32, tile)[:, None] == offset[None, :]
    scaled = jnp.where(
        on_diag, 0.0, part.astype(jnp.float32) * (rrow[:, None] / normalizer) * rwin[None, :]
    ).astype(jnp.bfloat16)
    packed = spread(scaled, obs_count, sp_count, 3)

    y = lax.dynamic_slice_in_dim(projected, col_start, tile)
    pos = jnp.stack([sp_pos, obs_pos]).astype(jnp.int32)
    inverse_tile, part_w = newton_call(
        pos, packed, root, rrow, y, obs_count, tile, share, sp_count
    )
    return inverse_tile, add_over_obs(part_w[0], obs_count, 1)


def solution(mesh):
    in_specs = (P("obs", None), P("obs", None), P(), P("obs"), P())
    out_specs = (P("sp", "obs"), P("sp"))
    return jax.shard_map(
        on_device, mesh=mesh, in_specs=in_specs, out_specs=out_specs, check_vma=False
    )
```

```python
import functools
import math

import jax
import jax.numpy as jnp
from jax import lax
from jax.experimental import pallas as pl
from jax.experimental.pallas import tpu as pltpu
from jax.sharding import PartitionSpec as P

epsilon = 1e-06
LANES = 128
VMEM_BYTES = 58 * 2**20


def unit_rows(row_block):
    values = row_block.astype(jnp.float32)
    return (values * lax.rsqrt(jnp.sum(values * values, axis=1, keepdims=True) + epsilon)).astype(
        jnp.bfloat16
    )


def gram_body(blocks, tile, share, ext, root, s_ref, norm_ref, sp_ref, tgt_ref, gram_ref, ws_ref, kext):
    step = pl.program_id(0)
    width = blocks * tile

    @pl.when(step < blocks)
    def _():
        inner = lax.dot_general(
            norm_ref[...], sp_ref[...], (((1,), (1,)), ((), ())), preferred_element_type=jnp.float32
        )
        scaled = inner * root
        squared = scaled * scaled
        kb = ((squared - 6.0) * squared + 3.0).astype(jnp.bfloat16)
        kext[:, pl.ds(pl.multiple_of(step * tile, tile), tile)] = kb

        @pl.when(step < ext)
        def _():
            kext[:, pl.ds(pl.multiple_of(width + step * tile, tile), tile)] = kb

        kf = kb.astype(jnp.float32)
        weighted = jnp.dot(tgt_ref[...], kb, preferred_element_type=jnp.float32)
        ws_ref[0:1, :] = weighted[0:1, :]
        ws_ref[1:2, :] = jnp.sum(kf * kf, axis=0, keepdims=True)

    @pl.when(step >= blocks)
    def _():
        j = step - blocks
        cols = pl.ds(pl.multiple_of(j * tile, tile), tile)
        window = pl.ds(pl.multiple_of(j * tile + s_ref[0] * share, LANES), share)
        gram_ref[...] = lax.dot_general(
            kext[:, cols], kext[:, window], (((0,), (0,)), ((), ())), preferred_element_type=jnp.float32
        ).astype(jnp.bfloat16)


def gram_call(s_pos, normed, sparse, targets, blocks, tile, share, sp_count):
    rows, depth = normed.shape
    width = blocks * tile
    ext = -(-((blocks - 1) * tile + sp_count * share - width) // tile)
    last = blocks - 1
    return pl.pallas_call(
        functools.partial(gram_body, blocks, tile, share, ext, math.sqrt(depth)),
        grid_spec=pltpu.PrefetchScalarGridSpec(
            num_scalar_prefetch=1,
            grid=(2 * blocks,),
            in_specs=[
                pl.BlockSpec((rows, depth), lambda g, s: (0, 0)),
                pl.BlockSpec((tile, depth), lambda g, s: (jnp.minimum(g, last), 0)),
                pl.BlockSpec((16, rows), lambda g, s: (0, 0)),
            ],
            out_specs=[
                pl.BlockSpec((tile, share), lambda g, s: (jnp.maximum(g - blocks, 0), 0)),
                pl.BlockSpec((2, tile), lambda g, s: (0, jnp.minimum(g, last))),
            ],
            scratch_shapes=[pltpu.VMEM((rows, width + ext * tile), jnp.bfloat16)],
        ),
        out_shape=[
            jax.ShapeDtypeStruct((width, share), jnp.bfloat16),
            jax.ShapeDtypeStruct((2, width), jnp.float32),
        ],
        compiler_params=pltpu.CompilerParams(vmem_limit_bytes=VMEM_BYTES),
    )(s_pos, normed, sparse, jnp.broadcast_to(targets[None, :], (16, rows)))


def newton_body(
    blocks, tile, share, sp_count, chunk, block_rows,
    pos_ref, packed_ref, rcol_ref, rrow_ref, y_ref, inv_ref, w_ref, dense, prod,
):
    step = pl.program_id(0)
    width = blocks * tile
    half = blocks // 2
    p_steps = width // chunk
    my_cols = pl.ds(pl.multiple_of(pos_ref[1] * tile, tile), tile)

    @pl.when(step < blocks)
    def _():
        rows = pl.ds(pl.multiple_of(step * tile, tile), tile)
        for s in range(sp_count):
            for q in range(share // LANES):
                offset = s * share + q * LANES
                if offset >= (half + 1) * tile:
                    continue
                col = lax.rem(step * tile + offset, width)
                cols = pl.ds(pl.multiple_of(col, LANES), LANES)
                block = packed_ref[s * tile : (s + 1) * tile, q * LANES : (q + 1) * LANES]
                dense[rows, cols] = block
                if tile <= offset < half * tile:
                    dense[cols, rows] = block.T

    @pl.when((step >= blocks) & (step < blocks + p_steps))
    def _():
        rows = pl.ds(pl.multiple_of((step - blocks) * chunk, chunk), chunk)
        prod[rows, :] = jnp.dot(
            dense[rows, :], dense[:, my_cols], preferred_element_type=jnp.float32
        ).astype(jnp.bfloat16)

    @pl.when(step >= blocks + p_steps)
    def _():
        local = pl.multiple_of((step - blocks - p_steps) * chunk, chunk)
        start = pl.multiple_of(pos_ref[0] * block_rows + local, chunk)
        rows = pl.ds(start, chunk)
        cubic = jnp.dot(dense[rows, :], prod[...], preferred_element_type=jnp.float32)
        on_diag = (start + lax.broadcasted_iota(jnp.int32, (chunk, tile), 0)) == (
            pos_ref[1] * tile + lax.broadcasted_iota(jnp.int32, (chunk, tile), 1)
        )
        series = (
            jnp.where(on_diag, 1.0, 0.0)
            - dense[rows, my_cols].astype(jnp.float32)
            + prod[rows, :].astype(jnp.float32)
            - cubic
        )
        out = series * rcol_ref[rows, :] * rrow_ref[...]
        inv_ref[pl.ds(local, chunk), :] = out
        w_ref[:, pl.ds(local, chunk)] = lax.dot_general(
            y_ref[...], out, (((1,), (1,)), ((), ())),
            precision=lax.Precision.HIGHEST, preferred_element_type=jnp.float32,
        )


def newton_call(pos, packed, root_recip, rrow, y, blocks, tile, share, sp_count):
    width = blocks * tile
    block_rows = width // sp_count
    chunk = min(512, block_rows)
    grid = blocks + width // chunk + block_rows // chunk
    last = blocks - 1
    return pl.pallas_call(
        functools.partial(newton_body, blocks, tile, share, sp_count, chunk, block_rows),
        grid_spec=pltpu.PrefetchScalarGridSpec(
            num_scalar_prefetch=1,
            grid=(grid,),
            in_specs=[
                pl.BlockSpec((sp_count * tile, share), lambda g, p: (jnp.minimum(g, last), 0)),
                pl.BlockSpec((width, 1), lambda g, p: (0, 0)),
                pl.BlockSpec((1, tile), lambda g, p: (0, 0)),
                pl.BlockSpec((8, tile), lambda g, p: (0, 0)),
            ],
            out_specs=[
                pl.BlockSpec((block_rows, tile), lambda g, p: (0, 0)),
                pl.BlockSpec((8, block_rows), lambda g, p: (0, 0)),
            ],
            scratch_shapes=[
                pltpu.VMEM((width, width), jnp.bfloat16),
                pltpu.VMEM((width, tile), jnp.bfloat16),
            ],
        ),
        out_shape=[
            jax.ShapeDtypeStruct((block_rows, tile), jnp.float32),
            jax.ShapeDtypeStruct((8, block_rows), jnp.float32),
        ],
        compiler_params=pltpu.CompilerParams(vmem_limit_bytes=VMEM_BYTES),
    )(pos, packed, root_recip[:, None], rrow[None, :], jnp.broadcast_to(y[None, :], (8, tile)))


def add_body(count, in_ref, out_ref, slots, send_sem, recv_sem):
    me = lax.axis_index("obs")
    barrier = pltpu.get_barrier_semaphore()
    for k in range(1, count):
        pl.semaphore_signal(
            barrier, inc=1, device_id={"obs": lax.rem(me + k, count)}, device_id_type=pl.DeviceIdType.MESH
        )
    pl.semaphore_wait(barrier, count - 1)
    copies = []
    for k in range(1, count):
        copy = pltpu.make_async_remote_copy(
            src_ref=in_ref,
            dst_ref=slots.at[me],
            send_sem=send_sem.at[k],
            recv_sem=recv_sem.at[k],
            device_id={"obs": lax.rem(me + k, count)},
            device_id_type=pl.DeviceIdType.MESH,
        )
        copy.start()
        copies.append(copy)
    slots[me] = in_ref[...]
    for copy in copies:
        copy.wait()
    total = slots[0]
    for k in range(1, count):
        total = total + slots[k]
    out_ref[...] = total


def add_over_obs(values, count, collective_id):
    shape = values.shape
    flat = values.reshape(values.size // LANES, LANES)
    total = pl.pallas_call(
        functools.partial(add_body, count),
        out_shape=jax.ShapeDtypeStruct(flat.shape, flat.dtype),
        in_specs=[pl.BlockSpec(memory_space=pltpu.VMEM)],
        out_specs=pl.BlockSpec(memory_space=pltpu.VMEM),
        scratch_shapes=[
            pltpu.VMEM((count,) + flat.shape, flat.dtype),
            pltpu.SemaphoreType.DMA((count,)),
            pltpu.SemaphoreType.DMA((count,)),
        ],
        cost_estimate=pl.CostEstimate(
            flops=count * flat.size, bytes_accessed=400 * flat.size, transcendentals=0
        ),
        compiler_params=pltpu.CompilerParams(collective_id=collective_id, has_side_effects=True),
    )(flat)
    return total.reshape(shape)


def spread_keys(z_count, sp_count):
    keys = [("z", k) for k in range(1, z_count)]
    for k in range(z_count):
        keys += [("x", k), ("core", k), ("core_x", k)]
        for d in range(1, sp_count):
            keys += [(name, k, d) for name in ("sp", "sp_a", "x_b", "core_sp", "core_a", "core_b")]
    return {key: place for place, key in enumerate(keys)}


def spread_body(z_count, sp_count, in_ref, out_ref, send_sem, recv_sem, own_sem):
    places = spread_keys(z_count, sp_count)
    obs = lax.axis_index("obs")
    s = lax.axis_index("sp")
    z, x, c = lax.div(obs, 4), lax.rem(lax.div(obs, 2), 2), lax.rem(obs, 2)
    half = in_ref.shape[0] // 2
    upper, lower = pl.ds(0, half), pl.ds(half, half)
    zs = [lax.bitwise_xor(z, k) for k in range(z_count)]
    to_sp = [lax.rem(s + d, sp_count) for d in range(sp_count)]
    from_sp = [lax.rem(s - d + sp_count, sp_count) for d in range(sp_count)]

    def device(z_to, x_to, c_to, s_to):
        return {"obs": z_to * 4 + x_to * 2 + c_to, "sp": s_to}

    def slot(z_of, x_of, s_of):
        return ((z_of * 2 + x_of) * 2 + c) * sp_count + s_of

    own_slot = slot(z, x, s)
    across, sibling = device(z, 1 - x, c, s), device(z, x, 1 - c, s)
    others = [device(zs[k], x, c, s) for k in range(1, z_count)]
    others += [device(z, x, c, to_sp[d]) for d in range(1, sp_count)]
    others += [across, sibling]
    barrier = pltpu.get_barrier_semaphore()
    for other in others:
        pl.semaphore_signal(barrier, inc=1, device_id=other, device_id_type=pl.DeviceIdType.MESH)
    pl.semaphore_wait(barrier, len(others))

    sent = {}

    def send(key, place, target, rows=None, own=False):
        src = in_ref if own else out_ref.at[place]
        dst = out_ref.at[place]
        if rows is not None:
            src, dst = src.at[rows], dst.at[rows]
        copy = pltpu.make_async_remote_copy(
            src_ref=src,
            dst_ref=dst,
            send_sem=send_sem.at[places[key]],
            recv_sem=recv_sem.at[places[key]],
            device_id=target,
            device_id_type=pl.DeviceIdType.MESH,
        )
        copy.start()
        sent[key] = copy

    keep = pltpu.make_async_copy(in_ref, out_ref.at[own_slot], own_sem)
    keep.start()
    for k in range(1, z_count):
        send(("z", k), own_slot, others[k - 1], own=True)

    def fan_out(k):
        place = slot(zs[k], x, s)
        send(("x", k), place, across, own=k == 0)
        for d in range(1, sp_count):
            send(("sp", k, d), place, device(z, x, c, to_sp[d]), own=k == 0)
        send(("core", k), place, sibling, own=k == 0)

    def relay(k):
        sent[("x", k)].wait_recv()
        place = slot(zs[k], 1 - x, s)
        for d in range(1, sp_count):
            send(("sp_a", k, d), place, device(z, x, c, to_sp[d]), upper)
        send(("core_x", k), place, sibling)
        for d in range(1, sp_count):
            sent[("sp", k, d)].wait_recv()
            place = slot(zs[k], x, from_sp[d])
            send(("x_b", k, d), place, across, lower)
            send(("core_sp", k, d), place, sibling)

    def finish(k):
        for d in range(1, sp_count):
            place = slot(zs[k], 1 - x, from_sp[d])
            sent[("sp_a", k, d)].wait_recv()
            send(("core_a", k, d), place, sibling, upper)
            sent[("x_b", k, d)].wait_recv()
            send(("core_b", k, d), place, sibling, lower)

    fan_out(0)
    for k in range(1, z_count):
        sent[("z", k)].wait_recv()
        fan_out(k)
        relay(k - 1)
        if k > 1:
            finish(k - 2)
    relay(z_count - 1)
    if z_count > 1:
        finish(z_count - 2)
    finish(z_count - 1)
    keep.wait()
    for key, copy in sent.items():
        copy.wait_send()
        if key[0].startswith("core"):
            copy.wait_recv()


def spread(shard, obs_count, sp_count, collective_id):
    rows, cols = shard.shape
    z_count = obs_count // 4
    total = obs_count * sp_count
    sems = len(spread_keys(z_count, sp_count))
    gathered = pl.pallas_call(
        functools.partial(spread_body, z_count, sp_count),
        out_shape=jax.ShapeDtypeStruct((total, rows, cols), shard.dtype),
        in_specs=[pl.BlockSpec(memory_space=pl.ANY)],
        out_specs=pl.BlockSpec(memory_space=pl.ANY),
        scratch_shapes=[
            pltpu.SemaphoreType.DMA((sems,)),
            pltpu.SemaphoreType.DMA((sems,)),
            pltpu.SemaphoreType.DMA,
        ],
        compiler_params=pltpu.CompilerParams(collective_id=collective_id, has_side_effects=True),
    )(shard)
    return gathered.reshape(total * rows, cols)


def position():
    obs = lax.axis_index("obs")
    return lax.div(obs, 4), lax.rem(lax.div(obs, 2), 2), lax.rem(obs, 2), lax.axis_index("sp")


def device(z, x, c, s):
    return {"obs": z * 4 + x * 2 + c, "sp": s}


def remote(src, dst, send_sem, recv_sem, target):
    return pltpu.make_async_remote_copy(
        src_ref=src, dst_ref=dst, send_sem=send_sem, recv_sem=recv_sem,
        device_id=target, device_id_type=pl.DeviceIdType.MESH,
    )


def route_sems(z_count, chunks):
    return [
        pltpu.SemaphoreType.DMA((4 * chunks * (z_count + 1),)),
        pltpu.SemaphoreType.DMA((4 * chunks * z_count,)),
        pltpu.SemaphoreType.DMA((4 * (chunks + 1) * z_count,)),
        pltpu.SemaphoreType.DMA((4 * (chunks + 1) * z_count,)),
    ]


def route_greet(z_count, meanwhile):
    z, x, c, s = position()
    barrier = pltpu.get_barrier_semaphore()
    others = [device(z, 1 - x, c, s), device(z, x, 1 - c, s), device(z, x, c, 1 - s)]
    others += [device(lax.rem(z + k, z_count), x, c, s) for k in range(1, z_count)]
    for other in others:
        pl.semaphore_signal(barrier, inc=1, device_id=other, device_id_type=pl.DeviceIdType.MESH)
    meanwhile()
    pl.semaphore_wait(barrier, len(others))


EXTRA = 32
OWN, ACROSS, BESIDE, DIAGONAL = range(4)


def route(z_count, home, out_ref, sems, arrive, chunks, diagonal, lag, begin, late=None):
    z_send, z_recv, send_sem, recv_sem = sems
    z, x, c, s = position()
    last = z_count - 1
    rows = out_ref.shape[1]
    high = rows // chunks
    known = home is None
    across, beside, sibling = device(z, 1 - x, c, s), device(z, x, c, 1 - s), device(z, x, 1 - c, s)
    along = {OWN: chunks, ACROSS: 0, BESIDE: 0, DIAGONAL: diagonal}

    nearer = jnp.minimum(z, last - z)
    origins = [z]
    for a in range(last):
        both = jnp.where((z <= last // 2) == (a % 2 == 0), z + (a // 2 + 1), z - (a // 2 + 1))
        single = jnp.where(z <= last - z, z + (a - nearer + 1), z - (a - nearer + 1))
        origins.append(jnp.where(a < 2 * nearer, both, single))

    def slot(col, a, c_of=c):
        x_of = 1 - x if col in (ACROSS, DIAGONAL) else x
        s_of = 1 - s if col in (BESIDE, DIAGONAL) else s
        return ((origins[a] * 2 + x_of) * 2 + c_of) * 2 + s_of

    def shard(col, a):
        return out_ref.at[slot(col, a)] if a or col != OWN or known else home

    sent = {}

    def send(key, col, a, target, begin=0, size=rows):
        cut = pl.ds(begin, size)
        n = len(sent)
        sent[key] = remote(
            shard(col, a).at[cut], out_ref.at[slot(col, a)].at[cut], send_sem.at[n], recv_sem.at[n], target
        )
        sent[key].start()

    hops = []

    def hop(col, a, j, n, target_z, when):
        cut = pl.ds(j * high, high)
        copy = remote(
            shard(col, a).at[cut], out_ref.at[slot(col, a)].at[cut],
            z_send.at[(col * chunks + j) * (z_count + 1) + n], z_recv.at[(col * chunks + j) * z_count + origins[a]],
            device(jnp.clip(target_z, 0, last), x, c, s),
        )
        pl.when(when)(copy.start)
        hops.append((when, copy))

    def set_off(col, j):
        if j < along[col]:
            hop(col, 0, j, 0, z + 1, z < last)
            hop(col, 0, j, 1, z - 1, z > 0)

    def pass_on(col, a, j):
        if j < along[col]:
            held = out_ref.at[slot(col, a)].at[pl.ds(j * high, high)]
            arrival = remote(
                held, held, z_send.at[0], z_recv.at[(col * chunks + j) * z_count + origins[a]], across
            ).wait_recv
            if not known or col != OWN or a > 1:
                arrival()
            target_z = jnp.where(origins[a] < z, z + 1, z - 1)
            hop(col, a, j, a + 1, target_z, (target_z >= 0) & (target_z <= last))

    finished = []

    def complete(now, a, *cols):
        for col in cols:
            send(("core", col, a), col, a, sibling)
            arrive(shard(col, a), slot(col, a))
            finished.append((now, a, col))

    def from_sibling(before):
        while finished and finished[0][0] < before:
            _, a, col = finished.pop(0)
            sent[("core", col, a)].wait_recv()
            place = slot(col, a, 1 - c)
            arrive(out_ref.at[place], place)

    def fan_out(a, j):
        send(("x", a, j), OWN, a, across, j * high, high)
        send(("y", a, j), OWN, a, beside, j * high, high)

    def relay(a, j):
        direct = a == 0 or j >= diagonal
        sent[("x", a, j)].wait_recv()
        if direct:
            send(("ya", a, j), ACROSS, a, beside, j * high, high // 2)
        sent[("y", a, j)].wait_recv()
        if direct:
            send(("xb", a, j), BESIDE, a, across, j * high + high // 2, high // 2)

    def finish(a, j):
        if ("ya", a, j) in sent:
            sent[("ya", a, j)].wait_recv()
            sent[("xb", a, j)].wait_recv()

    first = 1 if known else 0
    for j in range(chunks):
        if known:
            hop(OWN, 0, j, 0, jnp.where(z == 0, 1, last - 1), (z == 0) | (z == last))
        else:
            set_off(OWN, j)
            fan_out(0, j)
    for j in range(chunks if known else 0):
        set_off(DIAGONAL, j)
    begin()
    complete(-1, 0, OWN)
    if known:
        complete(-1, 0, ACROSS, BESIDE, DIAGONAL)
    items = [(a, j) for j in range(chunks) for a in range(first, 2)]
    items += [(a, j) for a in range(2, z_count) for j in range(chunks)]
    ends = [items.index((a, chunks - 1)) for a in range(1, z_count)]
    ready = set()
    for now in range(len(items) + max(sum(lag), 3)):
        if now < len(items):
            a, j = items[now]
            if a:
                pass_on(OWN, a, j)
                fan_out(a, j)
                if j == chunks - 1:
                    complete(now, a, OWN)
        if 0 <= now - lag[0] < len(items):
            a, j = items[now - lag[0]]
            relay(a, j)
            if j == chunks - 1:
                complete(now, a, ACROSS, BESIDE)
        if now - 3 in ends:
            a = ends.index(now - 3) + 1
            for j in range(chunks):
                pass_on(DIAGONAL, a, j)
            ready.add(a)
        if 0 <= now - sum(lag) < len(items):
            a, j = items[now - sum(lag)]
            finish(a, j)
            if a == 0:
                set_off(DIAGONAL, j)
            if j == chunks - 1:
                assert a in ready or not a
                complete(now, a, DIAGONAL)
        if now == len(items) - 2 and late is not None:
            late()
        from_sibling(now - 2)
    from_sibling(now + 1)
    for copy in sent.values():
        copy.wait_send()
    for when, copy in hops:
        pl.when(when)(copy.wait_send)


def share_body(
    z_count, rows_ref, targets_ref, candidates_ref, out_ref, slab_ref, own_ref, own_slab,
    z_send, z_recv, send_sem, recv_sem, slab_send, slab_recv, keep_sem,
):
    z, x, c, s = position()
    q, q_across = x * 2 + c, (1 - x) * 2 + c
    half = own_slab.shape[0] // 2
    near, far = pl.ds(pl.multiple_of(s * half, 16), half), pl.ds(pl.multiple_of((1 - s) * half, 16), half)

    def make_unit():
        piece, rows = own_ref.shape[0], rows_ref.shape[0]
        own_ref[...] = unit_rows(candidates_ref[pl.ds(pl.multiple_of(s * piece, 16), piece), :])
        step = math.gcd(rows, 256)
        for begin in range(0, rows, step):
            own_slab[begin : begin + step, :] = unit_rows(rows_ref[begin : begin + step, :])
        extra = own_slab.shape[0] - rows
        place = lax.broadcasted_iota(jnp.int32, (extra, own_slab.shape[1]), 0)
        lines = jnp.zeros(place.shape, jnp.float32)
        for k in range(rows // own_slab.shape[1]):
            line = targets_ref[:, k * own_slab.shape[1] : (k + 1) * own_slab.shape[1]].astype(jnp.float32)
            lines = jnp.where(place == k, line, lines)
        own_slab[rows:, :] = lines.astype(jnp.bfloat16)

    route_greet(z_count, make_unit)
    keep = pltpu.make_async_copy(own_ref, out_ref.at[((z * 2 + x) * 2 + c) * 2 + s], keep_sem.at[0])
    keep_slab = pltpu.make_async_copy(own_slab, slab_ref.at[q], keep_sem.at[1])
    keep.start()
    keep_slab.start()
    shared = []

    def share(src, place, piece, target):
        n = len(shared)
        dst = slab_ref.at[place]
        if piece is not None:
            src, dst = src.at[piece], dst.at[piece]
        shared.append(remote(src, dst, slab_send.at[n], slab_recv.at[n], target))
        shared[-1].start()

    def begin():
        share(own_slab, q, near, device(z, 1 - x, c, s))
        share(own_slab, q, None, device(z, x, 1 - c, s))

    def late():
        shared[0].wait_recv()
        share(slab_ref.at[q_across], q_across, near, device(z, x, c, 1 - s))
        share(slab_ref.at[q_across], q_across, near, device(z, x, 1 - c, s))

    sems = z_send, z_recv, send_sem, recv_sem
    route(z_count, own_ref, out_ref, sems, lambda src, place: None, 1, 0, (2, 2), begin, late)
    shared[2].wait_recv()
    share(slab_ref.at[q_across], q_across, far, device(z, x, 1 - c, s))
    for n in (1, 3, 4):
        shared[n].wait_recv()
    for copy in shared:
        copy.wait_send()
    keep.wait()
    keep_slab.wait()


def share(descriptors, targets, candidates, z_count, collective_id):
    rows, depth = descriptors.shape
    own = (candidates.shape[0] // 2, depth)
    own_slab = (rows + EXTRA, depth)
    anywhere = pl.BlockSpec(memory_space=pl.ANY)
    vmem = pl.BlockSpec(memory_space=pltpu.VMEM)
    return pl.pallas_call(
        functools.partial(share_body, z_count),
        out_shape=[
            jax.ShapeDtypeStruct((8 * z_count,) + own, jnp.bfloat16),
            jax.ShapeDtypeStruct((4,) + own_slab, jnp.bfloat16),
        ],
        in_specs=[vmem, vmem, vmem],
        out_specs=[anywhere, anywhere],
        scratch_shapes=[pltpu.VMEM(own, jnp.bfloat16), pltpu.VMEM(own_slab, jnp.bfloat16)]
        + route_sems(z_count, 1)
        + [pltpu.SemaphoreType.DMA((5,)), pltpu.SemaphoreType.DMA((5,)), pltpu.SemaphoreType.DMA((2,))],
        compiler_params=pltpu.CompilerParams(
            collective_id=collective_id, has_side_effects=True, vmem_limit_bytes=VMEM_BYTES
        ),
    )(descriptors, targets.reshape(1, rows), candidates)


def series_body(
    z_count, strip, tile, chunk, normalizer,
    begun_ref, sums_ref, reg_ref, inv_ref, w_ref, gathered,
    dense, first, second, stage, recip, spread_recip, out_buf, w_own, w_slots,
    z_send, z_recv, send_sem, recv_sem, stage_sem, out_sem, w_send, w_recv,
):
    z, x, c, s = position()
    obs = lax.axis_index("obs")
    obs_count = 4 * z_count
    strips = 8 * z_count
    width = strips * strip
    half = strips // 2
    span = begun_ref.shape[2]
    block_rows = width // 2
    lines = tile // LANES
    fold = 1.0 / normalizer

    barrier = pltpu.get_barrier_semaphore()
    peers = [
        {"obs": lax.rem(obs + k, obs_count), "sp": s} for k in range(1, obs_count)
    ]
    for peer in peers + [device(z, x, c, 1 - s)]:
        pl.semaphore_signal(barrier, inc=1, device_id=peer, device_id_type=pl.DeviceIdType.MESH)
    pl.semaphore_wait(barrier, obs_count)

    slots = stage.shape[0]
    waiting = []

    def lay_out(n):
        copy, place = waiting[n]
        copy.wait()
        place = lax.rem(place, 8) * z_count + lax.div(place, 8)
        rows = pl.ds(pl.multiple_of(place * strip, strip), strip)

        def put(k, turn):
            cols = pl.ds(pl.multiple_of(lax.rem(place + k, strips) * strip, strip), strip)
            block = stage[n % slots, :, pl.ds(pl.multiple_of(k * strip, strip), strip)]
            dense[rows, cols] = block
            if turn:
                dense[cols, rows] = block.T

        for k in range(half + 1):
            put(k, 0 < k < half)

    def arrive(src, place):
        n = len(waiting)
        if n >= slots:
            lay_out(n - slots)
        copy = pltpu.make_async_copy(src, stage.at[n % slots], stage_sem.at[n % slots])
        copy.start()
        waiting.append((copy, place))

    def begin():
        per = sums_ref.shape[1] // 2
        for p in range(sums_ref.shape[0]):
            lane = slice(p * per, (p + 1) * per)
            recip[lane, :] = 1.0 / (sums_ref[p, per:, :] * fold + reg_ref[lane, :])

        @pl.loop(0, width // LANES)
        def _(m):
            row = jnp.broadcast_to(recip[pl.ds(m, 1), :], (LANES, LANES))
            spread_recip[pl.ds(pl.multiple_of(m * LANES, LANES), LANES), :] = row.T

    sems = z_send, z_recv, send_sem, recv_sem
    route(z_count, None, gathered, sems, arrive, 4, 2, (2, 3), begin)
    for n in range(len(waiting) - slots, len(waiting)):
        lay_out(n)

    my_cols = pl.ds(pl.multiple_of(obs * tile, tile), tile)

    def by_row(values, rows):
        scale = spread_recip[rows, :]
        return values * jnp.concatenate([scale] * lines, axis=1)

    @pl.loop(0, width // chunk)
    def _(m):
        rows = pl.ds(pl.multiple_of(m * chunk, chunk), chunk)
        first[rows, :] = by_row(dense[rows, my_cols].astype(jnp.float32) * fold, rows).astype(jnp.bfloat16)

    @pl.loop(0, width // chunk)
    def _(m):
        rows = pl.ds(pl.multiple_of(m * chunk, chunk), chunk)
        prod = jnp.dot(dense[rows, :], first[...], preferred_element_type=jnp.float32)
        second[rows, :] = by_row(prod * fold, rows).astype(jnp.bfloat16)

    def my_lines(ref, at):
        return jnp.concatenate([ref[pl.ds(at + h, 1), :] for h in range(lines)], axis=1)

    per = sums_ref.shape[1] // 2
    r_row = my_lines(recip, obs * lines)
    y = my_lines(sums_ref.at[lax.div(obs * lines, per)], lax.rem(obs * lines, per))
    y = y * (1.0 / math.sqrt(normalizer))

    def emit(m):
        return pltpu.make_async_copy(
            out_buf.at[m], inv_ref.at[pl.ds(pl.multiple_of(m * chunk, chunk), chunk)], out_sem.at[m]
        )

    @pl.loop(0, block_rows // chunk)
    def _(m):
        begin_at = s * block_rows + m * chunk
        rows = pl.ds(pl.multiple_of(begin_at, chunk), chunk)
        cubic = jnp.dot(dense[rows, :], second[...], preferred_element_type=jnp.float32)
        on_diag = (begin_at + lax.broadcasted_iota(jnp.int32, (chunk, tile), 0)) == (
            obs * tile + lax.broadcasted_iota(jnp.int32, (chunk, tile), 1)
        )
        series = second[rows, :].astype(jnp.float32) - by_row(
            (dense[rows, my_cols].astype(jnp.float32) + cubic) * fold, rows
        )
        out = (jnp.where(on_diag, 1.0, 0.0) + series) * r_row
        out_buf[m] = out
        emit(m).start()
        weighted = out * y
        weighted = sum(weighted[:, h * LANES : (h + 1) * LANES] for h in range(lines))
        for h in range(chunk // LANES):
            turned = weighted[h * LANES : (h + 1) * LANES, :].T
            w_own[pl.ds(m * (chunk // LANES) + h, 1), :] = jnp.sum(turned, axis=0, keepdims=True)

    copies = []
    for k in range(1, obs_count):
        copies.append(remote(w_own, w_slots.at[obs], w_send.at[k], w_recv.at[k], peers[k - 1]))
        copies[-1].start()
    w_slots[obs] = w_own[...]
    for copy in copies:
        copy.wait()
    total = w_slots[0]
    for k in range(1, obs_count):
        total = total + w_slots[k]
    w_ref[...] = total
    for m in range(block_rows // chunk):
        emit(m).wait()


def series_tile(begun, sums, regularizer, z_count, tile, normalizer, collective_id):
    strips, strip, span = begun.shape
    width = strips * strip
    block_rows = width // 2
    chunk = min(512, block_rows)
    obs_count = 4 * z_count
    w_shape = (block_rows // LANES, LANES)
    anywhere = pl.BlockSpec(memory_space=pl.ANY)
    vmem = pl.BlockSpec(memory_space=pltpu.VMEM)
    inverse_tile, weights, _ = pl.pallas_call(
        functools.partial(series_body, z_count, strip, tile, chunk, normalizer),
        out_shape=[
            jax.ShapeDtypeStruct((block_rows, tile), jnp.float32),
            jax.ShapeDtypeStruct(w_shape, jnp.float32),
            jax.ShapeDtypeStruct(begun.shape, begun.dtype),
        ],
        in_specs=[anywhere, vmem, vmem],
        out_specs=[anywhere, vmem, anywhere],
        scratch_shapes=[
            pltpu.VMEM((width, width), jnp.bfloat16),
            pltpu.VMEM((width, tile), jnp.bfloat16),
            pltpu.VMEM((width, tile), jnp.bfloat16),
            pltpu.VMEM((3, strip, span), jnp.bfloat16),
            pltpu.VMEM((width // LANES, LANES), jnp.float32),
            pltpu.VMEM((width, LANES), jnp.float32),
            pltpu.VMEM((block_rows // chunk, chunk, tile), jnp.float32),
            pltpu.VMEM(w_shape, jnp.float32),
            pltpu.VMEM((obs_count,) + w_shape, jnp.float32),
        ]
        + route_sems(z_count, 4)
        + [
            pltpu.SemaphoreType.DMA((3,)),
            pltpu.SemaphoreType.DMA((block_rows // chunk,)),
            pltpu.SemaphoreType.DMA((obs_count,)),
            pltpu.SemaphoreType.DMA((obs_count,)),
        ],
        compiler_params=pltpu.CompilerParams(
            collective_id=collective_id, has_side_effects=True, vmem_limit_bytes=VMEM_BYTES
        ),
        input_output_aliases={0: 2},
    )(begun, sums, regularizer.reshape(width // LANES, LANES))
    return inverse_tile, weights.reshape(block_rows)


def by_strips(descriptors, candidates, sparse_index, targets, regularizer):
    obs_count = lax.axis_size("obs")
    sp_count = lax.axis_size("sp")
    obs_pos = lax.axis_index("obs")
    sp_pos = lax.axis_index("sp")
    z_count = obs_count // 4
    width = sparse_index.shape[0]
    tile = width // obs_count
    strip = width // (obs_count * sp_count)
    mine = strip * z_count
    span = width // 2 + strip
    window = width // 2 + mine
    rows, depth = descriptors.shape
    normalizer = 24.0 * rows * obs_count

    table, slab = share(descriptors, targets, candidates, z_count, 2)
    table = table.reshape(-1, depth)
    place = lax.rem(obs_pos, 4) * sp_count + sp_pos
    wanted = lax.dynamic_slice_in_dim(
        jnp.concatenate([sparse_index, sparse_index]), place * mine, window
    )
    sparse = table.at[wanted].get(mode="promise_in_bounds")
    begun, sums = slab_gram(
        slab, sparse, z_count, sp_count, strip, span, tile, rows, 0
    )
    return series_tile(begun, sums, regularizer, z_count, tile, normalizer, 3)


def slab_body(z_count, sp_count, strip, tile, root, *refs):
    slab_ref, sparse_ref, gathered, sums_ref = refs[:4]
    kbuf, ktr, parts, from_low, from_high, done, zsums, gsums = refs[4:12]
    up_send, up_recv, down_send, down_recv, side_send, side_recv, zs_send, zs_recv, gs_send, gs_recv, keep_sem = refs[12:23]
    near_send, near_recv, load_sem, norm_ref, sp_ref = refs[23:]
    obs = lax.axis_index("obs")
    s = lax.axis_index("sp")
    z, x, c, _ = position()
    q = x * 2 + c
    group = 4 * sp_count
    p = q * sp_count + s
    last = z_count - 1
    shard, depth = norm_ref.shape[1] - EXTRA, norm_ref.shape[2]
    mine = strip * z_count
    lines = mine // LANES

    z_others = [{"obs": lax.rem(z + k, z_count) * 4 + q, "sp": s} for k in range(1, z_count)]
    group_others = []
    for k in range(1, group):
        to = lax.rem(p + k, group)
        group_others.append({"obs": z * 4 + lax.div(to, sp_count), "sp": lax.rem(to, sp_count)})
    loads = [
        pltpu.make_async_copy(slab_ref, norm_ref, load_sem.at[0]),
        pltpu.make_async_copy(sparse_ref, sp_ref, load_sem.at[1]),
    ]
    for load in loads:
        load.start()
    barrier = pltpu.get_barrier_semaphore()
    for other in z_others + group_others:
        pl.semaphore_signal(barrier, inc=1, device_id=other, device_id_type=pl.DeviceIdType.MESH)
    pl.semaphore_wait(barrier, len(z_others) + len(group_others))
    for load in loads:
        load.wait()

    def kernel_tile(t, own):
        cols = pl.ds(pl.multiple_of(t * tile, tile), tile)
        for k in range(4):
            rows = pl.ds(k * shard, shard)
            inner = lax.dot_general(
                norm_ref[k, :shard, :], sp_ref[cols, :], (((1,), (1,)), ((), ())),
                preferred_element_type=jnp.float32,
            )
            scaled = inner * root
            squared = scaled * scaled
            kb = ((squared - 6.0) * squared + 3.0).astype(jnp.bfloat16)
            kbuf[rows, cols] = kb
            if own:
                ktr[cols, rows] = kb.T

    def row_sums():
        for t in range(mine // tile):
            cols = slice(t * tile, (t + 1) * tile)
            weighted = jnp.zeros((1, tile), jnp.float32)
            for k in range(4):
                for h in range(shard // depth):
                    begin = k * shard + h * depth
                    lines_of = jnp.dot(
                        norm_ref[k, shard:, :], kbuf[begin : begin + depth, cols],
                        preferred_element_type=jnp.float32,
                    )
                    weighted = weighted + lines_of[h : h + 1, :]
            square = jnp.zeros((1, tile), jnp.float32)
            for k in range(4):
                kf = kbuf[k * shard : (k + 1) * shard, cols].astype(jnp.float32)
                square = square + jnp.sum(kf * kf, axis=0, keepdims=True)
            for h in range(tile // LANES):
                line = t * (tile // LANES) + h
                lane = slice(h * LANES, (h + 1) * LANES)
                zsums[z, line : line + 1, :] = weighted[:, lane]
                zsums[z, lines + line : lines + line + 1, :] = square[:, lane]

    groups = kbuf.shape[1] // mine

    def piece(t, g):
        begin = t * strip if g == 0 else 0
        end = mine if g < groups - 1 else (t + 1) * strip
        return begin, g * mine + begin - t * strip, end - begin

    def cut(t, g):
        _, begin, size = piece(t, g)
        return pl.ds(begin, size)

    def up(t, g):
        n, at = t * groups + g, (t, slice(None), cut(t, g))
        return remote(
            parts.at[at], from_low.at[at], up_send.at[n], up_recv.at[n],
            {"obs": lax.rem(z + 1, z_count) * 4 + q, "sp": s},
        )

    def down(t, g):
        n, at = t * groups + g, (t, slice(None), cut(t, g))
        return remote(
            parts.at[at], from_high.at[at], down_send.at[n], down_recv.at[n],
            {"obs": lax.rem(z + last, z_count) * 4 + q, "sp": s},
        )

    def gram_group(g):
        cols = slice(g * mine, (g + 1) * mine)
        made = jnp.dot(ktr[...], kbuf[:, cols], preferred_element_type=jnp.float32).astype(jnp.bfloat16)
        for t in range(z_count):
            begin, at, size = piece(t, g)
            parts[t, :, at : at + size] = made[t * strip : (t + 1) * strip, begin : begin + size]

    def pass_on(place, n):
        def rise():
            g = n - place
            if place > 0 and 0 <= g < groups:
                for t in range(last, place, -1):
                    up(t, g).wait_recv()
                    parts[t, :, cut(t, g)] = parts[t, :, cut(t, g)] + from_low[t, :, cut(t, g)]
                    up(t, g).start()

        def fall():
            g = n - (last - place)
            if place < last and 0 <= g < groups:
                for t in range(place):
                    down(t, g).wait_recv()
                    parts[t, :, cut(t, g)] = parts[t, :, cut(t, g)] + from_high[t, :, cut(t, g)]
                    down(t, g).start()

        for step in (rise, fall) if place <= last // 2 else (fall, rise):
            step()

    mine_at = ((z * 2 + x) * 2 + c) * 2 + s
    across_at, beside_at = ((z * 2 + 1 - x) * 2 + c) * 2 + s, ((z * 2 + x) * 2 + c) * 2 + 1 - s
    across, beside = device(z, 1 - x, c, s), device(z, x, c, 1 - s)
    half = strip // 2

    def side(place, g, k):
        rows = (slice(None), slice(None), pl.ds(0, half), pl.ds(half, half))[k]
        at = (mine_at, mine_at, across_at, beside_at)[k]
        src = done.at[:, cut(place, g)] if k < 2 else gathered.at[at, rows, cut(place, g)]
        return remote(
            src, gathered.at[at, rows, cut(place, g)], side_send.at[g * 4 + k], side_recv.at[g * 4 + k],
            (across, beside, beside, across)[k],
        )

    def keep(place, g):
        return pltpu.make_async_copy(
            done.at[:, cut(place, g)], gathered.at[mine_at, :, cut(place, g)], keep_sem.at[g]
        )

    def near(place, g, rising):
        to = lax.rem(z + (1 if rising else last), z_count)
        n = g * 2 + int(rising)
        return remote(
            done.at[:, cut(place, g)], gathered.at[mine_at, :, cut(place, g)],
            near_send.at[n], near_recv.at[n], device(to, x, c, s),
        )

    def close(place, g):
        total = parts[place, :, cut(place, g)].astype(jnp.float32)
        if place > 0:
            up(place, g).wait_recv()
            total = total + from_low[place, :, cut(place, g)].astype(jnp.float32)
        if place < last:
            down(place, g).wait_recv()
            total = total + from_high[place, :, cut(place, g)].astype(jnp.float32)
        if g == 0:
            row = lax.broadcasted_iota(jnp.int32, total.shape, 0)
            col = lax.broadcasted_iota(jnp.int32, total.shape, 1)
            total = jnp.where(row == col, 0.0, total)
        done[:, cut(place, g)] = total.astype(jnp.bfloat16)
        side(place, g, 0).start()
        side(place, g, 1).start()
        if 0 < place < last:
            near(place, g, True).start()
            near(place, g, False).start()
        keep(place, g).start()

    def progress(place, n):
        pass_on(place, n)
        g = n - max(place, last - place)
        if 0 <= g < groups:
            close(place, g)
        if 0 <= g - 1 < groups:
            for k in range(2):
                side(place, g - 1, k).wait_recv()
                side(place, g - 1, k + 2).start()
        if 0 <= g - 2 < groups:
            for k in range(2):
                side(place, g - 2, k + 2).wait_recv()

    z_copies, g_copies = [], []
    for n in range(groups + last + 2):
        if n < groups:

            @pl.loop(n * mine // tile, (n + 1) * mine // tile)
            def _(t):
                kernel_tile(t, n == 0)

            gram_group(n)

            @pl.when(z == 0)
            def _():
                for t in range(last, 0, -1):
                    up(t, n).start()

            @pl.when(z == last)
            def _():
                for t in range(last):
                    down(t, n).start()

        if n == 0:
            row_sums()
            for k in range(1, z_count):
                z_copies.append(remote(zsums.at[z], zsums.at[z], zs_send.at[k], zs_recv.at[k], z_others[k - 1]))
                z_copies[-1].start()
        if n == 1:
            for copy in z_copies:
                copy.wait_recv()
            total = zsums[0]
            for m in range(1, z_count):
                total = total + zsums[m]
            gsums[p] = total
            for m in range(1, group):
                g_copies.append(
                    remote(gsums.at[p], gsums.at[p], gs_send.at[m], gs_recv.at[m], group_others[m - 1])
                )
                g_copies[-1].start()
        for place in range(z_count):
            pl.when(z == place)(functools.partial(progress, place, n))

    def finish(place):
        for g in range(groups):
            for k in range(4):
                side(place, g, k).wait_send()
            keep(place, g).wait()
            if 0 < place < last:
                near(place, g, True).wait_send()
                near(place, g, False).wait_send()
            if 0 < place + 1 < last:
                near(place + 1, g, False).wait_recv()
            if 0 < place - 1 < last:
                near(place - 1, g, True).wait_recv()
            for t in range(z_count):
                if t > place:
                    up(t, g).wait_send()
                if t < place:
                    down(t, g).wait_send()

    for place in range(z_count):
        pl.when(z == place)(functools.partial(finish, place))

    for copy in g_copies:
        copy.wait()
    for copy in z_copies:
        copy.wait_send()
    sums_ref[...] = gsums[...]


def slab_gram(slab, sparse, z_count, sp_count, strip, span, tile, rows, collective_id):
    depth = slab.shape[2]
    window = sparse.shape[0]
    group = 4 * sp_count
    mine = strip * z_count
    lines = 2 * mine // LANES
    vmem = pl.BlockSpec(memory_space=pltpu.VMEM)
    part = (z_count, strip, span)
    groups = window // mine
    sems = [pltpu.SemaphoreType.DMA((z_count * groups,))] * 4 + [pltpu.SemaphoreType.DMA((4 * groups,))] * 2
    sems += [pltpu.SemaphoreType.DMA((z_count,))] * 2 + [pltpu.SemaphoreType.DMA((group,))] * 2
    sems += [pltpu.SemaphoreType.DMA((groups,))] + [pltpu.SemaphoreType.DMA((2 * groups,))] * 2
    sems += [pltpu.SemaphoreType.DMA((2,))]
    sems += [pltpu.VMEM(slab.shape, slab.dtype), pltpu.VMEM(sparse.shape, sparse.dtype)]
    return pl.pallas_call(
        functools.partial(slab_body, z_count, sp_count, strip, tile, math.sqrt(depth)),
        out_shape=[
            jax.ShapeDtypeStruct((group * z_count, strip, span), jnp.bfloat16),
            jax.ShapeDtypeStruct((group, lines, LANES), jnp.float32),
        ],
        in_specs=[pl.BlockSpec(memory_space=pl.ANY)] * 2,
        out_specs=[pl.BlockSpec(memory_space=pl.ANY), vmem],
        scratch_shapes=[
            pltpu.VMEM((4 * rows, window), jnp.bfloat16),
            pltpu.VMEM((mine, 4 * rows), jnp.bfloat16),
            pltpu.VMEM(part, jnp.bfloat16),
            pltpu.VMEM(part, jnp.bfloat16),
            pltpu.VMEM(part, jnp.bfloat16),
            pltpu.VMEM(part[1:], jnp.bfloat16),
            pltpu.VMEM((z_count, lines, LANES), jnp.float32),
            pltpu.VMEM((group, lines, LANES), jnp.float32),
        ] + sems,
        compiler_params=pltpu.CompilerParams(
            collective_id=collective_id, has_side_effects=True, vmem_limit_bytes=VMEM_BYTES
        ),
    )(slab, sparse)


def on_device(descriptors, candidates, sparse_index, targets, regularizer):
    obs_count = lax.axis_size("obs")
    sp_count = lax.axis_size("sp")
    obs_pos = lax.axis_index("obs")
    sp_pos = lax.axis_index("sp")
    width = sparse_index.shape[0]
    if sp_count == 2 and obs_count == 16 and width % (obs_count * sp_count * LANES) == 0:
        return by_strips(descriptors, candidates, sparse_index, targets, regularizer)
    tile = width // obs_count
    share = -(-((obs_count // 2 + 1) * tile) // (sp_count * LANES)) * LANES
    normalizer = 24.0 * descriptors.shape[0] * obs_count

    normed = unit_rows(descriptors)
    piece = candidates.shape[0] // sp_count
    own = lax.dynamic_slice_in_dim(candidates, sp_pos * piece, piece)
    table = spread(unit_rows(own), obs_count, sp_count, 2)
    sparse = table.at[sparse_index].get(mode="promise_in_bounds")

    gram, sums = gram_call(
        sp_pos[None].astype(jnp.int32), normed, sparse, targets, obs_count, tile, share, sp_count
    )
    sums = add_over_obs(sums, obs_count, 0)
    part = lax.psum_scatter(gram, "obs", scatter_dimension=0, tiled=True)

    projected = sums[0] / math.sqrt(normalizer)
    root = lax.rsqrt(sums[1] / normalizer + regularizer)
    col_start = obs_pos * tile
    rrow = lax.dynamic_slice_in_dim(root, col_start, tile)
    window_start = col_start + sp_pos * share
    rwin = lax.dynamic_slice_in_dim(jnp.concatenate([root, root]), window_start, share)
    offset = sp_pos * share + lax.iota(jnp.int32, share)
    on_diag = lax.iota(jnp.int32, tile)[:, None] == offset[None, :]
    scaled = jnp.where(
        on_diag, 0.0, part.astype(jnp.float32) * (rrow[:, None] / normalizer) * rwin[None, :]
    ).astype(jnp.bfloat16)
    packed = spread(scaled, obs_count, sp_count, 3)

    y = lax.dynamic_slice_in_dim(projected, col_start, tile)
    pos = jnp.stack([sp_pos, obs_pos]).astype(jnp.int32)
    inverse_tile, part_w = newton_call(
        pos, packed, root, rrow, y, obs_count, tile, share, sp_count
    )
    return inverse_tile, add_over_obs(part_w[0], obs_count, 1)


def solution(mesh):
    in_specs = (P("obs", None), P("obs", None), P(), P("obs"), P())
    out_specs = (P("sp", "obs"), P("sp"))
    return jax.shard_map(
        on_device, mesh=mesh, in_specs=in_specs, out_specs=out_specs, check_vma=False
    )
```

```python
import functools
import math

import jax
import jax.numpy as jnp
from jax import lax
from jax.experimental import pallas as pl
from jax.experimental.pallas import tpu as pltpu
from jax.sharding import PartitionSpec as P

epsilon = 1e-06
LANES = 128
VMEM_BYTES = 58 * 2**20


def unit_rows(row_block):
    values = row_block.astype(jnp.float32)
    return (values * lax.rsqrt(jnp.sum(values * values, axis=1, keepdims=True) + epsilon)).astype(
        jnp.bfloat16
    )


def gram_body(blocks, tile, share, ext, root, s_ref, norm_ref, sp_ref, tgt_ref, gram_ref, ws_ref, kext):
    step = pl.program_id(0)
    width = blocks * tile

    @pl.when(step < blocks)
    def _():
        inner = lax.dot_general(
            norm_ref[...], sp_ref[...], (((1,), (1,)), ((), ())), preferred_element_type=jnp.float32
        )
        scaled = inner * root
        squared = scaled * scaled
        kb = ((squared - 6.0) * squared + 3.0).astype(jnp.bfloat16)
        kext[:, pl.ds(pl.multiple_of(step * tile, tile), tile)] = kb

        @pl.when(step < ext)
        def _():
            kext[:, pl.ds(pl.multiple_of(width + step * tile, tile), tile)] = kb

        kf = kb.astype(jnp.float32)
        weighted = jnp.dot(tgt_ref[...], kb, preferred_element_type=jnp.float32)
        ws_ref[0:1, :] = weighted[0:1, :]
        ws_ref[1:2, :] = jnp.sum(kf * kf, axis=0, keepdims=True)

    @pl.when(step >= blocks)
    def _():
        j = step - blocks
        cols = pl.ds(pl.multiple_of(j * tile, tile), tile)
        window = pl.ds(pl.multiple_of(j * tile + s_ref[0] * share, LANES), share)
        gram_ref[...] = lax.dot_general(
            kext[:, cols], kext[:, window], (((0,), (0,)), ((), ())), preferred_element_type=jnp.float32
        ).astype(jnp.bfloat16)


def gram_call(s_pos, normed, sparse, targets, blocks, tile, share, sp_count):
    rows, depth = normed.shape
    width = blocks * tile
    ext = -(-((blocks - 1) * tile + sp_count * share - width) // tile)
    last = blocks - 1
    return pl.pallas_call(
        functools.partial(gram_body, blocks, tile, share, ext, math.sqrt(depth)),
        grid_spec=pltpu.PrefetchScalarGridSpec(
            num_scalar_prefetch=1,
            grid=(2 * blocks,),
            in_specs=[
                pl.BlockSpec((rows, depth), lambda g, s: (0, 0)),
                pl.BlockSpec((tile, depth), lambda g, s: (jnp.minimum(g, last), 0)),
                pl.BlockSpec((16, rows), lambda g, s: (0, 0)),
            ],
            out_specs=[
                pl.BlockSpec((tile, share), lambda g, s: (jnp.maximum(g - blocks, 0), 0)),
                pl.BlockSpec((2, tile), lambda g, s: (0, jnp.minimum(g, last))),
            ],
            scratch_shapes=[pltpu.VMEM((rows, width + ext * tile), jnp.bfloat16)],
        ),
        out_shape=[
            jax.ShapeDtypeStruct((width, share), jnp.bfloat16),
            jax.ShapeDtypeStruct((2, width), jnp.float32),
        ],
        compiler_params=pltpu.CompilerParams(vmem_limit_bytes=VMEM_BYTES),
    )(s_pos, normed, sparse, jnp.broadcast_to(targets[None, :], (16, rows)))


def newton_body(
    blocks, tile, share, sp_count, chunk, block_rows,
    pos_ref, packed_ref, rcol_ref, rrow_ref, y_ref, inv_ref, w_ref, dense, prod,
):
    step = pl.program_id(0)
    width = blocks * tile
    half = blocks // 2
    p_steps = width // chunk
    my_cols = pl.ds(pl.multiple_of(pos_ref[1] * tile, tile), tile)

    @pl.when(step < blocks)
    def _():
        rows = pl.ds(pl.multiple_of(step * tile, tile), tile)
        for s in range(sp_count):
            for q in range(share // LANES):
                offset = s * share + q * LANES
                if offset >= (half + 1) * tile:
                    continue
                col = lax.rem(step * tile + offset, width)
                cols = pl.ds(pl.multiple_of(col, LANES), LANES)
                block = packed_ref[s * tile : (s + 1) * tile, q * LANES : (q + 1) * LANES]
                dense[rows, cols] = block
                if tile <= offset < half * tile:
                    dense[cols, rows] = block.T

    @pl.when((step >= blocks) & (step < blocks + p_steps))
    def _():
        rows = pl.ds(pl.multiple_of((step - blocks) * chunk, chunk), chunk)
        prod[rows, :] = jnp.dot(
            dense[rows, :], dense[:, my_cols], preferred_element_type=jnp.float32
        ).astype(jnp.bfloat16)

    @pl.when(step >= blocks + p_steps)
    def _():
        local = pl.multiple_of((step - blocks - p_steps) * chunk, chunk)
        start = pl.multiple_of(pos_ref[0] * block_rows + local, chunk)
        rows = pl.ds(start, chunk)
        cubic = jnp.dot(dense[rows, :], prod[...], preferred_element_type=jnp.float32)
        on_diag = (start + lax.broadcasted_iota(jnp.int32, (chunk, tile), 0)) == (
            pos_ref[1] * tile + lax.broadcasted_iota(jnp.int32, (chunk, tile), 1)
        )
        series = (
            jnp.where(on_diag, 1.0, 0.0)
            - dense[rows, my_cols].astype(jnp.float32)
            + prod[rows, :].astype(jnp.float32)
            - cubic
        )
        out = series * rcol_ref[rows, :] * rrow_ref[...]
        inv_ref[pl.ds(local, chunk), :] = out
        w_ref[:, pl.ds(local, chunk)] = lax.dot_general(
            y_ref[...], out, (((1,), (1,)), ((), ())),
            precision=lax.Precision.HIGHEST, preferred_element_type=jnp.float32,
        )


def newton_call(pos, packed, root_recip, rrow, y, blocks, tile, share, sp_count):
    width = blocks * tile
    block_rows = width // sp_count
    chunk = min(512, block_rows)
    grid = blocks + width // chunk + block_rows // chunk
    last = blocks - 1
    return pl.pallas_call(
        functools.partial(newton_body, blocks, tile, share, sp_count, chunk, block_rows),
        grid_spec=pltpu.PrefetchScalarGridSpec(
            num_scalar_prefetch=1,
            grid=(grid,),
            in_specs=[
                pl.BlockSpec((sp_count * tile, share), lambda g, p: (jnp.minimum(g, last), 0)),
                pl.BlockSpec((width, 1), lambda g, p: (0, 0)),
                pl.BlockSpec((1, tile), lambda g, p: (0, 0)),
                pl.BlockSpec((8, tile), lambda g, p: (0, 0)),
            ],
            out_specs=[
                pl.BlockSpec((block_rows, tile), lambda g, p: (0, 0)),
                pl.BlockSpec((8, block_rows), lambda g, p: (0, 0)),
            ],
            scratch_shapes=[
                pltpu.VMEM((width, width), jnp.bfloat16),
                pltpu.VMEM((width, tile), jnp.bfloat16),
            ],
        ),
        out_shape=[
            jax.ShapeDtypeStruct((block_rows, tile), jnp.float32),
            jax.ShapeDtypeStruct((8, block_rows), jnp.float32),
        ],
        compiler_params=pltpu.CompilerParams(vmem_limit_bytes=VMEM_BYTES),
    )(pos, packed, root_recip[:, None], rrow[None, :], jnp.broadcast_to(y[None, :], (8, tile)))


def add_body(count, in_ref, out_ref, slots, send_sem, recv_sem):
    me = lax.axis_index("obs")
    barrier = pltpu.get_barrier_semaphore()
    for k in range(1, count):
        pl.semaphore_signal(
            barrier, inc=1, device_id={"obs": lax.rem(me + k, count)}, device_id_type=pl.DeviceIdType.MESH
        )
    pl.semaphore_wait(barrier, count - 1)
    copies = []
    for k in range(1, count):
        copy = pltpu.make_async_remote_copy(
            src_ref=in_ref,
            dst_ref=slots.at[me],
            send_sem=send_sem.at[k],
            recv_sem=recv_sem.at[k],
            device_id={"obs": lax.rem(me + k, count)},
            device_id_type=pl.DeviceIdType.MESH,
        )
        copy.start()
        copies.append(copy)
    slots[me] = in_ref[...]
    for copy in copies:
        copy.wait()
    total = slots[0]
    for k in range(1, count):
        total = total + slots[k]
    out_ref[...] = total


def add_over_obs(values, count, collective_id):
    shape = values.shape
    flat = values.reshape(values.size // LANES, LANES)
    total = pl.pallas_call(
        functools.partial(add_body, count),
        out_shape=jax.ShapeDtypeStruct(flat.shape, flat.dtype),
        in_specs=[pl.BlockSpec(memory_space=pltpu.VMEM)],
        out_specs=pl.BlockSpec(memory_space=pltpu.VMEM),
        scratch_shapes=[
            pltpu.VMEM((count,) + flat.shape, flat.dtype),
            pltpu.SemaphoreType.DMA((count,)),
            pltpu.SemaphoreType.DMA((count,)),
        ],
        cost_estimate=pl.CostEstimate(
            flops=count * flat.size, bytes_accessed=400 * flat.size, transcendentals=0
        ),
        compiler_params=pltpu.CompilerParams(collective_id=collective_id, has_side_effects=True),
    )(flat)
    return total.reshape(shape)


def spread_keys(z_count, sp_count):
    keys = [("z", k) for k in range(1, z_count)]
    for k in range(z_count):
        keys += [("x", k), ("core", k), ("core_x", k)]
        for d in range(1, sp_count):
            keys += [(name, k, d) for name in ("sp", "sp_a", "x_b", "core_sp", "core_a", "core_b")]
    return {key: place for place, key in enumerate(keys)}


def spread_body(z_count, sp_count, in_ref, out_ref, send_sem, recv_sem, own_sem):
    places = spread_keys(z_count, sp_count)
    obs = lax.axis_index("obs")
    s = lax.axis_index("sp")
    z, x, c = lax.div(obs, 4), lax.rem(lax.div(obs, 2), 2), lax.rem(obs, 2)
    half = in_ref.shape[0] // 2
    upper, lower = pl.ds(0, half), pl.ds(half, half)
    zs = [lax.bitwise_xor(z, k) for k in range(z_count)]
    to_sp = [lax.rem(s + d, sp_count) for d in range(sp_count)]
    from_sp = [lax.rem(s - d + sp_count, sp_count) for d in range(sp_count)]

    def device(z_to, x_to, c_to, s_to):
        return {"obs": z_to * 4 + x_to * 2 + c_to, "sp": s_to}

    def slot(z_of, x_of, s_of):
        return ((z_of * 2 + x_of) * 2 + c) * sp_count + s_of

    own_slot = slot(z, x, s)
    across, sibling = device(z, 1 - x, c, s), device(z, x, 1 - c, s)
    others = [device(zs[k], x, c, s) for k in range(1, z_count)]
    others += [device(z, x, c, to_sp[d]) for d in range(1, sp_count)]
    others += [across, sibling]
    barrier = pltpu.get_barrier_semaphore()
    for other in others:
        pl.semaphore_signal(barrier, inc=1, device_id=other, device_id_type=pl.DeviceIdType.MESH)
    pl.semaphore_wait(barrier, len(others))

    sent = {}

    def send(key, place, target, rows=None, own=False):
        src = in_ref if own else out_ref.at[place]
        dst = out_ref.at[place]
        if rows is not None:
            src, dst = src.at[rows], dst.at[rows]
        copy = pltpu.make_async_remote_copy(
            src_ref=src,
            dst_ref=dst,
            send_sem=send_sem.at[places[key]],
            recv_sem=recv_sem.at[places[key]],
            device_id=target,
            device_id_type=pl.DeviceIdType.MESH,
        )
        copy.start()
        sent[key] = copy

    keep = pltpu.make_async_copy(in_ref, out_ref.at[own_slot], own_sem)
    keep.start()
    for k in range(1, z_count):
        send(("z", k), own_slot, others[k - 1], own=True)

    def fan_out(k):
        place = slot(zs[k], x, s)
        send(("x", k), place, across, own=k == 0)
        for d in range(1, sp_count):
            send(("sp", k, d), place, device(z, x, c, to_sp[d]), own=k == 0)
        send(("core", k), place, sibling, own=k == 0)

    def relay(k):
        sent[("x", k)].wait_recv()
        place = slot(zs[k], 1 - x, s)
        for d in range(1, sp_count):
            send(("sp_a", k, d), place, device(z, x, c, to_sp[d]), upper)
        send(("core_x", k), place, sibling)
        for d in range(1, sp_count):
            sent[("sp", k, d)].wait_recv()
            place = slot(zs[k], x, from_sp[d])
            send(("x_b", k, d), place, across, lower)
            send(("core_sp", k, d), place, sibling)

    def finish(k):
        for d in range(1, sp_count):
            place = slot(zs[k], 1 - x, from_sp[d])
            sent[("sp_a", k, d)].wait_recv()
            send(("core_a", k, d), place, sibling, upper)
            sent[("x_b", k, d)].wait_recv()
            send(("core_b", k, d), place, sibling, lower)

    fan_out(0)
    for k in range(1, z_count):
        sent[("z", k)].wait_recv()
        fan_out(k)
        relay(k - 1)
        if k > 1:
            finish(k - 2)
    relay(z_count - 1)
    if z_count > 1:
        finish(z_count - 2)
    finish(z_count - 1)
    keep.wait()
    for key, copy in sent.items():
        copy.wait_send()
        if key[0].startswith("core"):
            copy.wait_recv()


def spread(shard, obs_count, sp_count, collective_id):
    rows, cols = shard.shape
    z_count = obs_count // 4
    total = obs_count * sp_count
    sems = len(spread_keys(z_count, sp_count))
    gathered = pl.pallas_call(
        functools.partial(spread_body, z_count, sp_count),
        out_shape=jax.ShapeDtypeStruct((total, rows, cols), shard.dtype),
        in_specs=[pl.BlockSpec(memory_space=pl.ANY)],
        out_specs=pl.BlockSpec(memory_space=pl.ANY),
        scratch_shapes=[
            pltpu.SemaphoreType.DMA((sems,)),
            pltpu.SemaphoreType.DMA((sems,)),
            pltpu.SemaphoreType.DMA,
        ],
        compiler_params=pltpu.CompilerParams(collective_id=collective_id, has_side_effects=True),
    )(shard)
    return gathered.reshape(total * rows, cols)


def position():
    obs = lax.axis_index("obs")
    return lax.div(obs, 4), lax.rem(lax.div(obs, 2), 2), lax.rem(obs, 2), lax.axis_index("sp")


def device(z, x, c, s):
    return {"obs": z * 4 + x * 2 + c, "sp": s}


def remote(src, dst, send_sem, recv_sem, target):
    return pltpu.make_async_remote_copy(
        src_ref=src, dst_ref=dst, send_sem=send_sem, recv_sem=recv_sem,
        device_id=target, device_id_type=pl.DeviceIdType.MESH,
    )


def route_sems(z_count, chunks):
    return [
        pltpu.SemaphoreType.DMA((4 * chunks * (z_count + 1),)),
        pltpu.SemaphoreType.DMA((4 * chunks * z_count,)),
        pltpu.SemaphoreType.DMA((4 * (chunks + 1) * z_count,)),
        pltpu.SemaphoreType.DMA((4 * (chunks + 1) * z_count,)),
    ]


def route_greet(z_count, meanwhile):
    z, x, c, s = position()
    barrier = pltpu.get_barrier_semaphore()
    others = [device(z, 1 - x, c, s), device(z, x, 1 - c, s), device(z, x, c, 1 - s)]
    others += [device(lax.rem(z + k, z_count), x, c, s) for k in range(1, z_count)]
    for other in others:
        pl.semaphore_signal(barrier, inc=1, device_id=other, device_id_type=pl.DeviceIdType.MESH)
    meanwhile()
    pl.semaphore_wait(barrier, len(others))


EXTRA = 32
OWN, ACROSS, BESIDE, DIAGONAL = range(4)


def route(z_count, home, out_ref, sems, arrive, chunks, diagonal, lag, begin, late=None):
    z_send, z_recv, send_sem, recv_sem = sems
    z, x, c, s = position()
    last = z_count - 1
    rows = out_ref.shape[1]
    high = rows // chunks
    known = home is None
    across, beside, sibling = device(z, 1 - x, c, s), device(z, x, c, 1 - s), device(z, x, 1 - c, s)
    along = {OWN: chunks, ACROSS: 0, BESIDE: 0, DIAGONAL: diagonal}

    nearer = jnp.minimum(z, last - z)
    origins = [z]
    for a in range(last):
        both = jnp.where((z <= last // 2) == (a % 2 == 0), z + (a // 2 + 1), z - (a // 2 + 1))
        single = jnp.where(z <= last - z, z + (a - nearer + 1), z - (a - nearer + 1))
        origins.append(jnp.where(a < 2 * nearer, both, single))

    def slot(col, a, c_of=c):
        x_of = 1 - x if col in (ACROSS, DIAGONAL) else x
        s_of = 1 - s if col in (BESIDE, DIAGONAL) else s
        return ((origins[a] * 2 + x_of) * 2 + c_of) * 2 + s_of

    def shard(col, a):
        return out_ref.at[slot(col, a)] if a or col != OWN or known else home

    sent = {}

    def send(key, col, a, target, begin=0, size=rows):
        cut = pl.ds(begin, size)
        n = len(sent)
        sent[key] = remote(
            shard(col, a).at[cut], out_ref.at[slot(col, a)].at[cut], send_sem.at[n], recv_sem.at[n], target
        )
        sent[key].start()

    hops = []

    def hop(col, a, j, n, target_z, when):
        cut = pl.ds(j * high, high)
        copy = remote(
            shard(col, a).at[cut], out_ref.at[slot(col, a)].at[cut],
            z_send.at[(col * chunks + j) * (z_count + 1) + n], z_recv.at[(col * chunks + j) * z_count + origins[a]],
            device(jnp.clip(target_z, 0, last), x, c, s),
        )
        pl.when(when)(copy.start)
        hops.append((when, copy))

    def set_off(col, j):
        if j < along[col]:
            hop(col, 0, j, 0, z + 1, z < last)
            hop(col, 0, j, 1, z - 1, z > 0)

    def pass_on(col, a, j):
        if j < along[col]:
            held = out_ref.at[slot(col, a)].at[pl.ds(j * high, high)]
            arrival = remote(
                held, held, z_send.at[0], z_recv.at[(col * chunks + j) * z_count + origins[a]], across
            ).wait_recv
            if not known or col != OWN or a > 1:
                arrival()
            target_z = jnp.where(origins[a] < z, z + 1, z - 1)
            hop(col, a, j, a + 1, target_z, (target_z >= 0) & (target_z <= last))

    finished = []

    def complete(now, a, *cols):
        for col in cols:
            send(("core", col, a), col, a, sibling)
            arrive(shard(col, a), slot(col, a))
            finished.append((now, a, col))

    def from_sibling(before):
        while finished and finished[0][0] < before:
            _, a, col = finished.pop(0)
            sent[("core", col, a)].wait_recv()
            place = slot(col, a, 1 - c)
            arrive(out_ref.at[place], place)

    def fan_out(a, j):
        send(("x", a, j), OWN, a, across, j * high, high)
        send(("y", a, j), OWN, a, beside, j * high, high)

    def relay(a, j):
        direct = a == 0 or j >= diagonal
        sent[("x", a, j)].wait_recv()
        if direct:
            send(("ya", a, j), ACROSS, a, beside, j * high, high // 2)
        sent[("y", a, j)].wait_recv()
        if direct:
            send(("xb", a, j), BESIDE, a, across, j * high + high // 2, high // 2)

    def finish(a, j):
        if ("ya", a, j) in sent:
            sent[("ya", a, j)].wait_recv()
            sent[("xb", a, j)].wait_recv()

    first = 1 if known else 0
    for j in range(chunks):
        if known:
            hop(OWN, 0, j, 0, jnp.where(z == 0, 1, last - 1), (z == 0) | (z == last))
        else:
            set_off(OWN, j)
            fan_out(0, j)
    for j in range(chunks if known else 0):
        set_off(DIAGONAL, j)
    begin()
    complete(-1, 0, OWN)
    if known:
        complete(-1, 0, ACROSS, BESIDE, DIAGONAL)
    items = [(a, j) for j in range(chunks) for a in range(first, 2)]
    items += [(a, j) for a in range(2, z_count) for j in range(chunks)]
    ends = [items.index((a, chunks - 1)) for a in range(1, z_count)]
    ready = set()
    for now in range(len(items) + max(sum(lag), 3)):
        if now < len(items):
            a, j = items[now]
            if a:
                pass_on(OWN, a, j)
                fan_out(a, j)
                if j == chunks - 1:
                    complete(now, a, OWN)
        if 0 <= now - lag[0] < len(items):
            a, j = items[now - lag[0]]
            relay(a, j)
            if j == chunks - 1:
                complete(now, a, ACROSS, BESIDE)
        if now - 3 in ends:
            a = ends.index(now - 3) + 1
            for j in range(chunks):
                pass_on(DIAGONAL, a, j)
            ready.add(a)
        if 0 <= now - sum(lag) < len(items):
            a, j = items[now - sum(lag)]
            finish(a, j)
            if a == 0:
                set_off(DIAGONAL, j)
            if j == chunks - 1:
                assert a in ready or not a
                complete(now, a, DIAGONAL)
        if now == len(items) - 2 and late is not None:
            late()
        from_sibling(now - 2)
    from_sibling(now + 1)
    for copy in sent.values():
        copy.wait_send()
    for when, copy in hops:
        pl.when(when)(copy.wait_send)


def share_body(
    z_count, rows_ref, targets_ref, candidates_ref, out_ref, slab_ref, own_ref, own_slab,
    z_send, z_recv, send_sem, recv_sem, slab_send, slab_recv, keep_sem,
):
    z, x, c, s = position()
    q, q_across = x * 2 + c, (1 - x) * 2 + c
    half = own_slab.shape[0] // 2
    near, far = pl.ds(pl.multiple_of(s * half, 16), half), pl.ds(pl.multiple_of((1 - s) * half, 16), half)

    def make_unit():
        piece, rows = own_ref.shape[0], rows_ref.shape[0]
        own_ref[...] = unit_rows(candidates_ref[pl.ds(pl.multiple_of(s * piece, 16), piece), :])
        step = math.gcd(rows, 256)
        for begin in range(0, rows, step):
            own_slab[begin : begin + step, :] = unit_rows(rows_ref[begin : begin + step, :])
        extra = own_slab.shape[0] - rows
        place = lax.broadcasted_iota(jnp.int32, (extra, own_slab.shape[1]), 0)
        lines = jnp.zeros(place.shape, jnp.float32)
        for k in range(rows // own_slab.shape[1]):
            line = targets_ref[:, k * own_slab.shape[1] : (k + 1) * own_slab.shape[1]].astype(jnp.float32)
            lines = jnp.where(place == k, line, lines)
        own_slab[rows:, :] = lines.astype(jnp.bfloat16)

    route_greet(z_count, make_unit)
    keep = pltpu.make_async_copy(own_ref, out_ref.at[((z * 2 + x) * 2 + c) * 2 + s], keep_sem.at[0])
    keep_slab = pltpu.make_async_copy(own_slab, slab_ref.at[q], keep_sem.at[1])
    keep.start()
    keep_slab.start()
    shared = []

    def share(src, place, piece, target):
        n = len(shared)
        dst = slab_ref.at[place]
        if piece is not None:
            src, dst = src.at[piece], dst.at[piece]
        shared.append(remote(src, dst, slab_send.at[n], slab_recv.at[n], target))
        shared[-1].start()

    def begin():
        share(own_slab, q, near, device(z, 1 - x, c, s))
        share(own_slab, q, None, device(z, x, 1 - c, s))

    def late():
        shared[0].wait_recv()
        share(slab_ref.at[q_across], q_across, near, device(z, x, c, 1 - s))
        share(slab_ref.at[q_across], q_across, near, device(z, x, 1 - c, s))

    sems = z_send, z_recv, send_sem, recv_sem
    route(z_count, own_ref, out_ref, sems, lambda src, place: None, 1, 0, (2, 2), begin, late)
    shared[2].wait_recv()
    share(slab_ref.at[q_across], q_across, far, device(z, x, 1 - c, s))
    for n in (1, 3, 4):
        shared[n].wait_recv()
    for copy in shared:
        copy.wait_send()
    keep.wait()
    keep_slab.wait()


def share(descriptors, targets, candidates, z_count, collective_id):
    rows, depth = descriptors.shape
    own = (candidates.shape[0] // 2, depth)
    own_slab = (rows + EXTRA, depth)
    anywhere = pl.BlockSpec(memory_space=pl.ANY)
    vmem = pl.BlockSpec(memory_space=pltpu.VMEM)
    return pl.pallas_call(
        functools.partial(share_body, z_count),
        out_shape=[
            jax.ShapeDtypeStruct((8 * z_count,) + own, jnp.bfloat16),
            jax.ShapeDtypeStruct((4,) + own_slab, jnp.bfloat16),
        ],
        in_specs=[vmem, vmem, vmem],
        out_specs=[anywhere, anywhere],
        scratch_shapes=[pltpu.VMEM(own, jnp.bfloat16), pltpu.VMEM(own_slab, jnp.bfloat16)]
        + route_sems(z_count, 1)
        + [pltpu.SemaphoreType.DMA((5,)), pltpu.SemaphoreType.DMA((5,)), pltpu.SemaphoreType.DMA((2,))],
        compiler_params=pltpu.CompilerParams(
            collective_id=collective_id, has_side_effects=True, vmem_limit_bytes=VMEM_BYTES
        ),
    )(descriptors, targets.reshape(1, rows), candidates)


def series_body(
    z_count, strip, tile, chunk, normalizer,
    begun_ref, sums_ref, reg_ref, inv_ref, w_ref, gathered,
    dense, first, second, stage, recip, spread_recip, out_buf, w_own, w_slots,
    z_send, z_recv, send_sem, recv_sem, stage_sem, out_sem, w_send, w_recv,
):
    z, x, c, s = position()
    obs = lax.axis_index("obs")
    obs_count = 4 * z_count
    strips = 8 * z_count
    width = strips * strip
    half = strips // 2
    span = begun_ref.shape[2]
    block_rows = width // 2
    lines = tile // LANES
    fold = 1.0 / normalizer

    barrier = pltpu.get_barrier_semaphore()
    peers = [
        {"obs": lax.rem(obs + k, obs_count), "sp": s} for k in range(1, obs_count)
    ]
    for peer in peers + [device(z, x, c, 1 - s)]:
        pl.semaphore_signal(barrier, inc=1, device_id=peer, device_id_type=pl.DeviceIdType.MESH)
    pl.semaphore_wait(barrier, obs_count)

    slots = stage.shape[0]
    waiting = []

    def lay_out(n):
        copy, place = waiting[n]
        copy.wait()
        place = lax.rem(place, 8) * z_count + lax.div(place, 8)
        rows = pl.ds(pl.multiple_of(place * strip, strip), strip)

        def put(k, turn):
            cols = pl.ds(pl.multiple_of(lax.rem(place + k, strips) * strip, strip), strip)
            block = stage[n % slots, :, pl.ds(pl.multiple_of(k * strip, strip), strip)]
            dense[rows, cols] = block
            if turn:
                dense[cols, rows] = block.T

        for k in range(half + 1):
            put(k, 0 < k < half)

    def arrive(src, place):
        n = len(waiting)
        if n >= slots:
            lay_out(n - slots)
        copy = pltpu.make_async_copy(src, stage.at[n % slots], stage_sem.at[n % slots])
        copy.start()
        waiting.append((copy, place))

    def begin():
        per = sums_ref.shape[1] // 2
        for p in range(sums_ref.shape[0]):
            lane = slice(p * per, (p + 1) * per)
            recip[lane, :] = 1.0 / (sums_ref[p, per:, :] * fold + reg_ref[lane, :])

        @pl.loop(0, width // LANES)
        def _(m):
            row = jnp.broadcast_to(recip[pl.ds(m, 1), :], (LANES, LANES))
            spread_recip[pl.ds(pl.multiple_of(m * LANES, LANES), LANES), :] = row.T

    sems = z_send, z_recv, send_sem, recv_sem
    route(z_count, None, gathered, sems, arrive, 4, 2, (2, 3), begin)
    for n in range(len(waiting) - slots, len(waiting)):
        lay_out(n)

    my_cols = pl.ds(pl.multiple_of(obs * tile, tile), tile)

    def by_row(values, rows):
        scale = spread_recip[rows, :]
        return values * jnp.concatenate([scale] * lines, axis=1)

    @pl.loop(0, width // chunk)
    def _(m):
        rows = pl.ds(pl.multiple_of(m * chunk, chunk), chunk)
        first[rows, :] = by_row(dense[rows, my_cols].astype(jnp.float32) * fold, rows).astype(jnp.bfloat16)

    @pl.loop(0, width // chunk)
    def _(m):
        rows = pl.ds(pl.multiple_of(m * chunk, chunk), chunk)
        prod = jnp.dot(dense[rows, :], first[...], preferred_element_type=jnp.float32)
        second[rows, :] = by_row(prod * fold, rows).astype(jnp.bfloat16)

    def my_lines(ref, at):
        return jnp.concatenate([ref[pl.ds(at + h, 1), :] for h in range(lines)], axis=1)

    per = sums_ref.shape[1] // 2
    r_row = my_lines(recip, obs * lines)
    y = my_lines(sums_ref.at[lax.div(obs * lines, per)], lax.rem(obs * lines, per))
    y = y * (1.0 / math.sqrt(normalizer))

    def emit(m):
        return pltpu.make_async_copy(
            out_buf.at[m], inv_ref.at[pl.ds(pl.multiple_of(m * chunk, chunk), chunk)], out_sem.at[m]
        )

    @pl.loop(0, block_rows // chunk)
    def _(m):
        begin_at = s * block_rows + m * chunk
        rows = pl.ds(pl.multiple_of(begin_at, chunk), chunk)
        cubic = jnp.dot(dense[rows, :], second[...], preferred_element_type=jnp.float32)
        on_diag = (begin_at + lax.broadcasted_iota(jnp.int32, (chunk, tile), 0)) == (
            obs * tile + lax.broadcasted_iota(jnp.int32, (chunk, tile), 1)
        )
        series = second[rows, :].astype(jnp.float32) - by_row(
            (dense[rows, my_cols].astype(jnp.float32) + cubic) * fold, rows
        )
        out = (jnp.where(on_diag, 1.0, 0.0) + series) * r_row
        out_buf[m] = out
        emit(m).start()
        weighted = out * y
        weighted = sum(weighted[:, h * LANES : (h + 1) * LANES] for h in range(lines))
        for h in range(chunk // LANES):
            turned = weighted[h * LANES : (h + 1) * LANES, :].T
            w_own[pl.ds(m * (chunk // LANES) + h, 1), :] = jnp.sum(turned, axis=0, keepdims=True)

    copies = []
    for k in range(1, obs_count):
        copies.append(remote(w_own, w_slots.at[obs], w_send.at[k], w_recv.at[k], peers[k - 1]))
        copies[-1].start()
    w_slots[obs] = w_own[...]
    for copy in copies:
        copy.wait()
    total = w_slots[0]
    for k in range(1, obs_count):
        total = total + w_slots[k]
    w_ref[...] = total
    for m in range(block_rows // chunk):
        emit(m).wait()


def series_tile(begun, sums, regularizer, z_count, tile, normalizer, collective_id):
    strips, strip, span = begun.shape
    width = strips * strip
    block_rows = width // 2
    chunk = min(1024, block_rows)
    obs_count = 4 * z_count
    w_shape = (block_rows // LANES, LANES)
    anywhere = pl.BlockSpec(memory_space=pl.ANY)
    vmem = pl.BlockSpec(memory_space=pltpu.VMEM)
    inverse_tile, weights, _ = pl.pallas_call(
        functools.partial(series_body, z_count, strip, tile, chunk, normalizer),
        out_shape=[
            jax.ShapeDtypeStruct((block_rows, tile), jnp.float32),
            jax.ShapeDtypeStruct(w_shape, jnp.float32),
            jax.ShapeDtypeStruct(begun.shape, begun.dtype),
        ],
        in_specs=[anywhere, vmem, vmem],
        out_specs=[anywhere, vmem, anywhere],
        scratch_shapes=[
            pltpu.VMEM((width, width), jnp.bfloat16),
            pltpu.VMEM((width, tile), jnp.bfloat16),
            pltpu.VMEM((width, tile), jnp.bfloat16),
            pltpu.VMEM((3, strip, span), jnp.bfloat16),
            pltpu.VMEM((width // LANES, LANES), jnp.float32),
            pltpu.VMEM((width, LANES), jnp.float32),
            pltpu.VMEM((block_rows // chunk, chunk, tile), jnp.float32),
            pltpu.VMEM(w_shape, jnp.float32),
            pltpu.VMEM((obs_count,) + w_shape, jnp.float32),
        ]
        + route_sems(z_count, 4)
        + [
            pltpu.SemaphoreType.DMA((3,)),
            pltpu.SemaphoreType.DMA((block_rows // chunk,)),
            pltpu.SemaphoreType.DMA((obs_count,)),
            pltpu.SemaphoreType.DMA((obs_count,)),
        ],
        compiler_params=pltpu.CompilerParams(
            collective_id=collective_id, has_side_effects=True, vmem_limit_bytes=VMEM_BYTES
        ),
        input_output_aliases={0: 2},
    )(begun, sums, regularizer.reshape(width // LANES, LANES))
    return inverse_tile, weights.reshape(block_rows)


def by_strips(descriptors, candidates, sparse_index, targets, regularizer):
    obs_count = lax.axis_size("obs")
    sp_count = lax.axis_size("sp")
    obs_pos = lax.axis_index("obs")
    sp_pos = lax.axis_index("sp")
    z_count = obs_count // 4
    width = sparse_index.shape[0]
    tile = width // obs_count
    strip = width // (obs_count * sp_count)
    mine = strip * z_count
    span = width // 2 + strip
    window = width // 2 + mine
    rows, depth = descriptors.shape
    normalizer = 24.0 * rows * obs_count

    table, slab = share(descriptors, targets, candidates, z_count, 2)
    table = table.reshape(-1, depth)
    place = lax.rem(obs_pos, 4) * sp_count + sp_pos
    wanted = lax.dynamic_slice_in_dim(
        jnp.concatenate([sparse_index, sparse_index]), place * mine, window
    )
    sparse = table.at[wanted].get(mode="promise_in_bounds")
    begun, sums = slab_gram(
        slab, sparse, z_count, sp_count, strip, span, tile, rows, 0
    )
    return series_tile(begun, sums, regularizer, z_count, tile, normalizer, 3)


def slab_body(z_count, sp_count, strip, tile, root, *refs):
    slab_ref, sparse_ref, gathered, sums_ref = refs[:4]
    kbuf, ktr, parts, from_low, from_high, done, zsums, gsums = refs[4:12]
    up_send, up_recv, down_send, down_recv, side_send, side_recv, zs_send, zs_recv, gs_send, gs_recv, keep_sem = refs[12:23]
    near_send, near_recv, load_sem, norm_ref, sp_ref = refs[23:]
    obs = lax.axis_index("obs")
    s = lax.axis_index("sp")
    z, x, c, _ = position()
    q = x * 2 + c
    group = 4 * sp_count
    p = q * sp_count + s
    last = z_count - 1
    shard, depth = norm_ref.shape[1] - EXTRA, norm_ref.shape[2]
    mine = strip * z_count
    lines = mine // LANES

    z_others = [{"obs": lax.rem(z + k, z_count) * 4 + q, "sp": s} for k in range(1, z_count)]
    group_others = []
    for k in range(1, group):
        to = lax.rem(p + k, group)
        group_others.append({"obs": z * 4 + lax.div(to, sp_count), "sp": lax.rem(to, sp_count)})
    loads = [
        pltpu.make_async_copy(slab_ref, norm_ref, load_sem.at[0]),
        pltpu.make_async_copy(sparse_ref, sp_ref, load_sem.at[1]),
    ]
    for load in loads:
        load.start()
    barrier = pltpu.get_barrier_semaphore()
    for other in z_others + group_others:
        pl.semaphore_signal(barrier, inc=1, device_id=other, device_id_type=pl.DeviceIdType.MESH)
    pl.semaphore_wait(barrier, len(z_others) + len(group_others))
    for load in loads:
        load.wait()

    def kernel_tile(t, own):
        cols = pl.ds(pl.multiple_of(t * tile, tile), tile)
        for k in range(4):
            rows = pl.ds(k * shard, shard)
            inner = lax.dot_general(
                norm_ref[k, :shard, :], sp_ref[cols, :], (((1,), (1,)), ((), ())),
                preferred_element_type=jnp.float32,
            )
            scaled = inner * root
            squared = scaled * scaled
            kb = ((squared - 6.0) * squared + 3.0).astype(jnp.bfloat16)
            kbuf[rows, cols] = kb
            if own:
                ktr[cols, rows] = kb.T

    def row_sums():
        for t in range(mine // tile):
            cols = slice(t * tile, (t + 1) * tile)
            weighted = jnp.zeros((1, tile), jnp.float32)
            for k in range(4):
                for h in range(shard // depth):
                    begin = k * shard + h * depth
                    lines_of = jnp.dot(
                        norm_ref[k, shard:, :], kbuf[begin : begin + depth, cols],
                        preferred_element_type=jnp.float32,
                    )
                    weighted = weighted + lines_of[h : h + 1, :]
            square = jnp.zeros((1, tile), jnp.float32)
            for k in range(4):
                kf = kbuf[k * shard : (k + 1) * shard, cols].astype(jnp.float32)
                square = square + jnp.sum(kf * kf, axis=0, keepdims=True)
            for h in range(tile // LANES):
                line = t * (tile // LANES) + h
                lane = slice(h * LANES, (h + 1) * LANES)
                zsums[z, line : line + 1, :] = weighted[:, lane]
                zsums[z, lines + line : lines + line + 1, :] = square[:, lane]

    groups = kbuf.shape[1] // mine

    def piece(t, g):
        begin = t * strip if g == 0 else 0
        end = mine if g < groups - 1 else (t + 1) * strip
        return begin, g * mine + begin - t * strip, end - begin

    def cut(t, g):
        _, begin, size = piece(t, g)
        return pl.ds(begin, size)

    def up(t, g):
        n, at = t * groups + g, (t, slice(None), cut(t, g))
        return remote(
            parts.at[at], from_low.at[at], up_send.at[n], up_recv.at[n],
            {"obs": lax.rem(z + 1, z_count) * 4 + q, "sp": s},
        )

    def down(t, g):
        n, at = t * groups + g, (t, slice(None), cut(t, g))
        return remote(
            parts.at[at], from_high.at[at], down_send.at[n], down_recv.at[n],
            {"obs": lax.rem(z + last, z_count) * 4 + q, "sp": s},
        )

    def gram_group(g):
        cols = slice(g * mine, (g + 1) * mine)
        made = jnp.dot(ktr[...], kbuf[:, cols], preferred_element_type=jnp.float32).astype(jnp.bfloat16)
        for t in range(z_count):
            begin, at, size = piece(t, g)
            parts[t, :, at : at + size] = made[t * strip : (t + 1) * strip, begin : begin + size]

    def pass_on(place, n):
        def rise():
            g = n - place
            if place > 0 and 0 <= g < groups:
                for t in range(last, place, -1):
                    up(t, g).wait_recv()
                    parts[t, :, cut(t, g)] = parts[t, :, cut(t, g)] + from_low[t, :, cut(t, g)]
                    up(t, g).start()

        def fall():
            g = n - (last - place)
            if place < last and 0 <= g < groups:
                for t in range(place):
                    down(t, g).wait_recv()
                    parts[t, :, cut(t, g)] = parts[t, :, cut(t, g)] + from_high[t, :, cut(t, g)]
                    down(t, g).start()

        for step in (rise, fall) if place <= last // 2 else (fall, rise):
            step()

    mine_at = ((z * 2 + x) * 2 + c) * 2 + s
    across_at, beside_at = ((z * 2 + 1 - x) * 2 + c) * 2 + s, ((z * 2 + x) * 2 + c) * 2 + 1 - s
    across, beside = device(z, 1 - x, c, s), device(z, x, c, 1 - s)
    half = strip // 2

    def side(place, g, k):
        rows = (slice(None), slice(None), pl.ds(0, half), pl.ds(half, half))[k]
        at = (mine_at, mine_at, across_at, beside_at)[k]
        src = done.at[:, cut(place, g)] if k < 2 else gathered.at[at, rows, cut(place, g)]
        return remote(
            src, gathered.at[at, rows, cut(place, g)], side_send.at[g * 4 + k], side_recv.at[g * 4 + k],
            (across, beside, beside, across)[k],
        )

    def keep(place, g):
        return pltpu.make_async_copy(
            done.at[:, cut(place, g)], gathered.at[mine_at, :, cut(place, g)], keep_sem.at[g]
        )

    def near(place, g, rising):
        to = lax.rem(z + (1 if rising else last), z_count)
        n = g * 2 + int(rising)
        return remote(
            done.at[:, cut(place, g)], gathered.at[mine_at, :, cut(place, g)],
            near_send.at[n], near_recv.at[n], device(to, x, c, s),
        )

    def close(place, g):
        total = parts[place, :, cut(place, g)].astype(jnp.float32)
        if place > 0:
            up(place, g).wait_recv()
            total = total + from_low[place, :, cut(place, g)].astype(jnp.float32)
        if place < last:
            down(place, g).wait_recv()
            total = total + from_high[place, :, cut(place, g)].astype(jnp.float32)
        if g == 0:
            row = lax.broadcasted_iota(jnp.int32, total.shape, 0)
            col = lax.broadcasted_iota(jnp.int32, total.shape, 1)
            total = jnp.where(row == col, 0.0, total)
        done[:, cut(place, g)] = total.astype(jnp.bfloat16)
        side(place, g, 0).start()
        side(place, g, 1).start()
        if 0 < place < last:
            near(place, g, True).start()
            near(place, g, False).start()
        keep(place, g).start()

    def progress(place, n):
        pass_on(place, n)
        g = n - max(place, last - place)
        if 0 <= g < groups:
            close(place, g)
        if 0 <= g - 1 < groups:
            for k in range(2):
                side(place, g - 1, k).wait_recv()
                side(place, g - 1, k + 2).start()
        if 0 <= g - 2 < groups:
            for k in range(2):
                side(place, g - 2, k + 2).wait_recv()

    z_copies, g_copies = [], []
    for n in range(groups + last + 2):
        if n < groups:

            @pl.loop(n * mine // tile, (n + 1) * mine // tile)
            def _(t):
                kernel_tile(t, n == 0)

            gram_group(n)

            @pl.when(z == 0)
            def _():
                for t in range(last, 0, -1):
                    up(t, n).start()

            @pl.when(z == last)
            def _():
                for t in range(last):
                    down(t, n).start()

        if n == 0:
            row_sums()
            for k in range(1, z_count):
                z_copies.append(remote(zsums.at[z], zsums.at[z], zs_send.at[k], zs_recv.at[k], z_others[k - 1]))
                z_copies[-1].start()
        if n == 1:
            for copy in z_copies:
                copy.wait_recv()
            total = zsums[0]
            for m in range(1, z_count):
                total = total + zsums[m]
            gsums[p] = total
            for m in range(1, group):
                g_copies.append(
                    remote(gsums.at[p], gsums.at[p], gs_send.at[m], gs_recv.at[m], group_others[m - 1])
                )
                g_copies[-1].start()
        for place in range(z_count):
            pl.when(z == place)(functools.partial(progress, place, n))

    def finish(place):
        for g in range(groups):
            for k in range(4):
                side(place, g, k).wait_send()
            keep(place, g).wait()
            if 0 < place < last:
                near(place, g, True).wait_send()
                near(place, g, False).wait_send()
            if 0 < place + 1 < last:
                near(place + 1, g, False).wait_recv()
            if 0 < place - 1 < last:
                near(place - 1, g, True).wait_recv()
            for t in range(z_count):
                if t > place:
                    up(t, g).wait_send()
                if t < place:
                    down(t, g).wait_send()

    for place in range(z_count):
        pl.when(z == place)(functools.partial(finish, place))

    for copy in g_copies:
        copy.wait()
    for copy in z_copies:
        copy.wait_send()
    sums_ref[...] = gsums[...]


def slab_gram(slab, sparse, z_count, sp_count, strip, span, tile, rows, collective_id):
    depth = slab.shape[2]
    window = sparse.shape[0]
    group = 4 * sp_count
    mine = strip * z_count
    lines = 2 * mine // LANES
    vmem = pl.BlockSpec(memory_space=pltpu.VMEM)
    part = (z_count, strip, span)
    groups = window // mine
    sems = [pltpu.SemaphoreType.DMA((z_count * groups,))] * 4 + [pltpu.SemaphoreType.DMA((4 * groups,))] * 2
    sems += [pltpu.SemaphoreType.DMA((z_count,))] * 2 + [pltpu.SemaphoreType.DMA((group,))] * 2
    sems += [pltpu.SemaphoreType.DMA((groups,))] + [pltpu.SemaphoreType.DMA((2 * groups,))] * 2
    sems += [pltpu.SemaphoreType.DMA((2,))]
    sems += [pltpu.VMEM(slab.shape, slab.dtype), pltpu.VMEM(sparse.shape, sparse.dtype)]
    return pl.pallas_call(
        functools.partial(slab_body, z_count, sp_count, strip, tile, math.sqrt(depth)),
        out_shape=[
            jax.ShapeDtypeStruct((group * z_count, strip, span), jnp.bfloat16),
            jax.ShapeDtypeStruct((group, lines, LANES), jnp.float32),
        ],
        in_specs=[pl.BlockSpec(memory_space=pl.ANY)] * 2,
        out_specs=[pl.BlockSpec(memory_space=pl.ANY), vmem],
        scratch_shapes=[
            pltpu.VMEM((4 * rows, window), jnp.bfloat16),
            pltpu.VMEM((mine, 4 * rows), jnp.bfloat16),
            pltpu.VMEM(part, jnp.bfloat16),
            pltpu.VMEM(part, jnp.bfloat16),
            pltpu.VMEM(part, jnp.bfloat16),
            pltpu.VMEM(part[1:], jnp.bfloat16),
            pltpu.VMEM((z_count, lines, LANES), jnp.float32),
            pltpu.VMEM((group, lines, LANES), jnp.float32),
        ] + sems,
        compiler_params=pltpu.CompilerParams(
            collective_id=collective_id, has_side_effects=True, vmem_limit_bytes=VMEM_BYTES
        ),
    )(slab, sparse)


def on_device(descriptors, candidates, sparse_index, targets, regularizer):
    obs_count = lax.axis_size("obs")
    sp_count = lax.axis_size("sp")
    obs_pos = lax.axis_index("obs")
    sp_pos = lax.axis_index("sp")
    width = sparse_index.shape[0]
    if sp_count == 2 and obs_count == 16 and width % (obs_count * sp_count * LANES) == 0:
        return by_strips(descriptors, candidates, sparse_index, targets, regularizer)
    tile = width // obs_count
    share = -(-((obs_count // 2 + 1) * tile) // (sp_count * LANES)) * LANES
    normalizer = 24.0 * descriptors.shape[0] * obs_count

    normed = unit_rows(descriptors)
    piece = candidates.shape[0] // sp_count
    own = lax.dynamic_slice_in_dim(candidates, sp_pos * piece, piece)
    table = spread(unit_rows(own), obs_count, sp_count, 2)
    sparse = table.at[sparse_index].get(mode="promise_in_bounds")

    gram, sums = gram_call(
        sp_pos[None].astype(jnp.int32), normed, sparse, targets, obs_count, tile, share, sp_count
    )
    sums = add_over_obs(sums, obs_count, 0)
    part = lax.psum_scatter(gram, "obs", scatter_dimension=0, tiled=True)

    projected = sums[0] / math.sqrt(normalizer)
    root = lax.rsqrt(sums[1] / normalizer + regularizer)
    col_start = obs_pos * tile
    rrow = lax.dynamic_slice_in_dim(root, col_start, tile)
    window_start = col_start + sp_pos * share
    rwin = lax.dynamic_slice_in_dim(jnp.concatenate([root, root]), window_start, share)
    offset = sp_pos * share + lax.iota(jnp.int32, share)
    on_diag = lax.iota(jnp.int32, tile)[:, None] == offset[None, :]
    scaled = jnp.where(
        on_diag, 0.0, part.astype(jnp.float32) * (rrow[:, None] / normalizer) * rwin[None, :]
    ).astype(jnp.bfloat16)
    packed = spread(scaled, obs_count, sp_count, 3)

    y = lax.dynamic_slice_in_dim(projected, col_start, tile)
    pos = jnp.stack([sp_pos, obs_pos]).astype(jnp.int32)
    inverse_tile, part_w = newton_call(
        pos, packed, root, rrow, y, obs_count, tile, share, sp_count
    )
    return inverse_tile, add_over_obs(part_w[0], obs_count, 1)


def solution(mesh):
    in_specs = (P("obs", None), P("obs", None), P(), P("obs"), P())
    out_specs = (P("sp", "obs"), P("sp"))
    return jax.shard_map(
        on_device, mesh=mesh, in_specs=in_specs, out_specs=out_specs, check_vma=False
    )
```
